32 devices in a mesh: dp: 4 (over x, core), chan: 8 (over z, y).
Axes of the slice: x: 2, y: 2, z: 4, core: 2. Of those that a mesh axis runs over, the one named last changes fastest.
Arguments:
- patches: bfloat16 [8192, 768], P(('dp', 'chan')), may hold values from -6 to 6
- valid_mask: int32 [8192], P('dp'), may hold values from 0 to 1, as said below
- target_mask: int32 [8192], P('dp'), may hold values 0 or 1
- keep_mask: int32 [32, 2, 2], P('dp'), may hold values 0 or 1
- embed_weight: float32 [768, 384], replicated, may hold values from -0.21875 to 0.21875
- embed_moment: float32 [768, 384], replicated, may hold values from -0.0029296875 to 0.0029296875
- head_weight: float32 [384, 768], replicated, may hold values from -0.3125 to 0.3125
- head_moment: float32 [384, 768], replicated, may hold values from -0.0029296875 to 0.0029296875
- vectors: float32 [26, 384], replicated
- vector_moment: float32 [26, 384], replicated, may hold values from -0.015625 to 0.015625
- vector_average: float32 [26, 384], replicated
- focal_input: float32 [2, 384, 2, 384], P(None, None, None, 'chan'), may hold values from -0.3125 to 0.3125
- focal_moment: float32 [2, 384, 2, 384], P(None, None, None, 'chan'), may hold values from -0.0029296875 to 0.0029296875
- focal_average: float32 [2, 384, 2, 384], P(None, None, None, 'chan'), may hold values from -0.3125 to 0.3125
- mixers: float32 [2, 2, 384, 384], P(None, None, None, 'chan'), may hold values from -0.3125 to 0.3125
- mixer_moment: float32 [2, 2, 384, 384], P(None, None, None, 'chan'), may hold values from -0.0029296875 to 0.0029296875
- mixer_average: float32 [2, 2, 384, 384], P(None, None, None, 'chan'), may hold values from -0.3125 to 0.3125
- mlp_weights: float32 [2, 2, 384, 1536], P(None, None, None, 'chan'), may hold values from -0.3125 to 0.3125
- mlp_moment: float32 [2, 2, 384, 1536], P(None, None, None, 'chan'), may hold values from -0.0029296875 to 0.0029296875
- mlp_average: float32 [2, 2, 384, 1536], P(None, None, None, 'chan'), may hold values from -0.3125 to 0.3125
- kernels: float32 [2, 83, 384], P(None, None, 'chan'), may hold values from -1.25 to 1.25
- kernel_moment: float32 [2, 83, 384], P(None, None, 'chan'), may hold values from -0.0029296875 to 0.0029296875
- kernel_average: float32 [2, 83, 384], P(None, None, 'chan'), may hold values from -1.25 to 1.25
Outputs:
- loss: float32 [], replicated
- new_embed: float32 [768, 384], replicated
- new_embed_moment: float32 [768, 384], replicated
- new_head: float32 [384, 768], replicated
- new_head_moment: float32 [384, 768], replicated
- new_vectors: float32 [26, 384], replicated
- new_vector_moment: float32 [26, 384], replicated
- new_vector_average: float32 [26, 384], replicated
- new_focal: float32 [2, 384, 2, 384], P(None, None, None, 'chan')
- new_focal_moment: float32 [2, 384, 2, 384], P(None, None, None, 'chan')
- new_focal_average: float32 [2, 384, 2, 384], P(None, None, None, 'chan')
- new_mixers: float32 [2, 2, 384, 384], P(None, None, None, 'chan')
- new_mixer_moment: float32 [2, 2, 384, 384], P(None, None, None, 'chan')
- new_mixer_average: float32 [2, 2, 384, 384], P(None, None, None, 'chan')
- new_mlp: float32 [2, 2, 384, 1536], P(None, None, None, 'chan')
- new_mlp_moment: float32 [2, 2, 384, 1536], P(None, None, None, 'chan')
- new_mlp_average: float32 [2, 2, 384, 1536], P(None, None, None, 'chan')
- new_kernels: float32 [2, 83, 384], P(None, None, 'chan')
- new_kernel_moment: float32 [2, 83, 384], P(None, None, 'chan')
- new_kernel_average: float32 [2, 83, 384], P(None, None, 'chan')
The draws below stay inside these ranges and needn't reach their ends.
Inputs may be any that keep to these rules, and one draw needn't show every extreme that they name: `valid_mask`: each image's valid patches form its top-left rectangle with 8 to 16 rows and columns; image 0 is whole.
All inputs are finite; a program needn't handle non-finite values. No bound on the sum of `target_mask` or of `keep_mask` on one device may be relied on, other than what follows from the above.
Results may differ from the reference program's by a relative error of at most 0.012.
Values may be sent and summed in bfloat16 or wider, within the bound.
No kernel may reach another device: no remote copies, remote signals or barrier semaphores. Data moves between devices by JAX's collectives and lax.ppermute only.
A program may use at most 320 MiB of HBM per device.

```python
import math
import jax
import jax.numpy as jnp
import numpy as np
from jax import lax

C = 384
HID = 1536
PATCH_IN = 768
GRID = 16
BLOCKS = 2
TAPS = 83
IMAGES = 32
TOKENS = 8192
VROWS = 26


def draw_valid_mask(key, part):
    image_count = TOKENS // (GRID * GRID)
    extent = jax.random.randint(key, (image_count, 2), GRID // 2, GRID + 1)
    extent = extent.at[0].set(GRID)
    positions = jnp.arange(GRID)
    inside_rows = positions[None, :, None] < extent[:, 0, None, None]
    inside_cols = positions[None, None, :] < extent[:, 1, None, None]
    return (inside_rows & inside_cols).astype(jnp.int32).reshape(TOKENS)


def vector_rows(key):
    row_count = 10 * BLOCKS + 6
    kinds = np.zeros(row_count, np.int32)
    for block_index in range(BLOCKS):
        kinds[10 * block_index:10 * block_index + 10] = [0, 1, 0, 1, 1, 1, 2, 2, 2, 2]
    kinds[10 * BLOCKS:] = [1, 0, 1, 0, 1, 3]
    kind_col = jnp.asarray(kinds)[:, None]
    gains = 1.0 + 0.2 * jax.random.uniform(jax.random.fold_in(key, 1), (row_count, C), jnp.float32, -1.0, 1.0)
    shifts = 0.3 * jax.random.normal(jax.random.fold_in(key, 2), (row_count, C), jnp.float32)
    gate_rows = jax.random.normal(jax.random.fold_in(key, 3), (row_count, C), jnp.float32) / math.sqrt(C)
    token_rows = jax.random.normal(jax.random.fold_in(key, 4), (row_count, C), jnp.float32)
    values = jnp.where(kind_col == 0, gains, shifts)
    values = jnp.where(kind_col == 2, gate_rows, values)
    return jnp.where(kind_col == 3, token_rows, values)


def draw_vectors(key, part):
    return vector_rows(jax.random.fold_in(key, 11))


def draw_vector_average(key, part):
    return vector_rows(jax.random.fold_in(key, 23))


def plant(drawn, stream_key, smallest, top_value):
    longest = drawn.shape.index(max(drawn.shape))
    spots = []
    for shift in (0, 1):
        where = [jax.random.randint(jax.random.fold_in(stream_key, axis), (), 0, length) for axis, length in enumerate(drawn.shape)]
        where[longest] = (where[longest] + shift) % drawn.shape[longest]
        spots.append(tuple(where))
    return drawn.at[spots[0]].set(smallest).at[spots[1]].set(top_value)


def levels(rng, dims, cuts, low, largest):
    gain, own = 1.0, jax.random.fold_in(rng, 6)
    for axis_at, blocks in cuts:
        steps = jnp.exp(jax.random.uniform(jax.random.fold_in(own, axis_at), (blocks,), jnp.float32, low / len(cuts), largest / len(cuts)))
        gain = gain * jnp.repeat(steps, dims[axis_at] // blocks).reshape([-1 if axis == axis_at else 1 for axis in range(len(dims))])
    return gain


def scatter_about(key, shape, spread, reach, shards=(), dtype=jnp.bfloat16):
    factor_of = levels(key, shape, shards, -0.22, 0.18) if shards else 1.0
    result = jax.random.normal(key, shape, jnp.float32) * spread * factor_of
    return jnp.minimum(jnp.maximum(result, -reach), reach).astype(dtype)


def setup_inputs(seed: int = 0) -> dict:
    key_of = jax.random.split(jax.random.key(seed), 24)
    return {
        "patches": scatter_about(key_of[0], (TOKENS, PATCH_IN), 1.0, 6.0, ((0, 32),)),
        "valid_mask": draw_valid_mask(jax.random.fold_in(key_of[23], 71), 0),
        "target_mask": plant((jax.random.randint(key_of[2], (TOKENS,), 0, 2) < 1).astype(jnp.int32), jax.random.fold_in(key_of[2], 1), 0, 1),
        "keep_mask": plant((jax.random.randint(key_of[3], (IMAGES, BLOCKS, 2), 0, 5) < 4).astype(jnp.int32), jax.random.fold_in(key_of[3], 1), 0, 1),
        "embed_weight": scatter_about(key_of[4], (PATCH_IN, C), PATCH_IN ** -0.5, 0.21875, (), jnp.float32),
        "embed_moment": scatter_about(key_of[5], (PATCH_IN, C), (TOKENS * 500) ** -0.5, 0.0029296875, (), jnp.float32),
        "head_weight": scatter_about(key_of[6], (C, PATCH_IN), C ** -0.5, 0.3125, (), jnp.float32),
        "head_moment": scatter_about(key_of[7], (C, PATCH_IN), (TOKENS * 500) ** -0.5, 0.0029296875, (), jnp.float32),
        "vectors": draw_vectors(jax.random.fold_in(key_of[23], 71), 0),
        "vector_moment": scatter_about(key_of[9], (VROWS, C), (TOKENS * 20) ** -0.5, 0.015625, (), jnp.float32),
        "vector_average": draw_vector_average(jax.random.fold_in(key_of[23], 71), 0),
        "focal_input": scatter_about(key_of[11], (BLOCKS, C, 2, C), C ** -0.5, 0.3125, ((3, 8),), jnp.float32),
        "focal_moment": scatter_about(key_of[12], (BLOCKS, C, 2, C), (TOKENS * 500) ** -0.5, 0.0029296875, ((3, 8),), jnp.float32),
        "focal_average": scatter_about(key_of[13], (BLOCKS, C, 2, C), C ** -0.5, 0.3125, ((3, 8),), jnp.float32),
        "mixers": scatter_about(key_of[14], (BLOCKS, 2, C, C), C ** -0.5, 0.3125, ((3, 8),), jnp.float32),
        "mixer_moment": scatter_about(key_of[15], (BLOCKS, 2, C, C), (TOKENS * 500) ** -0.5, 0.0029296875, ((3, 8),), jnp.float32),
        "mixer_average": scatter_about(key_of[16], (BLOCKS, 2, C, C), C ** -0.5, 0.3125, ((3, 8),), jnp.float32),
        "mlp_weights": scatter_about(key_of[17], (BLOCKS, 2, C, HID), C ** -0.5, 0.3125, ((3, 8),), jnp.float32),
        "mlp_moment": scatter_about(key_of[18], (BLOCKS, 2, C, HID), (TOKENS * 500) ** -0.5, 0.0029296875, ((3, 8),), jnp.float32),
        "mlp_average": scatter_about(key_of[19], (BLOCKS, 2, C, HID), C ** -0.5, 0.3125, ((3, 8),), jnp.float32),
        "kernels": scatter_about(key_of[20], (BLOCKS, TAPS, C), 25 ** -0.5, 1.25, ((2, 8),), jnp.float32),
        "kernel_moment": scatter_about(key_of[21], (BLOCKS, TAPS, C), (TOKENS * 500) ** -0.5, 0.0029296875, ((2, 8),), jnp.float32),
        "kernel_average": scatter_about(key_of[22], (BLOCKS, TAPS, C), 25 ** -0.5, 1.25, ((2, 8),), jnp.float32),
    }


@jax.custom_vjp
def low(v):
    return lax.optimization_barrier(v.astype(jnp.bfloat16)).astype(jnp.float32)

@jax.custom_vjp
def low_back(v):
    return v

def low_keep(v):
    return (low(v), None)

def low_pass(kept, grad):
    return (grad,)

def back_keep(v):
    return (v, None)

def back_low(kept, grad):
    return (low(grad),)
low.defvjp(low_keep, low_pass)
low_back.defvjp(back_keep, back_low)
EPS = 1e-05
MOMENTUM = 0.9
AVERAGE = 0.5
KEEP_RATE = 0.8
KERNEL_SIZES = (3, 5, 7)
KERNEL_STARTS = (0, 9, 34)

def dense(left, right):
    return jnp.dot(left, right, preferred_element_type=jnp.float32, precision=lax.Precision.HIGHEST)

def layer_norm(values, norm_gain, norm_shift):
    average = lax.optimization_barrier(jnp.mean(values, axis=-1, keepdims=True))
    centred = values - average
    variance = lax.optimization_barrier(jnp.mean(centred * centred, axis=-1, keepdims=True))
    return centred * lax.rsqrt(variance + EPS) * norm_gain + norm_shift

def exact_gelu(values):
    return jax.nn.gelu(values, approximate=False)

def depthwise(field, kernel_taps, kernel_width):
    margin = kernel_width // 2
    padded = jnp.pad(field, ((0, 0), (margin, margin), (margin, margin), (0, 0)))
    summed = jnp.zeros_like(field)
    for kernel_row in range(kernel_width):
        for kernel_col in range(kernel_width):
            window = padded[:, kernel_row:kernel_row + GRID, kernel_col:kernel_col + GRID, :]
            summed = summed + window * kernel_taps[kernel_row * kernel_width + kernel_col]
    return summed

def focal_levels(context, gates, kernel_block, validity):
    image_count = validity.shape[0] // (GRID * GRID)
    channels = context.shape[-1]
    current = context.reshape(image_count, GRID, GRID, channels)
    gate_grid = gates.reshape(image_count, GRID, GRID, 4)
    summed = jnp.zeros_like(current)
    for level_index in range(3):
        kernel_width = KERNEL_SIZES[level_index]
        first_tap = KERNEL_STARTS[level_index]
        kernel_taps = kernel_block[first_tap:first_tap + kernel_width * kernel_width]
        current = exact_gelu(depthwise(current, kernel_taps, kernel_width))
        summed = summed + current * gate_grid[..., level_index:level_index + 1]
    valid_grid = validity.reshape(image_count, GRID, GRID, 1)
    valid_total = lax.optimization_barrier(jnp.sum(valid_grid, axis=(1, 2), keepdims=True))
    pooled = exact_gelu(lax.optimization_barrier(jnp.sum(current * valid_grid, axis=(1, 2), keepdims=True)) / valid_total)
    summed = summed + pooled * gate_grid[..., 3:4]
    return summed.reshape(image_count * GRID * GRID, channels)

def forward_group(patch_rows, validity, masked, keep_rows, denominator, embed_weight, head_weight, vectors, focal_input, mixers, mlp_weights, kernels):
    outer = 10 * BLOCKS
    embed_full = low_back(dense(patch_rows, low(embed_weight))) + vectors[outer]
    state = layer_norm(embed_full, vectors[outer + 1], vectors[outer + 2])
    residual = state * (1.0 - masked) + vectors[outer + 5] * masked
    for block_index in range(BLOCKS):
        block_vectors = vectors[10 * block_index:10 * block_index + 10]
        first = low(layer_norm(residual, block_vectors[0], block_vectors[1]))
        focal_block = low(focal_input[block_index])
        query = low_back(dense(first, focal_block[:, 0, :]))
        context = low_back(dense(first, focal_block[:, 1, :]))
        gates = dense(first, low(block_vectors[6:10]).T)
        context_sum = low(focal_levels(context, gates, kernels[block_index], validity))
        modulator = low_back(dense(context_sum, low(mixers[block_index, 0])))
        product = low(query * modulator)
        branch = low_back(dense(product, low(mixers[block_index, 1]).T))
        residual = residual + keep_rows[:, block_index, 0:1] * (branch + block_vectors[4])
        second = low(layer_norm(residual, block_vectors[2], block_vectors[3]))
        hidden = low(exact_gelu(low_back(dense(second, low(mlp_weights[block_index, 0])))))
        branch = low_back(dense(hidden, low(mlp_weights[block_index, 1]).T))
        residual = residual + keep_rows[:, block_index, 1:2] * (branch + block_vectors[5])
    final = low(layer_norm(residual, vectors[outer + 3], vectors[outer + 4]))
    prediction = low_back(dense(final, low(head_weight)))
    error = prediction - patch_rows
    loss_weight = masked * validity[:, None]
    return jnp.sum(loss_weight * error * error) / denominator

def nesterov(weight, moment, gradient, rate):
    new_moment = MOMENTUM * moment + gradient
    new_weight = weight - rate * (gradient + MOMENTUM * new_moment)
    return (new_weight, new_moment)

def reference(patches, valid_mask, target_mask, keep_mask, embed_weight, embed_moment, head_weight, head_moment, vectors, vector_moment, vector_average, focal_input, focal_moment, focal_average, mixers, mixer_moment, mixer_average, mlp_weights, mlp_moment, mlp_average, kernels, kernel_moment, kernel_average):
    validity = valid_mask.astype(jnp.float32)
    masked = target_mask.astype(jnp.float32)
    denominator = jnp.sum(masked * validity) * PATCH_IN
    keep_rows = jnp.repeat(keep_mask.astype(jnp.float32) / KEEP_RATE, GRID * GRID, axis=0)
    group_images = math.gcd(IMAGES, 16)
    group_count = IMAGES // group_images
    group_rows = group_images * GRID * GRID
    items = (patches.astype(jnp.float32).reshape(group_count, group_rows, PATCH_IN), validity.reshape(group_count, group_rows), masked.reshape(group_count, group_rows, 1), keep_rows.reshape(group_count, group_rows, BLOCKS, 2))
    weights = (embed_weight, head_weight, vectors, focal_input, mixers, mlp_weights, kernels)

    def group_step(carry, item):
        patch_rows, valid_rows, masked_rows, keep_group = item

        def loss_of(*params):
            return forward_group(patch_rows, valid_rows, masked_rows, keep_group, denominator, *params)
        value, pullback = jax.vjp(loss_of, *weights)
        grads = pullback(jnp.ones((), jnp.float32))
        summed = tuple((old + new for old, new in zip(carry[1], grads)))
        return ((carry[0] + value, summed), None)
    start = (jnp.zeros((), jnp.float32), tuple((jnp.zeros_like(weight) for weight in weights)))
    (loss, grads), unused = lax.scan(group_step, start, items)
    rate = 0.2 * math.sqrt(TOKENS)
    new_embed, new_embed_moment = nesterov(embed_weight, embed_moment, grads[0], rate)
    new_head, new_head_moment = nesterov(head_weight, head_moment, grads[1], rate)
    results = []
    for weight, moment, average, gradient in ((vectors, vector_moment, vector_average, grads[2]), (focal_input, focal_moment, focal_average, grads[3]), (mixers, mixer_moment, mixer_average, grads[4]), (mlp_weights, mlp_moment, mlp_average, grads[5]), (kernels, kernel_moment, kernel_average, grads[6])):
        new_weight, new_moment = nesterov(weight, moment, gradient, rate)
        results.append((new_weight, new_moment, AVERAGE * average + (1.0 - AVERAGE) * new_weight))
    return (loss, new_embed, new_embed_moment, new_head, new_head_moment, results[0][0], results[0][1], results[0][2], results[1][0], results[1][1], results[1][2], results[2][0], results[2][1], results[2][2], results[3][0], results[3][1], results[3][2], results[4][0], results[4][1], results[4][2])
```

```python
import math

import jax
import jax.numpy as jnp
from jax import lax
from jax.sharding import PartitionSpec as P

PATCH_IN = 768
GRID = 16
BLOCKS = 2
IMAGE_ROWS = GRID * GRID

EPS = 1e-05
MOMENTUM = 0.9
AVERAGE = 0.5
KEEP_RATE = 0.8
KERNEL_SIZES = (3, 5, 7)
KERNEL_STARTS = (0, 9, 34)
ROOT_HALF = math.sqrt(0.5)
DENSITY = 1.0 / math.sqrt(2.0 * math.pi)


def matmul(left, right):
    return jnp.dot(left, right, preferred_element_type=jnp.float32)


def contract_rows(left, right):
    return lax.dot_general(
        left, right, (((0,), (0,)), ((), ())), preferred_element_type=jnp.float32
    )


def times_transposed(left, right):
    return lax.dot_general(
        left, right, (((1,), (1,)), ((), ())), preferred_element_type=jnp.float32
    )


def split_low(values):
    high_part = values.astype(jnp.bfloat16)
    rest_part = (values - high_part.astype(jnp.float32)).astype(jnp.bfloat16)
    return (high_part, rest_part)


def normalize(values):
    average = jnp.mean(values, axis=-1, keepdims=True)
    centred = values - average
    variance = jnp.mean(centred * centred, axis=-1, keepdims=True)
    scale = lax.rsqrt(variance + EPS)
    return (centred * scale, scale)


def norm_backward(grad, unit, scale, gain):
    d_unit = grad * gain
    mean_one = jnp.mean(d_unit, axis=-1, keepdims=True)
    mean_two = jnp.mean(d_unit * unit, axis=-1, keepdims=True)
    d_values = (d_unit - mean_one - unit * mean_two) * scale
    return (
        d_values,
        jnp.sum(grad * unit, axis=0, keepdims=True),
        jnp.sum(grad, axis=0, keepdims=True),
    )


def gelu_pair(values):
    cumulative = 0.5 + 0.5 * lax.erf(values * ROOT_HALF)
    density = DENSITY * jnp.exp(-0.5 * values * values)
    return (values * cumulative, cumulative + values * density)


def depthwise(field, kernel_taps, kernel_width):
    margin = kernel_width // 2
    padded = jnp.pad(field, ((0, 0), (margin, margin), (margin, margin), (0, 0)))
    summed = jnp.zeros_like(field)
    for kernel_row in range(kernel_width):
        for kernel_col in range(kernel_width):
            window = padded[:, kernel_row : kernel_row + GRID, kernel_col : kernel_col + GRID, :]
            summed = summed + window * kernel_taps[kernel_row * kernel_width + kernel_col]
    return summed


def depthwise_taps(field, grad, kernel_width):
    margin = kernel_width // 2
    padded = jnp.pad(field, ((0, 0), (margin, margin), (margin, margin), (0, 0)))
    rows = []
    for kernel_row in range(kernel_width):
        for kernel_col in range(kernel_width):
            window = padded[:, kernel_row : kernel_row + GRID, kernel_col : kernel_col + GRID, :]
            rows.append(jnp.sum(window * grad, axis=(0, 1, 2)))
    return jnp.stack(rows)


def level_taps(kernel_block, level_index):
    kernel_width = KERNEL_SIZES[level_index]
    first_tap = KERNEL_STARTS[level_index]
    return kernel_block[first_tap : first_tap + kernel_width * kernel_width]


def focal_forward(context, gates, kernel_block, validity):
    images = validity.shape[0] // IMAGE_ROWS
    grid = lambda a: a.reshape(images, GRID, GRID, a.shape[-1])
    current = grid(context)
    gate_grid = grid(gates)
    valid_grid = grid(validity)
    summed = jnp.zeros_like(current)
    fields = [current]
    slopes = []
    for level_index in range(3):
        taps = level_taps(kernel_block, level_index)
        current, slope = gelu_pair(depthwise(current, taps, KERNEL_SIZES[level_index]))
        summed = summed + current * gate_grid[..., level_index : level_index + 1]
        fields.append(current)
        slopes.append(slope)
    valid_total = jnp.sum(valid_grid, axis=(1, 2), keepdims=True)
    pooled, pooled_slope = gelu_pair(
        jnp.sum(current * valid_grid, axis=(1, 2), keepdims=True) / valid_total
    )
    summed = summed + pooled * gate_grid[..., 3:4]
    return (
        summed.reshape(context.shape).astype(jnp.bfloat16),
        (fields, slopes, pooled, pooled_slope / valid_total),
    )


def focal_backward(d_summed, gates, kernel_block, validity, saved):
    fields, slopes, pooled, pooled_slope = saved
    images = validity.shape[0] // IMAGE_ROWS
    grid = lambda a: a.reshape(images, GRID, GRID, a.shape[-1])
    d_sum = grid(d_summed)
    gate_grid = grid(gates)
    valid_grid = grid(validity)
    d_pooled = jnp.sum(d_sum * gate_grid[..., 3:4], axis=(1, 2), keepdims=True)
    d_field = d_pooled * pooled_slope * valid_grid
    gate_cols = [None, None, None, jnp.sum(d_sum * pooled, axis=-1, keepdims=True)]
    tap_rows = [None, None, None]
    for level_index in reversed(range(3)):
        width = KERNEL_SIZES[level_index]
        gate_cols[level_index] = jnp.sum(d_sum * fields[level_index + 1], axis=-1, keepdims=True)
        d_pre = (d_field + d_sum * gate_grid[..., level_index : level_index + 1]) * slopes[
            level_index
        ]
        tap_rows[level_index] = depthwise_taps(fields[level_index], d_pre, width)
        d_field = depthwise(d_pre, level_taps(kernel_block, level_index)[::-1], width)
    d_gates = jnp.concatenate(gate_cols, axis=-1).reshape(gates.shape)
    return (d_field.reshape(d_summed.shape), d_gates, jnp.concatenate(tap_rows, axis=0))


class Shares:
    def __init__(self, local_rows, chan_size):
        self.count = max(1, IMAGE_ROWS // local_rows)
        self.groups = [
            list(range(first, first + self.count)) for first in range(0, chan_size, self.count)
        ]

    def to_images(self, values):
        if self.count == 1:
            return values
        return lax.all_to_all(
            values, "chan", 1, 0, axis_index_groups=self.groups, tiled=True
        )

    def to_rows(self, values):
        if self.count == 1:
            return values
        return lax.all_to_all(
            values, "chan", 0, 1, axis_index_groups=self.groups, tiled=True
        )

    def all_rows(self, values):
        if self.count == 1:
            return values
        return lax.all_gather(
            values, "chan", axis=0, axis_index_groups=self.groups, tiled=True
        )

    def sum_rows(self, values):
        if self.count == 1:
            return values
        return lax.psum_scatter(
            values, "chan", scatter_dimension=0, axis_index_groups=self.groups, tiled=True
        )

    def channels(self, values):
        if self.count == 1:
            return values
        size = values.shape[1] // self.count
        place = lax.axis_index("chan") % self.count
        return lax.dynamic_slice_in_dim(values, place * size, size, 1)

    def spread(self, values):
        if self.count == 1:
            return values
        size = values.shape[1]
        place = lax.axis_index("chan") % self.count
        whole = jnp.zeros((values.shape[0], size * self.count), values.dtype)
        return lax.dynamic_update_slice_in_dim(whole, values, place * size, 1)


def pack(parts, block_index):
    focal, mixer, mlp = parts
    return (
        jnp.concatenate(
            [
                focal[block_index, :, 0].T,
                focal[block_index, :, 1].T,
                mixer[block_index, 0].T,
                mixer[block_index, 1].T,
            ],
            axis=0,
        ),
        jnp.concatenate([mlp[block_index, 0].T, mlp[block_index, 1].T], axis=0),
    )


def gather_weights(packed, counts):
    size = lax.axis_size("chan")
    gathered = lax.all_gather(packed, "chan", axis=0, tiled=False)
    pieces = []
    start = 0
    for count in counts:
        pieces.append(
            gathered[:, start : start + count].reshape(size * count, packed.shape[-1])
        )
        start += count
    return pieces


def scatter_grads(grads):
    size = lax.axis_size("chan")
    stacked = jnp.concatenate(
        [grad.astype(jnp.bfloat16).reshape(size, -1, grad.shape[-1]) for grad in grads], axis=1
    )
    mine = lax.psum_scatter(stacked, "chan", scatter_dimension=0, tiled=False)
    return lax.psum(mine, "dp").astype(jnp.float32)


def nesterov(weight, moment, gradient, rate):
    new_moment = MOMENTUM * moment + gradient
    new_weight = weight - rate * (gradient + MOMENTUM * new_moment)
    return (new_weight, new_moment)


def block_forward(residual, vecs, focal_pieces, mlp_pieces, kernel_block, keep, validity, shares):
    query_w, key_w, mix_w, proj_w = focal_pieces
    up_w, down_w = mlp_pieces
    unit_one, scale_one = normalize(residual)
    first = (unit_one * vecs[0] + vecs[1]).astype(jnp.bfloat16)
    query = times_transposed(first, query_w)
    context = times_transposed(first, key_w)
    gates = times_transposed(first, vecs[6:10].astype(jnp.bfloat16))
    gates = shares.all_rows(gates)
    context_low, levels = focal_forward(
        shares.to_images(context), gates, shares.channels(kernel_block), validity
    )
    context_low = shares.to_rows(context_low)
    modulator = times_transposed(context_low, mix_w)
    product = (query * modulator).astype(jnp.bfloat16)
    middle = residual + keep[:, 0:1] * (matmul(product, proj_w) + vecs[4])
    unit_two, scale_two = normalize(middle)
    second = (unit_two * vecs[2] + vecs[3]).astype(jnp.bfloat16)
    hidden, slope = gelu_pair(times_transposed(second, up_w))
    hidden = hidden.astype(jnp.bfloat16)
    output = middle + keep[:, 1:2] * (matmul(hidden, down_w) + vecs[5])
    saved = (
        (unit_one, scale_one, first, query, gates),
        (context_low, levels, modulator, product),
        (unit_two, scale_two, second, hidden, slope),
    )
    return (output, saved)


def mlp_backward(d_residual, saved, vecs, mlp_pieces, keep):
    unit_two, scale_two, second, hidden, slope = saved
    up_w, down_w = mlp_pieces
    d_down = d_residual * keep[:, 1:2]
    d_low = d_down.astype(jnp.bfloat16)
    grad_down = contract_rows(hidden, d_low)
    d_pre = (times_transposed(d_low, down_w) * slope).astype(jnp.bfloat16)
    grad_up = contract_rows(d_pre, second)
    d_middle, grad_gain, grad_shift = norm_backward(
        matmul(d_pre, up_w), unit_two, scale_two, vecs[2]
    )
    bias = jnp.sum(d_down, axis=0, keepdims=True)
    return (d_middle + d_residual, (grad_up, grad_down), (grad_gain, grad_shift, bias))


def focal_block_backward(
    d_middle, saved_one, saved_two, vecs, focal_pieces, kernel_block, keep, validity, shares
):
    unit_one, scale_one, first, query, gates = saved_one
    context_low, levels, modulator, product = saved_two
    query_w, key_w, mix_w, proj_w = focal_pieces
    d_proj = d_middle * keep[:, 0:1]
    d_low = d_proj.astype(jnp.bfloat16)
    grad_proj = contract_rows(product, d_low)
    d_product = times_transposed(d_low, proj_w)
    d_query = (d_product * modulator).astype(jnp.bfloat16)
    d_modulator = (d_product * query).astype(jnp.bfloat16)
    grad_mix = contract_rows(d_modulator, context_low)
    d_context_sum = shares.to_images(matmul(d_modulator, mix_w))
    d_context, d_gates, grad_kernel = focal_backward(
        d_context_sum, gates, shares.channels(kernel_block), validity, levels
    )
    d_context = shares.to_rows(d_context.astype(jnp.bfloat16))
    d_gates = shares.sum_rows(d_gates)
    grad_kernel = shares.spread(grad_kernel)
    gate_high, gate_rest = split_low(d_gates)
    gate_low = vecs[6:10].astype(jnp.bfloat16)
    grad_gate = contract_rows(gate_high, first) + contract_rows(gate_rest, first)
    grad_query = contract_rows(d_query, first)
    grad_key = contract_rows(d_context, first)
    d_first = (
        matmul(d_query, query_w)
        + matmul(d_context, key_w)
        + matmul(gate_high, gate_low)
        + matmul(gate_rest, gate_low)
    )
    d_input, grad_gain, grad_shift = norm_backward(d_first, unit_one, scale_one, vecs[0])
    bias = jnp.sum(d_proj, axis=0, keepdims=True)
    return (
        d_input + d_middle,
        (grad_query, grad_key, grad_mix, grad_proj),
        grad_kernel,
        (grad_gain, grad_shift, bias, grad_gate),
    )


def shards(
    patches,
    valid_mask,
    target_mask,
    keep_mask,
    embed_weight,
    embed_moment,
    head_weight,
    head_moment,
    vectors,
    vector_moment,
    vector_average,
    focal_input,
    focal_moment,
    focal_average,
    mixers,
    mixer_moment,
    mixer_average,
    mlp_weights,
    mlp_moment,
    mlp_average,
    kernels,
    kernel_moment,
    kernel_average,
):
    local_rows = patches.shape[0]
    group_rows = valid_mask.shape[0]
    chan_size = lax.axis_size("chan")
    own = focal_input.shape[-1]
    own_hidden = mlp_weights.shape[-1]
    shares = Shares(local_rows, chan_size)
    outer = 10 * BLOCKS
    first_row = lax.axis_index("chan") * local_rows
    image_row = first_row // IMAGE_ROWS * IMAGE_ROWS
    image_rows = max(local_rows, IMAGE_ROWS)
    validity = valid_mask.astype(jnp.float32)
    valid_images = lax.dynamic_slice_in_dim(validity, image_row, image_rows)[:, None]
    valid_local = lax.dynamic_slice_in_dim(validity, first_row, local_rows)[:, None]
    masked_local = lax.dynamic_slice_in_dim(target_mask, first_row, local_rows).astype(jnp.float32)[
        :, None
    ]
    loss_weight = masked_local * valid_local
    group_count = jnp.sum(validity * target_mask.astype(jnp.float32))
    counted = lax.psum(group_count, "dp")
    denominator = counted * PATCH_IN
    keep_rows = jnp.repeat(keep_mask.astype(jnp.float32) / KEEP_RATE, IMAGE_ROWS, axis=0)
    keep_local = lax.dynamic_slice_in_dim(keep_rows, first_row, local_rows)

    low = tuple(part.astype(jnp.bfloat16) for part in (focal_input, mixers, mlp_weights))
    focal_pieces = []
    mlp_pieces = []
    for block_index in range(BLOCKS):
        focal_rows, mlp_rows = pack(low, block_index)
        focal_pieces.append(gather_weights(focal_rows, [own] * 4))
        mlp_pieces.append(gather_weights(mlp_rows, [own_hidden] * 2))
    kernels_full = lax.all_gather(kernels, "chan", axis=2, tiled=True)

    embed_low = embed_weight.astype(jnp.bfloat16)
    embed_full = matmul(patches, embed_low) + vectors[outer]
    embed_unit, embed_scale = normalize(embed_full)
    start_state = embed_unit * vectors[outer + 1] + vectors[outer + 2]
    residual = start_state * (1.0 - masked_local) + vectors[outer + 5] * masked_local
    saved_blocks = []
    for block_index in range(BLOCKS):
        residual, saved = block_forward(
            residual,
            vectors[10 * block_index : 10 * block_index + 10],
            focal_pieces[block_index],
            mlp_pieces[block_index],
            kernels_full[block_index],
            keep_local[:, block_index],
            valid_images,
            shares,
        )
        saved_blocks.append(saved)
    final_unit, final_scale = normalize(residual)
    final_low = (final_unit * vectors[outer + 3] + vectors[outer + 4]).astype(jnp.bfloat16)
    head_low = head_weight.astype(jnp.bfloat16)
    error = matmul(final_low, head_low) - patches.astype(jnp.float32)
    loss_part = jnp.sum(loss_weight * error * error) / denominator
    d_prediction = (2.0 * loss_weight * error / denominator).astype(jnp.bfloat16)
    grad_head = contract_rows(final_low, d_prediction)
    d_final = times_transposed(d_prediction, head_low)
    d_residual, grad_final_gain, grad_final_shift = norm_backward(
        d_final, final_unit, final_scale, vectors[outer + 3]
    )
    vector_parts = [None] * BLOCKS
    focal_grads = [None] * BLOCKS
    mlp_grads = [None] * BLOCKS
    kernel_parts = [None] * BLOCKS
    for block_index in reversed(range(BLOCKS)):
        vecs = vectors[10 * block_index : 10 * block_index + 10]
        keep = keep_local[:, block_index]
        saved_one, saved_two, saved_three = saved_blocks[block_index]
        d_middle, grads, (gain_two, shift_two, mlp_bias) = mlp_backward(
            d_residual, saved_three, vecs, mlp_pieces[block_index], keep
        )
        mlp_grads[block_index] = scatter_grads(grads)
        d_residual, grads, kernel_parts[block_index], (gain_one, shift_one, proj_bias, gate) = (
            focal_block_backward(
                d_middle,
                saved_one,
                saved_two,
                vecs,
                focal_pieces[block_index],
                kernels_full[block_index],
                keep,
                valid_images,
                shares,
            )
        )
        focal_grads[block_index] = scatter_grads(grads)
        vector_parts[block_index] = jnp.concatenate(
            [gain_one, shift_one, gain_two, shift_two, proj_bias, mlp_bias, gate], axis=0
        )
    d_start = d_residual * (1.0 - masked_local)
    grad_token = jnp.sum(d_residual * masked_local, axis=0, keepdims=True)
    d_embed, grad_embed_gain, grad_embed_shift = norm_backward(
        d_start, embed_unit, embed_scale, vectors[outer + 1]
    )
    grad_embed = contract_rows(patches, d_embed.astype(jnp.bfloat16))
    grad_vectors = jnp.concatenate(
        vector_parts
        + [
            jnp.sum(d_embed, axis=0, keepdims=True),
            grad_embed_gain,
            grad_embed_shift,
            grad_final_gain,
            grad_final_shift,
            grad_token,
        ],
        axis=0,
    )
    both = ("dp", "chan")
    grad_embed = lax.psum(grad_embed.astype(jnp.bfloat16), both).astype(jnp.float32)
    grad_head = lax.psum(grad_head.astype(jnp.bfloat16), both).astype(jnp.float32)
    grad_vectors, grad_kernel, loss = lax.psum(
        (grad_vectors, jnp.stack(kernel_parts), loss_part), both
    )
    grad_kernel = lax.dynamic_slice_in_dim(
        grad_kernel, lax.axis_index("chan") * own, own, 2
    )
    focal_stack = jnp.stack(focal_grads).reshape(BLOCKS, 4, own, -1)
    grad_focal = jnp.transpose(focal_stack[:, :2], (0, 3, 1, 2))
    grad_mixer = jnp.transpose(focal_stack[:, 2:], (0, 1, 3, 2))
    grad_mlp = jnp.transpose(
        jnp.stack(mlp_grads).reshape(BLOCKS, 2, own_hidden, -1), (0, 1, 3, 2)
    )
    rate = 0.2 * math.sqrt(group_rows * lax.axis_size("dp"))
    new_embed, new_embed_moment = nesterov(embed_weight, embed_moment, grad_embed, rate)
    new_head, new_head_moment = nesterov(head_weight, head_moment, grad_head, rate)
    results = []
    for weight, moment, average, gradient in (
        (vectors, vector_moment, vector_average, grad_vectors),
        (focal_input, focal_moment, focal_average, grad_focal),
        (mixers, mixer_moment, mixer_average, grad_mixer),
        (mlp_weights, mlp_moment, mlp_average, grad_mlp),
        (kernels, kernel_moment, kernel_average, grad_kernel),
    ):
        new_weight, new_moment = nesterov(weight, moment, gradient, rate)
        results.extend(
            (new_weight, new_moment, AVERAGE * average + (1.0 - AVERAGE) * new_weight)
        )
    return (loss, new_embed, new_embed_moment, new_head, new_head_moment, *results)


def solution(mesh):
    split = P(None, None, None, "chan")
    taps = P(None, None, "chan")
    return jax.shard_map(
        shards,
        mesh=mesh,
        in_specs=(P(("dp", "chan"), None), P("dp"), P("dp"), P("dp", None, None))
        + (P(),) * 7
        + (split,) * 9
        + (taps,) * 3,
        out_specs=(P(),) * 8 + (split,) * 9 + (taps,) * 3,
        check_vma=False,
    )
```

```python
import functools
import math

import jax
import jax.numpy as jnp
from jax import lax
from jax.experimental import pallas as pl
from jax.experimental.pallas import tpu as pltpu
from jax.sharding import PartitionSpec as P

PATCH_IN = 768
GRID = 16
BLOCKS = 2
IMAGE_ROWS = GRID * GRID
LANES = 128

EPS = 1e-05
MOMENTUM = 0.9
AVERAGE = 0.5
KEEP_RATE = 0.8
KERNEL_SIZES = (3, 5, 7)
KERNEL_STARTS = (0, 9, 34)
ROOT_HALF = math.sqrt(0.5)
DENSITY = 1.0 / math.sqrt(2.0 * math.pi)
VMEM_LIMIT = 50 << 20
F32 = jnp.float32
BF16 = jnp.bfloat16


def matmul(left, right):
    return jnp.dot(left, right, preferred_element_type=F32)


def contract_rows(left, right):
    return lax.dot_general(left, right, (((0,), (0,)), ((), ())), preferred_element_type=F32)


def times_transposed(left, right):
    return lax.dot_general(left, right, (((1,), (1,)), ((), ())), preferred_element_type=F32)


def normalize(values):
    average = jnp.mean(values, axis=-1, keepdims=True)
    centred = values - average
    variance = jnp.mean(centred * centred, axis=-1, keepdims=True)
    scale = lax.rsqrt(variance + EPS)
    return (centred * scale, scale)


def norm_backward(grad, unit, scale, gain):
    d_unit = grad * gain
    mean_one = jnp.mean(d_unit, axis=-1, keepdims=True)
    mean_two = jnp.mean(d_unit * unit, axis=-1, keepdims=True)
    return (d_unit - mean_one - unit * mean_two) * scale


def column_sum(values):
    return jnp.sum(values, axis=0, keepdims=True)


def gelu_pair(values):
    cumulative = 0.5 + 0.5 * lax.erf(values * ROOT_HALF)
    density = DENSITY * jnp.exp(-0.5 * values * values)
    return (values * cumulative, cumulative + values * density)


def shape_of(shape, dtype=F32):
    return jax.ShapeDtypeStruct(shape, dtype)


def whole_spec():
    return pl.BlockSpec(memory_space=pltpu.VMEM)


def far_spec():
    return pl.BlockSpec(memory_space=pl.ANY)


def scalar_spec():
    return pl.BlockSpec(memory_space=pltpu.SMEM)


def run_kernel(body, name, in_specs, outs, scratch, *args):
    return pl.pallas_call(
        body,
        name=name,
        in_specs=in_specs,
        out_specs=[whole_spec() for _ in outs],
        out_shape=outs,
        scratch_shapes=scratch,
        compiler_params=pltpu.CompilerParams(vmem_limit_bytes=VMEM_LIMIT),
    )(*args)


class Links:
    def __init__(self):
        chan = lax.axis_size("chan")
        self.ny = 1 << ((chan.bit_length() - 1) // 2)
        self.nz = chan // self.ny
        self.nc = 2
        self.nx = lax.axis_size("dp") // self.nc
        place = lax.axis_index("chan")
        self.chan = chan
        self.place = place
        self.z = place // self.ny
        self.y = place % self.ny
        self.core = lax.axis_index("dp") % self.nc
        slots = [
            (self.z - d) % self.nz * self.ny + (self.y - e) % self.ny
            for e in range(self.ny)
            for d in range(self.nz)
        ]
        self.where = jnp.stack([self.core] + slots).astype(jnp.int32)

    def shift_z(self, values, step):
        pairs = [
            (z * self.ny + y, (z + step) % self.nz * self.ny + y)
            for z in range(self.nz)
            for y in range(self.ny)
        ]
        return lax.ppermute(values, "chan", pairs)

    def shift_y(self, values, step):
        pairs = [
            (z * self.ny + y, z * self.ny + (y + step) % self.ny)
            for z in range(self.nz)
            for y in range(self.ny)
        ]
        return lax.ppermute(values, "chan", pairs)

    def shift_x(self, values, step):
        pairs = [
            (x * self.nc + c, (x + step) % self.nx * self.nc + c)
            for x in range(self.nx)
            for c in range(self.nc)
        ]
        return lax.ppermute(values, "dp", pairs)

    def swap_core(self, values):
        pairs = [(d, d ^ 1) for d in range(self.nx * self.nc)]
        return lax.ppermute(values, "dp", pairs)

    def spread_z(self, own):
        return [own] + [self.shift_z(own, d) for d in range(1, self.nz)]

    def spread_y(self, parts):
        stack = jnp.stack(parts)
        return [stack] + [self.shift_y(stack, e) for e in range(1, self.ny)]

    def own_half(self, halves):
        return lax.dynamic_index_in_dim(halves, self.core, 0, keepdims=False)

    def cross_x(self, values):
        total = values
        step = 1
        while step < self.nx:
            pairs = [
                (x * self.nc + c, (x ^ step) * self.nc + c)
                for x in range(self.nx)
                for c in range(self.nc)
            ]
            low = total.astype(BF16) if values.dtype == BF16 else total
            total = low.astype(F32) + lax.ppermute(low, "dp", pairs).astype(F32)
            step *= 2
        return total.astype(F32)

    def pick(self, values, axis, index):
        return lax.dynamic_index_in_dim(values, index, axis, keepdims=False)

    def add_core(self, kept, received):
        chan, rows, width = kept.shape
        total = (kept.astype(F32) + received.astype(F32)).astype(BF16)
        total = total.reshape(self.nz, self.ny, rows, width)
        return [self.pick(total, 1, (self.y + e) % self.ny) for e in range(self.ny)]

    def send_y(self, parts):
        return [parts[0]] + [self.shift_y(parts[e], e) for e in range(1, self.ny)]

    def add_y(self, parts):
        total = parts[0].astype(F32)
        for part in parts[1:]:
            total = total + part.astype(F32)
        return total.astype(BF16)

    def send_z(self, total):
        own = self.pick(total, 0, self.z)
        return [own] + [
            self.shift_z(self.pick(total, 0, (self.z + d) % self.nz), d)
            for d in range(1, self.nz)
        ]

    def add_z(self, parts):
        return self.add_y(parts)

    def both_halves(self, summed):
        other = self.swap_core(summed)
        first = self.core == 0
        return (jnp.where(first, summed, other), jnp.where(first, other, summed))


def after(value, *others):
    return lax.optimization_barrier((value, others))[0]


def piece_copies(where, near, far, half, first, count, target, sems):
    picks = []
    slot = 0
    for near_part, far_part in zip(near, far):
        for d in range(near_part.shape[0]):
            start = pl.multiple_of(where[1 + slot] * count, 8)
            room = target.at[pl.ds(start, count), :]
            source = pl.ds(first, count)
            picks.append(
                (
                    pltpu.make_async_copy(near_part.at[d, source, :], room, sems.at[slot]),
                    pltpu.make_async_copy(far_part.at[d, source, :], room, sems.at[slot]),
                )
            )
            slot += 1
    mine = where[0] == half

    def start():
        @pl.when(mine)
        def _():
            for near_copy, _far_copy in picks:
                near_copy.start()

        @pl.when(jnp.logical_not(mine))
        def _():
            for _near_copy, far_copy in picks:
                far_copy.start()

    def wait():
        for near_copy, _far_copy in picks:
            near_copy.wait()

    return (start, wait)


class Pieces:
    def __init__(self, links, near, far, matrices):
        self.where = links.where
        self.near = near
        self.far = far
        self.matrices = matrices
        self.slots = links.chan
        self.width = near[0].shape[-1]

    def args(self):
        return [self.where, *self.near, *self.far]

    def specs(self):
        return [scalar_spec()] + [far_spec() for _ in self.near + self.far]

    def scratch(self, names):
        shapes = []
        for name in names:
            count = self.matrices[name][2]
            shapes.append(pltpu.VMEM((count * self.slots, self.width), BF16))
            shapes.append(pltpu.SemaphoreType.DMA((self.slots,)))
        return shapes

    def loaders(self, names, refs, scratch):
        where, parts = refs[0], refs[1:]
        near, far = parts[: len(self.near)], parts[len(self.near) :]
        loads = []
        for at, name in enumerate(names):
            half, first, count = self.matrices[name]
            target, sems = scratch[2 * at], scratch[2 * at + 1]
            loads.append(
                (*piece_copies(where, near, far, half, first, count, target, sems), target)
            )
        return loads

    def size(self):
        return 1 + len(self.near) + len(self.far)


def low_gates(vecs):
    return vecs[6:10].astype(BF16)


def focal_inputs(x, vecs, pieces):
    rows, width = x.shape
    names = ("query", "key")
    size = pieces.size()

    def body(*refs):
        loads = pieces.loaders(names, refs[:size], refs[size + 2 + 6 :])
        x_ref, vec_ref = refs[size : size + 2]
        unit_ref, scale_ref, first_ref, query_ref, context_ref, gate_ref = refs[
            size + 2 : size + 8
        ]
        for start, _wait, _target in loads:
            start()
        vec = vec_ref[...]
        unit, scale = normalize(x_ref[...])
        unit_ref[...] = unit
        scale_ref[...] = scale
        first = (unit * vec[0:1] + vec[1:2]).astype(BF16)
        first_ref[...] = first
        gate_low = low_gates(vec)
        for level in range(4):
            spread = jnp.broadcast_to(gate_low[level : level + 1], (LANES, width))
            gate_ref[:, level * LANES : (level + 1) * LANES] = times_transposed(first, spread)
        loads[1][1]()
        context_ref[...] = times_transposed(first, loads[1][2][...])
        loads[0][1]()
        query_ref[...] = times_transposed(first, loads[0][2][...])

    return run_kernel(
        body,
        "focal_inputs",
        pieces.specs() + [whole_spec()] * 2,
        [
            shape_of((rows, width)),
            shape_of((rows, 1)),
            shape_of((rows, width), BF16),
            shape_of((rows, width)),
            shape_of((rows, width)),
            shape_of((rows, 4 * LANES)),
        ],
        pieces.scratch(names),
        *pieces.args(),
        x,
        vecs,
    )


def correlate(padded, taps, level, flip):
    width = KERNEL_SIZES[level]
    first = KERNEL_STARTS[level]
    margin = width // 2
    lanes = padded.shape[-1]
    sums = [None] * GRID
    for dx in range(width):
        weights = []
        for dy in range(width):
            tap = dy * width + dx
            if flip:
                tap = width * width - 1 - tap
            weights.append(jnp.broadcast_to(taps[first + tap : first + tap + 1, :], (GRID, lanes)))
        for row in range(GRID):
            window = padded[row, 8 - margin + dx : 8 - margin + dx + GRID, :]
            for dy in range(width):
                out = row - dy + margin
                if 0 <= out < GRID:
                    term = window * weights[dy]
                    sums[out] = term if sums[out] is None else sums[out] + term
    return sums


def correlate_taps(padded, grads, d_taps, level):
    width = KERNEL_SIZES[level]
    first = KERNEL_STARTS[level]
    margin = width // 2
    for dx in range(width):
        sums = [None] * width
        for row in range(GRID):
            window = padded[row, 8 - margin + dx : 8 - margin + dx + GRID, :]
            for dy in range(width):
                out = row - dy + margin
                if 0 <= out < GRID:
                    term = window * grads[out]
                    sums[dy] = term if sums[dy] is None else sums[dy] + term
        for dy in range(width):
            tap = first + dy * width + dx
            d_taps[tap : tap + 1, :] = column_sum(sums[dy])


def clear_margins(padded):
    lanes = padded.shape[-1]
    for row in range(GRID):
        padded[row, 0:8, :] = jnp.zeros((8, lanes), F32)
        padded[row, 8 + GRID : 16 + GRID, :] = jnp.zeros((8, lanes), F32)


def fill_padded(padded, rows):
    for row in range(GRID):
        padded[row, 8 : 8 + GRID, :] = rows[row]


def row_part(ref, row, lanes=None):
    if lanes is None:
        return ref[row * GRID : (row + 1) * GRID, :]
    return ref[row * GRID : (row + 1) * GRID, lanes]


def gate_part(gate_ref, row, level, lanes):
    part = gate_ref[row * GRID : (row + 1) * GRID, level * LANES : (level + 1) * LANES]
    return part if lanes == LANES else part[:, 0:1]


def lane_width(channels):
    return LANES if channels % LANES == 0 else channels


def focal_forward(context, gates, taps, validity):
    rows, channels = context.shape
    lanes = lane_width(channels)
    images = rows // IMAGE_ROWS

    def body(
        context_ref, gate_ref, tap_ref, valid_ref, low_ref, k1, k2, k3, s1, s2, s3, pool_ref, padded
    ):
        clear_margins(padded)
        fill_padded(padded, [row_part(context_ref, row) for row in range(GRID)])
        fields = (k1, k2, k3)
        slopes = (s1, s2, s3)
        for level in range(3):
            sums = correlate(padded, tap_ref, level, False)
            for row in range(GRID):
                value, slope = gelu_pair(sums[row])
                fields[level][row * GRID : (row + 1) * GRID, :] = value
                slopes[level][row * GRID : (row + 1) * GRID, :] = slope
                if level < 2:
                    padded[row, 8 : 8 + GRID, :] = value
        valid = valid_ref[...]
        total = jnp.sum(valid, axis=0, keepdims=True)
        mean = column_sum(k3[...] * valid) / total
        pooled, pooled_slope = gelu_pair(mean)
        pool_ref[0:1, :] = pooled
        pool_ref[1:2, :] = pooled_slope / total
        pool_ref[2:8, :] = jnp.zeros((6, lanes), F32)
        for row in range(GRID):
            summed = pooled * gate_part(gate_ref, row, 3, lanes)
            for level in range(3):
                summed = summed + row_part(fields[level], row) * gate_part(
                    gate_ref, row, level, lanes
                )
            low_ref[row * GRID : (row + 1) * GRID, :] = summed.astype(BF16)

    block = pl.BlockSpec((IMAGE_ROWS, lanes), lambda i, j: (i, j))
    pool_block = pl.BlockSpec((8, lanes), lambda i, j: (i, j))
    return pl.pallas_call(
        body,
        name="focal_forward",
        grid=(images, channels // lanes),
        in_specs=[
            block,
            pl.BlockSpec((IMAGE_ROWS, 4 * LANES), lambda i, j: (i, 0)),
            pl.BlockSpec((taps.shape[0], lanes), lambda i, j: (0, j)),
            pl.BlockSpec((IMAGE_ROWS, 1), lambda i, j: (i, 0)),
        ],
        out_specs=[block] * 7 + [pool_block],
        out_shape=[shape_of((rows, channels), BF16)]
        + [shape_of((rows, channels))] * 6
        + [shape_of((8 * images, channels))],
        scratch_shapes=[pltpu.VMEM((GRID, GRID + 16, lanes), F32)],
        compiler_params=pltpu.CompilerParams(
            vmem_limit_bytes=VMEM_LIMIT, dimension_semantics=("arbitrary", "arbitrary")
        ),
    )(context, gates, taps, validity)


def focal_backward(d_summed, gates, taps, validity, saved):
    context, k1, k2, k3, s1, s2, s3, pools = saved
    rows, channels = context.shape
    lanes = lane_width(channels)
    images = rows // IMAGE_ROWS
    groups = channels // lanes

    def body(
        d_ref,
        gate_ref,
        tap_ref,
        valid_ref,
        k0,
        k1,
        k2,
        k3,
        s1,
        s2,
        s3,
        pool_ref,
        d_context_ref,
        d_gate_ref,
        d_tap_ref,
        padded,
        d_padded,
        tap_sums,
    ):
        image = pl.program_id(1)
        fields = (k0, k1, k2, k3)
        slopes = (s1, s2, s3)
        clear_margins(padded)
        clear_margins(d_padded)
        pooled = pool_ref[0:1, :]
        d_pooled = jnp.zeros((1, lanes), F32)
        for row in range(GRID):
            d_row = row_part(d_ref, row)
            d_pooled = d_pooled + column_sum(d_row * gate_part(gate_ref, row, 3, lanes))
        d_mean = d_pooled * pool_ref[1:2, :]
        d_field = [d_mean * row_part(valid_ref, row) for row in range(GRID)]
        for level in (2, 1, 0):
            d_pre = []
            for row in range(GRID):
                d_row = row_part(d_ref, row)
                grad = (d_field[row] + d_row * gate_part(gate_ref, row, level, lanes)) * row_part(
                    slopes[level], row
                )
                d_pre.append(grad)
                d_padded[row, 8 : 8 + GRID, :] = grad
                padded[row, 8 : 8 + GRID, :] = row_part(fields[level], row)
            correlate_taps(padded, d_pre, tap_sums, level)
            d_field = correlate(d_padded, tap_ref, level, True)
        for row in range(GRID):
            d_context_ref[row * GRID : (row + 1) * GRID, :] = d_field[row].astype(BF16)
        d_all = d_ref[...]
        d_gate_ref[:, 0:LANES] = fold(d_all * k1[...])
        d_gate_ref[:, LANES : 2 * LANES] = fold(d_all * k2[...])
        d_gate_ref[:, 2 * LANES : 3 * LANES] = fold(d_all * k3[...])
        d_gate_ref[:, 3 * LANES : 4 * LANES] = fold(d_all * pooled)

        @pl.when(image == 0)
        def _():
            d_tap_ref[...] = tap_sums[...]

        @pl.when(image > 0)
        def _():
            d_tap_ref[...] = d_tap_ref[...] + tap_sums[...]

    def fold(values):
        if lanes == LANES:
            return values
        return jnp.broadcast_to(
            jnp.sum(values, axis=-1, keepdims=True) / LANES, (values.shape[0], LANES)
        )

    block = pl.BlockSpec((IMAGE_ROWS, lanes), lambda j, i: (i, j))
    return pl.pallas_call(
        body,
        name="focal_backward",
        grid=(groups, images),
        in_specs=[
            block,
            pl.BlockSpec((IMAGE_ROWS, 4 * LANES), lambda j, i: (i, 0)),
            pl.BlockSpec((taps.shape[0], lanes), lambda j, i: (0, j)),
            pl.BlockSpec((IMAGE_ROWS, 1), lambda j, i: (i, 0)),
        ]
        + [block] * 7
        + [pl.BlockSpec((8, lanes), lambda j, i: (i, j))],
        out_specs=[
            block,
            pl.BlockSpec((IMAGE_ROWS, 4 * LANES), lambda j, i: (i, j)),
            pl.BlockSpec((taps.shape[0], lanes), lambda j, i: (0, j)),
        ],
        out_shape=[
            shape_of((rows, channels), BF16),
            shape_of((rows, 4 * LANES * groups)),
            shape_of(taps.shape),
        ],
        scratch_shapes=[
            pltpu.VMEM((GRID, GRID + 16, lanes), F32),
            pltpu.VMEM((GRID, GRID + 16, lanes), F32),
            pltpu.VMEM(taps.shape[:1] + (lanes,), F32),
        ],
        compiler_params=pltpu.CompilerParams(
            vmem_limit_bytes=VMEM_LIMIT, dimension_semantics=("arbitrary", "arbitrary")
        ),
    )(d_summed, gates, taps, validity, context, k1, k2, k3, s1, s2, s3, pools)


def mix_forward(context_low, query, x, keep, vecs, pieces):
    rows, width = x.shape
    names = ("mix", "proj")
    size = pieces.size()

    def body(*refs):
        loads = pieces.loaders(names, refs[:size], refs[size + 5 + 6 :])
        low_ref, query_ref, x_ref, keep_ref, vec_ref = refs[size : size + 5]
        mod_ref, product_ref, middle_ref, unit_ref, scale_ref, second_ref = refs[
            size + 5 : size + 11
        ]
        for start, _wait, _target in loads:
            start()
        vec = vec_ref[...]
        loads[0][1]()
        modulator = times_transposed(low_ref[...], loads[0][2][...])
        mod_ref[...] = modulator
        product = (query_ref[...] * modulator).astype(BF16)
        product_ref[...] = product
        loads[1][1]()
        branch = matmul(product, loads[1][2][...]) + vec[4:5]
        middle = x_ref[...] + keep_ref[:, 0:1] * branch
        middle_ref[...] = middle
        unit, scale = normalize(middle)
        unit_ref[...] = unit
        scale_ref[...] = scale
        second_ref[...] = (unit * vec[2:3] + vec[3:4]).astype(BF16)

    return run_kernel(
        body,
        "mix_forward",
        pieces.specs() + [whole_spec()] * 5,
        [
            shape_of((rows, width)),
            shape_of((rows, width), BF16),
            shape_of((rows, width)),
            shape_of((rows, width)),
            shape_of((rows, 1)),
            shape_of((rows, width), BF16),
        ],
        pieces.scratch(names),
        *pieces.args(),
        context_low,
        query,
        x,
        keep,
        vecs,
    )


def mlp_forward(second, middle, keep, vecs, pieces):
    rows, width = middle.shape
    names = ("up", "down")
    size = pieces.size()
    hidden_width = pieces.matrices["up"][2] * pieces.slots

    def body(*refs):
        loads = pieces.loaders(names, refs[:size], refs[size + 4 + 3 :])
        second_ref, middle_ref, keep_ref, vec_ref = refs[size : size + 4]
        out_ref, hidden_ref, slope_ref = refs[size + 4 : size + 7]
        for start, _wait, _target in loads:
            start()
        loads[0][1]()
        second_value = second_ref[...]
        step = hidden_width // 4
        for part in range(4):
            at = slice(part * step, (part + 1) * step)
            value, slope = gelu_pair(times_transposed(second_value, loads[0][2][at, :]))
            hidden_ref[:, at] = value.astype(BF16)
            slope_ref[:, at] = slope
        loads[1][1]()
        lowered = matmul(hidden_ref[...], loads[1][2][...]) + vec_ref[5:6, :]
        out_ref[...] = middle_ref[...] + keep_ref[:, 1:2] * lowered

    return run_kernel(
        body,
        "mlp_forward",
        pieces.specs() + [whole_spec()] * 4,
        [
            shape_of((rows, width)),
            shape_of((rows, hidden_width), BF16),
            shape_of((rows, hidden_width)),
        ],
        pieces.scratch(names),
        *pieces.args(),
        second,
        middle,
        keep,
        vecs,
    )


def embed_forward(patches, embed_weight, vectors, masked):
    rows = patches.shape[0]
    width = embed_weight.shape[1]
    outer = 10 * BLOCKS

    def body(patch_ref, weight_ref, vec_ref, mask_ref, x_ref, unit_ref, scale_ref):
        embedded = matmul(patch_ref[...], weight_ref[...].astype(BF16)) + vec_ref[
            outer : outer + 1, :
        ]
        unit, scale = normalize(embedded)
        unit_ref[...] = unit
        scale_ref[...] = scale
        mask = mask_ref[...]
        state = unit * vec_ref[outer + 1 : outer + 2, :] + vec_ref[outer + 2 : outer + 3, :]
        x_ref[...] = state * (1.0 - mask) + vec_ref[outer + 5 : outer + 6, :] * mask

    return run_kernel(
        body,
        "embed_forward",
        [whole_spec()] * 4,
        [shape_of((rows, width)), shape_of((rows, width)), shape_of((rows, 1))],
        [],
        patches,
        embed_weight,
        vectors,
        masked,
    )


def head_step(links, x, patches, head_weight, vectors, loss_weight, denominator):
    rows, width = x.shape
    targets = head_weight.shape[1]
    part = targets // (2 * links.chan)
    outer = 10 * BLOCKS

    def body(
        core_ref,
        x_ref,
        patch_ref,
        weight_ref,
        vec_ref,
        weight_col,
        denom_ref,
        d_ref,
        kept_ref,
        sent_ref,
        sums_ref,
    ):
        gain = vec_ref[outer + 3 : outer + 4, :]
        unit, scale = normalize(x_ref[...])
        low = (unit * gain + vec_ref[outer + 4 : outer + 5, :]).astype(BF16)
        head_low = weight_ref[...].astype(BF16)
        error = matmul(low, head_low) - patch_ref[...].astype(F32)
        denom = denom_ref[0, 0]
        weighted = weight_col[...] * error
        loss = column_sum(jnp.sum(weighted * error, axis=-1, keepdims=True)) / denom
        d_pred = (2.0 * weighted / denom).astype(BF16)
        grad = contract_rows(d_pred, low)
        half = targets // 2
        store_halves(core_ref[0], kept_ref, sent_ref, 0, grad[:half], grad[half:])
        d_final = times_transposed(d_pred, head_low)
        d_ref[...] = norm_backward(d_final, unit, scale, gain)
        sums_ref[0:1, :] = column_sum(d_final * unit)
        sums_ref[1:2, :] = column_sum(d_final)
        sums_ref[2:3, :] = jnp.broadcast_to(loss, (1, width))
        sums_ref[3:8, :] = jnp.zeros((5, width), F32)

    return run_kernel(
        body,
        "head_step",
        [scalar_spec()] + [whole_spec()] * 5 + [scalar_spec()],
        [
            shape_of((rows, width)),
            shape_of((links.chan, part, width), BF16),
            shape_of((links.chan, part, width), BF16),
            shape_of((8, width)),
        ],
        [],
        links.where,
        x,
        patches,
        head_weight,
        vectors,
        loss_weight,
        denominator,
    )


def store_halves(core, kept_ref, sent_ref, at, first, second):
    chan, _rows, width = kept_ref.shape
    rows = first.shape[0] // chan
    first = first.reshape(chan, rows, width).astype(BF16)
    second = second.reshape(chan, rows, width).astype(BF16)

    @pl.when(core == 0)
    def _():
        kept_ref[:, at : at + rows, :] = first
        sent_ref[:, at : at + rows, :] = second

    @pl.when(core != 0)
    def _():
        kept_ref[:, at : at + rows, :] = second
        sent_ref[:, at : at + rows, :] = first


def append_halves(kept_ref, sent_ref, at, extra_refs):
    for ref, target in zip(extra_refs, (kept_ref, sent_ref)):
        target[:, at : at + ref.shape[1], :] = ref[...]


def mlp_backward(d_residual, hidden, slope, second, unit, scale, keep, vecs, pieces):
    rows, width = d_residual.shape
    hidden_width = hidden.shape[1]
    names = ("up", "down")
    size = pieces.size()

    def body(*refs):
        loads = pieces.loaders(names, refs[:size], refs[size + 8 + 4 :])
        d_ref, hidden_ref, slope_ref, second_ref, unit_ref, scale_ref, keep_ref, vec_ref = refs[
            size : size + 8
        ]
        out_ref, kept_ref, sent_ref, sums_ref = refs[size + 8 : size + 12]
        loads[1][0]()
        loads[0][0]()
        d_residual = d_ref[...]
        d_down = d_residual * keep_ref[:, 1:2]
        d_low = d_down.astype(BF16)
        grad_down = contract_rows(hidden_ref[...], d_low)
        loads[1][1]()
        d_pre = (times_transposed(d_low, loads[1][2][...]) * slope_ref[...]).astype(BF16)
        grad_up = contract_rows(d_pre, second_ref[...])
        store_halves(refs[0][0], kept_ref, sent_ref, 0, grad_up, grad_down)
        loads[0][1]()
        d_second = matmul(d_pre, loads[0][2][...])
        unit = unit_ref[...]
        out_ref[...] = d_residual + norm_backward(d_second, unit, scale_ref[...], vec_ref[2:3, :])
        sums_ref[0:1, :] = column_sum(d_second * unit)
        sums_ref[1:2, :] = column_sum(d_second)
        sums_ref[2:3, :] = column_sum(d_down)
        sums_ref[3:8, :] = jnp.zeros((5, width), F32)

    return run_kernel(
        body,
        "mlp_backward",
        pieces.specs() + [whole_spec()] * 8,
        [
            shape_of((rows, width)),
            shape_of((pieces.slots, hidden_width // pieces.slots, width), BF16),
            shape_of((pieces.slots, hidden_width // pieces.slots, width), BF16),
            shape_of((8, width)),
        ],
        pieces.scratch(names),
        *pieces.args(),
        d_residual,
        hidden,
        slope,
        second,
        unit,
        scale,
        keep,
        vecs,
    )


def mix_backward(d_middle, query, modulator, product, context_low, keep, vecs, pieces):
    rows, width = d_middle.shape
    names = ("mix", "proj")
    size = pieces.size()

    def body(*refs):
        loads = pieces.loaders(names, refs[:size], refs[size + 6 + 5 :])
        d_ref, query_ref, mod_ref, product_ref, low_ref, keep_ref = refs[size : size + 6]
        d_query_ref, d_sum_ref, kept_ref, sent_ref, sums_ref = refs[size + 6 : size + 11]
        loads[1][0]()
        loads[0][0]()
        d_proj = d_ref[...] * keep_ref[:, 0:1]
        d_low = d_proj.astype(BF16)
        grad_proj = contract_rows(product_ref[...], d_low)
        loads[1][1]()
        d_product = times_transposed(d_low, loads[1][2][...])
        d_query_ref[...] = (d_product * mod_ref[...]).astype(BF16)
        d_mod = (d_product * query_ref[...]).astype(BF16)
        loads[0][1]()
        d_sum_ref[...] = matmul(d_mod, loads[0][2][...])
        grad_mix = contract_rows(d_mod, low_ref[...])
        store_halves(refs[0][0], kept_ref, sent_ref, 0, grad_mix, grad_proj)
        sums_ref[0:1, :] = column_sum(d_proj)
        sums_ref[1:8, :] = jnp.zeros((7, width), F32)

    return run_kernel(
        body,
        "mix_backward",
        pieces.specs() + [whole_spec()] * 6,
        [
            shape_of((rows, width), BF16),
            shape_of((rows, width)),
            shape_of((pieces.slots, width // pieces.slots, width), BF16),
            shape_of((pieces.slots, width // pieces.slots, width), BF16),
            shape_of((8, width)),
        ],
        pieces.scratch(names),
        *pieces.args(),
        d_middle,
        query,
        modulator,
        product,
        context_low,
        keep,
    )


def inputs_backward(
    d_middle, d_query, d_context, d_gates, first, unit, scale, vecs, pieces, extras
):
    rows, width = d_middle.shape
    groups = d_gates.shape[1] // (4 * LANES)
    names = ("query", "key")
    size = pieces.size()
    own = width // pieces.slots
    more = [array for pair in extras for array in pair]
    total = own + sum(pair[0].shape[1] for pair in extras)

    def body(*refs):
        inputs = size + 8 + len(more)
        loads = pieces.loaders(names, refs[:size], refs[inputs + 4 :])
        d_ref, d_query_ref, d_context_ref, d_gate_ref, first_ref, unit_ref, scale_ref, vec_ref = (
            refs[size : size + 8]
        )
        more_refs = refs[size + 8 : inputs]
        out_ref, kept_ref, sent_ref, sums_ref = refs[inputs : inputs + 4]
        for start, _wait, _target in loads:
            start()
        first = first_ref[...]
        gate_low = low_gates(vec_ref[...]).astype(F32)
        sums_ref[...] = jnp.zeros((8, width), F32)
        gate_terms = jnp.zeros((rows, width), F32)
        first_wide = first.astype(F32)
        for level in range(4):
            gate_sum = jnp.zeros((rows, LANES), F32)
            for group in range(groups):
                at = (group * 4 + level) * LANES
                gate_sum = gate_sum + d_gate_ref[:, at : at + LANES]
            column = jnp.sum(gate_sum, axis=-1, keepdims=True)
            gate_terms = gate_terms + column * gate_low[level : level + 1]
            sums_ref[2 + level : 3 + level, :] = column_sum(column * first_wide)
        loads[0][1]()
        d_query = d_query_ref[...]
        d_context = d_context_ref[...]
        d_first = matmul(d_query, loads[0][2][...]) + gate_terms
        loads[1][1]()
        d_first = d_first + matmul(d_context, loads[1][2][...])
        unit = unit_ref[...]
        out_ref[...] = d_ref[...] + norm_backward(d_first, unit, scale_ref[...], vec_ref[0:1, :])
        sums_ref[0:1, :] = column_sum(d_first * unit)
        sums_ref[1:2, :] = column_sum(d_first)
        grad_query = contract_rows(d_query, first)
        grad_key = contract_rows(d_context, first)
        store_halves(refs[0][0], kept_ref, sent_ref, 0, grad_query, grad_key)
        at = own
        for index in range(len(extras)):
            append_halves(kept_ref, sent_ref, at, more_refs[2 * index : 2 * index + 2])
            at += more_refs[2 * index].shape[1]

    return run_kernel(
        body,
        "inputs_backward",
        pieces.specs() + [whole_spec()] * (8 + len(more)),
        [
            shape_of((rows, width)),
            shape_of((pieces.slots, total, width), BF16),
            shape_of((pieces.slots, total, width), BF16),
            shape_of((8, width)),
        ],
        pieces.scratch(names),
        *pieces.args(),
        d_middle,
        d_query,
        d_context,
        d_gates,
        first,
        unit,
        scale,
        vecs,
        *more,
    )


def small_offsets(tap_count):
    room = -(-tap_count // 8) * 8
    return ([b * room for b in range(BLOCKS)], BLOCKS * room)


def embed_backward(
    links, d_residual, patches, unit, scale, vectors, masked, tap_grads, sums, pair
):
    rows, width = d_residual.shape
    chan = links.chan
    outer = 10 * BLOCKS
    tap_at, sums_at = small_offsets(tap_grads[0].shape[0])
    used = sums_at + 8 * (len(sums) + 1)
    small_rows = -(-used // (16 * chan)) * (16 * chan)
    patch_in = patches.shape[1]
    embed_part = patch_in // (2 * chan)
    small_part = small_rows // (2 * chan)
    first_rows = pair[0].shape[1]
    total = first_rows + embed_part + small_part
    count = 7 + len(tap_grads) + len(sums) + 2

    def body(*refs):
        core_ref, d_ref, patch_ref, unit_ref, scale_ref, vec_ref, mask_ref = refs[:7]
        tap_refs = refs[7 : 7 + len(tap_grads)]
        sum_refs = refs[7 + len(tap_grads) : count - 2]
        pair_refs = refs[count - 2 : count]
        kept_ref, sent_ref, small = refs[count:]
        mask = mask_ref[...]
        d_residual = d_ref[...]
        d_start = d_residual * (1.0 - mask)
        unit = unit_ref[...]
        d_embed = norm_backward(d_start, unit, scale_ref[...], vec_ref[outer + 1 : outer + 2, :])
        small[...] = jnp.zeros(small.shape, F32)
        for at, ref in zip(tap_at, tap_refs):
            small[at : at + ref.shape[0], :] = ref[...]
        small[sums_at : sums_at + 1, :] = column_sum(d_embed)
        small[sums_at + 1 : sums_at + 2, :] = column_sum(d_start * unit)
        small[sums_at + 2 : sums_at + 3, :] = column_sum(d_start)
        small[sums_at + 3 : sums_at + 4, :] = column_sum(d_residual * mask)
        for index, ref in enumerate(sum_refs):
            at = sums_at + 8 * (index + 1)
            small[at : at + 8, :] = ref[...]
        grad = contract_rows(patch_ref[...], d_embed.astype(BF16))
        core = core_ref[0]
        half = patch_in // 2
        append_halves(kept_ref, sent_ref, 0, pair_refs)
        store_halves(core, kept_ref, sent_ref, first_rows, grad[:half], grad[half:])
        half = small_rows // 2
        store_halves(
            core, kept_ref, sent_ref, first_rows + embed_part, small[:half], small[half:]
        )

    return run_kernel(
        body,
        "embed_backward",
        [scalar_spec()] + [whole_spec()] * (count - 1),
        [shape_of((chan, total, width), BF16)] * 2,
        [pltpu.VMEM((small_rows, width), F32)],
        links.where,
        d_residual,
        patches,
        unit,
        scale,
        vectors,
        masked,
        *tap_grads,
        *sums,
        *pair,
    )


def taps_from_pieces(links, near, tap_count):
    own, lanes = near[0].shape[1:]
    channels = own * links.chan

    def body(*refs):
        parts = refs[1 : 1 + len(near)]
        out_ref, target, sems = refs[1 + len(near) :]
        copies = []
        slot = 0
        for part in parts:
            for d in range(part.shape[0]):
                start = pl.multiple_of(refs[0][1 + slot] * own, 8)
                copies.append(
                    pltpu.make_async_copy(
                        part.at[d], target.at[pl.ds(start, own), :], sems.at[slot]
                    )
                )
                slot += 1
        for copy in copies:
            copy.start()
        for copy in copies:
            copy.wait()
        turned = target[...].T
        for block_index in range(BLOCKS):
            out_ref[block_index] = turned[block_index * tap_count : (block_index + 1) * tap_count]

    return run_kernel(
        body,
        "taps_from_pieces",
        [scalar_spec()] + [far_spec() for _ in near],
        [shape_of((BLOCKS, tap_count, channels))],
        [pltpu.VMEM((channels, lanes), F32), pltpu.SemaphoreType.DMA((links.chan,))],
        links.where,
        *near,
    )[0]


def nesterov(weight, moment, gradient, rate):
    new_moment = MOMENTUM * moment + gradient
    new_weight = weight - rate * (gradient + MOMENTUM * new_moment)
    return (new_weight, new_moment)


def update_shared(links, pieces, tap_count, rate, head, embed, vectors, kernels):
    names = ("head0", "head1", "embed0", "embed1", "small0", "small1")
    size = pieces.size()
    width = pieces.width
    own = kernels[0].shape[-1]
    tap_at, sums_at = small_offsets(tap_count)
    spans = []
    for name in names:
        spans.append(pieces.matrices[name][2] * pieces.slots)
    patch_in = 2 * spans[0]
    small_rows = 2 * spans[4]

    def body(*refs):
        inputs = list(refs[size : size + 10])
        outputs = list(refs[size + 10 : size + 21])
        turned, target, small, *sems = refs[size + 21 :]
        views = [
            turned.at[0 : spans[0], :],
            turned.at[spans[0] : patch_in, :],
            target.at[0 : spans[2], :],
            target.at[spans[2] : patch_in, :],
            small.at[0 : spans[4], :],
            small.at[spans[4] : small_rows, :],
        ]
        scratch = [item for pair in zip(views, sems) for item in pair]
        loads = pieces.loaders(names, refs[:size], scratch)
        for start, _wait, _target in loads:
            start()
        for _start, wait, _target in loads:
            wait()
        head_ref, head_moment_ref, embed_ref, embed_moment_ref = inputs[:4]
        new_weight, new_moment = nesterov(
            head_ref[...], head_moment_ref[...], turned[...].astype(F32).T, rate
        )
        outputs[0][...] = new_weight
        outputs[1][...] = new_moment
        new_weight, new_moment = nesterov(
            embed_ref[...], embed_moment_ref[...], target[...].astype(F32), rate
        )
        outputs[2][...] = new_weight
        outputs[3][...] = new_moment
        grads = small[...].astype(F32)

        def sum_row(index, row):
            at = sums_at + 8 * index + row
            return grads[at : at + 1]

        rows = []
        for b in range(BLOCKS):
            inputs_at, mlp_at, mix_at = 1 + 3 * b, 2 + 3 * b, 3 + 3 * b
            rows += [sum_row(inputs_at, 0), sum_row(inputs_at, 1)]
            rows += [sum_row(mlp_at, 0), sum_row(mlp_at, 1)]
            rows += [sum_row(mix_at, 0), sum_row(mlp_at, 2)]
            rows += [sum_row(inputs_at, 2 + level) for level in range(4)]
        head_at = 1 + 3 * BLOCKS
        rows += [sum_row(0, 0), sum_row(0, 1), sum_row(0, 2)]
        rows += [sum_row(head_at, 0), sum_row(head_at, 1), sum_row(0, 3)]
        vec_ref, vec_moment_ref, vec_average_ref = inputs[4:7]
        for at, row in enumerate(rows):
            here = slice(at, at + 1)
            new_weight, new_moment = nesterov(
                vec_ref[here, :], vec_moment_ref[here, :], row, rate
            )
            outputs[4][here, :] = new_weight
            outputs[5][here, :] = new_moment
            outputs[6][here, :] = (
                AVERAGE * vec_average_ref[here, :] + (1.0 - AVERAGE) * new_weight
            )
        outputs[7][...] = sum_row(head_at, 2)[:, 0:LANES]
        first = refs[0][1] * own
        source = lax.broadcasted_iota(jnp.int32, (width, own), 0)
        wanted = first + lax.broadcasted_iota(jnp.int32, (width, own), 1)
        chosen = (source == wanted).astype(F32).astype(BF16)
        kernel_ref, kernel_moment_ref, kernel_average_ref = inputs[7:10]
        for b in range(BLOCKS):
            grad = matmul(small[tap_at[b] : tap_at[b] + tap_count, :], chosen)
            new_weight, new_moment = nesterov(kernel_ref[b], kernel_moment_ref[b], grad, rate)
            outputs[8][b] = new_weight
            outputs[9][b] = new_moment
            outputs[10][b] = AVERAGE * kernel_average_ref[b] + (1.0 - AVERAGE) * new_weight

    arrays = [*head, *embed, *vectors, *kernels]
    outs = [shape_of(array.shape) for array in arrays[:7]]
    outs += [shape_of((1, LANES))]
    outs += [shape_of(array.shape) for array in kernels]
    return run_kernel(
        body,
        "update_shared",
        pieces.specs() + [whole_spec()] * 10,
        outs,
        [
            pltpu.VMEM((patch_in, width), BF16),
            pltpu.VMEM((patch_in, width), BF16),
            pltpu.VMEM((small_rows, width), BF16),
        ]
        + [pltpu.SemaphoreType.DMA((pieces.slots,))] * 6,
        *pieces.args(),
        *arrays,
    )


class Shares:
    def __init__(self, local_rows, chan_size):
        self.count = max(1, IMAGE_ROWS // local_rows)
        self.groups = [
            list(range(first, first + self.count)) for first in range(0, chan_size, self.count)
        ]

    def to_images(self, values):
        if self.count == 1:
            return values
        return lax.all_to_all(values, "chan", 1, 0, axis_index_groups=self.groups, tiled=True)

    def to_rows(self, values):
        if self.count == 1:
            return values
        return lax.all_to_all(values, "chan", 0, 1, axis_index_groups=self.groups, tiled=True)

    def all_rows(self, values):
        if self.count == 1:
            return values
        return lax.all_gather(
            values, "chan", axis=0, axis_index_groups=self.groups, tiled=True
        )

    def sum_rows(self, values):
        if self.count == 1:
            return values
        return lax.psum_scatter(
            values, "chan", scatter_dimension=0, axis_index_groups=self.groups, tiled=True
        )

    def channels(self, values):
        if self.count == 1:
            return values
        size = values.shape[1] // self.count
        place = lax.axis_index("chan") % self.count
        return lax.dynamic_slice_in_dim(values, place * size, size, 1)

    def spread(self, values):
        if self.count == 1:
            return values
        size = values.shape[1]
        place = lax.axis_index("chan") % self.count
        whole = jnp.zeros((values.shape[0], size * self.count), values.dtype)
        return lax.dynamic_update_slice_in_dim(whole, values, place * size, 1)


def shards(
    patches,
    valid_mask,
    target_mask,
    keep_mask,
    embed_weight,
    embed_moment,
    head_weight,
    head_moment,
    vectors,
    vector_moment,
    vector_average,
    focal_input,
    focal_moment,
    focal_average,
    mixers,
    mixer_moment,
    mixer_average,
    mlp_weights,
    mlp_moment,
    mlp_average,
    kernels,
    kernel_moment,
    kernel_average,
):
    links = Links()
    local_rows = patches.shape[0]
    group_rows = valid_mask.shape[0]
    own = focal_input.shape[-1]
    own_hidden = mlp_weights.shape[-1]
    tap_count = kernels.shape[1]
    width = vectors.shape[1]
    shares = Shares(local_rows, links.chan)
    outer = 10 * BLOCKS

    focal_low = focal_input.astype(BF16)
    mixer_low = mixers.astype(BF16)
    mlp_low = mlp_weights.astype(BF16)
    chunks = []
    layouts = []
    for b in range(BLOCKS):
        chunks.append(
            jnp.stack(
                [
                    jnp.concatenate([focal_low[b, :, 0].T, mixer_low[b, 0].T], axis=0),
                    jnp.concatenate([focal_low[b, :, 1].T, mixer_low[b, 1].T], axis=0),
                ]
            )
        )
        layouts.append(
            {
                "query": (0, 0, own),
                "mix": (0, own, own),
                "key": (1, 0, own),
                "proj": (1, own, own),
            }
        )
        chunks.append(jnp.stack([mlp_low[b, 0].T, mlp_low[b, 1].T]))
        layouts.append({"up": (0, 0, own_hidden), "down": (1, 0, own_hidden)})
    columns = kernels.reshape(BLOCKS * tap_count, own).T
    lanes = -(-columns.shape[1] // LANES) * LANES
    columns = jnp.pad(columns, ((0, 0), (0, lanes - columns.shape[1])))

    spread = []
    for index, chunk in enumerate(chunks):
        own_part = links.own_half(chunk)
        if index == 1:
            own_part = after(own_part, spread[0][1], tap_parts[1])
        elif index > 1:
            own_part = after(own_part, spread[index - 1][1])
        spread.append(links.spread_z(own_part))
        if index == 0:
            tap_parts = links.spread_z(columns)
    near = [links.spread_y(parts) for parts in spread]
    taps_near = links.spread_y(tap_parts)
    pieces = [
        Pieces(links, part, [links.swap_core(item) for item in part], layout)
        for part, layout in zip(near, layouts)
    ]
    taps_full = taps_from_pieces(links, taps_near, tap_count)

    first_row = links.place * local_rows
    image_row = first_row // IMAGE_ROWS * IMAGE_ROWS
    image_rows = max(local_rows, IMAGE_ROWS)
    validity = valid_mask.astype(F32)
    valid_images = lax.dynamic_slice_in_dim(validity, image_row, image_rows)[:, None]
    valid_local = lax.dynamic_slice_in_dim(validity, first_row, local_rows)[:, None]
    masked_local = lax.dynamic_slice_in_dim(target_mask, first_row, local_rows).astype(F32)[
        :, None
    ]
    loss_weight = masked_local * valid_local
    group_count = jnp.broadcast_to(jnp.sum(validity * target_mask.astype(F32)), (8, LANES))
    counted = links.cross_x(group_count + links.swap_core(group_count))
    denominator = counted[0:1, 0:1] * PATCH_IN
    keep_rows = jnp.repeat(keep_mask.astype(F32) / KEEP_RATE, IMAGE_ROWS, axis=0)
    keep_local = lax.dynamic_slice_in_dim(keep_rows, first_row, local_rows)

    residual, embed_unit, embed_scale = embed_forward(
        patches, embed_weight, vectors, masked_local
    )
    saved = []
    for b in range(BLOCKS):
        vecs = vectors[10 * b : 10 * b + 10]
        keep = keep_local[:, b]
        focal_pieces = pieces[2 * b]
        mlp_pieces = pieces[2 * b + 1]
        residual = after(residual, near[2 * b + 1][0])
        unit_one, scale_one, first, query, context, gates = focal_inputs(
            residual, vecs, focal_pieces
        )
        gates = shares.all_rows(gates)
        context = shares.to_images(context)
        taps = shares.channels(taps_full[b])
        context_low, *levels = focal_forward(context, gates, taps, valid_images)
        context_low = shares.to_rows(context_low)
        if b + 1 < BLOCKS:
            context_low = after(context_low, near[2 * b + 2][0])
        modulator, product, middle, unit_two, scale_two, second = mix_forward(
            context_low, query, residual, keep, vecs, focal_pieces
        )
        residual, hidden, slope = mlp_forward(second, middle, keep, vecs, mlp_pieces)
        saved.append(
            (
                (unit_one, scale_one, first, query, gates, taps),
                (context_low, [context] + levels, modulator, product),
                (unit_two, scale_two, second, hidden, slope),
            )
        )
    d_residual, *head_pair, head_sums = head_step(
        links, residual, patches, head_weight, vectors, loss_weight, denominator
    )
    tap_grads = [None] * BLOCKS
    sums = [None] * BLOCKS
    whole_grads = [None] * BLOCKS
    waiting = None
    for b in reversed(range(BLOCKS)):
        last = b == 0
        vecs = vectors[10 * b : 10 * b + 10]
        keep = keep_local[:, b]
        unit_one, scale_one, first, query, gates, taps = saved[b][0]
        context_low, levels, modulator, product = saved[b][1]
        unit_two, scale_two, second, hidden, slope = saved[b][2]
        d_middle, kept, sent, mlp_sums = mlp_backward(
            d_residual, hidden, slope, second, unit_two, scale_two, keep, vecs, pieces[2 * b + 1]
        )
        mlp_received = links.swap_core(sent)
        mlp_kept = kept
        if waiting is not None:
            focal_parts = links.add_core(after(waiting[0], d_middle), waiting[1])
            d_middle = after(d_middle, *focal_parts)
            focal_parts = links.send_y(focal_parts)
        d_query, d_sum, *mix_pair, mix_sums = mix_backward(
            d_middle, query, modulator, product, context_low, keep, vecs, pieces[2 * b]
        )
        mlp_parts = links.add_core(after(mlp_kept, d_sum), mlp_received)
        d_sum = after(d_sum, *mlp_parts)
        mlp_parts = links.send_y(mlp_parts)
        d_context, d_gates, tap_grad = focal_backward(
            shares.to_images(d_sum), gates, taps, valid_images, levels
        )
        tap_grads[b] = shares.spread(tap_grad)
        if waiting is not None:
            upper = jnp.concatenate(
                [waiting[2], links.add_y([after(focal_parts[0], d_context)] + focal_parts[1:])],
                axis=1,
            )
            d_context = after(d_context, upper)
            upper_parts = links.send_z(upper)
        d_residual, kept, sent, input_sums = inputs_backward(
            d_middle,
            d_query,
            shares.to_rows(d_context),
            shares.sum_rows(d_gates),
            first,
            unit_one,
            scale_one,
            vecs,
            pieces[2 * b],
            [mix_pair] if last else [mix_pair, head_pair],
        )
        sums[b] = [input_sums, mlp_sums, mix_sums]
        mlp_total = links.add_y([after(mlp_parts[0], d_residual)] + mlp_parts[1:])
        if not last:
            waiting = (kept, links.swap_core(sent), mlp_total)
    kept, sent = embed_backward(
        links,
        d_residual,
        patches,
        embed_unit,
        embed_scale,
        vectors,
        masked_local,
        tap_grads,
        [item for parts in sums for item in parts] + [head_sums],
        (kept, sent),
    )
    focal_parts = links.send_y(links.add_core(kept, links.swap_core(sent)))
    mlp_parts = links.send_z(mlp_total)
    upper = links.cross_x(links.add_z(upper_parts))
    focal_parts = links.send_z(links.add_y(focal_parts))
    mlp_rows = links.cross_x(links.add_z(mlp_parts))
    lower = links.cross_x(links.add_z(focal_parts))
    edge = own_hidden + 2 * own
    head_rows = upper[edge:]
    common = jnp.concatenate([head_rows, lower[2 * own :]], axis=0).astype(BF16)
    common_near = links.spread_y(links.spread_z(common))
    head_part = head_rows.shape[0]
    embed_part = patches.shape[1] // (2 * links.chan)
    small_part = common.shape[0] - head_part - embed_part
    layout = {}
    for half in range(2):
        layout["head%d" % half] = (half, 0, head_part)
        layout["embed%d" % half] = (half, head_part, embed_part)
        layout["small%d" % half] = (half, head_part + embed_part, small_part)
    common_pieces = Pieces(
        links, common_near, [links.swap_core(item) for item in common_near], layout
    )
    whole_grads[1] = links.both_halves(upper[:edge])
    whole_grads[0] = links.both_halves(jnp.concatenate([mlp_rows, lower[: 2 * own]], axis=0))
    rate = 0.2 * math.sqrt(group_rows * lax.axis_size("dp"))
    updated = update_shared(
        links,
        common_pieces,
        tap_count,
        rate,
        (head_weight, head_moment),
        (embed_weight, embed_moment),
        (vectors, vector_moment, vector_average),
        (kernels, kernel_moment, kernel_average),
    )
    new_head, new_head_moment, new_embed, new_embed_moment = updated[:4]
    loss = updated[7][0, 0]
    focal_at = slice(own_hidden, own_hidden + own)
    mixer_at = slice(own_hidden + own, edge)
    grad_focal = jnp.stack(
        [jnp.stack([part[focal_at].T for part in grads], axis=1) for grads in whole_grads]
    )
    grad_mixer = jnp.stack(
        [jnp.stack([part[mixer_at].T for part in grads]) for grads in whole_grads]
    )
    grad_mlp = jnp.stack(
        [jnp.stack([part[:own_hidden].T for part in grads]) for grads in whole_grads]
    )
    results = []
    for weight, moment, average, gradient in (
        (focal_input, focal_moment, focal_average, grad_focal),
        (mixers, mixer_moment, mixer_average, grad_mixer),
        (mlp_weights, mlp_moment, mlp_average, grad_mlp),
    ):
        new_weight, new_moment = nesterov(weight, moment, gradient, rate)
        results.extend(
            (new_weight, new_moment, AVERAGE * average + (1.0 - AVERAGE) * new_weight)
        )
    return (
        loss,
        new_embed,
        new_embed_moment,
        new_head,
        new_head_moment,
        *updated[4:7],
        *results,
        *updated[8:11],
    )


def solution(mesh):
    split = P(None, None, None, "chan")
    taps = P(None, None, "chan")
    return jax.shard_map(
        shards,
        mesh=mesh,
        in_specs=(P(("dp", "chan"), None), P("dp"), P("dp"), P("dp", None, None))
        + (P(),) * 7
        + (split,) * 9
        + (taps,) * 3,
        out_specs=(P(),) * 8 + (split,) * 9 + (taps,) * 3,
        check_vma=False,
    )
```

```python
import math

import jax
import jax.numpy as jnp
from jax import lax
from jax.experimental import pallas as pl
from jax.experimental.pallas import tpu as pltpu
from jax.sharding import PartitionSpec as P

PATCH_IN = 768
GRID = 16
BLOCKS = 2
IMAGE_ROWS = GRID * GRID
LANES = 128

EPS = 1e-05
MOMENTUM = 0.9
AVERAGE = 0.5
KEEP_RATE = 0.8
KERNEL_SIZES = (3, 5, 7)
KERNEL_STARTS = (0, 9, 34)
ROOT_HALF = math.sqrt(0.5)
DENSITY = 1.0 / math.sqrt(2.0 * math.pi)
VMEM_LIMIT = 24 << 20
F32 = jnp.float32
BF16 = jnp.bfloat16


def matmul(left, right):
    return jnp.dot(left, right, preferred_element_type=F32)


def contract_rows(left, right):
    return lax.dot_general(left, right, (((0,), (0,)), ((), ())), preferred_element_type=F32)


def times_transposed(left, right):
    return lax.dot_general(left, right, (((1,), (1,)), ((), ())), preferred_element_type=F32)


def normalize(values):
    average = jnp.mean(values, axis=-1, keepdims=True)
    centred = values - average
    variance = jnp.mean(centred * centred, axis=-1, keepdims=True)
    scale = lax.rsqrt(variance + EPS)
    return (centred * scale, scale)


def norm_backward(grad, unit, scale, gain):
    d_unit = grad * gain
    mean_one = jnp.mean(d_unit, axis=-1, keepdims=True)
    mean_two = jnp.mean(d_unit * unit, axis=-1, keepdims=True)
    return (d_unit - mean_one - unit * mean_two) * scale


def column_sum(values):
    return jnp.sum(values, axis=0, keepdims=True)


def gelu_pair(values):
    cumulative = 0.5 + 0.5 * lax.erf(values * ROOT_HALF)
    density = DENSITY * jnp.exp(-0.5 * values * values)
    return (values * cumulative, cumulative + values * density)


def nesterov(weight, moment, gradient, rate):
    new_moment = MOMENTUM * moment + gradient
    new_weight = weight - rate * (gradient + MOMENTUM * new_moment)
    return (new_weight, new_moment)


def after(value, *others):
    return lax.optimization_barrier((value, others))[0]


class Links:
    def __init__(self):
        chan = lax.axis_size("chan")
        self.ny = 1 << ((chan.bit_length() - 1) // 2)
        self.nz = chan // self.ny
        self.nc = 2
        self.nx = lax.axis_size("dp") // self.nc
        self.chan = chan
        self.place = lax.axis_index("chan")
        self.z = self.place // self.ny
        self.y = self.place % self.ny
        group = lax.axis_index("dp")
        self.x = group // self.nc
        self.core = group % self.nc
        self.sizes = {"z": self.nz, "y": self.ny, "x": self.nx}

    def bits(self, axis):
        return [1 << k for k in reversed(range((self.sizes[axis] - 1).bit_length()))]

    def swap(self, values, axis, step):
        if axis in ("z", "y"):
            step = step * self.ny if axis == "z" else step
            return lax.ppermute(values, "chan", [(i, i ^ step) for i in range(self.chan)])
        step = step * self.nc if axis == "x" else step
        return lax.ppermute(values, "dp", [(i, i ^ step) for i in range(self.nx * self.nc)])

    def swap_core(self, values):
        return self.swap(values, "core", 1)

    def cross_x(self, values):
        total = values
        for step in self.bits("x"):
            low = total.astype(values.dtype)
            total = low.astype(F32) + self.swap(low, "x", step).astype(F32)
        return total.astype(F32)

    def mask_of(self, axis, step):
        return tuple(step if name == axis else 0 for name in ("z", "y", "x"))

    def here(self):
        return jnp.stack([self.core, self.place, self.x]).astype(jnp.int32)

    def slots(self, masks, split_x):
        places = []
        for mask_z, mask_y, mask_x in masks:
            place = (self.z ^ mask_z) * self.ny + (self.y ^ mask_y)
            places.append(place * self.nx + (self.x ^ mask_x) if split_x else place)
        return jnp.stack([self.core, self.place] + places).astype(jnp.int32)

    def open_sum(self, kept, received, parts=1):
        chan, rows, width = kept.shape
        bits = [2] * ((chan * parts).bit_length() - 1)
        return [term.reshape(*bits, rows // parts, width) for term in (kept, received)]

    def exchange(self, terms, axis, level):
        dims = terms[0].ndim - 2
        at = len(self.bits("z")) - 1 - level if axis == "z" else dims - 1
        index = self.index_on(axis) >> level & 1

        def pick(term, which):
            return lax.dynamic_index_in_dim(term, which, at, keepdims=False)

        sent = total([pick(term, 1 - index) for term in terms])

        def finish(received):
            return [pick(term, index) for term in terms] + [received]

        return ((sent, axis, 1 << level), finish)

    def index_on(self, axis):
        return self.y if axis == "y" else self.z if axis == "z" else self.x

    def early(self, terms, axis):
        levels = len(self.bits(axis))
        for level in range(levels - 1):
            move, finish = self.exchange(terms, axis, level)
            terms = finish(self.swap(*move))
        return self.exchange(terms, axis, levels - 1)

    def regather_x(self, rows):
        *steps, last = reversed(self.bits("x"))
        for step in steps:
            rows = self.beside_x(rows, self.swap(rows, "x", step), step)
        return ((rows, "x", last), lambda received: self.beside_x(rows, received, last))

    def beside_x(self, rows, received, step):
        first = jnp.concatenate([rows, received])
        second = jnp.concatenate([received, rows])
        return jnp.where(self.x & step == 0, first, second)

    def both_halves(self, summed):
        other = self.swap_core(summed)
        first = self.core == 0
        return (jnp.where(first, summed, other), jnp.where(first, other, summed))


def join(left, right):
    return tuple(a ^ b for a, b in zip(left, right))


def total(terms):
    result = terms[0].astype(F32)
    for term in terms[1:]:
        result = result + term.astype(F32)
    return result.astype(BF16)


class Gather:
    def __init__(self, links, own):
        self.links = links
        self.stack = own[None]
        self.masks = [(0, 0, 0)]
        self.parts = None

    def moves(self, axis, step):
        return [(self.stack, axis, step)]

    def take(self, received, axis, step, keep_apart=False):
        if keep_apart:
            self.parts = [self.stack, received]
        else:
            self.stack = jnp.concatenate([self.stack, received], axis=0)
        extra = self.links.mask_of(axis, step)
        self.masks = self.masks + [join(mask, extra) for mask in self.masks]

    def early(self, axis):
        *steps, last = self.links.bits(axis)
        for step in steps:
            self.take(self.links.swap(self.stack, axis, step), axis, step)
        return (axis, last)

    def direct(self):
        return [(self.stack, "z", step) for step in range(1, self.links.nz)]

    def take_direct(self, received):
        self.stack = jnp.concatenate([self.stack] + received, axis=0)
        self.masks = [self.links.mask_of("z", step) for step in range(self.links.nz)]


class Pieces:
    def __init__(self, where, near, far, matrices):
        self.where = where
        self.near = near
        self.far = far
        self.matrices = matrices
        self.slots = where.shape[0] - 2
        self.width = near[0].shape[-1]

    def rows(self, name):
        return self.matrices[name][2] * self.slots

    def arrays(self):
        return [*self.near, *self.far]

    def copies(self, name, where, parts, target, sems):
        half, first, count = self.matrices[name]
        near, far = parts[: len(self.near)], parts[len(self.near) :]
        pairs = []
        slot = 0
        for near_part, far_part in zip(near, far):
            for d in range(near_part.shape[0]):
                at = pl.multiple_of(where[2 + slot] * count, 8)
                room = target.at[pl.ds(at, count), :]
                rows = pl.ds(first, count)
                pairs.append(
                    (
                        pltpu.make_async_copy(near_part.at[d, rows, :], room, sems.at[slot]),
                        pltpu.make_async_copy(far_part.at[d, rows, :], room, sems.at[slot]),
                    )
                )
                slot += 1
        mine = where[0] == half

        def start():
            @pl.when(mine)
            def _():
                for pair in pairs:
                    pair[0].start()

            @pl.when(jnp.logical_not(mine))
            def _():
                for pair in pairs:
                    pair[1].start()

        def wait():
            for pair in pairs:
                pair[0].wait()

        return (start, wait)


class Room:
    def __init__(self):
        self.refs = {}
        self.waits = {}
        self.flushes = []
        self.pending = []

    def __getitem__(self, key):
        wait = self.waits.pop(key, None)
        if wait is not None:
            wait()
        return self.refs[key]

    def __getattr__(self, key):
        return self[key]

    def flush(self, *refs):
        rest = []
        for ref, copy in self.flushes:
            if any(ref is one for one in refs):
                copy.start()
                self.pending.append(copy)
            else:
                rest.append((ref, copy))
        self.flushes = rest

    def finish(self):
        self.flush(*[ref for ref, _copy in self.flushes])
        for copy in self.pending:
            copy.wait()


class Box(dict):
    __getattr__ = dict.__getitem__


class View:
    def __init__(self, room, names):
        self.room = room
        self.names = names

    def __getattr__(self, key):
        return self.room[self.names.get(key, key)]

    def flush(self, *refs):
        self.room.flush(*refs)


def renamed(stage, **names):
    def call(room):
        stage(View(room, names))

    call.__name__ = stage.__name__
    return call


HOLD, FETCH, SCALAR = range(3)


def run_kernel(stages, inputs, outputs, temps=(), weights=(), pinned=True):
    temps = dict(temps)
    operands, in_specs, scratch, plan = [], [], [], []

    def scratch_for(shape):
        scratch.append(shape)
        return len(scratch) - 1

    for key, (array, mode) in inputs.items():
        operands.append(array)
        if mode == HOLD:
            in_specs.append(pl.BlockSpec(memory_space=pltpu.VMEM))
            plan.append((key, mode, None))
        elif mode == SCALAR:
            in_specs.append(pl.BlockSpec(memory_space=pltpu.SMEM))
            plan.append((key, mode, None))
        else:
            operands[-1] = pltpu.with_memory_space_constraint(array, pltpu.HBM)
            in_specs.append(pl.BlockSpec(memory_space=pltpu.HBM))
            place = scratch_for(pltpu.VMEM(array.shape, array.dtype))
            plan.append((key, mode, (place, scratch_for(pltpu.SemaphoreType.DMA))))
    loads = []
    for pieces, names in weights:
        first = len(operands)
        operands.append(pieces.where)
        in_specs.append(pl.BlockSpec(memory_space=pltpu.SMEM))
        for array in pieces.arrays():
            if pinned:
                array = pltpu.with_memory_space_constraint(array, pltpu.HBM)
            operands.append(array)
            in_specs.append(pl.BlockSpec(memory_space=pltpu.HBM if pinned else pl.ANY))
        for matrix in names:
            place = scratch_for(pltpu.VMEM((pieces.rows(matrix), pieces.width), BF16))
            sems = scratch_for(pltpu.SemaphoreType.DMA((pieces.slots,)))
            loads.append((matrix, pieces, first, place, sems))
    out_specs, out_shapes, out_plan = [], [], []
    for key, (shape, dtype, mode) in outputs.items():
        if mode == HOLD:
            out_specs.append(pl.BlockSpec(memory_space=pltpu.VMEM))
            out_shapes.append(jax.ShapeDtypeStruct(shape, dtype))
            out_plan.append((key, None))
        else:
            out_specs.append(pl.BlockSpec(memory_space=pltpu.HBM))
            out_shapes.append(pltpu.HBM(shape, dtype))
            place = scratch_for(pltpu.VMEM(shape, dtype))
            out_plan.append((key, (place, scratch_for(pltpu.SemaphoreType.DMA))))
    temp_plan = [(key, scratch_for(shape)) for key, shape in temps.items()]

    def body(*refs):
        ins = refs[: len(operands)]
        outs = refs[len(operands) : len(operands) + len(out_specs)]
        rooms = refs[len(operands) + len(out_specs) :]
        room = Room()
        for ref, (key, mode, more) in zip(ins, plan):
            if mode == FETCH:
                place, sem = more
                copy = pltpu.make_async_copy(ref, rooms[place], rooms[sem])
                copy.start()
                room.refs[key] = rooms[place]
                room.waits[key] = copy.wait
            else:
                room.refs[key] = ref
        for matrix, pieces, first, place, sems in loads:
            where = ins[first]
            parts = ins[first + 1 : first + 1 + len(pieces.arrays())]
            start, wait = pieces.copies(matrix, where, parts, rooms[place], rooms[sems])
            start()
            room.refs[matrix] = rooms[place]
            room.waits[matrix] = wait
            room.refs.update(where=where)
        for ref, (key, more) in zip(outs, out_plan):
            if more is None:
                room.refs[key] = ref
            else:
                place, sem = more
                room.refs[key] = rooms[place]
                copy = pltpu.make_async_copy(rooms[place], ref, rooms[sem])
                room.flushes.append((rooms[place], copy))
        for key, place in temp_plan:
            room.refs[key] = rooms[place]
        for stage in stages:
            stage(room)
        for key in list(room.waits):
            room[key]
        room.finish()

    results = pl.pallas_call(
        body,
        name=stages[-1].__name__,
        in_specs=in_specs,
        out_specs=out_specs,
        out_shape=out_shapes,
        scratch_shapes=scratch,
        compiler_params=pltpu.CompilerParams(vmem_limit_bytes=VMEM_LIMIT),
    )(*operands)
    return Box(zip(outputs, results))


MASKED, COUNTED, VALID, KEEP = 0, 1, 2, 3


def column(room, index):
    return room.columns[:, index : index + 1]


def keep_of(room, block, branch):
    return column(room, KEEP + 2 * block + branch)


def vector(room, row):
    return room.vectors[row : row + 1, :]


def low_gates(room, block):
    return room.vectors[10 * block + 6 : 10 * block + 10, :].astype(BF16)


def correlate(padded, taps, level, flip):
    width = KERNEL_SIZES[level]
    first = KERNEL_STARTS[level]
    margin = width // 2
    lanes = padded.shape[-1]
    sums = [None] * GRID
    for dx in range(width):
        weights = []
        for dy in range(width):
            tap = dy * width + dx
            if flip:
                tap = width * width - 1 - tap
            weights.append(jnp.broadcast_to(taps[first + tap : first + tap + 1, :], (GRID, lanes)))
        for row in range(GRID):
            window = padded[row, 8 - margin + dx : 8 - margin + dx + GRID, :]
            for dy in range(width):
                out = row - dy + margin
                if 0 <= out < GRID:
                    term = window * weights[dy]
                    sums[out] = term if sums[out] is None else sums[out] + term
    return sums


def correlate_taps(padded, grads, d_taps, at_lanes, level):
    width = KERNEL_SIZES[level]
    first = KERNEL_STARTS[level]
    margin = width // 2
    for dx in range(width):
        sums = [None] * width
        for row in range(GRID):
            window = padded[row, 8 - margin + dx : 8 - margin + dx + GRID, :]
            for dy in range(width):
                out = row - dy + margin
                if 0 <= out < GRID:
                    term = window * grads[out]
                    sums[dy] = term if sums[dy] is None else sums[dy] + term
        for dy in range(width):
            tap = first + dy * width + dx
            d_taps[tap : tap + 1, at_lanes] = column_sum(sums[dy])


def clear_margins(padded):
    lanes = padded.shape[-1]
    for row in range(GRID):
        padded[row, 0:8, :] = jnp.zeros((8, lanes), F32)
        padded[row, 8 + GRID : 16 + GRID, :] = jnp.zeros((8, lanes), F32)


def rows_at(row):
    return slice(row * GRID, (row + 1) * GRID)


def gate_part(gates, row, level, lanes):
    part = gates[rows_at(row), level * LANES : (level + 1) * LANES]
    return part if lanes == LANES else part[:, 0:1]


def lane_range(group, groups, lanes):
    if groups == 1:
        return slice(0, lanes)
    return pl.ds(pl.multiple_of(group * lanes, lanes), lanes)


def tap_room(tap_count):
    return -(-tap_count // 8) * 8


def split_three(values):
    high = values.astype(BF16)
    rest = values - high.astype(F32)
    middle = rest.astype(BF16)
    return (high, middle, (rest - middle.astype(F32)).astype(BF16))


def pack_rows(here, sources, taps, parts):
    width = sources[0][0].shape[3]
    counts = [array.shape[2] // parts for array, _block in sources]
    rows = sum(counts) + (0 if taps is None else taps.shape[1])

    def body(here_ref, *refs):
        wide_refs = refs[: len(sources)]
        rest = refs[len(sources) :]
        out_ref = rest[0] if taps is None else rest[1]
        buffers = rest[-1 - len(sources) : -1]
        sems = rest[-1]
        copies = []
        for at, (ref, (_array, block)) in enumerate(zip(wide_refs, sources)):
            source = ref.at[block, here_ref[0]]
            if parts > 1:
                first = pl.multiple_of(here_ref[2] * counts[at], 8)
                source = source.at[pl.ds(first, counts[at]), :]
            copies.append(pltpu.make_async_copy(source, buffers[at], sems.at[at]))
            copies[-1].start()
        row = sum(counts)
        if taps is not None:
            own, count = taps.shape[1:]
            out_ref[row : row + own, :] = jnp.zeros((own, width), BF16)
            splits = [split_three(rest[0][b]) for b in range(BLOCKS)]
            wide = (splits[0][0], splits[1][0], splits[0][1])
            thin = (splits[1][1], splits[0][2], splits[1][2])
            for chosen, at_core in ((wide, 0), (thin, 1)):

                @pl.when(here_ref[0] == at_core)
                def _():
                    for index, part in enumerate(chosen):
                        at = index * LANES
                        out_ref[row : row + own, at : at + count] = part

        row = 0
        for copy, buffer, count in zip(copies, buffers, counts):
            copy.wait()
            out_ref[row : row + count, :] = buffer[...].astype(BF16)
            row += count

    extra = [] if taps is None else [taps]
    return pl.pallas_call(
        body,
        name=pack_rows.__name__,
        in_specs=[pl.BlockSpec(memory_space=pltpu.SMEM)]
        + [pl.BlockSpec(memory_space=pltpu.HBM) for _ in sources]
        + [pl.BlockSpec(memory_space=pltpu.VMEM) for _ in extra],
        out_specs=pl.BlockSpec(memory_space=pltpu.VMEM),
        out_shape=jax.ShapeDtypeStruct((rows, width), BF16),
        scratch_shapes=[pltpu.VMEM((count, width), F32) for count in counts]
        + [pltpu.SemaphoreType.DMA((len(sources),))],
        compiler_params=pltpu.CompilerParams(vmem_limit_bytes=VMEM_LIMIT),
    )(
        here,
        *[pltpu.with_memory_space_constraint(array, pltpu.HBM) for array, _block in sources],
        *extra,
    )


def taps_stage(tap_count, groups, lanes):
    room_rows = tap_room(tap_count)
    used = BLOCKS * room_rows

    def join_taps(room):
        wide = room.wide[...]
        thin = room.thin[...]
        shape = (used, wide.shape[1])
        row = lax.broadcasted_iota(jnp.int32, shape, 0)
        lane = lax.broadcasted_iota(jnp.int32, shape, 1)
        upper = row >= room_rows
        tap = jnp.where(upper, row - room_rows, row)
        tap = jnp.where(tap < tap_count, tap, -8 * LANES)

        def chosen(lower_places, upper_places):
            marks = jnp.zeros(shape, F32)
            for places, side in ((lower_places, False), (upper_places, True)):
                for place in places:
                    hit = jnp.logical_and(lane == tap + place * LANES, upper == side)
                    marks = jnp.where(hit, 1.0, marks)
            return marks.astype(BF16)

        taps = times_transposed(chosen((0, 2), (1,)), wide)
        taps = taps + times_transposed(chosen((1,), (0, 2)), thin)
        for b in range(BLOCKS):
            for j in range(groups):
                room.taps[b, j] = taps[
                    b * room_rows : (b + 1) * room_rows, j * lanes : (j + 1) * lanes
                ]

    return join_taps


def inputs_stage(block, groups, lanes):
    def focal_inputs(room):
        unit, _scale = normalize(room.x[...])
        first = unit * vector(room, 10 * block) + vector(room, 10 * block + 1)
        first = first.astype(BF16)
        width = first.shape[1]
        gate_low = low_gates(room, block)
        for level in range(4):
            spread = jnp.broadcast_to(gate_low[level : level + 1], (LANES, width))
            room.gates[:, level * LANES : (level + 1) * LANES] = times_transposed(
                first, spread
            )
        key = room.key
        for j in range(groups):
            room.context[j] = times_transposed(first, key[j * lanes : (j + 1) * lanes, :])
        room.query_out[...] = times_transposed(first, room.query[...])
        room.flush(room.gates, room.context, room.query_out)

    return focal_inputs


def focal_stage(block, groups, lanes):
    def focal_levels(room):
        padded = room.padded
        taps, context, gates, low, pool = room.taps, room.context, room.gates, room.low, room.pool
        fields = [room.k1, room.k2, room.k3]
        slopes = [room.s1, room.s2, room.s3]
        clear_margins(padded)
        valid = room.image_columns[:, VALID : VALID + 1]
        valid_total = column_sum(valid)

        def group(j, carry):
            tap = taps.at[block, j]
            for row in range(GRID):
                padded[row, 8 : 8 + GRID, :] = context[j, rows_at(row), :]
            for level in range(3):
                sums = correlate(padded, tap, level, False)
                for row in range(GRID):
                    value, slope = gelu_pair(sums[row])
                    fields[level][j, rows_at(row), :] = value
                    slopes[level][j, rows_at(row), :] = slope
                    if level < 2:
                        padded[row, 8 : 8 + GRID, :] = value
            mean = column_sum(fields[2][j] * valid) / valid_total
            pooled, pooled_slope = gelu_pair(mean)
            pool[j, 0:1, :] = pooled
            pool[j, 1:2, :] = pooled_slope / valid_total
            pool[j, 2:8, :] = jnp.zeros((6, lanes), F32)
            at = lane_range(j, groups, lanes)
            for row in range(GRID):
                summed = pooled * gate_part(gates, row, 3, lanes)
                for level in range(3):
                    summed = summed + fields[level][j, rows_at(row), :] * gate_part(
                        gates, row, level, lanes
                    )
                low[rows_at(row), at] = summed.astype(BF16)
            return carry

        if groups > 1:
            lax.fori_loop(0, groups, group, 0)
        else:
            group(0, 0)
        room.flush(room.k1, room.k2, room.k3, room.s1, room.s2, room.s3, room.pool, room.low)

    return focal_levels


def mix_stage(block):
    def mix_forward(room):
        modulator = times_transposed(room.low[...], room.mix[...])
        room.mod[...] = modulator
        room.flush(room.mod)
        product = (room.query_out[...] * modulator).astype(BF16)
        branch = matmul(product, room.proj[...]) + vector(room, 10 * block + 4)
        room.middle[...] = room.x[...] + keep_of(room, block, 0) * branch

    return mix_forward


def mlp_stage(block):
    def mlp_forward(room):
        middle = room.middle[...]
        unit, _scale = normalize(middle)
        second = unit * vector(room, 10 * block + 2) + vector(room, 10 * block + 3)
        second = second.astype(BF16)
        up = room.up
        step = up.shape[0] // 4
        for part in range(4):
            at = slice(part * step, (part + 1) * step)
            value, slope = gelu_pair(times_transposed(second, up[at, :]))
            room.hidden[:, at] = value.astype(BF16)
            room.slope[:, at] = slope
        room.flush(room.hidden, room.slope)
        lowered = matmul(room.hidden[...], room.down[...]) + vector(room, 10 * block + 5)
        room.out[...] = middle + keep_of(room, block, 1) * lowered

    return mlp_forward


def embed_stage(room):
    outer = 10 * BLOCKS
    embedded = matmul(room.patches[...], room.embed[...].astype(BF16))
    embedded = embedded + vector(room, outer)
    room.embedded[...] = embedded
    room.flush(room.embedded)
    unit, _scale = normalize(embedded)
    mask = column(room, MASKED)
    state = unit * vector(room, outer + 1) + vector(room, outer + 2)
    room.x[...] = state * (1.0 - mask) + vector(room, outer + 5) * mask


def store_halves(core, kept, sent, at, first, second):
    chan, _rows, width = kept.shape
    rows = first.shape[0] // chan
    first = first.reshape(chan, rows, width).astype(BF16)
    second = second.reshape(chan, rows, width).astype(BF16)

    @pl.when(core == 0)
    def _():
        kept[:, at : at + rows, :] = first
        sent[:, at : at + rows, :] = second

    @pl.when(core != 0)
    def _():
        kept[:, at : at + rows, :] = second
        sent[:, at : at + rows, :] = first


def head_stage(room):
    outer = 10 * BLOCKS
    gain = vector(room, outer + 3)
    unit, scale = normalize(room.x[...])
    low = (unit * gain + vector(room, outer + 4)).astype(BF16)
    head_low = room.head[...].astype(BF16)
    error = matmul(low, head_low) - room.patches[...].astype(F32)
    denom = room.denom[0, 0]
    weighted = column(room, COUNTED) * error
    loss = column_sum(jnp.sum(weighted * error, axis=-1, keepdims=True)) / denom
    d_pred = (2.0 * weighted / denom).astype(BF16)
    grad = contract_rows(low, d_pred)
    half = grad.shape[1] // 2
    core = room.where[0]
    store_halves(core, room.kept, room.sent, 0, grad[:, :half], grad[:, half:])
    room.flush(room.kept, room.sent)
    d_final = times_transposed(d_pred, head_low)
    room.d_out[...] = norm_backward(d_final, unit, scale, gain)
    sums = room.sums
    width = low.shape[1]
    sums[0:1, :] = column_sum(d_final * unit)
    sums[1:2, :] = column_sum(d_final)
    sums[2:3, :] = jnp.broadcast_to(loss, (1, width))
    sums[3:8, :] = jnp.zeros((5, width), F32)


def mlp_back_stage(block):
    def mlp_backward(room):
        d_residual = room.d_in[...]
        d_down = d_residual * keep_of(room, block, 1)
        d_low = d_down.astype(BF16)
        unit, scale = normalize(room.middle[...])
        gain = vector(room, 10 * block + 2)
        second = (unit * gain + vector(room, 10 * block + 3)).astype(BF16)
        grad_down = contract_rows(room.hidden[...], d_low)
        d_pre = (times_transposed(d_low, room.down[...]) * room.slope[...]).astype(BF16)
        grad_up = contract_rows(d_pre, second)
        core = room.where[0]
        store_halves(core, room.kept, room.sent, 0, grad_up, grad_down)
        room.flush(room.sent, room.kept)
        d_second = matmul(d_pre, room.up[...])
        room.d_out[...] = d_residual + norm_backward(d_second, unit, scale, gain)
        sums = room.sums
        width = d_low.shape[1]
        sums[0:1, :] = column_sum(d_second * unit)
        sums[1:2, :] = column_sum(d_second)
        sums[2:3, :] = column_sum(d_down)
        sums[3:8, :] = jnp.zeros((5, width), F32)

    return mlp_backward


def mix_back_stage(block, groups, lanes):
    def mix_backward(room):
        d_proj = room.d_in[...] * keep_of(room, block, 0)
        d_low = d_proj.astype(BF16)
        d_product = times_transposed(d_low, room.proj[...])
        modulator = room.mod[...]
        query = room.query_out[...]
        d_mod = (d_product * query).astype(BF16)
        mix = room.mix
        for j in range(groups):
            room.d_sum[j] = matmul(d_mod, mix[:, j * lanes : (j + 1) * lanes])
        room.d_query[...] = (d_product * modulator).astype(BF16)
        product = (query * modulator).astype(BF16)
        grad_proj = contract_rows(product, d_low)
        grad_mix = contract_rows(d_mod, room.low[...])
        core = room.where[0]
        store_halves(core, room.kept, room.sent, 0, grad_mix, grad_proj)
        sums = room.sums
        width = d_low.shape[1]
        sums[0:1, :] = column_sum(d_proj)
        sums[1:8, :] = jnp.zeros((7, width), F32)

    return mix_backward


def focal_back_stage(block, groups, lanes):
    def levels_backward(room):
        padded = room.padded
        d_padded = room.d_padded
        clear_margins(padded)
        clear_margins(d_padded)
        d_all, gates, taps, pool = room.d_sum, room.gates, room.taps, room.pool
        fields = [room.context, room.k1, room.k2, room.k3]
        slopes = [room.s1, room.s2, room.s3]
        d_context, d_gates, d_taps = room.d_context, room.d_gates, room.d_taps
        valid = room.image_columns[:, VALID : VALID + 1]
        d_gates[...] = jnp.zeros(d_gates.shape, F32)
        d_taps[...] = jnp.zeros(d_taps.shape, F32)

        def fold(values):
            if lanes == LANES:
                return values
            summed = jnp.sum(values, axis=-1, keepdims=True) / LANES
            return jnp.broadcast_to(summed, (values.shape[0], LANES))

        def group(j, carry):
            tap = taps.at[block, j]
            at = lane_range(j, groups, lanes)
            d_pooled = jnp.zeros((1, lanes), F32)
            for row in range(GRID):
                d_pooled = d_pooled + column_sum(
                    d_all[j, rows_at(row), :] * gate_part(gates, row, 3, lanes)
                )
            d_mean = d_pooled * pool[j, 1:2, :]
            d_field = [d_mean * valid[rows_at(row)] for row in range(GRID)]
            for level in (2, 1, 0):
                d_pre = []
                for row in range(GRID):
                    here = rows_at(row)
                    grad = d_field[row] + d_all[j, here, :] * gate_part(gates, row, level, lanes)
                    grad = grad * slopes[level][j, here, :]
                    d_pre.append(grad)
                    d_padded[row, 8 : 8 + GRID, :] = grad
                    padded[row, 8 : 8 + GRID, :] = fields[level][j, here, :]
                correlate_taps(padded, d_pre, d_taps, at, level)
                d_field = correlate(d_padded, tap, level, True)
            for row in range(GRID):
                d_context[rows_at(row), at] = d_field[row].astype(BF16)
            whole = d_all[j]
            for level in range(3):
                here = slice(level * LANES, (level + 1) * LANES)
                d_gates[:, here] = d_gates[:, here] + fold(whole * fields[level + 1][j])
            here = slice(3 * LANES, 4 * LANES)
            d_gates[:, here] = d_gates[:, here] + fold(whole * pool[j, 0:1, :])
            return carry

        if groups > 1:
            lax.fori_loop(0, groups, group, 0)
        else:
            group(0, 0)
        room.flush(room.d_taps)

    return levels_backward


def inputs_back_stage(block):
    def inputs_backward(room):
        unit, scale = normalize(room.x[...])
        gain = vector(room, 10 * block)
        first_wide = (unit * gain + vector(room, 10 * block + 1)).astype(BF16)
        first = first_wide
        first_wide = first.astype(F32)
        rows, width = first.shape
        gate_low = low_gates(room, block).astype(F32)
        sums = room.input_sums
        sums[...] = jnp.zeros((8, width), F32)
        d_first = jnp.zeros((rows, width), F32)
        d_gates = room.d_gates
        for level in range(4):
            here = slice(level * LANES, (level + 1) * LANES)
            col = jnp.sum(d_gates[:, here], axis=-1, keepdims=True)
            d_first = d_first + col * gate_low[level : level + 1]
            sums[2 + level : 3 + level, :] = column_sum(col * first_wide)
        d_query = room.d_query[...]
        d_context = room.d_context[...]
        d_first = d_first + matmul(d_query, room.query[...])
        d_first = d_first + matmul(d_context, room.key[...])
        room.d_out[...] = room.d_in[...] + norm_backward(d_first, unit, scale, gain)
        sums[0:1, :] = column_sum(d_first * unit)
        sums[1:2, :] = column_sum(d_first)
        grad_query = contract_rows(d_query, first)
        grad_key = contract_rows(d_context, first)
        kept, sent = room.kept, room.sent
        core = room.where[0]
        store_halves(core, kept, sent, 0, grad_query, grad_key)
        at = width // kept.shape[0]
        kept[:, at : 2 * at, :] = room.more_kept[...]
        sent[:, at : 2 * at, :] = room.more_sent[...]

    return inputs_backward


def sums_start(tap_count):
    return BLOCKS * tap_room(tap_count)


def small_rows_for(tap_count, chan):
    used = sums_start(tap_count) + 8 * (2 + 3 * BLOCKS)
    return -(-used // (16 * chan)) * (16 * chan)


def embed_back_stage(tap_count, sum_keys, tap_keys, first_row):
    outer = 10 * BLOCKS

    def embed_backward(room):
        mask = column(room, MASKED)
        d_residual = room.d_out[...]
        d_start = d_residual * (1.0 - mask)
        unit, scale = normalize(room.embedded[...])
        d_embed = norm_backward(d_start, unit, scale, vector(room, outer + 1))
        small = room.small
        small[...] = jnp.zeros(small.shape, F32)
        for b, key in enumerate(tap_keys):
            at = b * tap_room(tap_count)
            taps = room.d_taps if key is None else room[key]
            small[at : at + taps.shape[0], :] = taps[...]
        at = sums_start(tap_count)
        small[at : at + 1, :] = column_sum(d_embed)
        small[at + 1 : at + 2, :] = column_sum(d_start * unit)
        small[at + 2 : at + 3, :] = column_sum(d_start)
        small[at + 3 : at + 4, :] = column_sum(d_residual * mask)
        for key in sum_keys:
            at += 8
            sums = room.input_sums if key is None else room[key]
            small[at : at + 8, :] = sums[...]
        grad = contract_rows(room.patches[...], d_embed.astype(BF16))
        core = room.where[0]
        kept, sent = room.kept, room.sent
        half = grad.shape[0] // 2
        row = first_row
        store_halves(core, kept, sent, row, grad[:half], grad[half:])
        row += half // kept.shape[0]
        half = small.shape[0] // 2
        store_halves(core, kept, sent, row, small[:half], small[half:])

    return embed_backward


def update_head_stage(rate):
    def update_head(room):
        half = room.weight.shape[1] // 2
        for index in range(2):
            here = slice(index * half, (index + 1) * half)
            new_weight, new_moment = nesterov(
                room.weight[:, here],
                room.moment[:, here],
                (room.head0, room.head1)[index][...].astype(F32),
                rate,
            )
            room.new_weight[:, here] = new_weight
            room.new_moment[:, here] = new_moment

    return update_head


def update_shared_stage(tap_count, own, rate):
    def update_shared(room):
        half = room.embed0.shape[0]
        for index in range(2):
            here = slice(index * half, (index + 1) * half)
            gradient = (room.embed0, room.embed1)[index][...].astype(F32)
            new_weight, new_moment = nesterov(
                room.weight[here, :], room.moment[here, :], gradient, rate
            )
            room.new_weight[here, :] = new_weight
            room.new_moment[here, :] = new_moment
        room.flush(room.new_weight, room.new_moment)
        small = jnp.concatenate([room.small0[...], room.small1[...]], axis=0)
        grads = small.astype(F32)
        width = small.shape[1]

        def sum_row(index, row):
            at = sums_start(tap_count) + 8 * index + row
            return grads[at : at + 1]

        rows = []
        for b in range(BLOCKS):
            inputs_at, mlp_at, mix_at = 1 + 3 * b, 2 + 3 * b, 3 + 3 * b
            rows += [sum_row(inputs_at, 0), sum_row(inputs_at, 1)]
            rows += [sum_row(mlp_at, 0), sum_row(mlp_at, 1)]
            rows += [sum_row(mix_at, 0), sum_row(mlp_at, 2)]
            rows += [sum_row(inputs_at, 2 + level) for level in range(4)]
        head_at = 1 + 3 * BLOCKS
        rows += [sum_row(0, 0), sum_row(0, 1), sum_row(0, 2)]
        rows += [sum_row(head_at, 0), sum_row(head_at, 1), sum_row(0, 3)]
        packed = room.packed
        for at, row in enumerate(rows):
            packed[at : at + 1, :] = row
        gradient = packed[0 : len(rows), :]
        new_weight, new_moment = nesterov(
            room.vectors[...], room.vector_moment[...], gradient, rate
        )
        room.new_vectors[...] = new_weight
        room.new_vector_moment[...] = new_moment
        room.new_vector_average[...] = (
            AVERAGE * room.vector_average[...] + (1.0 - AVERAGE) * new_weight
        )
        room.loss[...] = sum_row(head_at, 2)[:, 0:LANES]
        first = room.where[1] * own
        source = lax.broadcasted_iota(jnp.int32, (own, width), 1)
        wanted = first + lax.broadcasted_iota(jnp.int32, (own, width), 0)
        chosen = (source == wanted).astype(F32).astype(BF16)
        for b in range(BLOCKS):
            at = b * tap_room(tap_count)
            gradient = times_transposed(chosen, small[at : at + tap_room(tap_count)])
            gradient = gradient[:, :tap_count]
            new_weight, new_moment = nesterov(
                room.kernels[b], room.kernel_moment[b], gradient, rate
            )
            room.new_kernels[b] = new_weight
            room.new_kernel_moment[b] = new_moment
            room.new_kernel_average[b] = (
                AVERAGE * room.kernel_average[b] + (1.0 - AVERAGE) * new_weight
            )

    return update_shared


class Shares:
    def __init__(self, local_rows, chan_size):
        self.count = max(1, IMAGE_ROWS // local_rows)
        self.groups = [
            list(range(first, first + self.count)) for first in range(0, chan_size, self.count)
        ]

    def to_images(self, values):
        whole = lax.all_to_all(
            values[0], "chan", 1, 0, axis_index_groups=self.groups, tiled=True
        )
        return whole[None]

    def to_rows(self, values):
        return lax.all_to_all(values, "chan", 0, 1, axis_index_groups=self.groups, tiled=True)

    def all_rows(self, values):
        return lax.all_gather(
            values, "chan", axis=0, axis_index_groups=self.groups, tiled=True
        )

    def sum_rows(self, values):
        return lax.psum_scatter(
            values, "chan", scatter_dimension=0, axis_index_groups=self.groups, tiled=True
        )

    def channels(self, values):
        size = values.shape[-1] // self.count
        place = lax.axis_index("chan") % self.count
        return lax.dynamic_slice_in_dim(values, place * size, size, values.ndim - 1)

    def spread(self, values):
        size = values.shape[1]
        place = lax.axis_index("chan") % self.count
        whole = jnp.zeros((values.shape[0], size * self.count), values.dtype)
        return lax.dynamic_update_slice_in_dim(whole, values, place * size, 1)


def hold(array):
    return (array, HOLD)


def fetch(array):
    return (array, FETCH)


def fetch_all(made, names):
    return {name: fetch(made[name]) for name in names}


def shards(
    patches,
    valid_mask,
    target_mask,
    keep_mask,
    embed_weight,
    embed_moment,
    head_weight,
    head_moment,
    vectors,
    vector_moment,
    vector_average,
    focal_input,
    focal_moment,
    focal_average,
    mixers,
    mixer_moment,
    mixer_average,
    mlp_weights,
    mlp_moment,
    mlp_average,
    kernels,
    kernel_moment,
    kernel_average,
):
    links = Links()
    rows, patch_in = patches.shape
    group_rows = valid_mask.shape[0]
    own = focal_input.shape[-1]
    own_hidden = mlp_weights.shape[-1]
    hidden_width = own_hidden * links.chan
    tap_count = kernels.shape[1]
    width = vectors.shape[1]
    shares = Shares(rows, links.chan)
    shared = shares.count > 1
    channels = width // shares.count
    lanes = LANES if channels % LANES == 0 else channels
    groups = channels // lanes
    room_rows = tap_room(tap_count)
    split_x = own_hidden % (8 * links.nx) == 0 and links.nx > 1

    def together(values, moves):
        got = [links.swap(*move) for move in moves]
        return lax.optimization_barrier((values, got))

    def beside(call, gate, moves):
        made = call(after(gate, *[move[0] for move in moves]))
        made, got = together(dict(made), moves)
        return (Box(made), got)

    here = links.here()
    focal_rows = jnp.transpose(focal_input, (0, 2, 3, 1))
    mixer_rows = jnp.transpose(mixers, (0, 1, 3, 2))
    mlp_rows = jnp.transpose(mlp_weights, (0, 1, 3, 2))
    kernel_rows = jnp.transpose(kernels, (0, 2, 1))
    focal_layout = dict(
        query=(0, 0, own), mix=(0, own, own), key=(1, 0, own), proj=(1, own, own)
    )
    first_layout = dict(focal_layout, wide=(0, 2 * own, own), thin=(1, 2 * own, own))

    def mlp_layout(count):
        return dict(up=(0, 0, count), down=(1, 0, count))

    first_row = links.place * rows
    validity = valid_mask.astype(F32)
    masked = target_mask.astype(F32)
    keep_rows = jnp.repeat(
        keep_mask.reshape(keep_mask.shape[0], -1).astype(F32) / KEEP_RATE, IMAGE_ROWS, axis=0
    )
    table = jnp.concatenate(
        [
            masked[:, None],
            (masked * validity)[:, None],
            validity[:, None],
            keep_rows,
            jnp.zeros((group_rows, 1), F32),
        ],
        axis=1,
    )
    columns = lax.dynamic_slice_in_dim(table, first_row, rows)
    image_columns = columns
    if shared:
        image_columns = lax.dynamic_slice_in_dim(
            table, first_row // IMAGE_ROWS * IMAGE_ROWS, IMAGE_ROWS
        )
    group_count = jnp.broadcast_to(jnp.sum(validity * masked), (8, LANES))
    basic = dict(vectors=fetch(vectors), columns=fetch(columns))
    grid_columns = dict(image_columns=fetch(image_columns))

    whole = (rows, width)
    focal = [None] * BLOCKS
    mlp = [None] * BLOCKS
    focal[0] = Gather(
        links, pack_rows(here, [(focal_rows, 0), (mixer_rows, 0)], kernel_rows, 1)
    )
    moves = focal[0].direct()
    embedded = run_kernel(
        [embed_stage],
        dict(patches=fetch(patches), embed=fetch(embed_weight), **basic),
        dict(x=(whole, F32, HOLD), embedded=(whole, F32, FETCH)),
    )
    parts_x = links.nx if split_x else 1
    packed = pack_rows(here, [(mlp_rows, 0)], None, parts_x)
    (x, packed), got = together((embedded.x, packed), moves)
    focal[0].take_direct(got)
    mlp[0] = Gather(links, packed)
    z_first, *z_rest = links.bits("z")
    y_move = focal[0].early("y")
    (move,) = mlp[0].moves("z", z_first)
    packed = (
        pack_rows(here, [(focal_rows, 1), (mixer_rows, 1)], None, 1),
        pack_rows(here, [(mlp_rows, 1)], None, 1),
    )
    packed, got = together(packed, [move])
    mlp[0].take(got[0], "z", z_first)
    focal[1] = Gather(links, packed[0])
    mlp[1] = Gather(links, packed[1])

    def take_z(gather, received):
        for step, one in zip(z_rest, received):
            gather.take(one, "z", step)

    moves = [(mlp[0].stack, "z", step) for step in z_rest]
    moves += [(focal[0].stack, *y_move), (focal[1].stack, "z", z_first)]
    moves += [(group_count, "core", 1)]
    x, got = together(x, moves)
    take_z(mlp[0], got[:-3])
    focal[0].take(got[-3], *y_move, True)
    focal[1].take(got[-2], "z", z_first)
    group_count = group_count + got[-1]

    def twins(gather, values):
        values, got = together(values, [(part, "core", 1) for part in gather.parts])
        return (values, got)

    def pieces_of(gather, far, layout, split):
        return Pieces(links.slots(gather.masks, split), gather.parts, far, layout)

    y_move = mlp[0].early("y")
    x, far = twins(focal[0], after(x, mlp[0].stack, group_count))
    focal_pieces = [pieces_of(focal[0], far, first_layout, False), None]
    mlp_pieces = [None, None]

    field_shape = (groups, IMAGE_ROWS, lanes)
    field = (field_shape, F32, FETCH)
    padded = pltpu.VMEM((GRID, GRID + 16, lanes), F32)
    gates_out = dict(gates=((IMAGE_ROWS, 4 * LANES), F32, FETCH))
    focal_out = dict(k1=field, k2=field, k3=field, s1=field, s2=field, s3=field)
    focal_out.update(pool=((groups, 8, lanes), F32, FETCH))
    mixed_out = dict(mod=(whole, F32, FETCH), middle=(whole, F32, HOLD))
    query_out = dict(query_out=(whole, F32, FETCH))
    low_out = dict(low=(whole, BF16, FETCH))
    mlp_out = dict(
        hidden=((rows, hidden_width), BF16, FETCH), slope=((rows, hidden_width), F32, FETCH)
    )
    weights_in = dict(key=0, query=0, mix=0, proj=0)
    up_down = dict(up=0, down=0)
    taps_shape = (BLOCKS, groups, room_rows, lanes)

    def focal_apart(b, x, taps):
        pieces = focal_pieces[b]
        made = run_kernel(
            [inputs_stage(b, 1, width)],
            dict(x=hold(x), **basic),
            dict(
                gates=((rows, 4 * LANES), F32, FETCH),
                context=((1, rows, width), F32, FETCH),
                **query_out,
            ),
            {},
            [(pieces, dict(key=0, query=0))],
        )
        made.update(gates=shares.all_rows(made.gates), context=shares.to_images(made.context))
        made.update(
            run_kernel(
                [focal_stage(b, groups, lanes)],
                dict(
                    context=fetch(made.context),
                    gates=fetch(made.gates),
                    taps=fetch(taps),
                    **grid_columns,
                ),
                dict(low=((IMAGE_ROWS, channels), BF16, FETCH), **focal_out),
                dict(padded=padded),
            )
        )
        made.update(low=shares.to_rows(made.low))
        made.update(
            run_kernel(
                [mix_stage(b)],
                dict(
                    x=hold(x), low=fetch(made.low), query_out=fetch(made.query_out), **basic
                ),
                mixed_out,
                {},
                [(pieces, dict(mix=0, proj=0))],
            )
        )
        return made

    def focal_stages(b):
        return [inputs_stage(b, groups, lanes), focal_stage(b, groups, lanes), mix_stage(b)]

    focal_made_out = dict(
        context=field, **gates_out, **query_out, **focal_out, **low_out, **mixed_out
    )

    def first_focal(x):
        if shared:
            taps = run_kernel(
                [taps_stage(tap_count, 1, width)],
                {},
                dict(taps=((BLOCKS, 1, room_rows, width), F32, FETCH)),
                {},
                [(focal_pieces[0], dict(wide=0, thin=0))],
            ).taps
            taps = shares.channels(taps)
            return Box(focal_apart(0, x, taps), taps=taps)
        return run_kernel(
            [taps_stage(tap_count, groups, lanes)] + focal_stages(0),
            dict(x=hold(x), **basic, **grid_columns),
            dict(taps=(taps_shape, F32, FETCH), **focal_made_out),
            dict(padded=padded),
            [(focal_pieces[0], dict(wide=0, thin=0, **weights_in))],
            False,
        )

    moves = [(mlp[0].stack, *y_move)]
    moves += [(focal[1].stack, "z", step) for step in z_rest[:1]]
    moves += [(mlp[1].stack, "z", z_first)]
    x_first, *x_rest = links.bits("x")
    moves += [(group_count, "x", x_first)]
    saved = [Box(x=x), Box()]
    made, got = beside(first_focal, x, moves)
    saved[0].update(made)
    taps = made.taps
    mlp[0].take(got[0], *y_move, not split_x)
    take_z(focal[1], got[1:-2])
    mlp[1].take(got[-2], "z", z_first)
    counted = group_count + got[-1]
    for step in x_rest:
        counted = counted + links.swap(counted, "x", step)
    denominator = counted[0:1, 0:1] * PATCH_IN
    y_move = focal[1].early("y")
    moves = [(focal[1].stack, *y_move)]
    moves += [(mlp[1].stack, "z", step) for step in z_rest]
    if split_x:
        x_move = mlp[0].early("x")
        moves += [(mlp[0].stack, *x_move)]
    middle, got = together(saved[0].middle, moves)
    focal[1].take(got[0], *y_move, True)
    take_z(mlp[1], got[1 : 1 + len(z_rest)])
    if split_x:
        mlp[0].take(got[-1], *x_move, True)
    y_move = mlp[1].early("y")
    moves = [(part, "core", 1) for part in mlp[0].parts + focal[1].parts]
    middle, got = together(after(middle, mlp[1].stack), moves)
    mlp_pieces[0] = pieces_of(mlp[0], got[:2], mlp_layout(own_hidden // parts_x), split_x)
    focal_pieces[1] = pieces_of(focal[1], got[2:], focal_layout, False)

    def second_focal(middle):
        inputs = dict(middle=hold(middle), **basic)
        outputs = dict(out=(whole, F32, FETCH), **mlp_out)
        if shared:
            made = run_kernel(
                [mlp_stage(0)], inputs, outputs, {}, [(mlp_pieces[0], up_down)]
            )
            lower = Box(hidden=made.hidden, slope=made.slope)
            return Box(focal_apart(1, made.out, taps), x=made.out, lower=dict(lower))
        made = run_kernel(
            [renamed(mlp_stage(0), middle=0, out=1)]
            + [renamed(stage, x=1) for stage in focal_stages(1)],
            {0: hold(middle), **basic, **grid_columns, **dict(taps=fetch(taps))},
            {1: (whole, F32, FETCH), **mlp_out, **focal_made_out},
            dict(padded=padded),
            [(mlp_pieces[0], up_down), (focal_pieces[1], weights_in)],
        )
        lower = dict(hidden=made.hidden, slope=made.slope)
        upper = Box({key: made[key] for key in focal_made_out})
        upper.update(x=made[1], lower=lower)
        return upper

    made, got = beside(second_focal, middle, [(mlp[1].stack, *y_move)])
    mlp[1].take(got[0], *y_move, True)
    saved[0].update(made.lower)
    saved[1].update(made)
    middle, far = twins(mlp[1], saved[1].middle)
    mlp_pieces[1] = pieces_of(mlp[1], far, mlp_layout(own_hidden), False)

    sums_out = ((8, width), F32, FETCH)
    head_part = (links.chan, patch_in // (2 * links.chan), width)
    hidden_part = (links.chan, own_hidden, width)
    own_part = (links.chan, own, width)
    made = run_kernel(
        [
            renamed(mlp_stage(1), out=0),
            renamed(head_stage, x=0, d_out=1, kept=2, sent=3, sums=4),
            renamed(mlp_back_stage(1), d_in=1),
        ],
        {
            **dict(middle=hold(middle), patches=fetch(patches), head=fetch(head_weight)),
            **dict(denom=(denominator, SCALAR), **basic),
        },
        {
            2: (head_part, BF16, HOLD),
            3: (head_part, BF16, HOLD),
            4: sums_out,
            **dict(
                d_out=(whole, F32, HOLD),
                kept=(hidden_part, BF16, HOLD),
                sent=(hidden_part, BF16, HOLD),
                sums=sums_out,
            ),
        },
        {
            0: pltpu.VMEM(whole, F32),
            1: pltpu.VMEM(whole, F32),
            **dict(
                hidden=pltpu.VMEM((rows, hidden_width), BF16),
                slope=pltpu.VMEM((rows, hidden_width), F32),
            ),
        },
        [(mlp_pieces[1], up_down)],
    )
    head_sums = made[4]
    sums = [[None] * 3 for _ in range(BLOCKS)]
    sums[1][1] = made.sums
    d_middle = made.d_out
    embed_rows = patch_in // (2 * links.chan)
    small_rows = small_rows_for(tap_count, links.chan)

    def mix_back(b, d_middle):
        shape = (1, rows, width) if shared else field_shape
        return run_kernel(
            [mix_back_stage(b, shape[0], shape[2])],
            dict(
                d_in=hold(d_middle),
                **fetch_all(saved[b], dict(query_out=0, mod=0, low=0)),
                **basic,
            ),
            dict(
                d_query=(whole, BF16, HOLD),
                d_sum=(shape, F32, HOLD),
                kept=(own_part, BF16, HOLD),
                sent=(own_part, BF16, HOLD),
                sums=sums_out,
            ),
            {},
            [(focal_pieces[b], dict(proj=0, mix=0))],
        )

    def focal_back(b, d_sum, d_middle, mixed):
        final = b == 0
        kept = saved[b]
        names = dict(context=0, gates=0, k1=0, k2=0, k3=0, s1=0, s2=0, s3=0, pool=0)
        levels_in = dict(taps=fetch(taps), **fetch_all(kept, names), **grid_columns)
        levels_temps = dict(padded=padded, d_padded=padded)
        inputs = dict(
            d_in=hold(d_middle),
            d_query=hold(mixed.d_query),
            x=fetch(kept.x),
            more_kept=hold(mixed.kept),
            more_sent=hold(mixed.sent),
            **basic,
        )
        part_rows = 2 * own
        if final:
            part_rows += embed_rows + small_rows // (2 * links.chan)
        part = (links.chan, part_rows, width)
        outputs = dict(kept=(part, BF16, HOLD), sent=(part, BF16, HOLD))
        temps = {}
        stages = [inputs_back_stage(b)]
        if final:
            sum_keys = [None]
            for c in range(BLOCKS):
                for kind in range(3):
                    if sums[c][kind] is not None:
                        key = 3 * c + kind
                        sum_keys.append(key)
                        inputs[key] = fetch(sums[c][kind])
            head_key, taps_key = 3 * BLOCKS, 3 * BLOCKS + 1
            inputs[head_key] = fetch(head_sums)
            inputs[taps_key] = fetch(d_taps)
            sum_keys.append(head_key)
            inputs.update(patches=fetch(patches), embedded=fetch(embedded.embedded))
            stages.append(embed_back_stage(tap_count, sum_keys, [None, taps_key], 2 * own))
            temps.update(
                small=pltpu.VMEM((small_rows, width), F32),
                input_sums=pltpu.VMEM((8, width), F32),
                d_out=pltpu.VMEM(whole, F32),
            )
        else:
            outputs.update(d_out=(whole, F32, HOLD), input_sums=sums_out)
        weights = [(focal_pieces[b], dict(query=0, key=0))]
        if shared:
            levels = run_kernel(
                [focal_back_stage(b, groups, lanes)],
                dict(d_sum=fetch(shares.to_images(d_sum)), **levels_in),
                dict(
                    d_context=((IMAGE_ROWS, channels), BF16, FETCH),
                    d_gates=((IMAGE_ROWS, 4 * LANES), F32, FETCH),
                    d_taps=((room_rows, channels), F32, FETCH),
                ),
                levels_temps,
            )
            tap_grad = shares.spread(levels.d_taps)
            inputs.update(
                d_context=fetch(shares.to_rows(levels.d_context)),
                d_gates=fetch(shares.sum_rows(levels.d_gates)),
            )
            if final:
                inputs.update(d_taps=fetch(tap_grad))
            made = run_kernel(stages, inputs, outputs, temps, weights)
            return Box(made, d_taps=tap_grad)
        temps.update(
            d_context=pltpu.VMEM(whole, BF16),
            d_gates=pltpu.VMEM((rows, 4 * LANES), F32),
            **levels_temps,
        )
        tap_shape = (room_rows, width)
        if final:
            temps.update(d_taps=pltpu.VMEM(tap_shape, F32))
        else:
            outputs.update(d_taps=(tap_shape, F32, FETCH))
        return run_kernel(
            [focal_back_stage(b, groups, lanes)] + stages,
            dict(d_sum=hold(d_sum), **levels_in) | inputs,
            outputs,
            temps,
            weights,
        )

    def mlp_back(b, d_x):
        return run_kernel(
            [mlp_back_stage(b)],
            dict(d_in=hold(d_x), **fetch_all(saved[b], dict(hidden=0, slope=0, middle=0)), **basic),
            dict(
                d_out=(whole, F32, HOLD),
                kept=(hidden_part, BF16, HOLD),
                sent=(hidden_part, BF16, HOLD),
                sums=sums_out,
            ),
            {},
            [(mlp_pieces[b], dict(down=0, up=0))],
        )

    z_last = len(links.bits("z")) - 1

    def open_mlp(kept, received):
        terms = links.open_sum(kept, received, parts_x)
        return links.early(terms, "x") if split_x else links.early(terms, "y")

    mixed, got = beside(
        lambda gate: mix_back(1, gate), d_middle, [(made.sent, "core", 1), (made[3], "core", 1)]
    )
    sums[1][2] = mixed.sums
    mlp_move, mlp_finish = open_mlp(made.kept, got[0])
    head_move, head_finish = links.early(links.open_sum(made[2], got[1]), "y")
    made, got = beside(
        lambda gate: focal_back(1, gate, d_middle, mixed), mixed.d_sum, [mlp_move, head_move]
    )
    mlp_sum = mlp_finish(got[0])
    sums[1][0] = made.input_sums
    d_taps = made.d_taps
    focal_kept = made.kept
    mlp_move, mlp_finish = links.early(mlp_sum, "y") if split_x else links.exchange(
        mlp_sum, "z", 0
    )
    head_move, head_finish = links.exchange(head_finish(got[1]), "z", 0)
    made, got = beside(
        lambda gate: mlp_back(0, gate),
        made.d_out,
        [(made.sent, "core", 1), mlp_move, head_move],
    )
    sums[0][1] = made.sums
    mlp_one = mlp_finish(got[1])
    d_middle = made.d_out
    focal_move, focal_finish = links.early(links.open_sum(focal_kept, got[0]), "y")
    one_move, one_finish = links.exchange(mlp_one, "z", 0 if split_x else z_last)
    head_move, head_finish = links.exchange(head_finish(got[2]), "z", z_last)
    mlp_kept = made.kept
    mixed, got = beside(
        lambda gate: mix_back(0, gate),
        d_middle,
        [(made.sent, "core", 1), focal_move, one_move, head_move],
    )
    sums[0][2] = mixed.sums
    mlp_move, mlp_finish = open_mlp(mlp_kept, got[0])
    focal_move, focal_finish = links.exchange(focal_finish(got[1]), "z", 0)
    mlp_one = one_finish(got[2])
    head_low = total(head_finish(got[3]))
    if split_x:
        one_move, one_finish = links.exchange(mlp_one, "z", z_last)
    else:
        one_low = total(mlp_one)
        one_move = (one_low, "x", x_first)
    moves = [mlp_move, focal_move, one_move, (head_low, "x", x_first)]
    made, got = beside(lambda gate: focal_back(0, gate, d_middle, mixed), mixed.d_sum, moves)
    mlp_sum = mlp_finish(got[0])

    def rest_x(low, received):
        summed = low.astype(F32) + received.astype(F32)
        for step in x_rest:
            low = summed.astype(BF16)
            summed = low.astype(F32) + links.swap(low, "x", step).astype(F32)
        return summed

    head = Gather(links, rest_x(head_low, got[3]).astype(BF16))
    rate = 0.2 * math.sqrt(group_rows * lax.axis_size("dp"))

    focal_move, focal_finish = links.exchange(focal_finish(got[1]), "z", z_last)
    if split_x:
        one_move, one_finish = links.regather_x(total(one_finish(got[2])).astype(F32))
        zero_move, zero_finish = links.early(mlp_sum, "y")
    else:
        mlp_one = rest_x(one_low, got[2])
        zero_move, zero_finish = links.exchange(mlp_sum, "z", 0)
    lower_kept, got = together(made.kept, [(made.sent, "core", 1)])
    lower_move, lower_finish = links.early(links.open_sum(lower_kept, got[0]), "y")
    moves = [lower_move, focal_move, (head.stack, "z", z_first)]
    if split_x:
        moves.append(one_move)
    gate, got = together(here, moves)
    lower_move, lower_finish = links.exchange(lower_finish(got[0]), "z", 0)
    focal_low = total(focal_finish(got[1]))
    head.take(got[2], "z", z_first)
    if split_x:
        mlp_one = one_finish(got[3])
    moves = [lower_move, zero_move] + [(head.stack, "z", step) for step in z_rest]
    gate, got = together(gate, moves)
    lower_move, lower_finish = links.exchange(lower_finish(got[0]), "z", z_last)
    take_z(head, got[2:])
    mlp_zero = zero_finish(got[1])
    zero_move, zero_finish = links.exchange(mlp_zero, "z", 0 if split_x else z_last)
    head_move = head.early("y")
    moves = [lower_move, (focal_low, "x", x_first), (head.stack, *head_move), zero_move]
    (gate, mlp_one), got = together((gate, mlp_one), moves)
    lower_low = total(lower_finish(got[0]))
    focal_one = rest_x(focal_low, got[1])
    head.take(got[2], *head_move, True)
    mlp_zero = zero_finish(got[3])
    if split_x:
        zero_move, zero_finish = links.exchange(mlp_zero, "z", z_last)
    else:
        zero_low = total(mlp_zero)
        zero_move = (zero_low, "x", x_first)
    moves = [(lower_low, "x", x_first), zero_move]
    moves += [(part, "core", 1) for part in head.parts]
    (focal_one, mlp_one), got = together((focal_one, mlp_one), moves)
    lower = rest_x(lower_low, got[0])
    head_far = got[2:]
    if split_x:
        zero_rows = total(zero_finish(got[1])).astype(F32)
        zero_move, zero_finish = links.regather_x(zero_rows)
    else:
        mlp_zero = rest_x(zero_low, got[1])
    common = Gather(links, lower[2 * own :].astype(BF16))
    moves = common.direct()
    count = len(moves)
    if split_x:
        moves.append(zero_move)
    (focal_one, mlp_one, late), got = together((focal_one, mlp_one, lower[: 2 * own]), moves)
    common.take_direct(got[:count])
    if split_x:
        mlp_zero = zero_finish(got[count])
    y_move = common.early("y")
    common.take(links.swap(common.stack, *y_move), *y_move, True)
    rows_early = jnp.concatenate([mlp_one, mlp_zero, focal_one, late], axis=0)
    rows_early, _stack = lax.optimization_barrier((rows_early, common.stack))
    halves = links.both_halves(rows_early)
    head_far, _stack = lax.optimization_barrier((head_far, common.stack))
    head_pieces = Pieces(
        links.slots(head.masks, False),
        head.parts,
        head_far,
        dict(head0=(0, 0, embed_rows), head1=(1, 0, embed_rows)),
    )
    weight_out = (head_weight.shape, F32, FETCH)
    new_head = run_kernel(
        [update_head_stage(rate)],
        dict(weight=fetch(head_weight), moment=fetch(head_moment)),
        dict(new_weight=weight_out, new_moment=weight_out),
        {},
        [(head_pieces, dict(head0=0, head1=0))],
    )
    ends = (own_hidden, 2 * own_hidden)
    grad_mlp = jnp.stack(
        [
            jnp.stack([part[ends[0] : ends[1]] for part in halves]),
            jnp.stack([part[: ends[0]] for part in halves]),
        ]
    )
    one = [part[ends[1] : ends[1] + 2 * own] for part in halves]
    late = [part[ends[1] + 2 * own :] for part in halves]
    grad_focal = jnp.stack([jnp.stack([part[:own] for part in parts]) for parts in (late, one)])
    grad_mixer = jnp.stack([jnp.stack([part[own:] for part in parts]) for parts in (late, one)])
    results = []
    for weight, moment, average, gradient, order, back in (
        (focal_input, focal_moment, focal_average, grad_focal, (0, 2, 3, 1), (0, 3, 1, 2)),
        (mixers, mixer_moment, mixer_average, grad_mixer, (0, 1, 3, 2), (0, 1, 3, 2)),
        (mlp_weights, mlp_moment, mlp_average, grad_mlp, (0, 1, 3, 2), (0, 1, 3, 2)),
    ):
        weight, moment, average = (
            jnp.transpose(array, order) for array in (weight, moment, average)
        )
        new_weight, new_moment = nesterov(weight, moment, gradient, rate)
        new_average = AVERAGE * average + (1.0 - AVERAGE) * new_weight
        results.extend(
            jnp.transpose(array, back) for array in (new_weight, new_moment, new_average)
        )
    there, results, *held = lax.optimization_barrier(
        (common.parts[1], results, new_head.new_weight, new_head.new_moment)
    )
    common_near = [common.parts[0], there]
    common_far = [links.swap_core(part) for part in common_near]
    small_part = small_rows // (2 * links.chan)
    common_pieces = Pieces(
        links.slots(common.masks, False),
        common_near,
        common_far,
        dict(
            embed0=(0, 0, embed_rows),
            embed1=(1, 0, embed_rows),
            small0=(0, embed_rows, small_part),
            small1=(1, embed_rows, small_part),
        ),
    )
    weight_out = (embed_weight.shape, F32, FETCH)
    vector_out = (vectors.shape, F32, HOLD)
    kernel_out = (kernel_rows.shape, F32, HOLD)
    made = run_kernel(
        [update_shared_stage(tap_count, own, rate)],
        dict(
            weight=hold(embed_weight),
            moment=hold(embed_moment),
            vectors=hold(vectors),
            vector_moment=hold(vector_moment),
            vector_average=hold(vector_average),
            kernels=hold(kernel_rows),
            kernel_moment=hold(jnp.transpose(kernel_moment, (0, 2, 1))),
            kernel_average=hold(jnp.transpose(kernel_average, (0, 2, 1))),
        ),
        dict(
            new_weight=weight_out,
            new_moment=weight_out,
            new_vectors=vector_out,
            new_vector_moment=vector_out,
            new_vector_average=vector_out,
            new_kernels=kernel_out,
            new_kernel_moment=kernel_out,
            new_kernel_average=kernel_out,
            loss=((1, LANES), F32, HOLD),
        ),
        dict(packed=pltpu.VMEM((-(-vectors.shape[0] // 8) * 8, width), F32)),
        [(common_pieces, dict(embed0=0, embed1=0, small0=0, small1=0))],
    )
    return (
        made.loss[0, 0],
        made.new_weight,
        made.new_moment,
        *held,
        made.new_vectors,
        made.new_vector_moment,
        made.new_vector_average,
        *results,
        *[
            jnp.transpose(array, (0, 2, 1))
            for array in (made.new_kernels, made.new_kernel_moment, made.new_kernel_average)
        ],
    )


def solution(mesh):
    split = P(None, None, None, "chan")
    taps = P(None, None, "chan")
    return jax.shard_map(
        shards,
        mesh=mesh,
        in_specs=(P(("dp", "chan"), None), P("dp"), P("dp"), P("dp", None, None))
        + (P(),) * 7
        + (split,) * 9
        + (taps,) * 3,
        out_specs=(P(),) * 8 + (split,) * 9 + (taps,) * 3,
        check_vma=False,
    )
```

```python
import math

import jax
import jax.numpy as jnp
from jax import lax
from jax.experimental import pallas as pl
from jax.experimental.pallas import tpu as pltpu
from jax.sharding import PartitionSpec as P

PATCH_IN = 768
GRID = 16
BLOCKS = 2
IMAGE_ROWS = GRID * GRID
LANES = 128

EPS = 1e-05
MOMENTUM = 0.9
AVERAGE = 0.5
KEEP_RATE = 0.8
KERNEL_SIZES = (3, 5, 7)
KERNEL_STARTS = (0, 9, 34)
ROOT_HALF = math.sqrt(0.5)
DENSITY = 1.0 / math.sqrt(2.0 * math.pi)
VMEM_LIMIT = 44 << 20
F32 = jnp.float32
BF16 = jnp.bfloat16


def matmul(left, right):
    return jnp.dot(left, right, preferred_element_type=F32)


def contract_rows(left, right):
    return lax.dot_general(left, right, (((0,), (0,)), ((), ())), preferred_element_type=F32)


def times_transposed(left, right):
    return lax.dot_general(left, right, (((1,), (1,)), ((), ())), preferred_element_type=F32)


def normalize(values):
    average = jnp.mean(values, axis=-1, keepdims=True)
    centred = values - average
    variance = jnp.mean(centred * centred, axis=-1, keepdims=True)
    scale = lax.rsqrt(variance + EPS)
    return (centred * scale, scale)


def norm_backward(grad, unit, scale, gain):
    d_unit = grad * gain
    mean_one = jnp.mean(d_unit, axis=-1, keepdims=True)
    mean_two = jnp.mean(d_unit * unit, axis=-1, keepdims=True)
    return (d_unit - mean_one - unit * mean_two) * scale


def column_sum(values):
    return jnp.sum(values, axis=0, keepdims=True)


def gelu_pair(values):
    cumulative = 0.5 + 0.5 * lax.erf(values * ROOT_HALF)
    density = DENSITY * jnp.exp(-0.5 * values * values)
    return (values * cumulative, cumulative + values * density)


def nesterov(weight, moment, gradient, rate):
    new_moment = MOMENTUM * moment + gradient
    new_weight = weight - rate * (gradient + MOMENTUM * new_moment)
    return (new_weight, new_moment)


def after(value, *others):
    return lax.optimization_barrier((value, others))[0]


class Links:
    def __init__(self):
        chan = lax.axis_size("chan")
        self.ny = 1 << ((chan.bit_length() - 1) // 2)
        self.nz = chan // self.ny
        self.nc = 2
        self.nx = lax.axis_size("dp") // self.nc
        self.chan = chan
        self.place = lax.axis_index("chan")
        self.z = self.place // self.ny
        self.y = self.place % self.ny
        group = lax.axis_index("dp")
        self.x = group // self.nc
        self.core = group % self.nc
        self.sizes = {"z": self.nz, "y": self.ny, "x": self.nx}

    def bits(self, axis):
        return [1 << k for k in reversed(range((self.sizes[axis] - 1).bit_length()))]

    def swap(self, values, axis, step):
        if axis in ("z", "y"):
            step = step * self.ny if axis == "z" else step
            return lax.ppermute(values, "chan", [(i, i ^ step) for i in range(self.chan)])
        step = step * self.nc if axis == "x" else step
        return lax.ppermute(values, "dp", [(i, i ^ step) for i in range(self.nx * self.nc)])

    def swap_core(self, values):
        return self.swap(values, "core", 1)

    def cross_x(self, values):
        total = values
        for step in self.bits("x"):
            low = total.astype(values.dtype)
            total = low.astype(F32) + self.swap(low, "x", step).astype(F32)
        return total.astype(F32)

    def mask_of(self, axis, step):
        return tuple(step if name == axis else 0 for name in ("z", "y", "x"))

    def here(self):
        return jnp.stack([self.core, self.place, self.x, self.y, self.z]).astype(jnp.int32)

    def slots(self, masks, split_x):
        places = []
        for mask_z, mask_y, mask_x in masks:
            place = (self.z ^ mask_z) * self.ny + (self.y ^ mask_y)
            places.append(place * self.nx + (self.x ^ mask_x) if split_x else place)
        return jnp.stack([self.core, self.place] + places).astype(jnp.int32)

    def both_halves(self, summed):
        other = self.swap_core(summed)
        first = self.core == 0
        return (jnp.where(first, summed, other), jnp.where(first, other, summed))


def join(left, right):
    return tuple(a ^ b for a, b in zip(left, right))


def total(terms):
    result = terms[0].astype(F32)
    for term in terms[1:]:
        result = result + term.astype(F32)
    return result.astype(BF16)


class Chain:
    def __init__(self, links, terms, rows, order):
        self.terms = terms
        self.rows = rows
        self.order = list(order)
        self.dims = [("z", k) for k in reversed(range(len(links.bits("z"))))]
        self.dims += [("y", k) for k in reversed(range(len(links.bits("y"))))]

    def low(self):
        parts = [
            lax.slice_in_dim(array[0], first, first + self.rows) for array, first in self.terms
        ]
        return total(parts)


def halve(links, chains):
    arrays = []
    plans = []
    groups = []
    outs = []
    for chain in chains:
        axis, level = chain.order.pop(0)
        places = []
        for array, _first in chain.terms:
            found = [k for k, other in enumerate(arrays) if other is array]
            if not found:
                arrays.append(array)
            places.append(found[0] if found else len(arrays) - 1)
        lead = 1 << len(chain.dims)
        if axis == "x":
            before, behind, rows, count = 0, lead, chain.rows // 2, lead
        else:
            at = chain.dims.index((axis, level))
            before, behind = 1 << at, lead >> (at + 1)
            rows, count = chain.rows, lead // 2
            chain.dims.pop(at)
        key = (axis, level, count)
        mates = [group for group in groups if group[0] == key]
        if mates:
            group = mates[0]
        else:
            group = [key, 0]
            groups.append(group)
        plans.append((chain, places, before, behind, rows, count, group, group[1]))
        group[1] += rows
    width = arrays[0].shape[-1]
    for key, rows in groups:
        outs.append(jax.ShapeDtypeStruct((key[2], rows, width), BF16))
    for _chain, _places, _before, _behind, rows, count, _group, _at in plans:
        outs.append(jax.ShapeDtypeStruct((count, rows, width), BF16))

    def body(here_ref, *refs):
        ins, sends = refs[: len(arrays)], refs[len(arrays) : len(arrays) + len(groups)]
        keeps = refs[len(arrays) + len(groups) :]
        index = dict(y=here_ref[3], z=here_ref[4], x=here_ref[2])
        for plan, keep in zip(plans, keeps):
            chain, places, before, behind, rows, count, group, at = plan
            axis, level, _count = group[0]
            bit = index[axis] >> level & 1
            send = sends[groups.index(group)]
            for side, target, first_row in ((1 - bit, send, at), (bit, keep, 0)):
                for out in range(count):
                    summed = None
                    for place, (_array, first) in zip(places, chain.terms):
                        if axis == "x":
                            start = pl.multiple_of(first + side * rows, 8)
                            value = ins[place][out, pl.ds(start, rows), :]
                        else:
                            source = (out // behind * 2 + side) * behind + out % behind
                            value = ins[place][source, first : first + rows, :]
                        value = value.astype(F32)
                        summed = value if summed is None else summed + value
                    target[out, first_row : first_row + rows, :] = summed.astype(BF16)

    made = pl.pallas_call(
        body,
        name=halve.__name__,
        in_specs=[pl.BlockSpec(memory_space=pltpu.SMEM)]
        + [pl.BlockSpec(memory_space=pltpu.VMEM) for _ in arrays],
        out_specs=[pl.BlockSpec(memory_space=pltpu.VMEM) for _ in outs],
        out_shape=outs,
        compiler_params=pltpu.CompilerParams(vmem_limit_bytes=VMEM_LIMIT),
    )(links.here(), *arrays)
    moves = [(sent, key[0], 1 << key[1]) for sent, (key, _rows) in zip(made, groups)]

    def take(received):
        for plan, keep in zip(plans, made[len(groups) :]):
            chain, _places, _before, _behind, rows, _count, group, at = plan
            chain.terms = [(keep, 0), (received[groups.index(group)], at)]
            chain.rows = rows

    return (moves, take)


class Reduction:
    def __init__(self, links, kept, received):
        self.links = links
        count = kept.shape[1]
        quantum = 16 * links.nx
        cut = 2 * count // 5 // quantum * quantum if links.nx > 1 else 0
        over_x = [("x", k) for k in reversed(range(len(links.bits("x"))))]
        over_y = [("y", k) for k in range(len(links.bits("y")))]
        over_z = [("z", k) for k in range(len(links.bits("z")))]
        terms = lambda first: [(kept, first), (received, first)]
        self.plain = Chain(links, terms(2 * cut), count - 2 * cut, over_y + over_z)
        self.cut = []
        if cut:
            self.cut = [
                Chain(links, terms(0), cut, over_x + over_y + over_z),
                Chain(links, terms(cut), cut, over_z[:1] + over_x + over_y + over_z[1:]),
            ]
        self.sums = links.bits("x")[::-1]
        self.gathers = list(self.sums) if cut else []
        self.plain_rows = None
        self.cut_rows = None

    def open(self):
        return [chain for chain in [self.plain] + self.cut if chain.order]

    def done(self):
        return not self.open() and not self.sums and not self.gathers

    def last_moves(self):
        moves, takes = [], []
        if not self.plain.order and self.sums:
            if self.plain_rows is None:
                self.plain_rows = self.plain.low()
            low = self.plain_rows.astype(BF16)
            moves.append((low, "x", self.sums.pop(0)))

            def take_sum(received):
                self.plain_rows = low.astype(F32) + received.astype(F32)

            takes.append(take_sum)
        if self.gathers and not any(chain.order for chain in self.cut):
            if self.cut_rows is None:
                self.cut_rows = jnp.stack([chain.low() for chain in self.cut])
            part = self.cut_rows
            step = self.gathers.pop(0)
            moves.append((part, "x", step))

            def take_part(received):
                first = jnp.concatenate([part, received], axis=1)
                second = jnp.concatenate([received, part], axis=1)
                self.cut_rows = jnp.where(self.links.x & step == 0, first, second)

            takes.append(take_part)
        return (moves, takes)

    def result(self):
        rows = self.plain_rows.astype(F32)
        if self.cut_rows is None:
            return rows
        width = rows.shape[-1]
        return jnp.concatenate([self.cut_rows.astype(F32).reshape(-1, width), rows])


def next_round(links, reductions):
    lasts = [reduction.last_moves() for reduction in reductions]
    chains = [chain for reduction in reductions for chain in reduction.open()]
    moves, take = halve(links, chains) if chains else ([], None)
    count = len(moves)
    for more, _takes in lasts:
        moves = moves + more
    takes = [one for _more, some in lasts for one in some]

    def take_all(received):
        if take is not None:
            take(received[:count])
        for one, part in zip(takes, received[count:]):
            one(part)

    return (moves, take_all)


class Gather:
    def __init__(self, links, own):
        self.links = links
        self.stack = own[None]
        self.masks = [(0, 0, 0)]
        self.parts = None

    def moves(self, axis, step):
        return [(self.stack, axis, step)]

    def take(self, received, axis, step, keep_apart=False):
        if keep_apart:
            self.parts = [self.stack, received]
        else:
            self.stack = jnp.concatenate([self.stack, received], axis=0)
        extra = self.links.mask_of(axis, step)
        self.masks = self.masks + [join(mask, extra) for mask in self.masks]

    def early(self, axis):
        *steps, last = self.links.bits(axis)
        for step in steps:
            self.take(self.links.swap(self.stack, axis, step), axis, step)
        return (axis, last)

    def direct(self):
        return [(self.stack, "z", step) for step in range(1, self.links.nz)]

    def take_direct(self, received):
        self.stack = jnp.concatenate([self.stack] + received, axis=0)
        self.masks = [self.links.mask_of("z", step) for step in range(self.links.nz)]


class Pieces:
    def __init__(self, where, near, far, matrices):
        self.where = where
        self.near = near
        self.far = far
        self.matrices = matrices
        self.slots = where.shape[0] - 2
        self.width = near[0].shape[-1]

    def rows(self, name):
        return self.matrices[name][2] * self.slots

    def arrays(self):
        return [*self.near, *self.far]

    def copies(self, name, where, parts, target, sems):
        half, first, count = self.matrices[name]
        near, far = parts[: len(self.near)], parts[len(self.near) :]
        pairs = []
        slot = 0
        for near_part, far_part in zip(near, far):
            for d in range(near_part.shape[0]):
                if len(target.shape) == 3:
                    room = target.at[where[2 + slot]]
                else:
                    at = pl.multiple_of(where[2 + slot] * count, 8)
                    room = target.at[pl.ds(at, count), :]
                rows = pl.ds(first, count)
                pairs.append(
                    (
                        pltpu.make_async_copy(near_part.at[d, rows, :], room, sems.at[slot]),
                        pltpu.make_async_copy(far_part.at[d, rows, :], room, sems.at[slot]),
                    )
                )
                slot += 1
        mine = where[0] == half

        def start():
            @pl.when(mine)
            def _():
                for pair in pairs:
                    pair[0].start()

            @pl.when(jnp.logical_not(mine))
            def _():
                for pair in pairs:
                    pair[1].start()

        def wait():
            for pair in pairs:
                pair[0].wait()

        return (start, wait)


class Room:
    def __init__(self):
        self.refs = {}
        self.waits = {}
        self.flushes = []
        self.pending = []

    def __getitem__(self, key):
        wait = self.waits.pop(key, None)
        if wait is not None:
            wait()
        return self.refs[key]

    def __getattr__(self, key):
        return self[key]

    def flush(self, *refs):
        rest = []
        for ref, copy in self.flushes:
            if any(ref is one for one in refs):
                copy.start()
                self.pending.append(copy)
            else:
                rest.append((ref, copy))
        self.flushes = rest

    def finish(self):
        self.flush(*[ref for ref, _copy in self.flushes])
        for copy in self.pending:
            copy.wait()


class Box(dict):
    __getattr__ = dict.__getitem__


class View:
    def __init__(self, room, names):
        self.room = room
        self.names = names

    def __getitem__(self, key):
        return self.room[self.names.get(key, key)]

    def __getattr__(self, key):
        return self[key]

    def flush(self, *refs):
        self.room.flush(*refs)


def renamed(stage, **names):
    def call(room):
        stage(View(room, names))

    call.__name__ = stage.__name__
    return call


HOLD, FETCH, SCALAR = range(3)


def run_kernel(stages, inputs, outputs, temps=(), weights=(), pinned=True):
    temps = dict(temps)
    operands, in_specs, scratch, plan = [], [], [], []

    def scratch_for(shape):
        scratch.append(shape)
        return len(scratch) - 1

    for key, (array, mode) in inputs.items():
        operands.append(array)
        if mode == HOLD:
            in_specs.append(pl.BlockSpec(memory_space=pltpu.VMEM))
            plan.append((key, mode, None))
        elif mode == SCALAR:
            in_specs.append(pl.BlockSpec(memory_space=pltpu.SMEM))
            plan.append((key, mode, None))
        else:
            operands[-1] = pltpu.with_memory_space_constraint(array, pltpu.HBM)
            in_specs.append(pl.BlockSpec(memory_space=pltpu.HBM))
            place = scratch_for(pltpu.VMEM(array.shape, array.dtype))
            plan.append((key, mode, (place, scratch_for(pltpu.SemaphoreType.DMA))))
    loads = []
    for pieces, names in weights:
        first = len(operands)
        operands.append(pieces.where)
        in_specs.append(pl.BlockSpec(memory_space=pltpu.SMEM))
        for array in pieces.arrays():
            if pinned:
                array = pltpu.with_memory_space_constraint(array, pltpu.HBM)
            operands.append(array)
            in_specs.append(pl.BlockSpec(memory_space=pltpu.HBM if pinned else pl.ANY))
        for matrix, apart in names.items():
            shape = (pieces.rows(matrix), pieces.width)
            if apart:
                shape = (pieces.slots, shape[0] // pieces.slots, shape[1])
            place = scratch_for(pltpu.VMEM(shape, BF16))
            sems = scratch_for(pltpu.SemaphoreType.DMA((pieces.slots,)))
            loads.append((matrix, pieces, first, place, sems))
    out_specs, out_shapes, out_plan = [], [], []
    for key, (shape, dtype, mode) in outputs.items():
        if mode == HOLD:
            out_specs.append(pl.BlockSpec(memory_space=pltpu.VMEM))
            out_shapes.append(jax.ShapeDtypeStruct(shape, dtype))
            out_plan.append((key, None))
        else:
            out_specs.append(pl.BlockSpec(memory_space=pltpu.HBM))
            out_shapes.append(pltpu.HBM(shape, dtype))
            place = scratch_for(pltpu.VMEM(shape, dtype))
            out_plan.append((key, (place, scratch_for(pltpu.SemaphoreType.DMA))))
    temp_plan = [(key, scratch_for(shape)) for key, shape in temps.items()]

    def body(*refs):
        ins = refs[: len(operands)]
        outs = refs[len(operands) : len(operands) + len(out_specs)]
        rooms = refs[len(operands) + len(out_specs) :]
        room = Room()
        def load(group):
            for matrix, pieces, first, place, sems in loads:
                if pieces is group:
                    where = ins[first]
                    parts = ins[first + 1 : first + 1 + len(pieces.arrays())]
                    start, wait = pieces.copies(matrix, where, parts, rooms[place], rooms[sems])
                    start()
                    room.refs[matrix] = rooms[place]
                    room.waits[matrix] = wait
                    room.refs.update(where=where)

        for pieces, _names in weights[:1]:
            load(pieces)
        for ref, (key, mode, more) in zip(ins, plan):
            if mode == FETCH:
                place, sem = more
                copy = pltpu.make_async_copy(ref, rooms[place], rooms[sem])
                copy.start()
                room.refs[key] = rooms[place]
                room.waits[key] = copy.wait
            else:
                room.refs[key] = ref
        for pieces, _names in weights[1:]:
            load(pieces)
        for ref, (key, more) in zip(outs, out_plan):
            if more is None:
                room.refs[key] = ref
            else:
                place, sem = more
                room.refs[key] = rooms[place]
                copy = pltpu.make_async_copy(rooms[place], ref, rooms[sem])
                room.flushes.append((rooms[place], copy))
        for key, place in temp_plan:
            room.refs[key] = rooms[place]
        for stage in stages:
            stage(room)
        for key in list(room.waits):
            room[key]
        room.finish()

    results = pl.pallas_call(
        body,
        name=stages[-1].__name__,
        in_specs=in_specs,
        out_specs=out_specs,
        out_shape=out_shapes,
        scratch_shapes=scratch,
        compiler_params=pltpu.CompilerParams(vmem_limit_bytes=VMEM_LIMIT),
    )(*operands)
    return Box(zip(outputs, results))


MASKED, COUNTED, VALID, KEEP = 0, 1, 2, 3


def column(room, index):
    return room.columns[:, index : index + 1]


def keep_of(room, block, branch):
    return column(room, KEEP + 2 * block + branch)


def vector(room, row):
    return room.vectors[row : row + 1, :]


def low_gates(room, block):
    return room.vectors[10 * block + 6 : 10 * block + 10, :].astype(BF16)


def correlate(padded, taps, level, flip):
    width = KERNEL_SIZES[level]
    first = KERNEL_STARTS[level]
    margin = width // 2
    lanes = padded.shape[-1]
    sums = [None] * GRID
    for dx in range(width):
        weights = []
        for dy in range(width):
            tap = dy * width + dx
            if flip:
                tap = width * width - 1 - tap
            weights.append(jnp.broadcast_to(taps[first + tap : first + tap + 1, :], (GRID, lanes)))
        for row in range(GRID):
            window = padded[row, 8 - margin + dx : 8 - margin + dx + GRID, :]
            for dy in range(width):
                out = row - dy + margin
                if 0 <= out < GRID:
                    term = window * weights[dy]
                    sums[out] = term if sums[out] is None else sums[out] + term
    return sums


def correlate_taps(padded, grads, d_taps, at_lanes, level):
    width = KERNEL_SIZES[level]
    first = KERNEL_STARTS[level]
    margin = width // 2
    for dx in range(width):
        sums = [None] * width
        for row in range(GRID):
            window = padded[row, 8 - margin + dx : 8 - margin + dx + GRID, :]
            for dy in range(width):
                out = row - dy + margin
                if 0 <= out < GRID:
                    term = window * grads[out]
                    sums[dy] = term if sums[dy] is None else sums[dy] + term
        for dy in range(width):
            tap = first + dy * width + dx
            d_taps[tap : tap + 1, at_lanes] = column_sum(sums[dy])


def clear_margins(padded):
    lanes = padded.shape[-1]
    for row in range(GRID):
        padded[row, 0:8, :] = jnp.zeros((8, lanes), F32)
        padded[row, 8 + GRID : 16 + GRID, :] = jnp.zeros((8, lanes), F32)


def rows_at(row):
    return slice(row * GRID, (row + 1) * GRID)


def gate_part(gates, row, level, lanes):
    part = gates[rows_at(row), level * LANES : (level + 1) * LANES]
    return part if lanes == LANES else part[:, 0:1]


def lane_range(group, groups, lanes):
    if groups == 1:
        return slice(0, lanes)
    return pl.ds(pl.multiple_of(group * lanes, lanes), lanes)


def tap_room(tap_count):
    return -(-tap_count // 8) * 8


def split_three(values):
    high = values.astype(BF16)
    rest = values - high.astype(F32)
    middle = rest.astype(BF16)
    return (high, middle, (rest - middle.astype(F32)).astype(BF16))


def pack_rows(here, sources, taps, parts):
    width = sources[0][0].shape[3]
    counts = [array.shape[2] // parts for array, _block in sources]
    rows = sum(counts) + (0 if taps is None else taps.shape[1])

    def body(here_ref, *refs):
        wide_refs = refs[: len(sources)]
        rest = refs[len(sources) :]
        out_ref = rest[0] if taps is None else rest[1]
        buffers = rest[-1 - len(sources) : -1]
        sems = rest[-1]
        copies = []
        for at, (ref, (_array, block)) in enumerate(zip(wide_refs, sources)):
            source = ref.at[block, here_ref[0]]
            if parts > 1:
                first = pl.multiple_of(here_ref[2] * counts[at], 8)
                source = source.at[pl.ds(first, counts[at]), :]
            copies.append(pltpu.make_async_copy(source, buffers[at], sems.at[at]))
            copies[-1].start()
        row = sum(counts)
        if taps is not None:
            own, count = taps.shape[1:]
            out_ref[row : row + own, :] = jnp.zeros((own, width), BF16)
            splits = [split_three(rest[0][b]) for b in range(BLOCKS)]
            wide = (splits[0][0], splits[1][0], splits[0][1])
            thin = (splits[1][1], splits[0][2], splits[1][2])
            for chosen, at_core in ((wide, 0), (thin, 1)):

                @pl.when(here_ref[0] == at_core)
                def _():
                    for index, part in enumerate(chosen):
                        at = index * LANES
                        out_ref[row : row + own, at : at + count] = part

        row = 0
        for copy, buffer, count in zip(copies, buffers, counts):
            copy.wait()
            out_ref[row : row + count, :] = buffer[...].astype(BF16)
            row += count

    extra = [] if taps is None else [taps]
    return pl.pallas_call(
        body,
        name=pack_rows.__name__,
        in_specs=[pl.BlockSpec(memory_space=pltpu.SMEM)]
        + [pl.BlockSpec(memory_space=pltpu.HBM) for _ in sources]
        + [pl.BlockSpec(memory_space=pltpu.VMEM) for _ in extra],
        out_specs=pl.BlockSpec(memory_space=pltpu.VMEM),
        out_shape=jax.ShapeDtypeStruct((rows, width), BF16),
        scratch_shapes=[pltpu.VMEM((count, width), F32) for count in counts]
        + [pltpu.SemaphoreType.DMA((len(sources),))],
        compiler_params=pltpu.CompilerParams(vmem_limit_bytes=VMEM_LIMIT),
    )(
        here,
        *[pltpu.with_memory_space_constraint(array, pltpu.HBM) for array, _block in sources],
        *extra,
    )


def taps_stage(tap_count, groups, lanes):
    room_rows = tap_room(tap_count)
    used = BLOCKS * room_rows

    def join_taps(room):
        wide = room.wide[...]
        thin = room.thin[...]
        shape = (used, wide.shape[1])
        row = lax.broadcasted_iota(jnp.int32, shape, 0)
        lane = lax.broadcasted_iota(jnp.int32, shape, 1)
        upper = row >= room_rows
        tap = jnp.where(upper, row - room_rows, row)
        tap = jnp.where(tap < tap_count, tap, -8 * LANES)

        def chosen(lower_places, upper_places):
            marks = jnp.zeros(shape, F32)
            for places, side in ((lower_places, False), (upper_places, True)):
                for place in places:
                    hit = jnp.logical_and(lane == tap + place * LANES, upper == side)
                    marks = jnp.where(hit, 1.0, marks)
            return marks.astype(BF16)

        taps = times_transposed(chosen((0, 2), (1,)), wide)
        taps = taps + times_transposed(chosen((1,), (0, 2)), thin)
        for b in range(BLOCKS):
            for j in range(groups):
                room.taps[b, j] = taps[
                    b * room_rows : (b + 1) * room_rows, j * lanes : (j + 1) * lanes
                ]

    return join_taps


def inputs_stage(block, groups, lanes):
    def focal_inputs(room):
        unit, _scale = normalize(room.x[...])
        first = unit * vector(room, 10 * block) + vector(room, 10 * block + 1)
        first = first.astype(BF16)
        width = first.shape[1]
        gate_low = low_gates(room, block)
        for level in range(4):
            spread = jnp.broadcast_to(gate_low[level : level + 1], (LANES, width))
            room.gates[:, level * LANES : (level + 1) * LANES] = times_transposed(
                first, spread
            )
        key = room.key
        for j in range(groups):
            room.context[j] = times_transposed(first, key[j * lanes : (j + 1) * lanes, :])
        room.query_out[...] = times_transposed(first, room.query[...])
        room.flush(room.gates, room.context, room.query_out)

    return focal_inputs


def focal_stage(block, groups, lanes):
    def focal_levels(room):
        padded = room.padded
        taps, context, gates, low, pool = room.taps, room.context, room.gates, room.low, room.pool
        fields = [room.k1, room.k2, room.k3]
        slopes = [room.s1, room.s2, room.s3]
        clear_margins(padded)
        valid = room.image_columns[:, VALID : VALID + 1]
        valid_total = column_sum(valid)

        def group(j, carry):
            tap = taps.at[block, j]
            for row in range(GRID):
                padded[row, 8 : 8 + GRID, :] = context[j, rows_at(row), :]
            for level in range(3):
                sums = correlate(padded, tap, level, False)
                for row in range(GRID):
                    value, slope = gelu_pair(sums[row])
                    fields[level][j, rows_at(row), :] = value
                    slopes[level][j, rows_at(row), :] = slope
                    if level < 2:
                        padded[row, 8 : 8 + GRID, :] = value
            mean = column_sum(fields[2][j] * valid) / valid_total
            pooled, pooled_slope = gelu_pair(mean)
            pool[j, 0:1, :] = pooled
            pool[j, 1:2, :] = pooled_slope / valid_total
            pool[j, 2:8, :] = jnp.zeros((6, lanes), F32)
            at = lane_range(j, groups, lanes)
            for row in range(GRID):
                summed = pooled * gate_part(gates, row, 3, lanes)
                for level in range(3):
                    summed = summed + fields[level][j, rows_at(row), :] * gate_part(
                        gates, row, level, lanes
                    )
                low[rows_at(row), at] = summed.astype(BF16)
            return carry

        if groups > 1:
            lax.fori_loop(0, groups, group, 0)
        else:
            group(0, 0)
        room.flush(room.k1, room.k2, room.k3, room.s1, room.s2, room.s3, room.pool, room.low)

    return focal_levels


def mix_stage(block):
    def mix_forward(room):
        modulator = times_transposed(room.low[...], room.mix[...])
        room.mod[...] = modulator
        room.flush(room.mod)
        product = (room.query_out[...] * modulator).astype(BF16)
        branch = matmul(product, room.proj[...]) + vector(room, 10 * block + 4)
        room.middle[...] = room.x[...] + keep_of(room, block, 0) * branch

    return mix_forward


def mlp_stage(block):
    def mlp_forward(room):
        middle = room.middle[...]
        unit, _scale = normalize(middle)
        second = unit * vector(room, 10 * block + 2) + vector(room, 10 * block + 3)
        second = second.astype(BF16)
        up = room.up
        step = up.shape[0] // 4
        for part in range(4):
            at = slice(part * step, (part + 1) * step)
            value, slope = gelu_pair(times_transposed(second, up[at, :]))
            room.hidden[:, at] = value.astype(BF16)
            room.slope[:, at] = slope
        room.flush(room.hidden, room.slope)
        lowered = matmul(room.hidden[...], room.down[...]) + vector(room, 10 * block + 5)
        room.out[...] = middle + keep_of(room, block, 1) * lowered

    return mlp_forward


def embed_stage(room):
    outer = 10 * BLOCKS
    embedded = matmul(room.patches[...], room.embed[...].astype(BF16))
    embedded = embedded + vector(room, outer)
    room.embedded[...] = embedded
    room.flush(room.embedded)
    unit, _scale = normalize(embedded)
    mask = column(room, MASKED)
    state = unit * vector(room, outer + 1) + vector(room, outer + 2)
    room.x[...] = state * (1.0 - mask) + vector(room, outer + 5) * mask


def store_halves(core, kept, sent, at, first, second):
    chan, _rows, width = kept.shape
    rows = first.shape[0] // chan
    first = first.reshape(chan, rows, width).astype(BF16)
    second = second.reshape(chan, rows, width).astype(BF16)

    @pl.when(core == 0)
    def _():
        kept[:, at : at + rows, :] = first
        sent[:, at : at + rows, :] = second

    @pl.when(core != 0)
    def _():
        kept[:, at : at + rows, :] = second
        sent[:, at : at + rows, :] = first


def head_stage(at):
    def head_step(room):
        outer = 10 * BLOCKS
        gain = vector(room, outer + 3)
        unit, scale = normalize(room.x[...])
        low = (unit * gain + vector(room, outer + 4)).astype(BF16)
        head_low = room.head[...].astype(BF16)
        error = matmul(low, head_low) - room.patches[...].astype(F32)
        denom = room.denom[0, 0]
        weighted = column(room, COUNTED) * error
        loss = column_sum(jnp.sum(weighted * error, axis=-1, keepdims=True)) / denom
        d_pred = (2.0 * weighted / denom).astype(BF16)
        grad = contract_rows(low, d_pred)
        half = grad.shape[1] // 2
        core = room.where[0]
        store_halves(core, room.kept, room.sent, at, grad[:, :half], grad[:, half:])
        d_final = times_transposed(d_pred, head_low)
        room.d_out[...] = norm_backward(d_final, unit, scale, gain)
        sums = room.sums
        width = low.shape[1]
        sums[0:1, :] = column_sum(d_final * unit)
        sums[1:2, :] = column_sum(d_final)
        sums[2:3, :] = jnp.broadcast_to(loss, (1, width))
        sums[3:8, :] = jnp.zeros((5, width), F32)

    return head_step


def mlp_back_stage(block, at):
    def mlp_backward(room):
        d_residual = room.d_in[...]
        d_down = d_residual * keep_of(room, block, 1)
        d_low = d_down.astype(BF16)
        unit, scale = normalize(room.middle[...])
        gain = vector(room, 10 * block + 2)
        second = (unit * gain + vector(room, 10 * block + 3)).astype(BF16)
        grad_down = contract_rows(room.hidden[...], d_low)
        d_pre = (times_transposed(d_low, room.down[...]) * room.slope[...]).astype(BF16)
        grad_up = contract_rows(d_pre, second)
        core = room.where[0]
        store_halves(core, room.kept, room.sent, at, grad_up, grad_down)
        d_second = matmul(d_pre, room.up[...])
        room.d_out[...] = d_residual + norm_backward(d_second, unit, scale, gain)
        sums = room.sums
        width = d_low.shape[1]
        sums[0:1, :] = column_sum(d_second * unit)
        sums[1:2, :] = column_sum(d_second)
        sums[2:3, :] = column_sum(d_down)
        sums[3:8, :] = jnp.zeros((5, width), F32)

    return mlp_backward


def mix_back_stage(block, groups, lanes, at):
    def mix_backward(room):
        d_proj = room.d_in[...] * keep_of(room, block, 0)
        d_low = d_proj.astype(BF16)
        d_product = times_transposed(d_low, room.proj[...])
        modulator = room.mod[...]
        query = room.query_out[...]
        d_mod = (d_product * query).astype(BF16)
        mix = room.mix
        for j in range(groups):
            room.d_sum[j] = matmul(d_mod, mix[:, j * lanes : (j + 1) * lanes])
        room.d_query[...] = (d_product * modulator).astype(BF16)
        product = (query * modulator).astype(BF16)
        grad_proj = contract_rows(product, d_low)
        grad_mix = contract_rows(d_mod, room.low[...])
        core = room.where[0]
        store_halves(core, room.kept, room.sent, at, grad_mix, grad_proj)
        sums = room.sums
        width = d_low.shape[1]
        sums[0:1, :] = column_sum(d_proj)
        sums[1:8, :] = jnp.zeros((7, width), F32)

    return mix_backward


def focal_back_stage(block, groups, lanes):
    def levels_backward(room):
        padded = room.padded
        d_padded = room.d_padded
        clear_margins(padded)
        clear_margins(d_padded)
        d_all, gates, taps, pool = room.d_sum, room.gates, room.taps, room.pool
        fields = [room.context, room.k1, room.k2, room.k3]
        slopes = [room.s1, room.s2, room.s3]
        d_context, d_gates, d_taps = room.d_context, room.d_gates, room.d_taps
        valid = room.image_columns[:, VALID : VALID + 1]
        d_gates[...] = jnp.zeros(d_gates.shape, F32)
        d_taps[...] = jnp.zeros(d_taps.shape, F32)

        def fold(values):
            if lanes == LANES:
                return values
            summed = jnp.sum(values, axis=-1, keepdims=True) / LANES
            return jnp.broadcast_to(summed, (values.shape[0], LANES))

        def group(j, carry):
            tap = taps.at[block, j]
            at = lane_range(j, groups, lanes)
            d_pooled = jnp.zeros((1, lanes), F32)
            for row in range(GRID):
                d_pooled = d_pooled + column_sum(
                    d_all[j, rows_at(row), :] * gate_part(gates, row, 3, lanes)
                )
            d_mean = d_pooled * pool[j, 1:2, :]
            d_field = [d_mean * valid[rows_at(row)] for row in range(GRID)]
            for level in (2, 1, 0):
                d_pre = []
                for row in range(GRID):
                    here = rows_at(row)
                    grad = d_field[row] + d_all[j, here, :] * gate_part(gates, row, level, lanes)
                    grad = grad * slopes[level][j, here, :]
                    d_pre.append(grad)
                    d_padded[row, 8 : 8 + GRID, :] = grad
                    padded[row, 8 : 8 + GRID, :] = fields[level][j, here, :]
                correlate_taps(padded, d_pre, d_taps, at, level)
                d_field = correlate(d_padded, tap, level, True)
            for row in range(GRID):
                d_context[rows_at(row), at] = d_field[row].astype(BF16)
            whole = d_all[j]
            for level in range(3):
                here = slice(level * LANES, (level + 1) * LANES)
                d_gates[:, here] = d_gates[:, here] + fold(whole * fields[level + 1][j])
            here = slice(3 * LANES, 4 * LANES)
            d_gates[:, here] = d_gates[:, here] + fold(whole * pool[j, 0:1, :])
            return carry

        if groups > 1:
            lax.fori_loop(0, groups, group, 0)
        else:
            group(0, 0)
        room.flush(room.d_taps)

    return levels_backward


def inputs_back_stage(block, at):
    def inputs_backward(room):
        unit, scale = normalize(room.x[...])
        gain = vector(room, 10 * block)
        first_wide = (unit * gain + vector(room, 10 * block + 1)).astype(BF16)
        first = first_wide
        first_wide = first.astype(F32)
        rows, width = first.shape
        gate_low = low_gates(room, block).astype(F32)
        sums = room.input_sums
        sums[...] = jnp.zeros((8, width), F32)
        d_first = jnp.zeros((rows, width), F32)
        d_gates = room.d_gates
        for level in range(4):
            here = slice(level * LANES, (level + 1) * LANES)
            col = jnp.sum(d_gates[:, here], axis=-1, keepdims=True)
            d_first = d_first + col * gate_low[level : level + 1]
            sums[2 + level : 3 + level, :] = column_sum(col * first_wide)
        d_query = room.d_query[...]
        d_context = room.d_context[...]
        d_first = d_first + matmul(d_query, room.query[...])
        d_first = d_first + matmul(d_context, room.key[...])
        room.d_out[...] = room.d_in[...] + norm_backward(d_first, unit, scale, gain)
        sums[0:1, :] = column_sum(d_first * unit)
        sums[1:2, :] = column_sum(d_first)
        grad_query = contract_rows(d_query, first)
        grad_key = contract_rows(d_context, first)
        kept, sent = room.kept, room.sent
        core = room.where[0]
        store_halves(core, kept, sent, at, grad_query, grad_key)

    return inputs_backward


def sums_start(tap_count):
    return BLOCKS * tap_room(tap_count)


def small_rows_for(tap_count, chan):
    used = sums_start(tap_count) + 8 * (2 + 3 * BLOCKS)
    return -(-used // (16 * chan)) * (16 * chan)


def embed_back_stage(tap_count, sum_keys, tap_keys, first_row):
    outer = 10 * BLOCKS

    def embed_backward(room):
        mask = column(room, MASKED)
        d_residual = room.d_out[...]
        d_start = d_residual * (1.0 - mask)
        unit, scale = normalize(room.embedded[...])
        d_embed = norm_backward(d_start, unit, scale, vector(room, outer + 1))
        small = room.small
        small[...] = jnp.zeros(small.shape, F32)
        for b, key in enumerate(tap_keys):
            at = b * tap_room(tap_count)
            taps = room.d_taps if key is None else room[key]
            small[at : at + taps.shape[0], :] = taps[...]
        at = sums_start(tap_count)
        small[at : at + 1, :] = column_sum(d_embed)
        small[at + 1 : at + 2, :] = column_sum(d_start * unit)
        small[at + 2 : at + 3, :] = column_sum(d_start)
        small[at + 3 : at + 4, :] = column_sum(d_residual * mask)
        for key in sum_keys:
            at += 8
            small[at : at + 8, :] = room[key][...]
        grad = contract_rows(room.patches[...], d_embed.astype(BF16))
        core = room.where[0]
        kept, sent = room.kept, room.sent
        half = grad.shape[0] // 2
        row = first_row
        store_halves(core, kept, sent, row, grad[:half], grad[half:])
        row += half // kept.shape[0]
        half = small.shape[0] // 2
        store_halves(core, kept, sent, row, small[:half], small[half:])

    return embed_backward


def update_shared_stage(tap_count, own, part, rate):
    def update_shared(room):
        slots = room.all0.shape[0]
        width = room.all0.shape[2]
        small_rows = []
        for index, ref in enumerate((room.all0, room.all1)):
            across = slice(index * width, (index + 1) * width)
            for slot in range(slots):
                gradient = ref[slot].astype(F32)
                down = slice(slot * part, (slot + 1) * part)
                new_weight, new_moment = nesterov(
                    room.head[down, across], room.head_moment[down, across], gradient[:part], rate
                )
                room.new_head[down, across] = new_weight
                room.new_head_moment[down, across] = new_moment
                at = (index * slots + slot) * part
                down = slice(at, at + part)
                new_weight, new_moment = nesterov(
                    room.embed[down, :], room.embed_moment[down, :], gradient[part : 2 * part], rate
                )
                room.new_embed[down, :] = new_weight
                room.new_embed_moment[down, :] = new_moment
                small_rows.append(gradient[2 * part :])
        room.flush(room.new_head, room.new_head_moment, room.new_embed, room.new_embed_moment)
        grads = jnp.concatenate(small_rows, axis=0)
        small = grads.astype(BF16)

        def sum_row(index, row):
            at = sums_start(tap_count) + 8 * index + row
            return grads[at : at + 1]

        rows = []
        for b in range(BLOCKS):
            inputs_at, mlp_at, mix_at = 1 + 3 * b, 2 + 3 * b, 3 + 3 * b
            rows += [sum_row(inputs_at, 0), sum_row(inputs_at, 1)]
            rows += [sum_row(mlp_at, 0), sum_row(mlp_at, 1)]
            rows += [sum_row(mix_at, 0), sum_row(mlp_at, 2)]
            rows += [sum_row(inputs_at, 2 + level) for level in range(4)]
        head_at = 1 + 3 * BLOCKS
        rows += [sum_row(0, 0), sum_row(0, 1), sum_row(0, 2)]
        rows += [sum_row(head_at, 0), sum_row(head_at, 1), sum_row(0, 3)]
        packed = room.packed
        for at, row in enumerate(rows):
            packed[at : at + 1, :] = row
        gradient = packed[0 : len(rows), :]
        new_weight, new_moment = nesterov(
            room.vectors[...], room.vector_moment[...], gradient, rate
        )
        room.new_vectors[...] = new_weight
        room.new_vector_moment[...] = new_moment
        room.new_vector_average[...] = (
            AVERAGE * room.vector_average[...] + (1.0 - AVERAGE) * new_weight
        )
        room.loss[...] = sum_row(head_at, 2)[:, 0:LANES]
        first = room.where[1] * own
        source = lax.broadcasted_iota(jnp.int32, (own, width), 1)
        wanted = first + lax.broadcasted_iota(jnp.int32, (own, width), 0)
        chosen = (source == wanted).astype(F32).astype(BF16)
        for b in range(BLOCKS):
            at = b * tap_room(tap_count)
            gradient = times_transposed(chosen, small[at : at + tap_room(tap_count)])
            gradient = gradient[:, :tap_count]
            new_weight, new_moment = nesterov(
                room.kernels[b], room.kernel_moment[b], gradient, rate
            )
            room.new_kernels[b] = new_weight
            room.new_kernel_moment[b] = new_moment
            room.new_kernel_average[b] = (
                AVERAGE * room.kernel_average[b] + (1.0 - AVERAGE) * new_weight
            )

    return update_shared


class Shares:
    def __init__(self, local_rows, chan_size):
        self.count = max(1, IMAGE_ROWS // local_rows)
        self.groups = [
            list(range(first, first + self.count)) for first in range(0, chan_size, self.count)
        ]

    def to_images(self, values):
        whole = lax.all_to_all(
            values[0], "chan", 1, 0, axis_index_groups=self.groups, tiled=True
        )
        return whole[None]

    def to_rows(self, values):
        return lax.all_to_all(values, "chan", 0, 1, axis_index_groups=self.groups, tiled=True)

    def all_rows(self, values):
        return lax.all_gather(
            values, "chan", axis=0, axis_index_groups=self.groups, tiled=True
        )

    def sum_rows(self, values):
        return lax.psum_scatter(
            values, "chan", scatter_dimension=0, axis_index_groups=self.groups, tiled=True
        )

    def channels(self, values):
        size = values.shape[-1] // self.count
        place = lax.axis_index("chan") % self.count
        return lax.dynamic_slice_in_dim(values, place * size, size, values.ndim - 1)

    def spread(self, values):
        size = values.shape[1]
        place = lax.axis_index("chan") % self.count
        whole = jnp.zeros((values.shape[0], size * self.count), values.dtype)
        return lax.dynamic_update_slice_in_dim(whole, values, place * size, 1)


def hold(array):
    return (array, HOLD)


def fetch(array):
    return (array, FETCH)


def fetch_all(made, names):
    return {name: fetch(made[name]) for name in names}


def shards(
    patches,
    valid_mask,
    target_mask,
    keep_mask,
    embed_weight,
    embed_moment,
    head_weight,
    head_moment,
    vectors,
    vector_moment,
    vector_average,
    focal_input,
    focal_moment,
    focal_average,
    mixers,
    mixer_moment,
    mixer_average,
    mlp_weights,
    mlp_moment,
    mlp_average,
    kernels,
    kernel_moment,
    kernel_average,
):
    links = Links()
    rows, patch_in = patches.shape
    group_rows = valid_mask.shape[0]
    own = focal_input.shape[-1]
    own_hidden = mlp_weights.shape[-1]
    hidden_width = own_hidden * links.chan
    tap_count = kernels.shape[1]
    width = vectors.shape[1]
    shares = Shares(rows, links.chan)
    shared = shares.count > 1
    channels = width // shares.count
    lanes = LANES if channels % LANES == 0 else channels
    groups = channels // lanes
    room_rows = tap_room(tap_count)
    split_x = own_hidden % (8 * links.nx) == 0 and links.nx > 1

    def together(values, moves):
        got = [links.swap(*move) for move in moves]
        return lax.optimization_barrier((values, got))

    def beside(call, gate, moves):
        made = call(after(gate, *[move[0] for move in moves]))
        made, got = together(dict(made), moves)
        return (Box(made), got)

    here = links.here()
    focal_rows = jnp.transpose(focal_input, (0, 2, 3, 1))
    mixer_rows = jnp.transpose(mixers, (0, 1, 3, 2))
    mlp_rows = jnp.transpose(mlp_weights, (0, 1, 3, 2))
    kernel_rows = jnp.transpose(kernels, (0, 2, 1))
    focal_layout = dict(
        query=(0, 0, own), mix=(0, own, own), key=(1, 0, own), proj=(1, own, own)
    )
    first_layout = dict(focal_layout, wide=(0, 2 * own, own), thin=(1, 2 * own, own))

    def mlp_layout(count):
        return dict(up=(0, 0, count), down=(1, 0, count))

    first_row = links.place * rows
    validity = valid_mask.astype(F32)
    masked = target_mask.astype(F32)
    keep_rows = jnp.repeat(
        keep_mask.reshape(keep_mask.shape[0], -1).astype(F32) / KEEP_RATE, IMAGE_ROWS, axis=0
    )
    table = jnp.concatenate(
        [
            masked[:, None],
            (masked * validity)[:, None],
            validity[:, None],
            keep_rows,
            jnp.zeros((group_rows, 1), F32),
        ],
        axis=1,
    )
    columns = lax.dynamic_slice_in_dim(table, first_row, rows)
    image_columns = columns
    if shared:
        image_columns = lax.dynamic_slice_in_dim(
            table, first_row // IMAGE_ROWS * IMAGE_ROWS, IMAGE_ROWS
        )
    group_count = jnp.broadcast_to(jnp.sum(validity * masked), (8, LANES))
    basic = dict(vectors=fetch(vectors), columns=fetch(columns))
    grid_columns = dict(image_columns=fetch(image_columns))

    whole = (rows, width)
    focal = [None] * BLOCKS
    mlp = [None] * BLOCKS
    focal[0] = Gather(
        links, pack_rows(here, [(focal_rows, 0), (mixer_rows, 0)], kernel_rows, 1)
    )
    moves = focal[0].direct()
    embedded = run_kernel(
        [embed_stage],
        dict(patches=fetch(patches), embed=fetch(embed_weight), **basic),
        dict(x=(whole, F32, HOLD), embedded=(whole, F32, FETCH)),
    )
    parts_x = links.nx if split_x else 1
    packed = pack_rows(here, [(mlp_rows, 0)], None, parts_x)
    (x, packed), got = together((embedded.x, packed), moves)
    focal[0].take_direct(got)
    mlp[0] = Gather(links, packed)
    z_first, *z_rest = links.bits("z")
    y_move = focal[0].early("y")
    (move,) = mlp[0].moves("z", z_first)
    packed = (
        pack_rows(here, [(focal_rows, 1), (mixer_rows, 1)], None, 1),
        pack_rows(here, [(mlp_rows, 1)], None, 1),
    )
    packed, got = together(packed, [move])
    mlp[0].take(got[0], "z", z_first)
    focal[1] = Gather(links, packed[0])
    mlp[1] = Gather(links, packed[1])

    def take_z(gather, received):
        for step, one in zip(z_rest, received):
            gather.take(one, "z", step)

    moves = [(mlp[0].stack, "z", step) for step in z_rest]
    moves += [(focal[0].stack, *y_move), (focal[1].stack, "z", z_first)]
    moves += [(group_count, "core", 1)]
    x, got = together(x, moves)
    take_z(mlp[0], got[:-3])
    focal[0].take(got[-3], *y_move, True)
    focal[1].take(got[-2], "z", z_first)
    group_count = group_count + got[-1]

    def twins(gather, values):
        values, got = together(values, [(part, "core", 1) for part in gather.parts])
        return (values, got)

    def pieces_of(gather, far, layout, split):
        return Pieces(links.slots(gather.masks, split), gather.parts, far, layout)

    y_move = mlp[0].early("y")
    x, far = twins(focal[0], after(x, mlp[0].stack, group_count))
    focal_pieces = [pieces_of(focal[0], far, first_layout, False), None]
    mlp_pieces = [None, None]

    field_shape = (groups, IMAGE_ROWS, lanes)
    field = (field_shape, F32, FETCH)
    padded = pltpu.VMEM((GRID, GRID + 16, lanes), F32)
    gates_out = dict(gates=((IMAGE_ROWS, 4 * LANES), F32, FETCH))
    focal_out = dict(k1=field, k2=field, k3=field, s1=field, s2=field, s3=field)
    focal_out.update(pool=((groups, 8, lanes), F32, FETCH))
    mixed_out = dict(mod=(whole, F32, FETCH), middle=(whole, F32, HOLD))
    query_out = dict(query_out=(whole, F32, FETCH))
    low_out = dict(low=(whole, BF16, FETCH))
    mlp_out = dict(
        hidden=((rows, hidden_width), BF16, FETCH), slope=((rows, hidden_width), F32, FETCH)
    )
    weights_in = dict(key=0, query=0, mix=0, proj=0)
    up_down = dict(up=0, down=0)
    taps_shape = (BLOCKS, groups, room_rows, lanes)

    def focal_apart(b, x, taps):
        pieces = focal_pieces[b]
        made = run_kernel(
            [inputs_stage(b, 1, width)],
            dict(x=hold(x), **basic),
            dict(
                gates=((rows, 4 * LANES), F32, FETCH),
                context=((1, rows, width), F32, FETCH),
                **query_out,
            ),
            {},
            [(pieces, dict(key=0, query=0))],
        )
        made.update(gates=shares.all_rows(made.gates), context=shares.to_images(made.context))
        made.update(
            run_kernel(
                [focal_stage(b, groups, lanes)],
                dict(
                    context=fetch(made.context),
                    gates=fetch(made.gates),
                    taps=fetch(taps),
                    **grid_columns,
                ),
                dict(low=((IMAGE_ROWS, channels), BF16, FETCH), **focal_out),
                dict(padded=padded),
            )
        )
        made.update(low=shares.to_rows(made.low))
        made.update(
            run_kernel(
                [mix_stage(b)],
                dict(
                    x=hold(x), low=fetch(made.low), query_out=fetch(made.query_out), **basic
                ),
                mixed_out,
                {},
                [(pieces, dict(mix=0, proj=0))],
            )
        )
        return made

    def focal_stages(b):
        return [inputs_stage(b, groups, lanes), focal_stage(b, groups, lanes), mix_stage(b)]

    focal_made_out = dict(
        context=field, **gates_out, **query_out, **focal_out, **low_out, **mixed_out
    )

    def first_focal(x):
        if shared:
            taps = run_kernel(
                [taps_stage(tap_count, 1, width)],
                {},
                dict(taps=((BLOCKS, 1, room_rows, width), F32, FETCH)),
                {},
                [(focal_pieces[0], dict(wide=0, thin=0))],
            ).taps
            taps = shares.channels(taps)
            return Box(focal_apart(0, x, taps), taps=taps)
        return run_kernel(
            [taps_stage(tap_count, groups, lanes)] + focal_stages(0),
            dict(x=hold(x), **basic, **grid_columns),
            dict(taps=(taps_shape, F32, FETCH), **focal_made_out),
            dict(padded=padded),
            [(focal_pieces[0], dict(wide=0, thin=0, **weights_in))],
            False,
        )

    moves = [(mlp[0].stack, *y_move)]
    moves += [(focal[1].stack, "z", step) for step in z_rest[:1]]
    moves += [(mlp[1].stack, "z", z_first)]
    x_first, *x_rest = links.bits("x")
    moves += [(group_count, "x", x_first)]
    saved = [Box(x=x), Box()]
    made, got = beside(first_focal, x, moves)
    saved[0].update(made)
    taps = made.taps
    mlp[0].take(got[0], *y_move, not split_x)
    take_z(focal[1], got[1:-2])
    mlp[1].take(got[-2], "z", z_first)
    counted = group_count + got[-1]
    for step in x_rest:
        counted = counted + links.swap(counted, "x", step)
    denominator = counted[0:1, 0:1] * PATCH_IN
    y_move = focal[1].early("y")
    moves = [(focal[1].stack, *y_move)]
    moves += [(mlp[1].stack, "z", step) for step in z_rest]
    if split_x:
        x_move = mlp[0].early("x")
        moves += [(mlp[0].stack, *x_move)]
    middle, got = together(saved[0].middle, moves)
    focal[1].take(got[0], *y_move, True)
    take_z(mlp[1], got[1 : 1 + len(z_rest)])
    if split_x:
        mlp[0].take(got[-1], *x_move, True)
    y_move = mlp[1].early("y")
    moves = [(part, "core", 1) for part in mlp[0].parts + focal[1].parts]
    middle, got = together(after(middle, mlp[1].stack), moves)
    mlp_pieces[0] = pieces_of(mlp[0], got[:2], mlp_layout(own_hidden // parts_x), split_x)
    focal_pieces[1] = pieces_of(focal[1], got[2:], focal_layout, False)

    def second_focal(middle):
        inputs = dict(middle=hold(middle), **basic)
        outputs = dict(out=(whole, F32, FETCH), **mlp_out)
        if shared:
            made = run_kernel(
                [mlp_stage(0)], inputs, outputs, {}, [(mlp_pieces[0], up_down)]
            )
            lower = Box(hidden=made.hidden, slope=made.slope)
            return Box(focal_apart(1, made.out, taps), x=made.out, lower=dict(lower))
        made = run_kernel(
            [renamed(mlp_stage(0), middle=0, out=1)]
            + [renamed(stage, x=1) for stage in focal_stages(1)],
            {0: hold(middle), **basic, **grid_columns, **dict(taps=fetch(taps))},
            {1: (whole, F32, FETCH), **mlp_out, **focal_made_out},
            dict(padded=padded),
            [(mlp_pieces[0], up_down), (focal_pieces[1], weights_in)],
        )
        lower = dict(hidden=made.hidden, slope=made.slope)
        upper = Box({key: made[key] for key in focal_made_out})
        upper.update(x=made[1], lower=lower)
        return upper

    made, got = beside(second_focal, middle, [(mlp[1].stack, *y_move)])
    mlp[1].take(got[0], *y_move, True)
    saved[0].update(made.lower)
    saved[1].update(made)
    middle, far = twins(mlp[1], saved[1].middle)
    mlp_pieces[1] = pieces_of(mlp[1], far, mlp_layout(own_hidden), False)

    sums_out = ((8, width), F32, FETCH)
    embed_rows = patch_in // (2 * links.chan)
    small_rows = small_rows_for(tap_count, links.chan)
    small_part = small_rows // (2 * links.chan)
    hidden_shape = (rows, hidden_width)
    mix_at = own_hidden
    upper_lead = own_hidden + own + embed_rows
    lower_lead = own_hidden + own
    upper_count = upper_lead + own
    lower_count = lower_lead + own + embed_rows + small_part
    d_shape = (1, rows, width) if shared else field_shape
    levels_names = dict(context=0, gates=0, k1=0, k2=0, k3=0, s1=0, s2=0, s3=0, pool=0)
    mix_names = dict(query_out=0, mod=0, low=0)
    levels_temps = dict(padded=padded, d_padded=padded)
    between = dict(
        d_context=pltpu.VMEM(whole, BF16),
        d_gates=pltpu.VMEM((rows, 4 * LANES), F32),
        **levels_temps,
    )
    tap_shape = (room_rows, width)

    def pair_of(count):
        shape = (links.chan, count, width)
        return dict(kept=(shape, BF16, HOLD), sent=(shape, BF16, HOLD))

    def levels_in(b):
        return dict(taps=fetch(taps), **fetch_all(saved[b], levels_names), **grid_columns)

    head_names = dict(x=0, d_out=1, sums=5)
    first_stages = [
        renamed(mlp_stage(1), out=0),
        renamed(head_stage(own_hidden + own), **head_names),
        renamed(mlp_back_stage(1, 0), d_in=1, d_out=2, sums=3),
        renamed(mix_back_stage(1, d_shape[0], d_shape[2], mix_at), d_in=2, sums=4),
    ]
    first_in = dict(
        middle=hold(middle),
        head=fetch(head_weight),
        patches=fetch(patches),
        denom=(denominator, SCALAR),
        **basic,
        **fetch_all(saved[1], mix_names),
    )
    first_temps = {
        0: pltpu.VMEM(whole, F32),
        1: pltpu.VMEM(whole, F32),
        **dict(hidden=pltpu.VMEM(hidden_shape, BF16), slope=pltpu.VMEM(hidden_shape, F32)),
    }
    sums_outs = {3: sums_out, 4: sums_out, 5: sums_out}
    mlp_weights_in = (mlp_pieces[1], up_down)
    mixer_in = dict(proj=0, mix=0)
    inputs_in = dict(query=0, key=0)

    def levels_apart(b, d_sum):
        made = run_kernel(
            [focal_back_stage(b, groups, lanes)],
            dict(d_sum=fetch(shares.to_images(d_sum)), **levels_in(b)),
            dict(
                d_context=((IMAGE_ROWS, channels), BF16, FETCH),
                d_gates=((IMAGE_ROWS, 4 * LANES), F32, FETCH),
                d_taps=((room_rows, channels), F32, FETCH),
            ),
            levels_temps,
        )
        return Box(
            d_context=shares.to_rows(made.d_context),
            d_gates=shares.sum_rows(made.d_gates),
            d_taps=shares.spread(made.d_taps),
        )

    def joined(first, second):
        return Box(
            kept=jnp.concatenate([first.kept, second.kept], axis=1),
            sent=jnp.concatenate([first.sent, second.sent], axis=1),
        )

    if shared:
        first = run_kernel(
            first_stages,
            first_in,
            {
                2: (whole, F32, HOLD),
                **sums_outs,
                **dict(d_query=(whole, BF16, HOLD), d_sum=(d_shape, F32, HOLD)),
                **pair_of(upper_lead),
            },
            first_temps,
            [mlp_weights_in, (focal_pieces[1], mixer_in)],
        )
        levels = levels_apart(1, first.d_sum)
        second = run_kernel(
            [inputs_back_stage(1, 0)],
            dict(
                d_in=hold(first[2]),
                d_query=hold(first.d_query),
                d_context=fetch(levels.d_context),
                d_gates=fetch(levels.d_gates),
                x=fetch(saved[1].x),
                **basic,
            ),
            dict(d_out=(whole, F32, HOLD), input_sums=sums_out, **pair_of(own)),
            {},
            [(focal_pieces[1], inputs_in)],
        )
        pair = joined(first, second)
        d_x, d_taps = second.d_out, levels.d_taps
        upper_sums = [second.input_sums, first[3], first[4], first[5]]
    else:
        first = run_kernel(
            first_stages
            + [
                focal_back_stage(1, groups, lanes),
                renamed(inputs_back_stage(1, upper_lead), d_in=2),
            ],
            dict(x=fetch(saved[1].x), **levels_in(1)) | first_in,
            {
                **sums_outs,
                **dict(
                    d_out=(whole, F32, HOLD),
                    input_sums=sums_out,
                    d_taps=(tap_shape, F32, FETCH),
                ),
                **pair_of(upper_count),
            },
            {
                2: pltpu.VMEM(whole, F32),
                **first_temps,
                **dict(d_query=pltpu.VMEM(whole, BF16), d_sum=pltpu.VMEM(d_shape, F32)),
                **between,
            },
            [mlp_weights_in, (focal_pieces[1], mixer_in | inputs_in)],
        )
        pair = first
        d_x, d_taps = first.d_out, first.d_taps
        upper_sums = [first.input_sums, first[3], first[4], first[5]]

    lower_stages = [
        renamed(mlp_back_stage(0, 0), d_out=2, sums=3),
        renamed(mix_back_stage(0, d_shape[0], d_shape[2], mix_at), d_in=2, sums=4),
    ]
    lower_names = dict(hidden=0, slope=0, middle=0)
    sum_keys = [10, 3, 4, 11, 12, 13, 14]
    last_in = {
        **dict(zip(sum_keys[3:], (fetch(array) for array in upper_sums))),
        15: fetch(d_taps),
        **dict(patches=fetch(patches), embedded=fetch(embedded.embedded), x=fetch(saved[0].x)),
    }

    def last_stages(at):
        return [
            renamed(inputs_back_stage(0, at), d_in=2, d_out=1, input_sums=10),
            renamed(
                embed_back_stage(tap_count, sum_keys, [None, 15], at + own), d_out=1
            ),
        ]

    last_temps = {
        1: pltpu.VMEM(whole, F32),
        10: pltpu.VMEM((8, width), F32),
        **dict(small=pltpu.VMEM((small_rows, width), F32)),
    }

    def lower_back(d_x):
        inputs = dict(
            d_in=hold(d_x),
            **fetch_all(saved[0], lower_names),
            **basic,
            **fetch_all(saved[0], mix_names),
        )
        weights = [(mlp_pieces[0], dict(down=0, up=0)), (focal_pieces[0], mixer_in)]
        if shared:
            first = run_kernel(
                lower_stages,
                inputs,
                {
                    2: (whole, F32, HOLD),
                    3: sums_out,
                    4: sums_out,
                    **dict(d_query=(whole, BF16, HOLD), d_sum=(d_shape, F32, HOLD)),
                    **pair_of(lower_lead),
                },
                {},
                weights,
            )
            levels = levels_apart(0, first.d_sum)
            second = run_kernel(
                last_stages(0),
                {
                    2: hold(first[2]),
                    3: fetch(first[3]),
                    4: fetch(first[4]),
                    **last_in,
                    **dict(
                        d_query=hold(first.d_query),
                        d_context=fetch(levels.d_context),
                        d_gates=fetch(levels.d_gates),
                        d_taps=fetch(levels.d_taps),
                        **basic,
                    ),
                },
                pair_of(lower_count - lower_lead),
                last_temps,
                [(focal_pieces[0], inputs_in)],
            )
            return joined(first, second)
        return run_kernel(
            lower_stages + [focal_back_stage(0, groups, lanes)] + last_stages(lower_lead),
            {**inputs, **levels_in(0), **last_in},
            pair_of(lower_count),
            {
                2: pltpu.VMEM(whole, F32),
                3: pltpu.VMEM((8, width), F32),
                4: pltpu.VMEM((8, width), F32),
                **last_temps,
                **dict(d_query=pltpu.VMEM(whole, BF16), d_sum=pltpu.VMEM(d_shape, F32)),
                **dict(d_taps=pltpu.VMEM(tap_shape, F32)),
                **between,
            },
            [weights[0], (focal_pieces[0], mixer_in | inputs_in)],
        )

    (d_x, upper_kept), got = together((d_x, pair.kept), [(pair.sent, "core", 1)])
    upper = Reduction(links, upper_kept, got[0])
    moves, take = next_round(links, [upper])
    made, got = beside(lower_back, d_x, moves)
    take(got)
    moves, take = next_round(links, [upper])
    lower_kept, got = together(made.kept, moves + [(made.sent, "core", 1)])
    take(got[:-1])
    lower = Reduction(links, lower_kept, got[-1])
    rate = 0.2 * math.sqrt(group_rows * lax.axis_size("dp"))
    gate = here
    turn = [lower]
    while not (lower.done() and upper.done()):
        moves, take = next_round(links, turn)
        gate, got = together(gate, moves)
        take(got)
        turn = [lower, upper]
    upper_rows, lower_rows = upper.result(), lower.result()
    head_at = own_hidden + own
    common = Gather(
        links,
        jnp.concatenate(
            [
                upper_rows[head_at : head_at + embed_rows].astype(BF16),
                lower_rows[lower_lead + own :].astype(BF16),
            ]
        ),
    )
    got = [links.swap(*move) for move in common.direct()]
    common.take_direct(got)
    y_move = common.early("y")
    common.take(links.swap(common.stack, *y_move), *y_move, True)
    rows_early = jnp.concatenate(
        [
            upper_rows[:own_hidden],
            lower_rows[:own_hidden],
            upper_rows[mix_at : mix_at + own],
            upper_rows[upper_lead:],
            lower_rows[mix_at : lower_lead + own],
        ]
    )
    rows_early, _stack = lax.optimization_barrier((rows_early, common.stack))
    halves = links.both_halves(rows_early)
    ends = (own_hidden, 2 * own_hidden)
    grad_mlp = jnp.stack(
        [
            jnp.stack([part[ends[0] : ends[1]] for part in halves]),
            jnp.stack([part[: ends[0]] for part in halves]),
        ]
    )
    places = [ends[1] + k * own for k in range(5)]
    mix_one, inputs_one, mix_zero, inputs_zero = (
        [part[first:end] for part in halves] for first, end in zip(places, places[1:])
    )
    grad_focal = jnp.stack([jnp.stack(inputs_zero), jnp.stack(inputs_one)])
    grad_mixer = jnp.stack([jnp.stack(mix_zero), jnp.stack(mix_one)])
    results = []
    for weight, moment, average, gradient, order, back in (
        (focal_input, focal_moment, focal_average, grad_focal, (0, 2, 3, 1), (0, 3, 1, 2)),
        (mixers, mixer_moment, mixer_average, grad_mixer, (0, 1, 3, 2), (0, 1, 3, 2)),
        (mlp_weights, mlp_moment, mlp_average, grad_mlp, (0, 1, 3, 2), (0, 1, 3, 2)),
    ):
        weight, moment, average = (
            jnp.transpose(array, order) for array in (weight, moment, average)
        )
        new_weight, new_moment = nesterov(weight, moment, gradient, rate)
        new_average = AVERAGE * average + (1.0 - AVERAGE) * new_weight
        results.extend(
            jnp.transpose(array, back) for array in (new_weight, new_moment, new_average)
        )
    there, results = lax.optimization_barrier((common.parts[1], results))
    common_near = [common.parts[0], there]
    common_far = [links.swap_core(part) for part in common_near]
    count = 2 * embed_rows + small_part
    common_pieces = Pieces(
        links.slots(common.masks, False),
        common_near,
        common_far,
        dict(all0=(0, 0, count), all1=(1, 0, count)),
    )
    head_out = (head_weight.shape, F32, FETCH)
    embed_out = (embed_weight.shape, F32, FETCH)
    vector_out = (vectors.shape, F32, HOLD)
    kernel_out = (kernel_rows.shape, F32, HOLD)
    made = run_kernel(
        [update_shared_stage(tap_count, own, embed_rows, rate)],
        dict(
            head=hold(head_weight),
            head_moment=hold(head_moment),
            embed=hold(embed_weight),
            embed_moment=hold(embed_moment),
            vectors=hold(vectors),
            vector_moment=hold(vector_moment),
            vector_average=hold(vector_average),
            kernels=hold(kernel_rows),
            kernel_moment=hold(jnp.transpose(kernel_moment, (0, 2, 1))),
            kernel_average=hold(jnp.transpose(kernel_average, (0, 2, 1))),
        ),
        dict(
            new_head=head_out,
            new_head_moment=head_out,
            new_embed=embed_out,
            new_embed_moment=embed_out,
            new_vectors=vector_out,
            new_vector_moment=vector_out,
            new_vector_average=vector_out,
            new_kernels=kernel_out,
            new_kernel_moment=kernel_out,
            new_kernel_average=kernel_out,
            loss=((1, LANES), F32, HOLD),
        ),
        dict(packed=pltpu.VMEM((-(-vectors.shape[0] // 8) * 8, width), F32)),
        [(common_pieces, dict(all0=1, all1=1))],
        False,
    )
    return (
        made.loss[0, 0],
        made.new_embed,
        made.new_embed_moment,
        made.new_head,
        made.new_head_moment,
        made.new_vectors,
        made.new_vector_moment,
        made.new_vector_average,
        *results,
        *[
            jnp.transpose(array, (0, 2, 1))
            for array in (made.new_kernels, made.new_kernel_moment, made.new_kernel_average)
        ],
    )


def solution(mesh):
    split = P(None, None, None, "chan")
    taps = P(None, None, "chan")
    return jax.shard_map(
        shards,
        mesh=mesh,
        in_specs=(P(("dp", "chan"), None), P("dp"), P("dp"), P("dp", None, None))
        + (P(),) * 7
        + (split,) * 9
        + (taps,) * 3,
        out_specs=(P(),) * 8 + (split,) * 9 + (taps,) * 3,
        check_vma=False,
    )
```

```python
import math

import jax
import jax.numpy as jnp
from jax import lax
from jax.experimental import pallas as pl
from jax.experimental.pallas import tpu as pltpu
from jax.sharding import PartitionSpec as P

PATCH_IN = 768
GRID = 16
BLOCKS = 2
IMAGE_ROWS = GRID * GRID
LANES = 128

EPS = 1e-05
MOMENTUM = 0.9
AVERAGE = 0.5
KEEP_RATE = 0.8
KERNEL_SIZES = (3, 5, 7)
KERNEL_STARTS = (0, 9, 34)
ROOT_HALF = math.sqrt(0.5)
DENSITY = 1.0 / math.sqrt(2.0 * math.pi)
VMEM_LIMIT = 44 << 20
F32 = jnp.float32
BF16 = jnp.bfloat16


def matmul(left, right):
    return jnp.dot(left, right, preferred_element_type=F32)


def contract_rows(left, right):
    return lax.dot_general(left, right, (((0,), (0,)), ((), ())), preferred_element_type=F32)


def times_transposed(left, right):
    return lax.dot_general(left, right, (((1,), (1,)), ((), ())), preferred_element_type=F32)


def normalize(values):
    average = jnp.mean(values, axis=-1, keepdims=True)
    centred = values - average
    variance = jnp.mean(centred * centred, axis=-1, keepdims=True)
    scale = lax.rsqrt(variance + EPS)
    return (centred * scale, scale)


def norm_backward(grad, unit, scale, gain):
    d_unit = grad * gain
    mean_one = jnp.mean(d_unit, axis=-1, keepdims=True)
    mean_two = jnp.mean(d_unit * unit, axis=-1, keepdims=True)
    return (d_unit - mean_one - unit * mean_two) * scale


def column_sum(values):
    return jnp.sum(values, axis=0, keepdims=True)


def gelu_pair(values):
    cumulative = 0.5 + 0.5 * lax.erf(values * ROOT_HALF)
    density = DENSITY * jnp.exp(-0.5 * values * values)
    return (values * cumulative, cumulative + values * density)


def nesterov(weight, moment, gradient, rate):
    new_moment = MOMENTUM * moment + gradient
    new_weight = weight - rate * (gradient + MOMENTUM * new_moment)
    return (new_weight, new_moment)


def after(value, *others):
    return lax.optimization_barrier((value, others))[0]


class Links:
    def __init__(self):
        chan = lax.axis_size("chan")
        self.ny = 1 << ((chan.bit_length() - 1) // 2)
        self.nz = chan // self.ny
        self.nc = 2
        self.nx = lax.axis_size("dp") // self.nc
        self.chan = chan
        self.place = lax.axis_index("chan")
        self.z = self.place // self.ny
        self.y = self.place % self.ny
        group = lax.axis_index("dp")
        self.x = group // self.nc
        self.core = group % self.nc
        self.sizes = {"z": self.nz, "y": self.ny, "x": self.nx}

    def bits(self, axis):
        return [1 << k for k in reversed(range((self.sizes[axis] - 1).bit_length()))]

    def swap(self, values, axis, step):
        if axis in ("z", "y"):
            step = step * self.ny if axis == "z" else step
            return lax.ppermute(values, "chan", [(i, i ^ step) for i in range(self.chan)])
        step = step * self.nc if axis == "x" else step
        return lax.ppermute(values, "dp", [(i, i ^ step) for i in range(self.nx * self.nc)])

    def swap_core(self, values):
        return self.swap(values, "core", 1)

    def cross_x(self, values):
        total = values
        for step in self.bits("x"):
            low = total.astype(values.dtype)
            total = low.astype(F32) + self.swap(low, "x", step).astype(F32)
        return total.astype(F32)

    def mask_of(self, axis, step):
        return tuple(step if name == axis else 0 for name in ("z", "y", "x"))

    def here(self):
        return jnp.stack([self.core, self.place, self.x, self.y, self.z]).astype(jnp.int32)

    def places(self, masks):
        return [
            ((self.z ^ mask_z) * self.ny + (self.y ^ mask_y), self.x ^ mask_x)
            for mask_z, mask_y, mask_x in masks
        ]

    def where(self, rows):
        return jnp.stack([self.core, self.place] + rows).astype(jnp.int32)

    def both_halves(self, summed):
        other = self.swap_core(summed)
        first = self.core == 0
        return (jnp.where(first, summed, other), jnp.where(first, other, summed))


def join(left, right):
    return tuple(a ^ b for a, b in zip(left, right))


def total(terms):
    result = terms[0].astype(F32)
    for term in terms[1:]:
        result = result + term.astype(F32)
    return result.astype(BF16)


class Chain:
    def __init__(self, links, terms, rows, order):
        self.terms = terms
        self.rows = rows
        self.order = list(order)
        self.dims = [("z", k) for k in reversed(range(len(links.bits("z"))))]
        self.dims += [("y", k) for k in reversed(range(len(links.bits("y"))))]

    def low(self):
        parts = [
            lax.slice_in_dim(array[0], first, first + self.rows) for array, first in self.terms
        ]
        return total(parts)


def halve(links, chains):
    arrays = []
    plans = []
    groups = []
    outs = []
    for chain in chains:
        axis, level = chain.order.pop(0)
        places = []
        for array, _first in chain.terms:
            found = [k for k, other in enumerate(arrays) if other is array]
            if not found:
                arrays.append(array)
            places.append(found[0] if found else len(arrays) - 1)
        lead = 1 << len(chain.dims)
        if axis == "x":
            before, behind, rows, count = 0, lead, chain.rows // 2, lead
        else:
            at = chain.dims.index((axis, level))
            before, behind = 1 << at, lead >> (at + 1)
            rows, count = chain.rows, lead // 2
            chain.dims.pop(at)
        key = (axis, level, count)
        mates = [group for group in groups if group[0] == key]
        if mates:
            group = mates[0]
        else:
            group = [key, 0]
            groups.append(group)
        plans.append((chain, places, before, behind, rows, count, group, group[1]))
        group[1] += rows
    width = arrays[0].shape[-1]
    for key, rows in groups:
        outs.append(jax.ShapeDtypeStruct((key[2], rows, width), BF16))
    for _chain, _places, _before, _behind, rows, count, _group, _at in plans:
        outs.append(jax.ShapeDtypeStruct((count, rows, width), BF16))

    def body(here_ref, *refs):
        ins, sends = refs[: len(arrays)], refs[len(arrays) : len(arrays) + len(groups)]
        keeps = refs[len(arrays) + len(groups) :]
        index = dict(y=here_ref[3], z=here_ref[4], x=here_ref[2])
        for plan, keep in zip(plans, keeps):
            chain, places, before, behind, rows, count, group, at = plan
            axis, level, _count = group[0]
            bit = index[axis] >> level & 1
            send = sends[groups.index(group)]
            for side, target, first_row in ((1 - bit, send, at), (bit, keep, 0)):
                for out in range(count):
                    summed = None
                    for place, (_array, first) in zip(places, chain.terms):
                        if axis == "x":
                            start = pl.multiple_of(first + side * rows, 8 if rows % 16 else 16)
                            value = ins[place][out, pl.ds(start, rows), :]
                        else:
                            source = (out // behind * 2 + side) * behind + out % behind
                            value = ins[place][source, first : first + rows, :]
                        value = value.astype(F32)
                        summed = value if summed is None else summed + value
                    target[out, first_row : first_row + rows, :] = summed.astype(BF16)

    made = pl.pallas_call(
        body,
        name=halve.__name__,
        in_specs=[pl.BlockSpec(memory_space=pltpu.SMEM)]
        + [pl.BlockSpec(memory_space=pltpu.VMEM) for _ in arrays],
        out_specs=[pl.BlockSpec(memory_space=pltpu.VMEM) for _ in outs],
        out_shape=outs,
        compiler_params=pltpu.CompilerParams(vmem_limit_bytes=VMEM_LIMIT),
    )(links.here(), *arrays)
    moves = [(sent, key[0], 1 << key[1]) for sent, (key, _rows) in zip(made, groups)]

    def take(received):
        for plan, keep in zip(plans, made[len(groups) :]):
            chain, _places, _before, _behind, rows, _count, group, at = plan
            chain.terms = [(keep, 0), (received[groups.index(group)], at)]
            chain.rows = rows

    return (moves, take)


class Reduction:
    def __init__(self, links, kept, received):
        self.links = links
        count = kept.shape[1]
        quantum = 16 * links.nx
        cut = 2 * count // 5 // quantum * quantum if links.nx > 1 else 0
        over_x = [("x", k) for k in reversed(range(len(links.bits("x"))))]
        over_y = [("y", k) for k in range(len(links.bits("y")))]
        over_z = [("z", k) for k in range(len(links.bits("z")))]
        terms = lambda first: [(kept, first), (received, first)]
        self.plain = Chain(links, terms(2 * cut), count - 2 * cut, over_y + over_z)
        self.cut = []
        if cut:
            self.cut = [
                Chain(links, terms(0), cut, over_x + over_y + over_z),
                Chain(links, terms(cut), cut, over_z[:1] + over_x + over_y + over_z[1:]),
            ]
        self.sums = links.bits("x")[::-1]
        self.gathers = list(self.sums) if cut else []
        self.plain_rows = None
        self.cut_rows = None

    def open(self):
        return [chain for chain in [self.plain] + self.cut if chain.order]

    def done(self):
        return not self.open() and not self.sums and not self.gathers

    def ready(self):
        return not self.open() and not self.sums

    def last_moves(self):
        moves, takes = [], []
        if not self.plain.order and self.sums:
            if self.plain_rows is None:
                self.plain_rows = self.plain.low()
            low = self.plain_rows.astype(BF16)
            moves.append((low, "x", self.sums.pop(0)))

            def take_sum(received):
                self.plain_rows = low.astype(F32) + received.astype(F32)

            takes.append(take_sum)
        if self.gathers and not any(chain.order for chain in self.cut):
            if self.cut_rows is None:
                self.cut_rows = jnp.stack([chain.low() for chain in self.cut])
            part = self.cut_rows
            step = self.gathers.pop(0)
            moves.append((part, "x", step))

            def take_part(received):
                first = jnp.concatenate([part, received], axis=1)
                second = jnp.concatenate([received, part], axis=1)
                self.cut_rows = jnp.where(self.links.x & step == 0, first, second)

            takes.append(take_part)
        return (moves, takes)

    def tail(self, count):
        return self.plain_rows[self.plain_rows.shape[0] - count :]

    def result(self):
        rows = self.plain_rows.astype(F32)
        if self.cut_rows is None:
            return rows
        width = rows.shape[-1]
        return jnp.concatenate([self.cut_rows.astype(F32).reshape(-1, width), rows])


def next_round(links, reductions):
    lasts = [reduction.last_moves() for reduction in reductions]
    chains = [chain for reduction in reductions for chain in reduction.open()]
    moves, take = halve(links, chains) if chains else ([], None)
    count = len(moves)
    for more, _takes in lasts:
        moves = moves + more
    takes = [one for _more, some in lasts for one in some]

    def take_all(received):
        if take is not None:
            take(received[:count])
        for one, part in zip(takes, received[count:]):
            one(part)

    return (moves, take_all)


class Gather:
    def __init__(self, links, own):
        self.links = links
        self.stack = own[None]
        self.masks = [(0, 0, 0)]
        self.parts = None

    def moves(self, axis, step):
        return [(self.stack, axis, step)]

    def take(self, received, axis, step, keep_apart=False):
        if keep_apart:
            self.parts = [self.stack, received]
        else:
            self.stack = jnp.concatenate([self.stack, received], axis=0)
        extra = self.links.mask_of(axis, step)
        self.masks = self.masks + [join(mask, extra) for mask in self.masks]

    def early(self, axis):
        *steps, last = self.links.bits(axis)
        for step in steps:
            self.take(self.links.swap(self.stack, axis, step), axis, step)
        return (axis, last)

    def direct(self):
        return [(self.stack, "z", step) for step in range(1, self.links.nz)]

    def take_direct(self, received):
        self.stack = jnp.concatenate([self.stack] + received, axis=0)
        self.masks = [self.links.mask_of("z", step) for step in range(self.links.nz)]


class Pieces:
    def __init__(self, where, near, far, matrices, slots):
        self.where = where
        self.near = near
        self.far = far
        self.matrices = matrices
        self.slots = slots
        self.width = near[0].shape[-1]

    def rows(self, name):
        return sum(entry[3] for entry in self.matrices[name][1])

    def count(self, name):
        return len(self.matrices[name][1])

    def arrays(self):
        return [*self.near, *self.far]

    def copies(self, name, where, parts, target, sems):
        half, entries = self.matrices[name]
        near, far = parts[: len(self.near)], parts[len(self.near) :]
        pairs = []
        for at, (array, slot, first, count, entry) in enumerate(entries):
            if len(target.shape) == 3:
                room = target.at[where[2 + entry]]
            else:
                start = pl.multiple_of(where[2 + entry], 8 if count % 16 else 16)
                room = target.at[pl.ds(start, count), :]
            rows = pl.ds(first, count)
            pairs.append(
                tuple(
                    pltpu.make_async_copy(part[array].at[slot, rows, :], room, sems.at[at])
                    for part in (near, far)
                )
            )
        mine = where[0] == half

        def start():
            @pl.when(mine)
            def _():
                for pair in pairs:
                    pair[0].start()

            @pl.when(jnp.logical_not(mine))
            def _():
                for pair in pairs:
                    pair[1].start()

        def wait():
            for pair in pairs:
                pair[0].wait()

        return (start, wait)


class Room:
    def __init__(self):
        self.refs = {}
        self.waits = {}
        self.flushes = []
        self.pending = []

    def __getitem__(self, key):
        wait = self.waits.pop(key, None)
        if wait is not None:
            wait()
        return self.refs[key]

    def __getattr__(self, key):
        return self[key]

    def flush(self, *refs):
        rest = []
        for ref, copy in self.flushes:
            if any(ref is one for one in refs):
                copy.start()
                self.pending.append(copy)
            else:
                rest.append((ref, copy))
        self.flushes = rest

    def flush_next(self, *refs):
        for ref in refs:
            at = [k for k, item in enumerate(self.flushes) if item[0] is ref][0]
            copy = self.flushes.pop(at)[1]
            copy.start()
            self.pending.append(copy)

    def finish(self):
        self.flush(*[ref for ref, _copy in self.flushes])
        for copy in self.pending:
            copy.wait()


class Box(dict):
    __getattr__ = dict.__getitem__


class View:
    def __init__(self, room, names):
        self.room = room
        self.names = names

    def __getitem__(self, key):
        return self.room[self.names.get(key, key)]

    def __getattr__(self, key):
        return self[key]

    def flush(self, *refs):
        self.room.flush(*refs)


def renamed(stage, **names):
    def call(room):
        stage(View(room, names))

    call.__name__ = stage.__name__
    return call


HOLD, FETCH, SCALAR = range(3)


def run_kernel(stages, inputs, outputs, temps=(), weights=(), pinned=True):
    temps = dict(temps)
    operands, in_specs, scratch, plan = [], [], [], []

    def scratch_for(shape):
        scratch.append(shape)
        return len(scratch) - 1

    for key, (array, mode) in inputs.items():
        operands.append(array)
        if mode == HOLD:
            in_specs.append(pl.BlockSpec(memory_space=pltpu.VMEM))
            plan.append((key, mode, None))
        elif mode == SCALAR:
            in_specs.append(pl.BlockSpec(memory_space=pltpu.SMEM))
            plan.append((key, mode, None))
        else:
            operands[-1] = pltpu.with_memory_space_constraint(array, pltpu.HBM)
            in_specs.append(pl.BlockSpec(memory_space=pltpu.HBM))
            place = scratch_for(pltpu.VMEM(array.shape, array.dtype))
            plan.append((key, mode, (place, scratch_for(pltpu.SemaphoreType.DMA))))
    loads = []
    for pieces, names in weights:
        first = len(operands)
        operands.append(pieces.where)
        in_specs.append(pl.BlockSpec(memory_space=pltpu.SMEM))
        for array in pieces.arrays():
            if pinned:
                array = pltpu.with_memory_space_constraint(array, pltpu.HBM)
            operands.append(array)
            in_specs.append(pl.BlockSpec(memory_space=pltpu.HBM if pinned else pl.ANY))
        for matrix, apart in names.items():
            shape = (pieces.rows(matrix), pieces.width)
            if apart:
                shape = (pieces.slots, shape[0] // pieces.slots, shape[1])
            place = scratch_for(pltpu.VMEM(shape, BF16))
            sems = scratch_for(pltpu.SemaphoreType.DMA((pieces.count(matrix),)))
            loads.append((matrix, pieces, first, place, sems))
    out_specs, out_shapes, out_plan = [], [], []
    for key, (shape, dtype, mode, *cuts) in outputs.items():
        if mode == HOLD:
            out_specs.append(pl.BlockSpec(memory_space=pltpu.VMEM))
            out_shapes.append(jax.ShapeDtypeStruct(shape, dtype))
            out_plan.append((key, None))
        else:
            out_specs.append(pl.BlockSpec(memory_space=pltpu.HBM))
            out_shapes.append(pltpu.HBM(shape, dtype))
            place = scratch_for(pltpu.VMEM(shape, dtype))
            cuts = cuts or [()]
            sems = [scratch_for(pltpu.SemaphoreType.DMA) for _ in cuts]
            out_plan.append((key, (place, sems, cuts)))
    temp_plan = [(key, scratch_for(shape)) for key, shape in temps.items()]

    def body(*refs):
        ins = refs[: len(operands)]
        outs = refs[len(operands) : len(operands) + len(out_specs)]
        rooms = refs[len(operands) + len(out_specs) :]
        room = Room()
        def load(group):
            for matrix, pieces, first, place, sems in loads:
                if pieces is group:
                    where = ins[first]
                    parts = ins[first + 1 : first + 1 + len(pieces.arrays())]
                    start, wait = pieces.copies(matrix, where, parts, rooms[place], rooms[sems])
                    start()
                    room.refs[matrix] = rooms[place]
                    room.waits[matrix] = wait
                    room.refs.update(where=where)

        for pieces, _names in weights[:1]:
            load(pieces)
        for ref, (key, mode, more) in zip(ins, plan):
            if mode == FETCH:
                place, sem = more
                copy = pltpu.make_async_copy(ref, rooms[place], rooms[sem])
                copy.start()
                room.refs[key] = rooms[place]
                room.waits[key] = copy.wait
            else:
                room.refs[key] = ref
        for pieces, _names in weights[1:]:
            load(pieces)
        for ref, (key, more) in zip(outs, out_plan):
            if more is None:
                room.refs[key] = ref
            else:
                place, sems, cuts = more
                room.refs[key] = rooms[place]
                for sem, cut in zip(sems, cuts):
                    source, target = rooms[place], ref
                    if cut:
                        source, target = source.at[cut], target.at[cut]
                    copy = pltpu.make_async_copy(source, target, rooms[sem])
                    room.flushes.append((rooms[place], copy))
        for key, place in temp_plan:
            room.refs[key] = rooms[place]
        for stage in stages:
            stage(room)
        for key in list(room.waits):
            room[key]
        room.finish()

    results = pl.pallas_call(
        body,
        name=stages[-1].__name__,
        in_specs=in_specs,
        out_specs=out_specs,
        out_shape=out_shapes,
        scratch_shapes=scratch,
        compiler_params=pltpu.CompilerParams(vmem_limit_bytes=VMEM_LIMIT),
    )(*operands)
    return Box(zip(outputs, results))


MASKED, COUNTED, VALID, KEEP = 0, 1, 2, 3


def column(room, index):
    return room.columns[:, index : index + 1]


def keep_of(room, block, branch):
    return column(room, KEEP + 2 * block + branch)


def vector(room, row):
    return room.vectors[row : row + 1, :]


def low_gates(room, block):
    return room.vectors[10 * block + 6 : 10 * block + 10, :].astype(BF16)


def correlate(padded, taps, level, flip):
    width = KERNEL_SIZES[level]
    first = KERNEL_STARTS[level]
    margin = width // 2
    lanes = padded.shape[-1]
    sums = [None] * GRID
    for dx in range(width):
        weights = []
        for dy in range(width):
            tap = dy * width + dx
            if flip:
                tap = width * width - 1 - tap
            weights.append(jnp.broadcast_to(taps[first + tap : first + tap + 1, :], (GRID, lanes)))
        for row in range(GRID):
            window = padded[row, 8 - margin + dx : 8 - margin + dx + GRID, :]
            for dy in range(width):
                out = row - dy + margin
                if 0 <= out < GRID:
                    term = window * weights[dy]
                    sums[out] = term if sums[out] is None else sums[out] + term
    return sums


def correlate_taps(padded, grads, d_taps, at_lanes, level):
    width = KERNEL_SIZES[level]
    first = KERNEL_STARTS[level]
    margin = width // 2
    for dx in range(width):
        sums = [None] * width
        for row in range(GRID):
            window = padded[row, 8 - margin + dx : 8 - margin + dx + GRID, :]
            for dy in range(width):
                out = row - dy + margin
                if 0 <= out < GRID:
                    term = window * grads[out]
                    sums[dy] = term if sums[dy] is None else sums[dy] + term
        for dy in range(width):
            tap = first + dy * width + dx
            d_taps[tap : tap + 1, at_lanes] = column_sum(sums[dy])


def clear_margins(padded):
    lanes = padded.shape[-1]
    for row in range(GRID):
        padded[row, 0:8, :] = jnp.zeros((8, lanes), F32)
        padded[row, 8 + GRID : 16 + GRID, :] = jnp.zeros((8, lanes), F32)


def rows_at(row):
    return slice(row * GRID, (row + 1) * GRID)


def gate_part(gates, row, level, lanes):
    part = gates[rows_at(row), level * LANES : (level + 1) * LANES]
    return part if lanes == LANES else part[:, 0:1]


def lane_range(group, groups, lanes):
    if groups == 1:
        return slice(0, lanes)
    return pl.ds(pl.multiple_of(group * lanes, lanes), lanes)


def tap_room(tap_count):
    return -(-tap_count // 8) * 8


def split_three(values):
    high = values.astype(BF16)
    rest = values - high.astype(F32)
    middle = rest.astype(BF16)
    return (high, middle, (rest - middle.astype(F32)).astype(BF16))


def pack_rows(here, sources, taps):
    width = sources[0][0].shape[3]
    counts = [rows // parts for _array, _block, _first, rows, parts in sources]
    rows = sum(counts) + (0 if taps is None else taps.shape[1])

    def body(here_ref, *refs):
        wide_refs = refs[: len(sources)]
        rest = refs[len(sources) :]
        out_ref = rest[0] if taps is None else rest[1]
        buffers = rest[-1 - len(sources) : -1]
        sems = rest[-1]
        copies = []
        for at, (ref, (_array, block, first, _rows, parts)) in enumerate(zip(wide_refs, sources)):
            if parts > 1:
                first = pl.multiple_of(first + here_ref[2] * counts[at], 8)
            source = ref.at[block, here_ref[0], pl.ds(first, counts[at]), :]
            copies.append(pltpu.make_async_copy(source, buffers[at], sems.at[at]))
            copies[-1].start()
        row = sum(counts)
        if taps is not None:
            own, count = taps.shape[1:]
            out_ref[row : row + own, :] = jnp.zeros((own, width), BF16)
            splits = [split_three(rest[0][b]) for b in range(BLOCKS)]
            wide = (splits[0][0], splits[1][0], splits[0][1])
            thin = (splits[1][1], splits[0][2], splits[1][2])
            for chosen, at_core in ((wide, 0), (thin, 1)):

                @pl.when(here_ref[0] == at_core)
                def _():
                    for index, part in enumerate(chosen):
                        at = index * LANES
                        out_ref[row : row + own, at : at + count] = part

        row = 0
        for copy, buffer, count in zip(copies, buffers, counts):
            copy.wait()
            out_ref[row : row + count, :] = buffer[...].astype(BF16)
            row += count

    extra = [] if taps is None else [taps]
    return pl.pallas_call(
        body,
        name=pack_rows.__name__,
        in_specs=[pl.BlockSpec(memory_space=pltpu.SMEM)]
        + [pl.BlockSpec(memory_space=pltpu.HBM) for _ in sources]
        + [pl.BlockSpec(memory_space=pltpu.VMEM) for _ in extra],
        out_specs=pl.BlockSpec(memory_space=pltpu.VMEM),
        out_shape=jax.ShapeDtypeStruct((rows, width), BF16),
        scratch_shapes=[pltpu.VMEM((count, width), F32) for count in counts]
        + [pltpu.SemaphoreType.DMA((len(sources),))],
        compiler_params=pltpu.CompilerParams(vmem_limit_bytes=VMEM_LIMIT),
    )(
        here,
        *[pltpu.with_memory_space_constraint(array, pltpu.HBM) for array, *_rest in sources],
        *extra,
    )


def taps_stage(tap_count, groups, lanes):
    room_rows = tap_room(tap_count)
    used = BLOCKS * room_rows

    def join_taps(room):
        wide = room.wide[...]
        thin = room.thin[...]
        shape = (used, wide.shape[1])
        row = lax.broadcasted_iota(jnp.int32, shape, 0)
        lane = lax.broadcasted_iota(jnp.int32, shape, 1)
        upper = row >= room_rows
        tap = jnp.where(upper, row - room_rows, row)
        tap = jnp.where(tap < tap_count, tap, -8 * LANES)

        def chosen(lower_places, upper_places):
            marks = jnp.zeros(shape, F32)
            for places, side in ((lower_places, False), (upper_places, True)):
                for place in places:
                    hit = jnp.logical_and(lane == tap + place * LANES, upper == side)
                    marks = jnp.where(hit, 1.0, marks)
            return marks.astype(BF16)

        taps = times_transposed(chosen((0, 2), (1,)), wide)
        taps = taps + times_transposed(chosen((1,), (0, 2)), thin)
        for b in range(BLOCKS):
            for j in range(groups):
                room.taps[b, j] = taps[
                    b * room_rows : (b + 1) * room_rows, j * lanes : (j + 1) * lanes
                ]

    return join_taps


def inputs_stage(block, groups, lanes):
    def focal_inputs(room):
        unit, _scale = normalize(room.x[...])
        first = unit * vector(room, 10 * block) + vector(room, 10 * block + 1)
        first = first.astype(BF16)
        width = first.shape[1]
        gate_low = low_gates(room, block)
        for level in range(4):
            spread = jnp.broadcast_to(gate_low[level : level + 1], (LANES, width))
            room.gates[:, level * LANES : (level + 1) * LANES] = times_transposed(
                first, spread
            )
        key = room.key
        for j in range(groups):
            room.context[j] = times_transposed(first, key[j * lanes : (j + 1) * lanes, :])
        room.query_out[...] = times_transposed(first, room.query[...])
        room.flush(room.gates, room.context, room.query_out)

    return focal_inputs


def focal_stage(block, groups, lanes):
    def focal_levels(room):
        padded = room.padded
        taps, context, gates, low, pool = room.taps, room.context, room.gates, room.low, room.pool
        fields = [room.k1, room.k2, room.k3]
        slopes = [room.s1, room.s2, room.s3]
        clear_margins(padded)
        valid = room.image_columns[:, VALID : VALID + 1]
        valid_total = column_sum(valid)

        def group(j, carry):
            tap = taps.at[block, j]
            for row in range(GRID):
                padded[row, 8 : 8 + GRID, :] = context[j, rows_at(row), :]
            for level in range(3):
                sums = correlate(padded, tap, level, False)
                for row in range(GRID):
                    value, slope = gelu_pair(sums[row])
                    fields[level][j, rows_at(row), :] = value
                    slopes[level][j, rows_at(row), :] = slope
                    if level < 2:
                        padded[row, 8 : 8 + GRID, :] = value
            mean = column_sum(fields[2][j] * valid) / valid_total
            pooled, pooled_slope = gelu_pair(mean)
            pool[j, 0:1, :] = pooled
            pool[j, 1:2, :] = pooled_slope / valid_total
            pool[j, 2:8, :] = jnp.zeros((6, lanes), F32)
            at = lane_range(j, groups, lanes)
            for row in range(GRID):
                summed = pooled * gate_part(gates, row, 3, lanes)
                for level in range(3):
                    summed = summed + fields[level][j, rows_at(row), :] * gate_part(
                        gates, row, level, lanes
                    )
                low[rows_at(row), at] = summed.astype(BF16)
            return carry

        if groups > 1:
            lax.fori_loop(0, groups, group, 0)
        else:
            group(0, 0)
        room.flush(room.k1, room.k2, room.k3, room.s1, room.s2, room.s3, room.pool, room.low)

    return focal_levels


def mix_stage(block):
    def mix_forward(room):
        modulator = times_transposed(room.low[...], room.mix[...])
        room.mod[...] = modulator
        room.flush(room.mod)
        product = (room.query_out[...] * modulator).astype(BF16)
        branch = matmul(product, room.proj[...]) + vector(room, 10 * block + 4)
        room.middle[...] = room.x[...] + keep_of(room, block, 0) * branch

    return mix_forward


def mlp_stage(block):
    def mlp_forward(room):
        middle = room.middle[...]
        unit, _scale = normalize(middle)
        second = unit * vector(room, 10 * block + 2) + vector(room, 10 * block + 3)
        second = second.astype(BF16)
        up = room.up
        step = up.shape[0] // 4
        for part in range(4):
            at = slice(part * step, (part + 1) * step)
            value, slope = gelu_pair(times_transposed(second, up[at, :]))
            room.hidden[:, at] = value.astype(BF16)
            room.slope[:, at] = slope
        room.flush(room.hidden, room.slope)
        lowered = matmul(room.hidden[...], room.down[...]) + vector(room, 10 * block + 5)
        room.out[...] = middle + keep_of(room, block, 1) * lowered

    return mlp_forward


def embed_stage(room):
    outer = 10 * BLOCKS
    embedded = matmul(room.patches[...], room.embed[...].astype(BF16))
    embedded = embedded + vector(room, outer)
    room.embedded[...] = embedded
    room.flush(room.embedded)
    unit, _scale = normalize(embedded)
    mask = column(room, MASKED)
    state = unit * vector(room, outer + 1) + vector(room, outer + 2)
    room.x[...] = state * (1.0 - mask) + vector(room, outer + 5) * mask


def store_halves(core, kept, sent, at, first, second):
    chan, _rows, width = kept.shape
    rows = first.shape[0] // chan
    first = first.reshape(chan, rows, width).astype(BF16)
    second = second.reshape(chan, rows, width).astype(BF16)

    @pl.when(core == 0)
    def _():
        kept[:, at : at + rows, :] = first
        sent[:, at : at + rows, :] = second

    @pl.when(core != 0)
    def _():
        kept[:, at : at + rows, :] = second
        sent[:, at : at + rows, :] = first


def head_stage(at):
    def head_step(room):
        outer = 10 * BLOCKS
        gain = vector(room, outer + 3)
        unit, scale = normalize(room.x[...])
        low = (unit * gain + vector(room, outer + 4)).astype(BF16)
        head_low = room.head[...].astype(BF16)
        error = matmul(low, head_low) - room.patches[...].astype(F32)
        denom = room.denom[0, 0]
        weighted = column(room, COUNTED) * error
        loss = column_sum(weighted * error) / denom
        d_pred = (2.0 * weighted / denom).astype(BF16)
        grad = contract_rows(low, d_pred)
        half = grad.shape[1] // 2
        core = room.where[0]
        store_halves(core, room.kept, room.sent, at, grad[:, :half], grad[:, half:])
        d_final = times_transposed(d_pred, head_low)
        room.d_out[...] = norm_backward(d_final, unit, scale, gain)
        sums = room.sums
        width = low.shape[1]
        sums[0:1, :] = column_sum(d_final * unit)
        sums[1:2, :] = column_sum(d_final)
        parts = [loss[:, at : at + width] for at in range(0, loss.shape[1], width)]
        sums[2:3, :] = sum(parts[1:], parts[0])
        sums[3:8, :] = jnp.zeros((5, width), F32)

    return head_step


def mlp_back_stage(block, at):
    def mlp_backward(room):
        d_residual = room.d_in[...]
        d_down = d_residual * keep_of(room, block, 1)
        d_low = d_down.astype(BF16)
        unit, scale = normalize(room.middle[...])
        gain = vector(room, 10 * block + 2)
        second = (unit * gain + vector(room, 10 * block + 3)).astype(BF16)
        grad_down = contract_rows(room.hidden[...], d_low)
        d_pre = (times_transposed(d_low, room.down[...]) * room.slope[...]).astype(BF16)
        grad_up = contract_rows(d_pre, second)
        core = room.where[0]
        store_halves(core, room.kept, room.sent, at, grad_up, grad_down)
        d_second = matmul(d_pre, room.up[...])
        room.d_out[...] = d_residual + norm_backward(d_second, unit, scale, gain)
        sums = room.sums
        width = d_low.shape[1]
        sums[0:1, :] = column_sum(d_second * unit)
        sums[1:2, :] = column_sum(d_second)
        sums[2:3, :] = column_sum(d_down)
        sums[3:8, :] = jnp.zeros((5, width), F32)

    return mlp_backward


def mix_back_stage(block, groups, lanes, at):
    def mix_backward(room):
        d_proj = room.d_in[...] * keep_of(room, block, 0)
        d_low = d_proj.astype(BF16)
        d_product = times_transposed(d_low, room.proj[...])
        modulator = room.mod[...]
        query = room.query_out[...]
        d_mod = (d_product * query).astype(BF16)
        mix = room.mix
        for j in range(groups):
            room.d_sum[j] = matmul(d_mod, mix[:, j * lanes : (j + 1) * lanes])
        room.d_query[...] = (d_product * modulator).astype(BF16)
        product = (query * modulator).astype(BF16)
        grad_proj = contract_rows(product, d_low)
        grad_mix = contract_rows(d_mod, room.low[...])
        core = room.where[0]
        store_halves(core, room.kept, room.sent, at, grad_mix, grad_proj)
        sums = room.sums
        width = d_low.shape[1]
        sums[0:1, :] = column_sum(d_proj)
        sums[1:8, :] = jnp.zeros((7, width), F32)

    return mix_backward


def focal_back_stage(block, groups, lanes):
    def levels_backward(room):
        padded = room.padded
        d_padded = room.d_padded
        clear_margins(padded)
        clear_margins(d_padded)
        d_all, gates, taps, pool = room.d_sum, room.gates, room.taps, room.pool
        fields = [room.context, room.k1, room.k2, room.k3]
        slopes = [room.s1, room.s2, room.s3]
        d_context, d_gates, d_taps = room.d_context, room.d_gates, room.d_taps
        valid = room.image_columns[:, VALID : VALID + 1]
        d_gates[...] = jnp.zeros(d_gates.shape, F32)
        d_taps[...] = jnp.zeros(d_taps.shape, F32)

        def fold(values):
            if lanes == LANES:
                return values
            summed = jnp.sum(values, axis=-1, keepdims=True) / LANES
            return jnp.broadcast_to(summed, (values.shape[0], LANES))

        def group(j, carry):
            tap = taps.at[block, j]
            at = lane_range(j, groups, lanes)
            d_pooled = jnp.zeros((1, lanes), F32)
            for row in range(GRID):
                d_pooled = d_pooled + column_sum(
                    d_all[j, rows_at(row), :] * gate_part(gates, row, 3, lanes)
                )
            d_mean = d_pooled * pool[j, 1:2, :]
            d_field = [d_mean * valid[rows_at(row)] for row in range(GRID)]
            for level in (2, 1, 0):
                d_pre = []
                for row in range(GRID):
                    here = rows_at(row)
                    grad = d_field[row] + d_all[j, here, :] * gate_part(gates, row, level, lanes)
                    grad = grad * slopes[level][j, here, :]
                    d_pre.append(grad)
                    d_padded[row, 8 : 8 + GRID, :] = grad
                    padded[row, 8 : 8 + GRID, :] = fields[level][j, here, :]
                correlate_taps(padded, d_pre, d_taps, at, level)
                d_field = correlate(d_padded, tap, level, True)
            for row in range(GRID):
                d_context[rows_at(row), at] = d_field[row].astype(BF16)
            whole = d_all[j]
            for level in range(3):
                here = slice(level * LANES, (level + 1) * LANES)
                d_gates[:, here] = d_gates[:, here] + fold(whole * fields[level + 1][j])
            here = slice(3 * LANES, 4 * LANES)
            d_gates[:, here] = d_gates[:, here] + fold(whole * pool[j, 0:1, :])
            return carry

        if groups > 1:
            lax.fori_loop(0, groups, group, 0)
        else:
            group(0, 0)
        room.flush(room.d_taps)

    return levels_backward


def inputs_back_stage(block, at):
    def inputs_backward(room):
        unit, scale = normalize(room.x[...])
        gain = vector(room, 10 * block)
        first_wide = (unit * gain + vector(room, 10 * block + 1)).astype(BF16)
        first = first_wide
        first_wide = first.astype(F32)
        rows, width = first.shape
        gate_low = low_gates(room, block).astype(F32)
        sums = room.input_sums
        sums[...] = jnp.zeros((8, width), F32)
        d_first = jnp.zeros((rows, width), F32)
        d_gates = room.d_gates
        for level in range(4):
            here = slice(level * LANES, (level + 1) * LANES)
            col = jnp.sum(d_gates[:, here], axis=-1, keepdims=True)
            d_first = d_first + col * gate_low[level : level + 1]
            sums[2 + level : 3 + level, :] = column_sum(col * first_wide)
        d_query = room.d_query[...]
        d_context = room.d_context[...]
        d_first = d_first + matmul(d_query, room.query[...])
        d_first = d_first + matmul(d_context, room.key[...])
        room.d_out[...] = room.d_in[...] + norm_backward(d_first, unit, scale, gain)
        sums[0:1, :] = column_sum(d_first * unit)
        sums[1:2, :] = column_sum(d_first)
        grad_query = contract_rows(d_query, first)
        grad_key = contract_rows(d_context, first)
        kept, sent = room.kept, room.sent
        core = room.where[0]
        store_halves(core, kept, sent, at, grad_query, grad_key)

    return inputs_backward


def sums_start(tap_count):
    return BLOCKS * tap_room(tap_count)


def small_rows_for(tap_count, chan):
    used = sums_start(tap_count) + 8 * (2 + 3 * BLOCKS)
    return -(-used // (16 * chan)) * (16 * chan)


def embed_back_stage(tap_count, sum_keys, tap_keys, first_row):
    outer = 10 * BLOCKS

    def embed_backward(room):
        mask = column(room, MASKED)
        d_residual = room.d_out[...]
        d_start = d_residual * (1.0 - mask)
        unit, scale = normalize(room.embedded[...])
        d_embed = norm_backward(d_start, unit, scale, vector(room, outer + 1))
        small = room.small
        small[...] = jnp.zeros(small.shape, F32)
        for b, key in enumerate(tap_keys):
            at = b * tap_room(tap_count)
            taps = room.d_taps if key is None else room[key]
            small[at : at + taps.shape[0], :] = taps[...]
        at = sums_start(tap_count)
        small[at : at + 1, :] = column_sum(d_embed)
        small[at + 1 : at + 2, :] = column_sum(d_start * unit)
        small[at + 2 : at + 3, :] = column_sum(d_start)
        small[at + 3 : at + 4, :] = column_sum(d_residual * mask)
        for key in sum_keys:
            at += 8
            small[at : at + 8, :] = room[key][...]
        grad = contract_rows(room.patches[...], d_embed.astype(BF16))
        core = room.where[0]
        kept, sent = room.kept, room.sent
        half = grad.shape[0] // 2
        row = first_row
        store_halves(core, kept, sent, row, grad[:half], grad[half:])
        row += half // kept.shape[0]
        half = small.shape[0] // 2
        store_halves(core, kept, sent, row, small[:half], small[half:])

    return embed_backward


def update_shared_stage(tap_count, own, part, rate):
    def update_shared(room):
        width = room.near0.shape[2]
        core = room.where[0]
        small_half = room.small.shape[0] // 2
        small_part = room.near0.shape[1] - 2 * part
        half_rows = room.embed.shape[0] // 2
        for half, parts in ((core, (room.near0, room.near1)), (1 - core, (room.far0, room.far1))):
            across = pl.ds(pl.multiple_of(half * width, width), width)
            entry = 2
            for ref in parts:
                for slot in range(ref.shape[0]):
                    place = room.where[entry]
                    entry += 1
                    gradient = ref[slot].astype(F32)
                    down = pl.ds(pl.multiple_of(place * part, 8), part)
                    new_weight, new_moment = nesterov(
                        room.head[down, across],
                        room.head_moment[down, across],
                        gradient[:part],
                        rate,
                    )
                    room.new_head[down, across] = new_weight
                    room.new_head_moment[down, across] = new_moment
                    down = pl.ds(pl.multiple_of(half * half_rows + place * part, 8), part)
                    new_weight, new_moment = nesterov(
                        room.embed[down, :],
                        room.embed_moment[down, :],
                        gradient[part : 2 * part],
                        rate,
                    )
                    room.new_embed[down, :] = new_weight
                    room.new_embed_moment[down, :] = new_moment
                    at = pl.multiple_of(half * small_half + place * small_part, 8)
                    room.small[pl.ds(at, small_part), :] = gradient[2 * part :]
        room.flush(room.new_head, room.new_head_moment, room.new_embed, room.new_embed_moment)
        grads = room.small[...]
        small = grads.astype(BF16)

        def sum_row(index, row):
            at = sums_start(tap_count) + 8 * index + row
            return grads[at : at + 1]

        rows = []
        for b in range(BLOCKS):
            inputs_at, mlp_at, mix_at = 1 + 3 * b, 2 + 3 * b, 3 + 3 * b
            rows += [sum_row(inputs_at, 0), sum_row(inputs_at, 1)]
            rows += [sum_row(mlp_at, 0), sum_row(mlp_at, 1)]
            rows += [sum_row(mix_at, 0), sum_row(mlp_at, 2)]
            rows += [sum_row(inputs_at, 2 + level) for level in range(4)]
        head_at = 1 + 3 * BLOCKS
        rows += [sum_row(0, 0), sum_row(0, 1), sum_row(0, 2)]
        rows += [sum_row(head_at, 0), sum_row(head_at, 1), sum_row(0, 3)]
        packed = room.packed
        for at, row in enumerate(rows):
            packed[at : at + 1, :] = row
        gradient = packed[0 : len(rows), :]
        new_weight, new_moment = nesterov(
            room.vectors[...], room.vector_moment[...], gradient, rate
        )
        room.new_vectors[...] = new_weight
        room.new_vector_moment[...] = new_moment
        room.new_vector_average[...] = (
            AVERAGE * room.vector_average[...] + (1.0 - AVERAGE) * new_weight
        )
        loss = jnp.sum(sum_row(head_at, 2), axis=-1, keepdims=True)
        room.loss[...] = jnp.broadcast_to(loss, room.loss.shape)
        first = room.where[1] * own
        source = lax.broadcasted_iota(jnp.int32, (own, width), 1)
        wanted = first + lax.broadcasted_iota(jnp.int32, (own, width), 0)
        chosen = (source == wanted).astype(F32).astype(BF16)
        for b in range(BLOCKS):
            at = b * tap_room(tap_count)
            gradient = times_transposed(chosen, small[at : at + tap_room(tap_count)])
            gradient = gradient[:, :tap_count]
            new_weight, new_moment = nesterov(
                room.kernels[b], room.kernel_moment[b], gradient, rate
            )
            room.new_kernels[b] = new_weight
            room.new_kernel_moment[b] = new_moment
            room.new_kernel_average[b] = (
                AVERAGE * room.kernel_average[b] + (1.0 - AVERAGE) * new_weight
            )

    return update_shared


class Shares:
    def __init__(self, local_rows, chan_size):
        self.count = max(1, IMAGE_ROWS // local_rows)
        self.groups = [
            list(range(first, first + self.count)) for first in range(0, chan_size, self.count)
        ]

    def to_images(self, values):
        whole = lax.all_to_all(
            values[0], "chan", 1, 0, axis_index_groups=self.groups, tiled=True
        )
        return whole[None]

    def to_rows(self, values):
        return lax.all_to_all(values, "chan", 0, 1, axis_index_groups=self.groups, tiled=True)

    def all_rows(self, values):
        return lax.all_gather(
            values, "chan", axis=0, axis_index_groups=self.groups, tiled=True
        )

    def sum_rows(self, values):
        return lax.psum_scatter(
            values, "chan", scatter_dimension=0, axis_index_groups=self.groups, tiled=True
        )

    def channels(self, values):
        size = values.shape[-1] // self.count
        place = lax.axis_index("chan") % self.count
        return lax.dynamic_slice_in_dim(values, place * size, size, values.ndim - 1)

    def spread(self, values):
        size = values.shape[1]
        place = lax.axis_index("chan") % self.count
        whole = jnp.zeros((values.shape[0], size * self.count), values.dtype)
        return lax.dynamic_update_slice_in_dim(whole, values, place * size, 1)


def hold(array):
    return (array, HOLD)


def fetch(array):
    return (array, FETCH)


def fetch_all(made, names):
    return {name: fetch(made[name]) for name in names}


def shards(
    patches,
    valid_mask,
    target_mask,
    keep_mask,
    embed_weight,
    embed_moment,
    head_weight,
    head_moment,
    vectors,
    vector_moment,
    vector_average,
    focal_input,
    focal_moment,
    focal_average,
    mixers,
    mixer_moment,
    mixer_average,
    mlp_weights,
    mlp_moment,
    mlp_average,
    kernels,
    kernel_moment,
    kernel_average,
):
    links = Links()
    rows, patch_in = patches.shape
    group_rows = valid_mask.shape[0]
    own = focal_input.shape[-1]
    own_hidden = mlp_weights.shape[-1]
    hidden_width = own_hidden * links.chan
    tap_count = kernels.shape[1]
    width = vectors.shape[1]
    shares = Shares(rows, links.chan)
    shared = shares.count > 1
    channels = width // shares.count
    lanes = LANES if channels % LANES == 0 else channels
    groups = channels // lanes
    room_rows = tap_room(tap_count)
    cut_rows = own_hidden // 2 if links.nx > 1 and own_hidden % (16 * links.nx) == 0 else 0
    plain_rows = own_hidden - cut_rows
    cut_part = cut_rows // links.nx

    def together(values, moves):
        got = [links.swap(*move) for move in moves]
        return lax.optimization_barrier((values, got))

    def beside(call, gate, moves):
        made = call(after(gate, *[move[0] for move in moves]))
        made, got = together(dict(made), moves)
        return (Box(made), got)

    here = links.here()
    focal_rows = jnp.transpose(focal_input, (0, 2, 3, 1))
    mixer_rows = jnp.transpose(mixers, (0, 1, 3, 2))
    mlp_rows = jnp.transpose(mlp_weights, (0, 1, 3, 2))
    kernel_rows = jnp.transpose(kernels, (0, 2, 1))
    focal_layout = dict(query=(0, 0), mix=(0, own), key=(1, 0), proj=(1, own))
    first_layout = dict(focal_layout, wide=(0, 2 * own), thin=(1, 2 * own))
    mlp_layout = dict(up=(0, 0), down=(1, 0))

    def slots_of(parts):
        return [(k, d) for k, part in enumerate(parts) for d in range(part.shape[0])]

    def pieces_of(gather, far, layout, count, apart=False):
        rows = [place * (1 if apart else count) for place, _x in links.places(gather.masks)]
        slots = slots_of(gather.parts)
        matrices = {
            name: (half, [(k, d, first, count, at) for at, (k, d) in enumerate(slots)])
            for name, (half, first) in layout.items()
        }
        return Pieces(links.where(rows), gather.parts, far, matrices, len(slots))

    def cut_pieces(gather, crossed, masks, far):
        rows, entries = [], []
        for (k, d), (place, x) in zip(slots_of(gather.parts), links.places(gather.masks)):
            entries.append((k, d, 0, plain_rows, len(rows)))
            rows.append(place * own_hidden)
            entries.append((k, d, plain_rows, cut_part, len(rows)))
            rows.append(place * own_hidden + plain_rows + x * cut_part)
        for (k, d), (place, x) in zip(slots_of(crossed), links.places(masks)):
            entries.append((k + len(gather.parts), d, 0, cut_part, len(rows)))
            rows.append(place * own_hidden + plain_rows + x * cut_part)
        matrices = dict(up=(0, entries), down=(1, entries))
        return Pieces(links.where(rows), gather.parts + crossed, far, matrices, links.chan)

    first_row = links.place * rows
    validity = valid_mask.astype(F32)
    masked = target_mask.astype(F32)
    keep_rows = jnp.repeat(
        keep_mask.reshape(keep_mask.shape[0], -1).astype(F32) / KEEP_RATE, IMAGE_ROWS, axis=0
    )
    table = jnp.concatenate(
        [
            masked[:, None],
            (masked * validity)[:, None],
            validity[:, None],
            keep_rows,
            jnp.zeros((group_rows, 1), F32),
        ],
        axis=1,
    )
    columns = lax.dynamic_slice_in_dim(table, first_row, rows)
    image_columns = columns
    if shared:
        image_columns = lax.dynamic_slice_in_dim(
            table, first_row // IMAGE_ROWS * IMAGE_ROWS, IMAGE_ROWS
        )
    group_count = jnp.broadcast_to(jnp.sum(validity * masked), (8, LANES))
    basic = dict(vectors=fetch(vectors), columns=fetch(columns))
    grid_columns = dict(image_columns=fetch(image_columns))

    whole = (rows, width)
    focal = [None] * BLOCKS
    mlp = [None] * BLOCKS
    focal[0] = Gather(
        links, pack_rows(
            here, [(focal_rows, 0, 0, own, 1), (mixer_rows, 0, 0, own, 1)], kernel_rows
        )
    )
    moves = focal[0].direct()
    embedded = run_kernel(
        [embed_stage],
        dict(patches=fetch(patches), embed=fetch(embed_weight), **basic),
        dict(x=(whole, F32, HOLD), embedded=(whole, F32, FETCH)),
    )
    sources = [(mlp_rows, 0, 0, plain_rows, 1)]
    if cut_rows:
        sources.append((mlp_rows, 0, plain_rows, cut_rows, links.nx))
    packed = pack_rows(here, sources, None)
    (x, packed), got = together((embedded.x, packed), moves)
    focal[0].take_direct(got)
    mlp[0] = Gather(links, packed)
    z_first, *z_rest = links.bits("z")
    y_move = focal[0].early("y")
    (move,) = mlp[0].moves("z", z_first)
    packed = (
        pack_rows(here, [(focal_rows, 1, 0, own, 1), (mixer_rows, 1, 0, own, 1)], None),
        pack_rows(here, [(mlp_rows, 1, 0, own_hidden, 1)], None),
    )
    packed, got = together(packed, [move])
    mlp[0].take(got[0], "z", z_first)
    focal[1] = Gather(links, packed[0])
    mlp[1] = Gather(links, packed[1])

    def take_z(gather, received):
        for step, one in zip(z_rest, received):
            gather.take(one, "z", step)

    moves = [(mlp[0].stack, "z", step) for step in z_rest]
    moves += [(focal[0].stack, *y_move), (focal[1].stack, "z", z_first)]
    x, got = together(x, moves)
    take_z(mlp[0], got[:-2])
    focal[0].take(got[-2], *y_move, True)
    focal[1].take(got[-1], "z", z_first)

    def twins(gather, values):
        values, got = together(values, [(part, "core", 1) for part in gather.parts])
        return (values, got)

    y_move = mlp[0].early("y")
    x, far = twins(focal[0], after(x, mlp[0].stack))
    focal_pieces = [pieces_of(focal[0], far, first_layout, own), None]
    mlp_pieces = [None, None]

    field_shape = (groups, IMAGE_ROWS, lanes)
    field = (field_shape, F32, FETCH)
    padded = pltpu.VMEM((GRID, GRID + 16, lanes), F32)
    gates_out = dict(gates=((IMAGE_ROWS, 4 * LANES), F32, FETCH))
    focal_out = dict(k1=field, k2=field, k3=field, s1=field, s2=field, s3=field)
    focal_out.update(pool=((groups, 8, lanes), F32, FETCH))
    mixed_out = dict(mod=(whole, F32, FETCH), middle=(whole, F32, HOLD))
    query_out = dict(query_out=(whole, F32, FETCH))
    low_out = dict(low=(whole, BF16, FETCH))
    mlp_out = dict(
        hidden=((rows, hidden_width), BF16, FETCH), slope=((rows, hidden_width), F32, FETCH)
    )
    weights_in = dict(key=0, query=0, mix=0, proj=0)
    up_down = dict(up=0, down=0)
    taps_shape = (BLOCKS, groups, room_rows, lanes)

    def focal_apart(b, x, taps):
        pieces = focal_pieces[b]
        made = run_kernel(
            [inputs_stage(b, 1, width)],
            dict(x=hold(x), **basic),
            dict(
                gates=((rows, 4 * LANES), F32, FETCH),
                context=((1, rows, width), F32, FETCH),
                **query_out,
            ),
            {},
            [(pieces, dict(key=0, query=0))],
        )
        made.update(gates=shares.all_rows(made.gates), context=shares.to_images(made.context))
        made.update(
            run_kernel(
                [focal_stage(b, groups, lanes)],
                dict(
                    context=fetch(made.context),
                    gates=fetch(made.gates),
                    taps=fetch(taps),
                    **grid_columns,
                ),
                dict(low=((IMAGE_ROWS, channels), BF16, FETCH), **focal_out),
                dict(padded=padded),
            )
        )
        made.update(low=shares.to_rows(made.low))
        made.update(
            run_kernel(
                [mix_stage(b)],
                dict(
                    x=hold(x), low=fetch(made.low), query_out=fetch(made.query_out), **basic
                ),
                mixed_out,
                {},
                [(pieces, dict(mix=0, proj=0))],
            )
        )
        return made

    def focal_stages(b):
        return [inputs_stage(b, groups, lanes), focal_stage(b, groups, lanes), mix_stage(b)]

    focal_made_out = dict(
        context=field, **gates_out, **query_out, **focal_out, **low_out, **mixed_out
    )

    def first_focal(x):
        if shared:
            taps = run_kernel(
                [taps_stage(tap_count, 1, width)],
                {},
                dict(taps=((BLOCKS, 1, room_rows, width), F32, FETCH)),
                {},
                [(focal_pieces[0], dict(wide=0, thin=0))],
            ).taps
            taps = shares.channels(taps)
            return Box(focal_apart(0, x, taps), taps=taps)
        return run_kernel(
            [taps_stage(tap_count, groups, lanes)] + focal_stages(0),
            dict(x=hold(x), **basic, **grid_columns),
            dict(taps=(taps_shape, F32, FETCH), **focal_made_out),
            dict(padded=padded),
            [(focal_pieces[0], dict(wide=0, thin=0, **weights_in))],
            False,
        )

    moves = [(mlp[0].stack, *y_move)]
    moves += [(focal[1].stack, "z", step) for step in z_rest[:1]]
    moves += [(mlp[1].stack, "z", z_first)]
    x_first, *x_rest = links.bits("x")
    saved = [Box(x=x), Box()]
    made, got = beside(first_focal, x, moves)
    saved[0].update(made)
    taps = made.taps
    mlp[0].take(got[0], *y_move, True)
    take_z(focal[1], got[1:-1])
    mlp[1].take(got[-1], "z", z_first)
    y_move = focal[1].early("y")
    moves = [(focal[1].stack, *y_move)]
    moves += [(mlp[1].stack, "z", step) for step in z_rest]
    crossed, crossed_masks = [], []
    if cut_rows:
        cut_stack = jnp.concatenate([part[:, plain_rows:] for part in mlp[0].parts])
        cut_gather = Gather(links, cut_stack[0])
        cut_gather.stack, cut_gather.masks = cut_stack, mlp[0].masks
        x_move = cut_gather.early("x")
        moves += [(cut_gather.stack, *x_move)]
    group_count = after(group_count, saved[0].middle)
    moves.insert(0, (group_count, "core", 1))
    middle, got = together(saved[0].middle, moves)
    group_count = group_count + got.pop(0)
    focal[1].take(got[0], *y_move, True)
    take_z(mlp[1], got[1 : 1 + len(z_rest)])
    if cut_rows:
        held = cut_stack.shape[0]
        cut_gather.take(got[-1], *x_move, True)
        crossed = [cut_gather.parts[0][held:], cut_gather.parts[1]]
        crossed = [part for part in crossed if part.shape[0]]
        crossed_masks = cut_gather.masks[held:]
    y_move = mlp[1].early("y")
    arrays = mlp[0].parts + crossed
    moves = [(part, "core", 1) for part in arrays + focal[1].parts]
    middle, got = together(after(middle, mlp[1].stack), moves)
    far, far_focal = got[: len(arrays)], got[len(arrays) :]
    if cut_rows:
        mlp_pieces[0] = cut_pieces(mlp[0], crossed, crossed_masks, far)
    else:
        mlp_pieces[0] = pieces_of(mlp[0], far, mlp_layout, own_hidden)
    focal_pieces[1] = pieces_of(focal[1], far_focal, focal_layout, own)

    def second_focal(middle):
        inputs = dict(middle=hold(middle), **basic)
        outputs = dict(out=(whole, F32, FETCH), **mlp_out)
        if shared:
            made = run_kernel(
                [mlp_stage(0)], inputs, outputs, {}, [(mlp_pieces[0], up_down)]
            )
            lower = Box(hidden=made.hidden, slope=made.slope)
            return Box(focal_apart(1, made.out, taps), x=made.out, lower=dict(lower))
        made = run_kernel(
            [renamed(mlp_stage(0), middle=0, out=1)]
            + [renamed(stage, x=1) for stage in focal_stages(1)],
            {0: hold(middle), **basic, **grid_columns, **dict(taps=fetch(taps))},
            {1: (whole, F32, FETCH), **mlp_out, **focal_made_out},
            dict(padded=padded),
            [(mlp_pieces[0], up_down), (focal_pieces[1], weights_in)],
        )
        lower = dict(hidden=made.hidden, slope=made.slope)
        upper = Box({key: made[key] for key in focal_made_out})
        upper.update(x=made[1], lower=lower)
        return upper

    moves = [(mlp[1].stack, *y_move), (group_count, "x", x_first)]
    made, got = beside(second_focal, middle, moves)
    mlp[1].take(got[0], *y_move, True)
    counted = group_count + got[1]
    for step in x_rest:
        counted = counted + links.swap(counted, "x", step)
    denominator = counted[0:1, 0:1] * PATCH_IN
    saved[0].update(made.lower)
    saved[1].update(made)
    middle, far = twins(mlp[1], saved[1].middle)
    mlp_pieces[1] = pieces_of(mlp[1], far, mlp_layout, own_hidden)

    sums_out = ((8, width), F32, FETCH)
    embed_rows = patch_in // (2 * links.chan)
    small_rows = small_rows_for(tap_count, links.chan)
    small_part = small_rows // (2 * links.chan)
    hidden_shape = (rows, hidden_width)
    mix_at = own_hidden
    upper_lead = own_hidden + own
    head_at = upper_lead + own
    lower_lead = own_hidden + own
    upper_count = head_at + embed_rows
    lower_count = lower_lead + own + embed_rows + small_part
    d_shape = (1, rows, width) if shared else field_shape
    levels_names = dict(context=0, gates=0, k1=0, k2=0, k3=0, s1=0, s2=0, s3=0, pool=0)
    mix_names = dict(query_out=0, mod=0, low=0)
    levels_temps = dict(padded=padded, d_padded=padded)
    between = dict(
        d_context=pltpu.VMEM(whole, BF16),
        d_gates=pltpu.VMEM((rows, 4 * LANES), F32),
        **levels_temps,
    )
    tap_shape = (room_rows, width)

    def pair_of(count):
        shape = (links.chan, count, width)
        return dict(kept=(shape, BF16, HOLD), sent=(shape, BF16, HOLD))

    def levels_in(b):
        return dict(taps=fetch(taps), **fetch_all(saved[b], levels_names), **grid_columns)

    head_names = dict(x=0, d_out=1, sums=5)
    head_first = upper_lead if shared else head_at
    first_stages = [
        renamed(mlp_stage(1), out=0),
        renamed(head_stage(head_first), **head_names),
        renamed(mlp_back_stage(1, 0), d_in=1, d_out=2, sums=3),
        renamed(mix_back_stage(1, d_shape[0], d_shape[2], mix_at), d_in=2, sums=4),
    ]
    first_in = dict(
        middle=hold(middle),
        head=fetch(head_weight),
        patches=fetch(patches),
        denom=(denominator, SCALAR),
        **basic,
        **fetch_all(saved[1], mix_names),
    )
    first_temps = {
        0: pltpu.VMEM(whole, F32),
        1: pltpu.VMEM(whole, F32),
        **dict(hidden=pltpu.VMEM(hidden_shape, BF16), slope=pltpu.VMEM(hidden_shape, F32)),
    }
    sums_outs = {3: sums_out, 4: sums_out, 5: sums_out}
    mlp_weights_in = (mlp_pieces[1], up_down)
    mixer_in = dict(proj=0, mix=0)
    inputs_in = dict(query=0, key=0)

    def levels_apart(b, d_sum):
        made = run_kernel(
            [focal_back_stage(b, groups, lanes)],
            dict(d_sum=fetch(shares.to_images(d_sum)), **levels_in(b)),
            dict(
                d_context=((IMAGE_ROWS, channels), BF16, FETCH),
                d_gates=((IMAGE_ROWS, 4 * LANES), F32, FETCH),
                d_taps=((room_rows, channels), F32, FETCH),
            ),
            levels_temps,
        )
        return Box(
            d_context=shares.to_rows(made.d_context),
            d_gates=shares.sum_rows(made.d_gates),
            d_taps=shares.spread(made.d_taps),
        )

    def joined(first, second):
        return Box(
            kept=jnp.concatenate([first.kept, second.kept], axis=1),
            sent=jnp.concatenate([first.sent, second.sent], axis=1),
        )

    if shared:
        first = run_kernel(
            first_stages,
            first_in,
            {
                2: (whole, F32, HOLD),
                **sums_outs,
                **dict(d_query=(whole, BF16, HOLD), d_sum=(d_shape, F32, HOLD)),
                **pair_of(upper_lead + embed_rows),
            },
            first_temps,
            [mlp_weights_in, (focal_pieces[1], mixer_in)],
        )
        levels = levels_apart(1, first.d_sum)
        second = run_kernel(
            [inputs_back_stage(1, 0)],
            dict(
                d_in=hold(first[2]),
                d_query=hold(first.d_query),
                d_context=fetch(levels.d_context),
                d_gates=fetch(levels.d_gates),
                x=fetch(saved[1].x),
                **basic,
            ),
            dict(d_out=(whole, F32, HOLD), input_sums=sums_out, **pair_of(own)),
            {},
            [(focal_pieces[1], inputs_in)],
        )
        pair = joined(first, second)
        pair = Box(
            (key, jnp.concatenate([array[:, :upper_lead], array[:, -own:], array[:, upper_lead:-own]], 1))
            for key, array in pair.items()
        )
        d_x, d_taps = second.d_out, levels.d_taps
        upper_sums = [second.input_sums, first[3], first[4], first[5]]
    else:
        first = run_kernel(
            first_stages
            + [
                focal_back_stage(1, groups, lanes),
                renamed(inputs_back_stage(1, upper_lead), d_in=2),
            ],
            dict(x=fetch(saved[1].x), **levels_in(1)) | first_in,
            {
                **sums_outs,
                **dict(
                    d_out=(whole, F32, HOLD),
                    input_sums=sums_out,
                    d_taps=(tap_shape, F32, FETCH),
                ),
                **pair_of(upper_count),
            },
            {
                2: pltpu.VMEM(whole, F32),
                **first_temps,
                **dict(d_query=pltpu.VMEM(whole, BF16), d_sum=pltpu.VMEM(d_shape, F32)),
                **between,
            },
            [mlp_weights_in, (focal_pieces[1], mixer_in | inputs_in)],
        )
        pair = first
        d_x, d_taps = first.d_out, first.d_taps
        upper_sums = [first.input_sums, first[3], first[4], first[5]]

    lower_stages = [
        renamed(mlp_back_stage(0, 0), d_out=2, sums=3),
        renamed(mix_back_stage(0, d_shape[0], d_shape[2], mix_at), d_in=2, sums=4),
    ]
    lower_names = dict(hidden=0, slope=0, middle=0)
    sum_keys = [10, 3, 4, 11, 12, 13, 14]
    last_in = {
        **dict(zip(sum_keys[3:], (fetch(array) for array in upper_sums))),
        15: fetch(d_taps),
        **dict(patches=fetch(patches), embedded=fetch(embedded.embedded), x=fetch(saved[0].x)),
    }

    def last_stages(at):
        return [
            renamed(inputs_back_stage(0, at), d_in=2, d_out=1, input_sums=10),
            renamed(
                embed_back_stage(tap_count, sum_keys, [None, 15], at + own), d_out=1
            ),
        ]

    last_temps = {
        1: pltpu.VMEM(whole, F32),
        10: pltpu.VMEM((8, width), F32),
        **dict(small=pltpu.VMEM((small_rows, width), F32)),
    }

    def lower_back(d_x):
        inputs = dict(
            d_in=hold(d_x),
            **fetch_all(saved[0], lower_names),
            **basic,
            **fetch_all(saved[0], mix_names),
        )
        weights = [(mlp_pieces[0], dict(down=0, up=0)), (focal_pieces[0], mixer_in)]
        if shared:
            first = run_kernel(
                lower_stages,
                inputs,
                {
                    2: (whole, F32, HOLD),
                    3: sums_out,
                    4: sums_out,
                    **dict(d_query=(whole, BF16, HOLD), d_sum=(d_shape, F32, HOLD)),
                    **pair_of(lower_lead),
                },
                {},
                weights,
            )
            levels = levels_apart(0, first.d_sum)
            second = run_kernel(
                last_stages(0),
                {
                    2: hold(first[2]),
                    3: fetch(first[3]),
                    4: fetch(first[4]),
                    **last_in,
                    **dict(
                        d_query=hold(first.d_query),
                        d_context=fetch(levels.d_context),
                        d_gates=fetch(levels.d_gates),
                        d_taps=fetch(levels.d_taps),
                        **basic,
                    ),
                },
                pair_of(lower_count - lower_lead),
                last_temps,
                [(focal_pieces[0], inputs_in)],
            )
            return joined(first, second)
        return run_kernel(
            lower_stages + [focal_back_stage(0, groups, lanes)] + last_stages(lower_lead),
            {**inputs, **levels_in(0), **last_in},
            pair_of(lower_count),
            {
                2: pltpu.VMEM(whole, F32),
                3: pltpu.VMEM((8, width), F32),
                4: pltpu.VMEM((8, width), F32),
                **last_temps,
                **dict(d_query=pltpu.VMEM(whole, BF16), d_sum=pltpu.VMEM(d_shape, F32)),
                **dict(d_taps=pltpu.VMEM(tap_shape, F32)),
                **between,
            },
            [weights[0], (focal_pieces[0], mixer_in | inputs_in)],
        )

    (d_x, upper_kept), got = together((d_x, pair.kept), [(pair.sent, "core", 1)])
    upper = Reduction(links, upper_kept, got[0])
    moves, take = next_round(links, [upper])
    made, got = beside(lower_back, d_x, moves)
    take(got)
    moves, take = next_round(links, [upper])
    lower_kept, got = together(made.kept, moves + [(made.sent, "core", 1)])
    take(got[:-1])
    lower = Reduction(links, lower_kept, got[-1])
    rate = 0.2 * math.sqrt(group_rows * lax.axis_size("dp"))
    gate = here
    turn = [lower]
    while not (lower.ready() and upper.done()):
        moves, take = next_round(links, turn)
        gate, got = together(gate, moves)
        take(got)
        turn = [lower, upper]
    common = Gather(
        links,
        jnp.concatenate(
            [
                upper.tail(embed_rows).astype(BF16),
                lower.tail(embed_rows + small_part).astype(BF16),
            ]
        ),
    )
    moves = common.direct()
    count = len(moves)
    more, takes = lower.last_moves()
    gate, got = together(gate, moves + more)
    common.take_direct(got[:count])
    for one, part in zip(takes, got[count:]):
        one(part)
    while not lower.done():
        more, takes = lower.last_moves()
        takes[0](links.swap(*more[0]))
    upper_rows, lower_rows = upper.result(), lower.result()
    y_move = common.early("y")
    common.take(links.swap(common.stack, *y_move), *y_move, True)
    rows_early = jnp.concatenate(
        [
            upper_rows[:own_hidden],
            lower_rows[:own_hidden],
            upper_rows[mix_at : mix_at + own],
            upper_rows[upper_lead:head_at],
            lower_rows[mix_at : lower_lead + own],
        ]
    )
    rows_early, _stack = lax.optimization_barrier((rows_early, common.stack))
    halves = links.both_halves(rows_early)
    ends = (own_hidden, 2 * own_hidden)
    grad_mlp = jnp.stack(
        [
            jnp.stack([part[ends[0] : ends[1]] for part in halves]),
            jnp.stack([part[: ends[0]] for part in halves]),
        ]
    )
    places = [ends[1] + k * own for k in range(5)]
    mix_one, inputs_one, mix_zero, inputs_zero = (
        [part[first:end] for part in halves] for first, end in zip(places, places[1:])
    )
    grad_focal = jnp.stack([jnp.stack(inputs_zero), jnp.stack(inputs_one)])
    grad_mixer = jnp.stack([jnp.stack(mix_zero), jnp.stack(mix_one)])
    results = []
    for weight, moment, average, gradient, order, back in (
        (focal_input, focal_moment, focal_average, grad_focal, (0, 2, 3, 1), (0, 3, 1, 2)),
        (mixers, mixer_moment, mixer_average, grad_mixer, (0, 1, 3, 2), (0, 1, 3, 2)),
        (mlp_weights, mlp_moment, mlp_average, grad_mlp, (0, 1, 3, 2), (0, 1, 3, 2)),
    ):
        weight, moment, average = (
            jnp.transpose(array, order) for array in (weight, moment, average)
        )
        new_weight, new_moment = nesterov(weight, moment, gradient, rate)
        new_average = AVERAGE * average + (1.0 - AVERAGE) * new_weight
        results.extend(
            jnp.transpose(array, back) for array in (new_weight, new_moment, new_average)
        )
    there, results = lax.optimization_barrier((common.parts[1], results))
    common_near = [common.parts[0], there]
    common_far = [links.swap_core(part) for part in common_near]
    common_where = links.where([place for place, _x in links.places(common.masks)])
    head_out = (head_weight.shape, F32, FETCH)
    embed_out = (embed_weight.shape, F32, FETCH)
    vector_out = (vectors.shape, F32, HOLD)
    kernel_out = (kernel_rows.shape, F32, HOLD)
    made = run_kernel(
        [update_shared_stage(tap_count, own, embed_rows, rate)],
        dict(
            where=(common_where, SCALAR),
            near0=hold(common_near[0]),
            near1=hold(common_near[1]),
            far0=hold(common_far[0]),
            far1=hold(common_far[1]),
            head=fetch(head_weight),
            head_moment=fetch(head_moment),
            embed=fetch(embed_weight),
            embed_moment=fetch(embed_moment),
            vectors=fetch(vectors),
            vector_moment=fetch(vector_moment),
            vector_average=fetch(vector_average),
            kernels=fetch(kernel_rows),
            kernel_moment=fetch(jnp.transpose(kernel_moment, (0, 2, 1))),
            kernel_average=fetch(jnp.transpose(kernel_average, (0, 2, 1))),
        ),
        dict(
            new_head=head_out,
            new_head_moment=head_out,
            new_embed=embed_out,
            new_embed_moment=embed_out,
            new_vectors=vector_out,
            new_vector_moment=vector_out,
            new_vector_average=vector_out,
            new_kernels=kernel_out,
            new_kernel_moment=kernel_out,
            new_kernel_average=kernel_out,
            loss=((1, LANES), F32, HOLD),
        ),
        dict(
            packed=pltpu.VMEM((-(-vectors.shape[0] // 8) * 8, width), F32),
            small=pltpu.VMEM((small_rows, width), F32),
        ),
    )
    return (
        made.loss[0, 0],
        made.new_embed,
        made.new_embed_moment,
        made.new_head,
        made.new_head_moment,
        made.new_vectors,
        made.new_vector_moment,
        made.new_vector_average,
        *results,
        *[
            jnp.transpose(array, (0, 2, 1))
            for array in (made.new_kernels, made.new_kernel_moment, made.new_kernel_average)
        ],
    )


def solution(mesh):
    split = P(None, None, None, "chan")
    taps = P(None, None, "chan")
    return jax.shard_map(
        shards,
        mesh=mesh,
        in_specs=(P(("dp", "chan"), None), P("dp"), P("dp"), P("dp", None, None))
        + (P(),) * 7
        + (split,) * 9
        + (taps,) * 3,
        out_specs=(P(),) * 8 + (split,) * 9 + (taps,) * 3,
        check_vma=False,
    )
```

```python
import math

import jax
import jax.numpy as jnp
from jax import lax
from jax.experimental import pallas as pl
from jax.experimental.pallas import tpu as pltpu
from jax.sharding import PartitionSpec as P

PATCH_IN = 768
GRID = 16
BLOCKS = 2
IMAGE_ROWS = GRID * GRID
LANES = 128

EPS = 1e-05
MOMENTUM = 0.9
AVERAGE = 0.5
KEEP_RATE = 0.8
KERNEL_SIZES = (3, 5, 7)
KERNEL_STARTS = (0, 9, 34)
MLP_PARTS = 1
ROOT_HALF = math.sqrt(0.5)
DENSITY = 1.0 / math.sqrt(2.0 * math.pi)
VMEM_LIMIT = 44 << 20
SMALL_LIMIT = 14 << 20
F32 = jnp.float32
BF16 = jnp.bfloat16


def matmul(left, right):
    return jnp.dot(left, right, preferred_element_type=F32)


def contract_rows(left, right):
    return lax.dot_general(left, right, (((0,), (0,)), ((), ())), preferred_element_type=F32)


def times_transposed(left, right):
    return lax.dot_general(left, right, (((1,), (1,)), ((), ())), preferred_element_type=F32)


def normalize(values):
    average = jnp.mean(values, axis=-1, keepdims=True)
    centred = values - average
    variance = jnp.mean(centred * centred, axis=-1, keepdims=True)
    scale = lax.rsqrt(variance + EPS)
    return (centred * scale, scale)


def norm_backward(grad, unit, scale, gain):
    d_unit = grad * gain
    mean_one = jnp.mean(d_unit, axis=-1, keepdims=True)
    mean_two = jnp.mean(d_unit * unit, axis=-1, keepdims=True)
    return (d_unit - mean_one - unit * mean_two) * scale


def column_sum(values):
    return jnp.sum(values, axis=0, keepdims=True)


def gelu_pair(values):
    cumulative = 0.5 + 0.5 * lax.erf(values * ROOT_HALF)
    density = DENSITY * jnp.exp(-0.5 * values * values)
    return (values * cumulative, cumulative + values * density)


def nesterov(weight, moment, gradient, rate):
    new_moment = MOMENTUM * moment + gradient
    new_weight = weight - rate * (gradient + MOMENTUM * new_moment)
    return (new_weight, new_moment)


def after(value, *others):
    return lax.optimization_barrier((value, others))[0]


class Links:
    def __init__(self):
        chan = lax.axis_size("chan")
        self.ny = 1 << ((chan.bit_length() - 1) // 2)
        self.nz = chan // self.ny
        self.nc = 2
        self.nx = lax.axis_size("dp") // self.nc
        self.chan = chan
        self.place = lax.axis_index("chan")
        self.z = self.place // self.ny
        self.y = self.place % self.ny
        group = lax.axis_index("dp")
        self.x = group // self.nc
        self.core = group % self.nc
        self.sizes = {"z": self.nz, "y": self.ny, "x": self.nx}

    def bits(self, axis):
        return [1 << k for k in reversed(range((self.sizes[axis] - 1).bit_length()))]

    def swap(self, values, axis, step):
        if axis in ("z", "y"):
            step = step * self.ny if axis == "z" else step
            return lax.ppermute(values, "chan", [(i, i ^ step) for i in range(self.chan)])
        step = step * self.nc if axis == "x" else step
        return lax.ppermute(values, "dp", [(i, i ^ step) for i in range(self.nx * self.nc)])

    def swap_core(self, values):
        return self.swap(values, "core", 1)

    def cross_x(self, values):
        total = values
        for step in self.bits("x"):
            low = total.astype(values.dtype)
            total = low.astype(F32) + self.swap(low, "x", step).astype(F32)
        return total.astype(F32)

    def mask_of(self, axis, step):
        return tuple(step if name == axis else 0 for name in ("z", "y", "x"))

    def here(self):
        return jnp.stack([self.core, self.place, self.x, self.y, self.z]).astype(jnp.int32)

    def places(self, masks):
        return [
            ((self.z ^ mask_z) * self.ny + (self.y ^ mask_y), self.x ^ mask_x)
            for mask_z, mask_y, mask_x in masks
        ]

    def where(self, rows):
        return jnp.stack([self.core, self.place] + rows).astype(jnp.int32)

    def both_halves(self, summed):
        other = self.swap_core(summed)
        first = self.core == 0
        return (jnp.where(first, summed, other), jnp.where(first, other, summed))


def join(left, right):
    return tuple(a ^ b for a, b in zip(left, right))


def total(terms):
    result = terms[0].astype(F32)
    for term in terms[1:]:
        result = result + term.astype(F32)
    return result.astype(BF16)


class Chain:
    def __init__(self, links, terms, rows, order):
        self.terms = terms
        self.rows = rows
        self.order = list(order)
        self.dims = [("z", k) for k in reversed(range(len(links.bits("z"))))]
        self.dims += [("y", k) for k in reversed(range(len(links.bits("y"))))]

    def low(self):
        parts = [
            lax.slice_in_dim(array[0], first, first + self.rows) for array, first in self.terms
        ]
        return total(parts)


def halve(links, chains):
    arrays = []
    plans = []
    groups = []
    outs = []
    for chain in chains:
        axis, level = chain.order.pop(0)
        places = []
        for array, _first in chain.terms:
            found = [k for k, other in enumerate(arrays) if other is array]
            if not found:
                arrays.append(array)
            places.append(found[0] if found else len(arrays) - 1)
        lead = 1 << len(chain.dims)
        if axis == "x":
            before, behind, rows, count = 0, lead, chain.rows // 2, lead
        else:
            at = chain.dims.index((axis, level))
            before, behind = 1 << at, lead >> (at + 1)
            rows, count = chain.rows, lead // 2
            chain.dims.pop(at)
        key = (axis, level, count)
        mates = [group for group in groups if group[0] == key]
        if mates:
            group = mates[0]
        else:
            group = [key, 0]
            groups.append(group)
        plans.append((chain, places, before, behind, rows, count, group, group[1]))
        group[1] += rows
    width = arrays[0].shape[-1]
    for key, rows in groups:
        outs.append(jax.ShapeDtypeStruct((key[2], rows, width), BF16))
    for _chain, _places, _before, _behind, rows, count, _group, _at in plans:
        outs.append(jax.ShapeDtypeStruct((count, rows, width), BF16))

    def body(here_ref, *refs):
        ins, sends = refs[: len(arrays)], refs[len(arrays) : len(arrays) + len(groups)]
        keeps = refs[len(arrays) + len(groups) :]
        index = dict(y=here_ref[3], z=here_ref[4], x=here_ref[2])
        for plan, keep in zip(plans, keeps):
            chain, places, before, behind, rows, count, group, at = plan
            axis, level, _count = group[0]
            bit = index[axis] >> level & 1
            send = sends[groups.index(group)]
            for side, target, first_row in ((1 - bit, send, at), (bit, keep, 0)):
                for out in range(count):
                    summed = None
                    for place, (_array, first) in zip(places, chain.terms):
                        if axis == "x":
                            start = pl.multiple_of(first + side * rows, 8 if rows % 16 else 16)
                            value = ins[place][out, pl.ds(start, rows), :]
                        else:
                            source = (out // behind * 2 + side) * behind + out % behind
                            value = ins[place][source, first : first + rows, :]
                        value = value.astype(F32)
                        summed = value if summed is None else summed + value
                    target[out, first_row : first_row + rows, :] = summed.astype(BF16)

    made = pl.pallas_call(
        body,
        name=halve.__name__,
        in_specs=[pl.BlockSpec(memory_space=pltpu.SMEM)]
        + [pl.BlockSpec(memory_space=pltpu.VMEM) for _ in arrays],
        out_specs=[pl.BlockSpec(memory_space=pltpu.VMEM) for _ in outs],
        out_shape=outs,
        compiler_params=pltpu.CompilerParams(vmem_limit_bytes=SMALL_LIMIT),
    )(links.here(), *arrays)
    moves = [(sent, key[0], 1 << key[1]) for sent, (key, _rows) in zip(made, groups)]

    def take(received):
        for plan, keep in zip(plans, made[len(groups) :]):
            chain, _places, _before, _behind, rows, _count, group, at = plan
            chain.terms = [(keep, 0), (received[groups.index(group)], at)]
            chain.rows = rows

    return (moves, take)


class Reduction:
    def __init__(self, links, kept, received, cuts):
        self.links = links
        count = kept.shape[1]
        quantum = 16 * links.nx
        cut = 2 * count // (3 + cuts) // quantum * quantum if links.nx > 1 else 0
        over_x = [("x", k) for k in reversed(range(len(links.bits("x"))))]
        over_y = [("y", k) for k in range(len(links.bits("y")))]
        over_z = [("z", k) for k in range(len(links.bits("z")))]
        terms = lambda first: [(kept, first), (received, first)]
        self.plain = Chain(links, terms(cuts * cut), count - cuts * cut, over_y + over_z)
        self.cut = []
        if cut:
            orders = [over_x + over_y + over_z, over_z[:1] + over_x + over_y + over_z[1:]]
            self.cut = [
                Chain(links, terms(k * cut), cut, order) for k, order in enumerate(orders[:cuts])
            ]
        self.sums = links.bits("x")[::-1]
        self.gathers = list(self.sums) if cut else []
        self.plain_rows = None
        self.cut_rows = None

    def open(self):
        return [chain for chain in [self.plain] + self.cut if chain.order]

    def done(self):
        return not self.open() and not self.sums and not self.gathers

    def ready(self):
        return not self.open() and not self.sums

    def last_moves(self):
        moves, takes = [], []
        if not self.plain.order and self.sums:
            if self.plain_rows is None:
                self.plain_rows = self.plain.low()
            low = self.plain_rows.astype(BF16)
            moves.append((low, "x", self.sums.pop(0)))

            def take_sum(received):
                self.plain_rows = low.astype(F32) + received.astype(F32)

            takes.append(take_sum)
        if self.gathers and not any(chain.order for chain in self.cut):
            if self.cut_rows is None:
                self.cut_rows = jnp.stack([chain.low() for chain in self.cut])
            part = self.cut_rows
            step = self.gathers.pop(0)
            moves.append((part, "x", step))

            def take_part(received):
                first = jnp.concatenate([part, received], axis=1)
                second = jnp.concatenate([received, part], axis=1)
                self.cut_rows = jnp.where(self.links.x & step == 0, first, second)

            takes.append(take_part)
        return (moves, takes)

    def tail(self, count):
        return self.plain_rows[self.plain_rows.shape[0] - count :]

    def result(self):
        rows = self.plain_rows.astype(F32)
        if self.cut_rows is None:
            return rows
        width = rows.shape[-1]
        return jnp.concatenate([self.cut_rows.astype(F32).reshape(-1, width), rows])


def next_round(links, reductions):
    lasts = [reduction.last_moves() for reduction in reductions]
    chains = [chain for reduction in reductions for chain in reduction.open()]
    moves, take = halve(links, chains) if chains else ([], None)
    count = len(moves)
    for more, _takes in lasts:
        moves = moves + more
    takes = [one for _more, some in lasts for one in some]

    def take_all(received):
        if take is not None:
            take(received[:count])
        for one, part in zip(takes, received[count:]):
            one(part)

    return (moves, take_all)


class Gather:
    def __init__(self, links, own):
        self.links = links
        self.stack = own[None]
        self.masks = [(0, 0, 0)]
        self.parts = None

    def moves(self, axis, step):
        return [(self.stack, axis, step)]

    def take(self, received, axis, step, keep_apart=False):
        if keep_apart:
            self.parts = [self.stack, received]
        else:
            self.stack = jnp.concatenate([self.stack, received], axis=0)
        extra = self.links.mask_of(axis, step)
        self.masks = self.masks + [join(mask, extra) for mask in self.masks]

    def early(self, axis):
        *steps, last = self.links.bits(axis)
        for step in steps:
            self.take(self.links.swap(self.stack, axis, step), axis, step)
        return (axis, last)

    def direct(self):
        return [(self.stack, "z", step) for step in range(1, self.links.nz)]

    def take_direct(self, received):
        self.stack = jnp.concatenate([self.stack] + received, axis=0)
        self.masks = [self.links.mask_of("z", step) for step in range(self.links.nz)]


class Pieces:
    def __init__(self, where, near, far, matrices, slots):
        self.where = where
        self.near = near
        self.far = far
        self.matrices = matrices
        self.slots = slots
        self.width = near[0].shape[-1]

    def rows(self, name):
        return sum(entry[3] for entry in self.matrices[name][1])

    def count(self, name):
        return len(self.matrices[name][1])

    def arrays(self):
        return [*self.near, *self.far]

    def copies(self, name, where, parts, target, sems):
        half, entries = self.matrices[name]
        near, far = parts[: len(self.near)], parts[len(self.near) :]
        pairs = []
        for at, (array, slot, first, count, entry) in enumerate(entries):
            if len(target.shape) == 3:
                room = target.at[where[2 + entry]]
            else:
                start = pl.multiple_of(where[2 + entry], 8 if count % 16 else 16)
                room = target.at[pl.ds(start, count), :]
            rows = pl.ds(first, count)
            pairs.append(
                tuple(
                    pltpu.make_async_copy(part[array].at[slot, rows, :], room, sems.at[at])
                    for part in (near, far)
                )
            )
        mine = where[0] == half

        def start():
            @pl.when(mine)
            def _():
                for pair in pairs:
                    pair[0].start()

            @pl.when(jnp.logical_not(mine))
            def _():
                for pair in pairs:
                    pair[1].start()

        def wait():
            for pair in pairs:
                pair[0].wait()

        return (start, wait)


class Room:
    def __init__(self):
        self.refs = {}
        self.waits = {}
        self.flushes = []
        self.pending = []

    def __getitem__(self, key):
        wait = self.waits.pop(key, None)
        if wait is not None:
            wait()
        return self.refs[key]

    def __getattr__(self, key):
        return self[key]

    def flush(self, *refs):
        rest = []
        for ref, copy in self.flushes:
            if any(ref is one for one in refs):
                copy.start()
                self.pending.append(copy)
            else:
                rest.append((ref, copy))
        self.flushes = rest

    def flush_next(self, *refs):
        for ref in refs:
            at = [k for k, item in enumerate(self.flushes) if item[0] is ref][0]
            copy = self.flushes.pop(at)[1]
            copy.start()
            self.pending.append(copy)

    def finish(self):
        self.flush(*[ref for ref, _copy in self.flushes])
        for copy in self.pending:
            copy.wait()


class Box(dict):
    __getattr__ = dict.__getitem__


class View:
    def __init__(self, room, names):
        self.room = room
        self.names = names

    def __getitem__(self, key):
        return self.room[self.names.get(key, key)]

    def __getattr__(self, key):
        return self[key]

    def flush(self, *refs):
        self.room.flush(*refs)


def renamed(stage, **names):
    def call(room):
        stage(View(room, names))

    call.__name__ = stage.__name__
    return call


HOLD, FETCH, SCALAR = range(3)


def run_kernel(stages, inputs, outputs, temps=(), weights=(), pinned=True, limit=VMEM_LIMIT):
    temps = dict(temps)
    operands, in_specs, scratch, plan = [], [], [], []

    def scratch_for(shape):
        scratch.append(shape)
        return len(scratch) - 1

    for key, (array, mode) in inputs.items():
        operands.append(array)
        if mode == HOLD:
            in_specs.append(pl.BlockSpec(memory_space=pltpu.VMEM))
            plan.append((key, mode, None))
        elif mode == SCALAR:
            in_specs.append(pl.BlockSpec(memory_space=pltpu.SMEM))
            plan.append((key, mode, None))
        else:
            operands[-1] = pltpu.with_memory_space_constraint(array, pltpu.HBM)
            in_specs.append(pl.BlockSpec(memory_space=pltpu.HBM))
            place = scratch_for(pltpu.VMEM(array.shape, array.dtype))
            plan.append((key, mode, (place, scratch_for(pltpu.SemaphoreType.DMA))))
    loads = []
    for pieces, names in weights:
        first = len(operands)
        operands.append(pieces.where)
        in_specs.append(pl.BlockSpec(memory_space=pltpu.SMEM))
        for array in pieces.arrays():
            if pinned:
                array = pltpu.with_memory_space_constraint(array, pltpu.HBM)
            operands.append(array)
            in_specs.append(pl.BlockSpec(memory_space=pltpu.HBM if pinned else pl.ANY))
        for matrix, apart in names.items():
            shape = (pieces.rows(matrix), pieces.width)
            if apart:
                shape = (pieces.slots, shape[0] // pieces.slots, shape[1])
            place = scratch_for(pltpu.VMEM(shape, BF16))
            sems = scratch_for(pltpu.SemaphoreType.DMA((pieces.count(matrix),)))
            loads.append((matrix, pieces, first, place, sems))
    out_specs, out_shapes, out_plan = [], [], []
    for key, (shape, dtype, mode, *cuts) in outputs.items():
        if mode == HOLD:
            out_specs.append(pl.BlockSpec(memory_space=pltpu.VMEM))
            out_shapes.append(jax.ShapeDtypeStruct(shape, dtype))
            out_plan.append((key, None))
        else:
            out_specs.append(pl.BlockSpec(memory_space=pltpu.HBM))
            out_shapes.append(pltpu.HBM(shape, dtype))
            place = scratch_for(pltpu.VMEM(shape, dtype))
            cuts = cuts or [()]
            sems = [scratch_for(pltpu.SemaphoreType.DMA) for _ in cuts]
            out_plan.append((key, (place, sems, cuts)))
    temp_plan = [(key, scratch_for(shape)) for key, shape in temps.items()]

    def body(*refs):
        ins = refs[: len(operands)]
        outs = refs[len(operands) : len(operands) + len(out_specs)]
        rooms = refs[len(operands) + len(out_specs) :]
        room = Room()
        def load(group):
            for matrix, pieces, first, place, sems in loads:
                if pieces is group:
                    where = ins[first]
                    parts = ins[first + 1 : first + 1 + len(pieces.arrays())]
                    start, wait = pieces.copies(matrix, where, parts, rooms[place], rooms[sems])
                    start()
                    room.refs[matrix] = rooms[place]
                    room.waits[matrix] = wait
                    room.refs.update(where=where)

        for pieces, _names in weights[:1]:
            load(pieces)
        for ref, (key, mode, more) in zip(ins, plan):
            if mode == FETCH:
                place, sem = more
                copy = pltpu.make_async_copy(ref, rooms[place], rooms[sem])
                copy.start()
                room.refs[key] = rooms[place]
                room.waits[key] = copy.wait
            else:
                room.refs[key] = ref
        for pieces, _names in weights[1:]:
            load(pieces)
        for ref, (key, more) in zip(outs, out_plan):
            if more is None:
                room.refs[key] = ref
            else:
                place, sems, cuts = more
                room.refs[key] = rooms[place]
                for sem, cut in zip(sems, cuts):
                    source, target = rooms[place], ref
                    if cut:
                        source, target = source.at[cut], target.at[cut]
                    copy = pltpu.make_async_copy(source, target, rooms[sem])
                    room.flushes.append((rooms[place], copy))
        for key, place in temp_plan:
            room.refs[key] = rooms[place]
        for stage in stages:
            stage(room)
        for key in list(room.waits):
            room[key]
        room.finish()

    results = pl.pallas_call(
        body,
        name=stages[-1].__name__,
        in_specs=in_specs,
        out_specs=out_specs,
        out_shape=out_shapes,
        scratch_shapes=scratch,
        compiler_params=pltpu.CompilerParams(vmem_limit_bytes=limit),
    )(*operands)
    return Box(zip(outputs, results))


MASKED, COUNTED, VALID, KEEP = 0, 1, 2, 3


def column(room, index):
    return room.columns[:, index : index + 1]


def keep_of(room, block, branch):
    return column(room, KEEP + 2 * block + branch)


def vector(room, row):
    return room.vectors[row : row + 1, :]


def low_gates(room, block):
    return room.vectors[10 * block + 6 : 10 * block + 10, :].astype(BF16)


def correlate(padded, taps, level, flip):
    width = KERNEL_SIZES[level]
    first = KERNEL_STARTS[level]
    margin = width // 2
    lanes = padded.shape[-1]
    sums = [None] * GRID
    for dx in range(width):
        weights = []
        for dy in range(width):
            tap = dy * width + dx
            if flip:
                tap = width * width - 1 - tap
            weights.append(jnp.broadcast_to(taps[first + tap : first + tap + 1, :], (GRID, lanes)))
        for row in range(GRID):
            window = padded[row, 8 - margin + dx : 8 - margin + dx + GRID, :]
            for dy in range(width):
                out = row - dy + margin
                if 0 <= out < GRID:
                    term = window * weights[dy]
                    sums[out] = term if sums[out] is None else sums[out] + term
    return sums


def correlate_taps(padded, grads, d_taps, at_lanes, level):
    width = KERNEL_SIZES[level]
    first = KERNEL_STARTS[level]
    margin = width // 2
    for dx in range(width):
        sums = [None] * width
        for row in range(GRID):
            window = padded[row, 8 - margin + dx : 8 - margin + dx + GRID, :]
            for dy in range(width):
                out = row - dy + margin
                if 0 <= out < GRID:
                    term = window * grads[out]
                    sums[dy] = term if sums[dy] is None else sums[dy] + term
        for dy in range(width):
            tap = first + dy * width + dx
            d_taps[tap : tap + 1, at_lanes] = column_sum(sums[dy])


def clear_margins(padded):
    lanes = padded.shape[-1]
    for row in range(GRID):
        padded[row, 0:8, :] = jnp.zeros((8, lanes), F32)
        padded[row, 8 + GRID : 16 + GRID, :] = jnp.zeros((8, lanes), F32)


def rows_at(row):
    return slice(row * GRID, (row + 1) * GRID)


def gate_part(gates, row, level, lanes):
    part = gates[rows_at(row), level * LANES : (level + 1) * LANES]
    return part if lanes == LANES else part[:, 0:1]


def lane_range(group, groups, lanes):
    if groups == 1:
        return slice(0, lanes)
    if isinstance(group, int):
        return slice(group * lanes, (group + 1) * lanes)
    return pl.ds(pl.multiple_of(group * lanes, lanes), lanes)


def tap_room(tap_count):
    return -(-tap_count // 8) * 8


def split_three(values):
    high = values.astype(BF16)
    rest = values - high.astype(F32)
    middle = rest.astype(BF16)
    return (high, middle, (rest - middle.astype(F32)).astype(BF16))


def pack_rows(here, sources, taps):
    width = sources[0][0].shape[3]
    counts = [rows // parts for _array, _block, _first, rows, parts in sources]
    rows = sum(counts) + (0 if taps is None else taps.shape[1])

    def body(here_ref, *refs):
        wide_refs = refs[: len(sources)]
        rest = refs[len(sources) :]
        out_ref = rest[0] if taps is None else rest[1]
        buffers = rest[-1 - len(sources) : -1]
        sems = rest[-1]
        if taps is not None:
            tap_buffer, tap_sem = rest[2:4]
            tap_copy = pltpu.make_async_copy(rest[0], tap_buffer, tap_sem)
            tap_copy.start()
        copies = []
        for at, (ref, (_array, block, first, _rows, parts)) in enumerate(zip(wide_refs, sources)):
            if parts > 1:
                first = pl.multiple_of(first + here_ref[2] * counts[at], 8)
            source = ref.at[block, here_ref[0], pl.ds(first, counts[at]), :]
            copies.append(pltpu.make_async_copy(source, buffers[at], sems.at[at]))
            copies[-1].start()
        row = sum(counts)
        if taps is not None:
            own, count = taps.shape[1:]
            out_ref[row : row + own, :] = jnp.zeros((own, width), BF16)
            tap_copy.wait()
            splits = [split_three(tap_buffer[b]) for b in range(BLOCKS)]
            wide = (splits[0][0], splits[1][0], splits[0][1])
            thin = (splits[1][1], splits[0][2], splits[1][2])
            for chosen, at_core in ((wide, 0), (thin, 1)):

                @pl.when(here_ref[0] == at_core)
                def _():
                    for index, part in enumerate(chosen):
                        at = index * LANES
                        out_ref[row : row + own, at : at + count] = part

        row = 0
        for copy, buffer, count in zip(copies, buffers, counts):
            copy.wait()
            out_ref[row : row + count, :] = buffer[...].astype(BF16)
            row += count

    extra = [] if taps is None else [taps]
    return pl.pallas_call(
        body,
        name=pack_rows.__name__,
        in_specs=[pl.BlockSpec(memory_space=pltpu.SMEM)]
        + [pl.BlockSpec(memory_space=pltpu.HBM) for _ in sources]
        + [pl.BlockSpec(memory_space=pltpu.HBM) for _ in extra],
        out_specs=pl.BlockSpec(memory_space=pltpu.VMEM),
        out_shape=jax.ShapeDtypeStruct((rows, width), BF16),
        scratch_shapes=[
            item
            for array in extra
            for item in (pltpu.VMEM(array.shape, F32), pltpu.SemaphoreType.DMA)
        ]
        + [pltpu.VMEM((count, width), F32) for count in counts]
        + [pltpu.SemaphoreType.DMA((len(sources),))],
        compiler_params=pltpu.CompilerParams(vmem_limit_bytes=SMALL_LIMIT),
    )(
        here,
        *[pltpu.with_memory_space_constraint(array, pltpu.HBM) for array, *_rest in sources],
        *[pltpu.with_memory_space_constraint(array, pltpu.HBM) for array in extra],
    )


def taps_stage(tap_count, groups, lanes):
    room_rows = tap_room(tap_count)
    used = BLOCKS * room_rows

    def join_taps(room):
        wide = room.wide[...]
        thin = room.thin[...]
        shape = (used, wide.shape[1])
        row = lax.broadcasted_iota(jnp.int32, shape, 0)
        lane = lax.broadcasted_iota(jnp.int32, shape, 1)
        upper = row >= room_rows
        tap = jnp.where(upper, row - room_rows, row)
        tap = jnp.where(tap < tap_count, tap, -8 * LANES)

        def chosen(lower_places, upper_places):
            marks = jnp.zeros(shape, F32)
            for places, side in ((lower_places, False), (upper_places, True)):
                for place in places:
                    hit = jnp.logical_and(lane == tap + place * LANES, upper == side)
                    marks = jnp.where(hit, 1.0, marks)
            return marks.astype(BF16)

        taps = times_transposed(chosen((0, 2), (1,)), wide)
        taps = taps + times_transposed(chosen((1,), (0, 2)), thin)
        for b in range(BLOCKS):
            for j in range(groups):
                room.taps[b, j] = taps[
                    b * room_rows : (b + 1) * room_rows, j * lanes : (j + 1) * lanes
                ]

    return join_taps


def inputs_stage(block, groups, lanes):
    def focal_inputs(room):
        unit, _scale = normalize(room.x[...])
        first = unit * vector(room, 10 * block) + vector(room, 10 * block + 1)
        first = first.astype(BF16)
        width = first.shape[1]
        gate_low = low_gates(room, block)
        for level in range(4):
            spread = jnp.broadcast_to(gate_low[level : level + 1], (LANES, width))
            room.gates[:, level * LANES : (level + 1) * LANES] = times_transposed(
                first, spread
            )
        key = room.key
        for j in range(groups):
            room.context[j] = times_transposed(first, key[j * lanes : (j + 1) * lanes, :])
        room.query_out[...] = times_transposed(first, room.query[...])
        room.flush(room.gates, room.context, room.query_out)

    return focal_inputs


def focal_stage(block, groups, lanes):
    def focal_levels(room):
        padded = room.padded
        taps, context, gates, low, pool = room.taps, room.context, room.gates, room.low, room.pool
        fields = [room.k1, room.k2, room.k3]
        slopes = [room.s1, room.s2, room.s3]
        clear_margins(padded)
        valid = room.image_columns[:, VALID : VALID + 1]
        valid_total = column_sum(valid)

        def group(j, carry):
            tap = taps.at[block, j]
            for row in range(GRID):
                padded[row, 8 : 8 + GRID, :] = context[j, rows_at(row), :]
            for level in range(3):
                sums = correlate(padded, tap, level, False)
                for row in range(GRID):
                    value, slope = gelu_pair(sums[row])
                    fields[level][j, rows_at(row), :] = value
                    slopes[level][j, rows_at(row), :] = slope
                    if level < 2:
                        padded[row, 8 : 8 + GRID, :] = value
            mean = column_sum(fields[2][j] * valid) / valid_total
            pooled, pooled_slope = gelu_pair(mean)
            pool[j, 0:1, :] = pooled
            pool[j, 1:2, :] = pooled_slope / valid_total
            pool[j, 2:8, :] = jnp.zeros((6, lanes), F32)
            at = lane_range(j, groups, lanes)
            for row in range(GRID):
                summed = pooled * gate_part(gates, row, 3, lanes)
                for level in range(3):
                    summed = summed + fields[level][j, rows_at(row), :] * gate_part(
                        gates, row, level, lanes
                    )
                low[rows_at(row), at] = summed.astype(BF16)
            return carry

        if groups > 1:
            lax.fori_loop(0, groups, group, 0)
        else:
            group(0, 0)
        room.flush(room.k1, room.k2, room.k3, room.s1, room.s2, room.s3, room.pool, room.low)

    return focal_levels


def mix_stage(block):
    def mix_forward(room):
        modulator = times_transposed(room.low[...], room.mix[...])
        room.mod[...] = modulator
        room.flush(room.mod)
        product = (room.query_out[...] * modulator).astype(BF16)
        branch = matmul(product, room.proj[...]) + vector(room, 10 * block + 4)
        room.middle[...] = room.x[...] + keep_of(room, block, 0) * branch

    return mix_forward


def mlp_stage(block):
    def mlp_forward(room):
        middle = room.middle[...]
        unit, _scale = normalize(middle)
        second = unit * vector(room, 10 * block + 2) + vector(room, 10 * block + 3)
        second = second.astype(BF16)
        up = room.up
        step = up.shape[0] // 4
        for part in range(4):
            at = slice(part * step, (part + 1) * step)
            value, slope = gelu_pair(times_transposed(second, up[at, :]))
            room.hidden[:, at] = value.astype(BF16)
            room.slope[:, at] = slope
        room.flush(room.hidden, room.slope)
        lowered = matmul(room.hidden[...], room.down[...]) + vector(room, 10 * block + 5)
        room.out[...] = middle + keep_of(room, block, 1) * lowered

    return mlp_forward


def embed_stage(room):
    outer = 10 * BLOCKS
    embedded = matmul(room.patches[...], room.embed[...].astype(BF16))
    embedded = embedded + vector(room, outer)
    room.embedded[...] = embedded
    room.flush(room.embedded)
    unit, _scale = normalize(embedded)
    mask = column(room, MASKED)
    state = unit * vector(room, outer + 1) + vector(room, outer + 2)
    room.x[...] = state * (1.0 - mask) + vector(room, outer + 5) * mask


def store_halves(core, kept, sent, at, first, second):
    chan, _rows, width = kept.shape
    rows = first.shape[0] // chan
    first = first.reshape(chan, rows, width).astype(BF16)
    second = second.reshape(chan, rows, width).astype(BF16)

    @pl.when(core == 0)
    def _():
        kept[:, at : at + rows, :] = first
        sent[:, at : at + rows, :] = second

    @pl.when(core != 0)
    def _():
        kept[:, at : at + rows, :] = second
        sent[:, at : at + rows, :] = first


def head_stage(at):
    def head_step(room):
        outer = 10 * BLOCKS
        gain = vector(room, outer + 3)
        unit, scale = normalize(room.x[...])
        low = (unit * gain + vector(room, outer + 4)).astype(BF16)
        head_low = room.head[...].astype(BF16)
        error = matmul(low, head_low) - room.patches[...].astype(F32)
        denom = jnp.max(room.counts[...] + room.counts_twin[...]) * PATCH_IN
        weighted = column(room, COUNTED) * error
        loss = column_sum(weighted * error) / denom
        d_pred = (2.0 * weighted / denom).astype(BF16)
        grad = contract_rows(low, d_pred)
        half = grad.shape[1] // 2
        core = room.where[0]
        store_halves(core, room.kept, room.sent, at, grad[:, :half], grad[:, half:])
        d_final = times_transposed(d_pred, head_low)
        room.d_out[...] = norm_backward(d_final, unit, scale, gain)
        sums = room.sums
        width = low.shape[1]
        sums[0:1, :] = column_sum(d_final * unit)
        sums[1:2, :] = column_sum(d_final)
        parts = [loss[:, at : at + width] for at in range(0, loss.shape[1], width)]
        sums[2:3, :] = sum(parts[1:], parts[0])
        sums[3:8, :] = jnp.zeros((5, width), F32)

    return head_step


def mlp_back_stage(block, at):
    def mlp_backward(room):
        d_residual = room.d_in[...]
        d_down = d_residual * keep_of(room, block, 1)
        d_low = d_down.astype(BF16)
        unit, scale = normalize(room.middle[...])
        gain = vector(room, 10 * block + 2)
        second = (unit * gain + vector(room, 10 * block + 3)).astype(BF16)
        down, hidden, slope, up = room.down, room.hidden, room.slope, room.up
        d_second = None
        count = MLP_PARTS
        step = down.shape[0] // count
        grads = []
        for part in range(count):
            here = slice(part * step, (part + 1) * step)
            d_pre = (times_transposed(d_low, down[here, :]) * slope[:, here]).astype(BF16)
            grads.append((contract_rows(d_pre, second), contract_rows(hidden[:, here], d_low)))
            term = matmul(d_pre, up[here, :])
            d_second = term if d_second is None else d_second + term
        core = room.where[0]
        chan = room.kept.shape[0]
        for part, (grad_up, grad_down) in enumerate(grads):
            places = slice(part * (chan // count), (part + 1) * (chan // count))
            kept, sent = room.kept.at[places], room.sent.at[places]
            store_halves(core, kept, sent, at, grad_up, grad_down)
        room.d_out[...] = d_residual + norm_backward(d_second, unit, scale, gain)
        sums = room.sums
        width = d_low.shape[1]
        sums[0:1, :] = column_sum(d_second * unit)
        sums[1:2, :] = column_sum(d_second)
        sums[2:3, :] = column_sum(d_down)
        sums[3:8, :] = jnp.zeros((5, width), F32)

    return mlp_backward


def mix_back_stage(block, groups, lanes, at):
    def mix_backward(room):
        d_proj = room.d_in[...] * keep_of(room, block, 0)
        d_low = d_proj.astype(BF16)
        d_product = times_transposed(d_low, room.proj[...])
        modulator = room.mod[...]
        query = room.query_out[...]
        d_mod = (d_product * query).astype(BF16)
        mix = room.mix
        for j in range(groups):
            room.d_sum[j] = matmul(d_mod, mix[:, j * lanes : (j + 1) * lanes])
        room.d_query[...] = (d_product * modulator).astype(BF16)
        product = (query * modulator).astype(BF16)
        grad_proj = contract_rows(product, d_low)
        grad_mix = contract_rows(d_mod, room.low[...])
        core = room.where[0]
        store_halves(core, room.kept, room.sent, at, grad_mix, grad_proj)
        sums = room.sums
        width = d_low.shape[1]
        sums[0:1, :] = column_sum(d_proj)
        sums[1:8, :] = jnp.zeros((7, width), F32)

    return mix_backward


def focal_back_stage(block, groups, lanes):
    def levels_backward(room):
        padded = room.padded
        d_padded = room.d_padded
        clear_margins(padded)
        clear_margins(d_padded)
        d_all, gates, taps, pool = room.d_sum, room.gates, room.taps, room.pool
        fields = [room.context, room.k1, room.k2, room.k3]
        slopes = [room.s1, room.s2, room.s3]
        d_context, d_gates, d_taps = room.d_context, room.d_gates, room.d_taps
        valid = room.image_columns[:, VALID : VALID + 1]
        d_gates[...] = jnp.zeros(d_gates.shape, F32)
        d_taps[...] = jnp.zeros(d_taps.shape, F32)

        def fold(values):
            if lanes == LANES:
                return values
            summed = jnp.sum(values, axis=-1, keepdims=True) / LANES
            return jnp.broadcast_to(summed, (values.shape[0], LANES))

        def group(j, carry):
            tap = taps.at[block, j]
            at = lane_range(j, groups, lanes)
            d_pooled = jnp.zeros((1, lanes), F32)
            for row in range(GRID):
                d_pooled = d_pooled + column_sum(
                    d_all[j, rows_at(row), :] * gate_part(gates, row, 3, lanes)
                )
            d_mean = d_pooled * pool[j, 1:2, :]
            d_field = [d_mean * valid[rows_at(row)] for row in range(GRID)]
            for level in (2, 1, 0):
                d_pre = []
                for row in range(GRID):
                    here = rows_at(row)
                    grad = d_field[row] + d_all[j, here, :] * gate_part(gates, row, level, lanes)
                    grad = grad * slopes[level][j, here, :]
                    d_pre.append(grad)
                    d_padded[row, 8 : 8 + GRID, :] = grad
                    padded[row, 8 : 8 + GRID, :] = fields[level][j, here, :]
                correlate_taps(padded, d_pre, d_taps, at, level)
                d_field = correlate(d_padded, tap, level, True)
            for row in range(GRID):
                d_context[rows_at(row), at] = d_field[row].astype(BF16)
            whole = d_all[j]
            for level in range(3):
                here = slice(level * LANES, (level + 1) * LANES)
                d_gates[:, here] = d_gates[:, here] + fold(whole * fields[level + 1][j])
            here = slice(3 * LANES, 4 * LANES)
            d_gates[:, here] = d_gates[:, here] + fold(whole * pool[j, 0:1, :])
            return carry

        for j in range(groups):
            group(j, 0)
        room.flush(room.d_taps)

    return levels_backward


def inputs_back_stage(block, at):
    def inputs_backward(room):
        unit, scale = normalize(room.x[...])
        gain = vector(room, 10 * block)
        first_wide = (unit * gain + vector(room, 10 * block + 1)).astype(BF16)
        first = first_wide
        first_wide = first.astype(F32)
        rows, width = first.shape
        gate_low = low_gates(room, block).astype(F32)
        sums = room.input_sums
        sums[...] = jnp.zeros((8, width), F32)
        d_first = jnp.zeros((rows, width), F32)
        d_gates = room.d_gates
        for level in range(4):
            here = slice(level * LANES, (level + 1) * LANES)
            col = jnp.sum(d_gates[:, here], axis=-1, keepdims=True)
            d_first = d_first + col * gate_low[level : level + 1]
            sums[2 + level : 3 + level, :] = column_sum(col * first_wide)
        d_query = room.d_query[...]
        d_context = room.d_context[...]
        d_first = d_first + matmul(d_query, room.query[...])
        d_first = d_first + matmul(d_context, room.key[...])
        room.d_out[...] = room.d_in[...] + norm_backward(d_first, unit, scale, gain)
        sums[0:1, :] = column_sum(d_first * unit)
        sums[1:2, :] = column_sum(d_first)
        grad_query = contract_rows(d_query, first)
        grad_key = contract_rows(d_context, first)
        kept, sent = room.kept, room.sent
        core = room.where[0]
        store_halves(core, kept, sent, at, grad_query, grad_key)

    return inputs_backward


def sums_start(tap_count):
    return BLOCKS * tap_room(tap_count)


def small_rows_for(tap_count, chan):
    used = sums_start(tap_count) + 8 * (2 + 3 * BLOCKS)
    return -(-used // (16 * chan)) * (16 * chan)


def embed_back_stage(tap_count, sum_keys, tap_keys, first_row):
    outer = 10 * BLOCKS

    def embed_backward(room):
        mask = column(room, MASKED)
        d_residual = room.d_out[...]
        d_start = d_residual * (1.0 - mask)
        unit, scale = normalize(room.embedded[...])
        d_embed = norm_backward(d_start, unit, scale, vector(room, outer + 1))
        small = room.small
        small[...] = jnp.zeros(small.shape, F32)
        for b, key in enumerate(tap_keys):
            at = b * tap_room(tap_count)
            taps = room.d_taps if key is None else room[key]
            small[at : at + taps.shape[0], :] = taps[...]
        at = sums_start(tap_count)
        small[at : at + 1, :] = column_sum(d_embed)
        small[at + 1 : at + 2, :] = column_sum(d_start * unit)
        small[at + 2 : at + 3, :] = column_sum(d_start)
        small[at + 3 : at + 4, :] = column_sum(d_residual * mask)
        for key in sum_keys:
            at += 8
            small[at : at + 8, :] = room[key][...]
        grad = contract_rows(room.patches[...], d_embed.astype(BF16))
        core = room.where[0]
        kept, sent = room.kept, room.sent
        half = grad.shape[0] // 2
        row = first_row
        store_halves(core, kept, sent, row, grad[:half], grad[half:])
        row += half // kept.shape[0]
        half = small.shape[0] // 2
        store_halves(core, kept, sent, row, small[:half], small[half:])

    return embed_backward


def update_shared_stage(tap_count, own, part, rate):
    def update_shared(room):
        width = room.near0.shape[2]
        core = room.where[0]
        small_half = room.small.shape[0] // 2
        small_part = room.near0.shape[1] - 2 * part
        half_rows = room.embed.shape[0] // 2
        for half, parts in ((core, (room.near0, room.near1)), (1 - core, (room.far0, room.far1))):
            across = pl.ds(pl.multiple_of(half * width, width), width)
            entry = 2
            for ref in parts:
                for slot in range(ref.shape[0]):
                    place = room.where[entry]
                    entry += 1
                    gradient = ref[slot].astype(F32)
                    down = pl.ds(pl.multiple_of(place * part, 8), part)
                    new_weight, new_moment = nesterov(
                        room.head[down, across],
                        room.head_moment[down, across],
                        gradient[:part],
                        rate,
                    )
                    room.new_head[down, across] = new_weight
                    room.new_head_moment[down, across] = new_moment
                    down = pl.ds(pl.multiple_of(half * half_rows + place * part, 8), part)
                    new_weight, new_moment = nesterov(
                        room.embed[down, :],
                        room.embed_moment[down, :],
                        gradient[part : 2 * part],
                        rate,
                    )
                    room.new_embed[down, :] = new_weight
                    room.new_embed_moment[down, :] = new_moment
                    at = pl.multiple_of(half * small_half + place * small_part, 8)
                    room.small[pl.ds(at, small_part), :] = gradient[2 * part :]
        room.flush(room.new_head, room.new_head_moment, room.new_embed, room.new_embed_moment)
        grads = room.small[...]
        small = grads.astype(BF16)

        def sum_row(index, row):
            at = sums_start(tap_count) + 8 * index + row
            return grads[at : at + 1]

        rows = []
        for b in range(BLOCKS):
            inputs_at, mlp_at, mix_at = 1 + 3 * b, 2 + 3 * b, 3 + 3 * b
            rows += [sum_row(inputs_at, 0), sum_row(inputs_at, 1)]
            rows += [sum_row(mlp_at, 0), sum_row(mlp_at, 1)]
            rows += [sum_row(mix_at, 0), sum_row(mlp_at, 2)]
            rows += [sum_row(inputs_at, 2 + level) for level in range(4)]
        head_at = 1 + 3 * BLOCKS
        rows += [sum_row(0, 0), sum_row(0, 1), sum_row(0, 2)]
        rows += [sum_row(head_at, 0), sum_row(head_at, 1), sum_row(0, 3)]
        packed = room.packed
        for at, row in enumerate(rows):
            packed[at : at + 1, :] = row
        gradient = packed[0 : len(rows), :]
        new_weight, new_moment = nesterov(
            room.vectors[...], room.vector_moment[...], gradient, rate
        )
        room.new_vectors[...] = new_weight
        room.new_vector_moment[...] = new_moment
        room.new_vector_average[...] = (
            AVERAGE * room.vector_average[...] + (1.0 - AVERAGE) * new_weight
        )
        loss = jnp.sum(sum_row(head_at, 2), axis=-1, keepdims=True)
        room.loss[...] = jnp.broadcast_to(loss, room.loss.shape)
        first = room.where[1] * own
        source = lax.broadcasted_iota(jnp.int32, (own, width), 1)
        wanted = first + lax.broadcasted_iota(jnp.int32, (own, width), 0)
        chosen = (source == wanted).astype(F32).astype(BF16)
        for b in range(BLOCKS):
            at = b * tap_room(tap_count)
            gradient = times_transposed(chosen, small[at : at + tap_room(tap_count)])
            gradient = gradient[:, :tap_count]
            new_weight, new_moment = nesterov(
                room.kernels[b], room.kernel_moment[b], gradient, rate
            )
            room.new_kernels[b] = new_weight
            room.new_kernel_moment[b] = new_moment
            room.new_kernel_average[b] = (
                AVERAGE * room.kernel_average[b] + (1.0 - AVERAGE) * new_weight
            )

    return update_shared


class Shares:
    def __init__(self, local_rows, chan_size):
        self.count = max(1, IMAGE_ROWS // local_rows)
        self.groups = [
            list(range(first, first + self.count)) for first in range(0, chan_size, self.count)
        ]

    def to_images(self, values):
        whole = lax.all_to_all(
            values[0], "chan", 1, 0, axis_index_groups=self.groups, tiled=True
        )
        return whole[None]

    def to_rows(self, values):
        return lax.all_to_all(values, "chan", 0, 1, axis_index_groups=self.groups, tiled=True)

    def all_rows(self, values):
        return lax.all_gather(
            values, "chan", axis=0, axis_index_groups=self.groups, tiled=True
        )

    def sum_rows(self, values):
        return lax.psum_scatter(
            values, "chan", scatter_dimension=0, axis_index_groups=self.groups, tiled=True
        )

    def channels(self, values):
        size = values.shape[-1] // self.count
        place = lax.axis_index("chan") % self.count
        return lax.dynamic_slice_in_dim(values, place * size, size, values.ndim - 1)

    def spread(self, values):
        size = values.shape[1]
        place = lax.axis_index("chan") % self.count
        whole = jnp.zeros((values.shape[0], size * self.count), values.dtype)
        return lax.dynamic_update_slice_in_dim(whole, values, place * size, 1)


def hold(array):
    return (array, HOLD)


def fetch(array):
    return (array, FETCH)


def fetch_all(made, names):
    return {name: fetch(made[name]) for name in names}


def shards(
    patches,
    valid_mask,
    target_mask,
    keep_mask,
    embed_weight,
    embed_moment,
    head_weight,
    head_moment,
    vectors,
    vector_moment,
    vector_average,
    focal_input,
    focal_moment,
    focal_average,
    mixers,
    mixer_moment,
    mixer_average,
    mlp_weights,
    mlp_moment,
    mlp_average,
    kernels,
    kernel_moment,
    kernel_average,
):
    links = Links()
    rows, patch_in = patches.shape
    group_rows = valid_mask.shape[0]
    own = focal_input.shape[-1]
    own_hidden = mlp_weights.shape[-1]
    hidden_width = own_hidden * links.chan
    tap_count = kernels.shape[1]
    width = vectors.shape[1]
    shares = Shares(rows, links.chan)
    shared = shares.count > 1
    channels = width // shares.count
    lanes = LANES if channels % LANES == 0 else channels
    groups = channels // lanes
    room_rows = tap_room(tap_count)
    cut_rows = own_hidden // 2 if links.nx > 1 and own_hidden % (16 * links.nx) == 0 else 0
    plain_rows = own_hidden - cut_rows
    cut_part = cut_rows // links.nx

    def together(values, moves):
        got = [links.swap(*move) for move in moves]
        return lax.optimization_barrier((values, got))

    def beside(call, gate, moves):
        made = call(after(gate, *[move[0] for move in moves]))
        made, got = together(dict(made), moves)
        return (Box(made), got)

    here = links.here()
    focal_rows = jnp.transpose(focal_input, (0, 2, 3, 1))
    mixer_rows = jnp.transpose(mixers, (0, 1, 3, 2))
    mlp_rows = jnp.transpose(mlp_weights, (0, 1, 3, 2))
    kernel_rows = jnp.transpose(kernels, (0, 2, 1))
    focal_layout = dict(query=(0, 0), mix=(0, own), key=(1, 0), proj=(1, own))
    first_layout = dict(focal_layout, wide=(0, 2 * own), thin=(1, 2 * own))
    mlp_layout = dict(up=(0, 0), down=(1, 0))

    def slots_of(parts):
        return [(k, d) for k, part in enumerate(parts) for d in range(part.shape[0])]

    def pieces_of(gather, far, layout, count, apart=False):
        rows = [place * (1 if apart else count) for place, _x in links.places(gather.masks)]
        slots = slots_of(gather.parts)
        matrices = {
            name: (half, [(k, d, first, count, at) for at, (k, d) in enumerate(slots)])
            for name, (half, first) in layout.items()
        }
        return Pieces(links.where(rows), gather.parts, far, matrices, len(slots))

    def cut_pieces(gather, crossed, masks, far):
        rows, entries = [], []
        for (k, d), (place, x) in zip(slots_of(gather.parts), links.places(gather.masks)):
            entries.append((k, d, 0, plain_rows, len(rows)))
            rows.append(place * own_hidden)
            entries.append((k, d, plain_rows, cut_part, len(rows)))
            rows.append(place * own_hidden + plain_rows + x * cut_part)
        for (k, d), (place, x) in zip(slots_of(crossed), links.places(masks)):
            entries.append((k + len(gather.parts), d, 0, cut_part, len(rows)))
            rows.append(place * own_hidden + plain_rows + x * cut_part)
        matrices = dict(up=(0, entries), down=(1, entries))
        return Pieces(links.where(rows), gather.parts + crossed, far, matrices, links.chan)

    first_row = links.place * rows
    validity = valid_mask.astype(F32)
    masked = target_mask.astype(F32)
    keep_rows = jnp.repeat(
        keep_mask.reshape(keep_mask.shape[0], -1).astype(F32) / KEEP_RATE, IMAGE_ROWS, axis=0
    )
    table = jnp.concatenate(
        [
            masked[:, None],
            (masked * validity)[:, None],
            validity[:, None],
            keep_rows,
            jnp.zeros((group_rows, 1), F32),
        ],
        axis=1,
    )
    columns = lax.dynamic_slice_in_dim(table, first_row, rows)
    image_columns = columns
    if shared:
        image_columns = lax.dynamic_slice_in_dim(
            table, first_row // IMAGE_ROWS * IMAGE_ROWS, IMAGE_ROWS
        )
    group_count = jnp.broadcast_to(jnp.sum(validity * masked), (8, LANES))
    basic = dict(vectors=fetch(vectors), columns=fetch(columns))
    grid_columns = dict(image_columns=fetch(image_columns))

    whole = (rows, width)
    focal = [None] * BLOCKS
    mlp = [None] * BLOCKS
    focal[0] = Gather(
        links, pack_rows(
            here, [(focal_rows, 0, 0, own, 1), (mixer_rows, 0, 0, own, 1)], kernel_rows
        )
    )
    moves = focal[0].direct()
    embedded = run_kernel(
        [embed_stage],
        dict(patches=fetch(patches), embed=fetch(embed_weight), **basic),
        dict(x=(whole, F32, HOLD), embedded=(whole, F32, FETCH)),
    )
    sources = [(mlp_rows, 0, 0, plain_rows, 1)]
    if cut_rows:
        sources.append((mlp_rows, 0, plain_rows, cut_rows, links.nx))
    packed = pack_rows(here, sources, None)
    (x, packed), got = together((embedded.x, packed), moves)
    focal[0].take_direct(got)
    mlp[0] = Gather(links, packed)
    z_first, *z_rest = links.bits("z")
    y_move = focal[0].early("y")
    (move,) = mlp[0].moves("z", z_first)
    packed = (
        pack_rows(here, [(focal_rows, 1, 0, own, 1), (mixer_rows, 1, 0, own, 1)], None),
        pack_rows(here, [(mlp_rows, 1, 0, own_hidden, 1)], None),
    )
    packed, got = together(packed, [move])
    mlp[0].take(got[0], "z", z_first)
    focal[1] = Gather(links, packed[0])
    mlp[1] = Gather(links, packed[1])

    def take_z(gather, received):
        for step, one in zip(z_rest, received):
            gather.take(one, "z", step)

    moves = [(mlp[0].stack, "z", step) for step in z_rest]
    moves += [(focal[0].stack, *y_move), (focal[1].stack, "z", z_first)]
    x, got = together(x, moves)
    take_z(mlp[0], got[:-2])
    focal[0].take(got[-2], *y_move, True)
    focal[1].take(got[-1], "z", z_first)

    def twins(gather, values):
        values, got = together(values, [(part, "core", 1) for part in gather.parts])
        return (values, got)

    y_move = mlp[0].early("y")
    x, far = twins(focal[0], after(x, mlp[0].stack))
    focal_pieces = [pieces_of(focal[0], far, first_layout, own), None]
    mlp_pieces = [None, None]

    field_shape = (groups, IMAGE_ROWS, lanes)
    field = (field_shape, F32, FETCH)
    padded = pltpu.VMEM((GRID, GRID + 16, lanes), F32)
    gates_out = dict(gates=((IMAGE_ROWS, 4 * LANES), F32, FETCH))
    focal_out = dict(k1=field, k2=field, k3=field, s1=field, s2=field, s3=field)
    focal_out.update(pool=((groups, 8, lanes), F32, FETCH))
    mixed_out = dict(mod=(whole, F32, FETCH), middle=(whole, F32, HOLD))
    query_out = dict(query_out=(whole, F32, FETCH))
    low_out = dict(low=(whole, BF16, FETCH))
    mlp_out = dict(
        hidden=((rows, hidden_width), BF16, FETCH), slope=((rows, hidden_width), F32, FETCH)
    )
    weights_in = dict(key=0, query=0, mix=0, proj=0)
    up_down = dict(up=0, down=0)
    taps_shape = (BLOCKS, groups, room_rows, lanes)

    def focal_apart(b, x, taps):
        pieces = focal_pieces[b]
        made = run_kernel(
            [inputs_stage(b, 1, width)],
            dict(x=hold(x), **basic),
            dict(
                gates=((rows, 4 * LANES), F32, FETCH),
                context=((1, rows, width), F32, FETCH),
                **query_out,
            ),
            {},
            [(pieces, dict(key=0, query=0))],
        )
        made.update(gates=shares.all_rows(made.gates), context=shares.to_images(made.context))
        made.update(
            run_kernel(
                [focal_stage(b, groups, lanes)],
                dict(
                    context=fetch(made.context),
                    gates=fetch(made.gates),
                    taps=fetch(taps),
                    **grid_columns,
                ),
                dict(low=((IMAGE_ROWS, channels), BF16, FETCH), **focal_out),
                dict(padded=padded),
            )
        )
        made.update(low=shares.to_rows(made.low))
        made.update(
            run_kernel(
                [mix_stage(b)],
                dict(
                    x=hold(x), low=fetch(made.low), query_out=fetch(made.query_out), **basic
                ),
                mixed_out,
                {},
                [(pieces, dict(mix=0, proj=0))],
            )
        )
        return made

    def focal_stages(b):
        return [inputs_stage(b, groups, lanes), focal_stage(b, groups, lanes), mix_stage(b)]

    focal_made_out = dict(
        context=field, **gates_out, **query_out, **focal_out, **low_out, **mixed_out
    )

    def first_focal(x):
        if shared:
            taps = run_kernel(
                [taps_stage(tap_count, 1, width)],
                {},
                dict(taps=((BLOCKS, 1, room_rows, width), F32, FETCH)),
                {},
                [(focal_pieces[0], dict(wide=0, thin=0))],
            ).taps
            taps = shares.channels(taps)
            return Box(focal_apart(0, x, taps), taps=taps)
        return run_kernel(
            [taps_stage(tap_count, groups, lanes)] + focal_stages(0),
            dict(x=hold(x), **basic, **grid_columns),
            dict(taps=(taps_shape, F32, FETCH), **focal_made_out),
            dict(padded=padded),
            [(focal_pieces[0], dict(wide=0, thin=0, **weights_in))],
            False,
        )

    moves = [(mlp[0].stack, *y_move)]
    moves += [(focal[1].stack, "z", step) for step in z_rest[:1]]
    moves += [(mlp[1].stack, "z", z_first)]
    x_first, *x_rest = links.bits("x")
    saved = [Box(x=x), Box()]
    made, got = beside(first_focal, x, moves)
    saved[0].update(made)
    taps = made.taps
    mlp[0].take(got[0], *y_move, True)
    take_z(focal[1], got[1:-1])
    mlp[1].take(got[-1], "z", z_first)
    y_move = focal[1].early("y")
    moves = [(focal[1].stack, *y_move)]
    moves += [(mlp[1].stack, "z", step) for step in z_rest]
    crossed, crossed_masks = [], []
    if cut_rows:
        cut_stack = jnp.concatenate([part[:, plain_rows:] for part in mlp[0].parts])
        cut_gather = Gather(links, cut_stack[0])
        cut_gather.stack, cut_gather.masks = cut_stack, mlp[0].masks
        x_move = cut_gather.early("x")
        moves += [(cut_gather.stack, *x_move)]
    group_count = after(group_count, saved[0].middle)
    moves.insert(0, (group_count, "core", 1))
    middle, got = together(saved[0].middle, moves)
    group_count = group_count + got.pop(0)
    focal[1].take(got[0], *y_move, True)
    take_z(mlp[1], got[1 : 1 + len(z_rest)])
    if cut_rows:
        held = cut_stack.shape[0]
        cut_gather.take(got[-1], *x_move, True)
        crossed = [cut_gather.parts[0][held:], cut_gather.parts[1]]
        crossed = [part for part in crossed if part.shape[0]]
        crossed_masks = cut_gather.masks[held:]
    y_move = mlp[1].early("y")
    arrays = mlp[0].parts + crossed
    moves = [(part, "core", 1) for part in arrays + focal[1].parts]
    middle, got = together(after(middle, mlp[1].stack), moves)
    far, far_focal = got[: len(arrays)], got[len(arrays) :]
    if cut_rows:
        mlp_pieces[0] = cut_pieces(mlp[0], crossed, crossed_masks, far)
    else:
        mlp_pieces[0] = pieces_of(mlp[0], far, mlp_layout, own_hidden)
    focal_pieces[1] = pieces_of(focal[1], far_focal, focal_layout, own)

    def second_focal(middle):
        inputs = dict(middle=hold(middle), **basic)
        outputs = dict(out=(whole, F32, FETCH), **mlp_out)
        if shared:
            made = run_kernel(
                [mlp_stage(0)], inputs, outputs, {}, [(mlp_pieces[0], up_down)]
            )
            lower = Box(hidden=made.hidden, slope=made.slope)
            return Box(focal_apart(1, made.out, taps), x=made.out, lower=dict(lower))
        made = run_kernel(
            [renamed(mlp_stage(0), middle=0, out=1)]
            + [renamed(stage, x=1) for stage in focal_stages(1)],
            {0: hold(middle), **basic, **grid_columns, **dict(taps=fetch(taps))},
            {1: (whole, F32, FETCH), **mlp_out, **focal_made_out},
            dict(padded=padded),
            [(mlp_pieces[0], up_down), (focal_pieces[1], weights_in)],
        )
        lower = dict(hidden=made.hidden, slope=made.slope)
        upper = Box({key: made[key] for key in focal_made_out})
        upper.update(x=made[1], lower=lower)
        return upper

    moves = [(mlp[1].stack, *y_move), (group_count, "x", x_first)]
    made, got = beside(second_focal, middle, moves)
    mlp[1].take(got[0], *y_move, True)
    counts_twin = got[1]
    for step in x_rest:
        group_count = group_count + counts_twin
        counts_twin = links.swap(group_count, "x", step)
    saved[0].update(made.lower)
    saved[1].update(made)
    middle, far = twins(mlp[1], saved[1].middle)
    mlp_pieces[1] = pieces_of(mlp[1], far, mlp_layout, own_hidden)

    sums_out = ((8, width), F32, FETCH)
    embed_rows = patch_in // (2 * links.chan)
    small_rows = small_rows_for(tap_count, links.chan)
    small_part = small_rows // (2 * links.chan)
    hidden_shape = (rows, hidden_width)
    mix_at = own_hidden
    upper_lead = own_hidden + own
    head_at = upper_lead + own
    lower_lead = own_hidden + own
    upper_count = head_at + embed_rows
    lower_count = lower_lead + own + embed_rows + small_part
    d_shape = (1, rows, width) if shared else field_shape
    levels_names = dict(context=0, gates=0, k1=0, k2=0, k3=0, s1=0, s2=0, s3=0, pool=0)
    mix_names = dict(query_out=0, mod=0, low=0)
    levels_temps = dict(padded=padded, d_padded=padded)
    between = dict(
        d_context=pltpu.VMEM(whole, BF16),
        d_gates=pltpu.VMEM((rows, 4 * LANES), F32),
        **levels_temps,
    )
    tap_shape = (room_rows, width)

    def pair_of(count):
        shape = (links.chan, count, width)
        return dict(kept=(shape, BF16, HOLD), sent=(shape, BF16, HOLD))

    def levels_in(b):
        return dict(taps=fetch(taps), **fetch_all(saved[b], levels_names), **grid_columns)

    head_names = dict(x=0, d_out=1, sums=5)
    head_first = upper_lead if shared else head_at
    first_stages = [
        renamed(mlp_stage(1), out=0),
        renamed(head_stage(head_first), **head_names),
        renamed(mlp_back_stage(1, 0), d_in=1, d_out=2, sums=3),
        renamed(mix_back_stage(1, d_shape[0], d_shape[2], mix_at), d_in=2, sums=4),
    ]
    first_in = dict(
        middle=hold(middle),
        head=fetch(head_weight),
        patches=fetch(patches),
        counts=hold(group_count),
        counts_twin=hold(counts_twin),
        **basic,
        **fetch_all(saved[1], mix_names),
    )
    first_temps = {
        0: pltpu.VMEM(whole, F32),
        1: pltpu.VMEM(whole, F32),
        **dict(hidden=pltpu.VMEM(hidden_shape, BF16), slope=pltpu.VMEM(hidden_shape, F32)),
    }
    sums_outs = {3: sums_out, 4: sums_out, 5: sums_out}
    mlp_weights_in = (mlp_pieces[1], up_down)
    mixer_in = dict(proj=0, mix=0)
    inputs_in = dict(query=0, key=0)

    def levels_apart(b, d_sum):
        made = run_kernel(
            [focal_back_stage(b, groups, lanes)],
            dict(d_sum=fetch(shares.to_images(d_sum)), **levels_in(b)),
            dict(
                d_context=((IMAGE_ROWS, channels), BF16, FETCH),
                d_gates=((IMAGE_ROWS, 4 * LANES), F32, FETCH),
                d_taps=((room_rows, channels), F32, FETCH),
            ),
            levels_temps,
        )
        return Box(
            d_context=shares.to_rows(made.d_context),
            d_gates=shares.sum_rows(made.d_gates),
            d_taps=shares.spread(made.d_taps),
        )

    def joined(first, second):
        return Box(
            kept=jnp.concatenate([first.kept, second.kept], axis=1),
            sent=jnp.concatenate([first.sent, second.sent], axis=1),
        )

    if shared:
        first = run_kernel(
            first_stages,
            first_in,
            {
                2: (whole, F32, HOLD),
                **sums_outs,
                **dict(d_query=(whole, BF16, HOLD), d_sum=(d_shape, F32, HOLD)),
                **pair_of(upper_lead + embed_rows),
            },
            first_temps,
            [mlp_weights_in, (focal_pieces[1], mixer_in)],
        )
        levels = levels_apart(1, first.d_sum)
        second = run_kernel(
            [inputs_back_stage(1, 0)],
            dict(
                d_in=hold(first[2]),
                d_query=hold(first.d_query),
                d_context=fetch(levels.d_context),
                d_gates=fetch(levels.d_gates),
                x=fetch(saved[1].x),
                **basic,
            ),
            dict(d_out=(whole, F32, HOLD), input_sums=sums_out, **pair_of(own)),
            {},
            [(focal_pieces[1], inputs_in)],
        )
        pair = joined(first, second)
        pair = Box(
            (key, jnp.concatenate([array[:, :upper_lead], array[:, -own:], array[:, upper_lead:-own]], 1))
            for key, array in pair.items()
        )
        d_x, d_taps = second.d_out, levels.d_taps
        upper_sums = [second.input_sums, first[3], first[4], first[5]]
    else:
        first = run_kernel(
            first_stages
            + [
                focal_back_stage(1, groups, lanes),
                renamed(inputs_back_stage(1, upper_lead), d_in=2),
            ],
            dict(x=fetch(saved[1].x), **levels_in(1)) | first_in,
            {
                **sums_outs,
                **dict(
                    d_out=(whole, F32, HOLD),
                    input_sums=sums_out,
                    d_taps=(tap_shape, F32, FETCH),
                ),
                **pair_of(upper_count),
            },
            {
                2: pltpu.VMEM(whole, F32),
                **first_temps,
                **dict(d_query=pltpu.VMEM(whole, BF16), d_sum=pltpu.VMEM(d_shape, F32)),
                **between,
            },
            [mlp_weights_in, (focal_pieces[1], mixer_in | inputs_in)],
        )
        pair = first
        d_x, d_taps = first.d_out, first.d_taps
        upper_sums = [first.input_sums, first[3], first[4], first[5]]

    lower_stages = [
        renamed(mlp_back_stage(0, 0), d_out=2, sums=3),
        renamed(mix_back_stage(0, d_shape[0], d_shape[2], mix_at), d_in=2, sums=4),
    ]
    lower_names = dict(hidden=0, slope=0, middle=0)
    sum_keys = [10, 3, 4, 11, 12, 13, 14]
    last_in = {
        **dict(zip(sum_keys[3:], (fetch(array) for array in upper_sums))),
        15: fetch(d_taps),
        **dict(patches=fetch(patches), embedded=fetch(embedded.embedded), x=fetch(saved[0].x)),
    }

    def last_stages(at):
        return [
            renamed(inputs_back_stage(0, at), d_in=2, d_out=1, input_sums=10),
            renamed(
                embed_back_stage(tap_count, sum_keys, [None, 15], at + own), d_out=1
            ),
        ]

    last_temps = {
        1: pltpu.VMEM(whole, F32),
        10: pltpu.VMEM((8, width), F32),
        **dict(small=pltpu.VMEM((small_rows, width), F32)),
    }

    def lower_back(d_x):
        inputs = dict(
            d_in=hold(d_x),
            **fetch_all(saved[0], lower_names),
            **basic,
            **fetch_all(saved[0], mix_names),
        )
        weights = [(mlp_pieces[0], dict(down=0, up=0)), (focal_pieces[0], mixer_in)]
        if shared:
            first = run_kernel(
                lower_stages,
                inputs,
                {
                    2: (whole, F32, HOLD),
                    3: sums_out,
                    4: sums_out,
                    **dict(d_query=(whole, BF16, HOLD), d_sum=(d_shape, F32, HOLD)),
                    **pair_of(lower_lead),
                },
                {},
                weights,
            )
            levels = levels_apart(0, first.d_sum)
            second = run_kernel(
                last_stages(0),
                {
                    2: hold(first[2]),
                    3: fetch(first[3]),
                    4: fetch(first[4]),
                    **last_in,
                    **dict(
                        d_query=hold(first.d_query),
                        d_context=fetch(levels.d_context),
                        d_gates=fetch(levels.d_gates),
                        d_taps=fetch(levels.d_taps),
                        **basic,
                    ),
                },
                pair_of(lower_count - lower_lead),
                last_temps,
                [(focal_pieces[0], inputs_in)],
            )
            return joined(first, second)
        return run_kernel(
            lower_stages + [focal_back_stage(0, groups, lanes)] + last_stages(lower_lead),
            {**inputs, **levels_in(0), **last_in},
            pair_of(lower_count),
            {
                2: pltpu.VMEM(whole, F32),
                3: pltpu.VMEM((8, width), F32),
                4: pltpu.VMEM((8, width), F32),
                **last_temps,
                **dict(d_query=pltpu.VMEM(whole, BF16), d_sum=pltpu.VMEM(d_shape, F32)),
                **dict(d_taps=pltpu.VMEM(tap_shape, F32)),
                **between,
            },
            [weights[0], (focal_pieces[0], mixer_in | inputs_in)],
        )

    (d_x, upper_kept), got = together((d_x, pair.kept), [(pair.sent, "core", 1)])
    upper = Reduction(links, upper_kept, got[0], 1)
    moves, take = next_round(links, [upper])
    made, got = beside(lower_back, d_x, moves)
    take(got)
    moves, take = next_round(links, [upper])
    lower_kept, got = together(made.kept, moves + [(made.sent, "core", 1)])
    take(got[:-1])
    lower = Reduction(links, lower_kept, got[-1], 2)
    rate = 0.2 * math.sqrt(group_rows * lax.axis_size("dp"))
    gate = here
    turn = [lower]
    while not (lower.ready() and upper.done()):
        moves, take = next_round(links, turn)
        gate, got = together(gate, moves)
        take(got)
        turn = [lower, upper]
    common = Gather(
        links,
        jnp.concatenate(
            [
                upper.tail(embed_rows).astype(BF16),
                lower.tail(embed_rows + small_part).astype(BF16),
            ]
        ),
    )
    moves = common.direct()
    count = len(moves)
    more, takes = lower.last_moves()
    gate, got = together(gate, moves + more)
    common.take_direct(got[:count])
    for one, part in zip(takes, got[count:]):
        one(part)
    while not lower.done():
        more, takes = lower.last_moves()
        takes[0](links.swap(*more[0]))
    upper_rows, lower_rows = upper.result(), lower.result()
    y_move = common.early("y")
    common.take(links.swap(common.stack, *y_move), *y_move, True)
    rows_early = jnp.concatenate(
        [
            upper_rows[:own_hidden],
            lower_rows[:own_hidden],
            upper_rows[mix_at : mix_at + own],
            upper_rows[upper_lead:head_at],
            lower_rows[mix_at : lower_lead + own],
        ]
    )
    rows_early, _stack = lax.optimization_barrier((rows_early, common.stack))
    halves = links.both_halves(rows_early)
    ends = (own_hidden, 2 * own_hidden)
    grad_mlp = jnp.stack(
        [
            jnp.stack([part[ends[0] : ends[1]] for part in halves]),
            jnp.stack([part[: ends[0]] for part in halves]),
        ]
    )
    places = [ends[1] + k * own for k in range(5)]
    mix_one, inputs_one, mix_zero, inputs_zero = (
        [part[first:end] for part in halves] for first, end in zip(places, places[1:])
    )
    grad_focal = jnp.stack([jnp.stack(inputs_zero), jnp.stack(inputs_one)])
    grad_mixer = jnp.stack([jnp.stack(mix_zero), jnp.stack(mix_one)])
    results = []
    for weight, moment, average, gradient, order, back in (
        (focal_input, focal_moment, focal_average, grad_focal, (0, 2, 3, 1), (0, 3, 1, 2)),
        (mixers, mixer_moment, mixer_average, grad_mixer, (0, 1, 3, 2), (0, 1, 3, 2)),
        (mlp_weights, mlp_moment, mlp_average, grad_mlp, (0, 1, 3, 2), (0, 1, 3, 2)),
    ):
        weight, moment, average = (
            jnp.transpose(array, order) for array in (weight, moment, average)
        )
        new_weight, new_moment = nesterov(weight, moment, gradient, rate)
        new_average = AVERAGE * average + (1.0 - AVERAGE) * new_weight
        results.extend(
            jnp.transpose(array, back) for array in (new_weight, new_moment, new_average)
        )
    there, results = lax.optimization_barrier((common.parts[1], results))
    common_near = [common.parts[0], there]
    common_far = [links.swap_core(part) for part in common_near]
    common_where = links.where([place for place, _x in links.places(common.masks)])
    head_out = (head_weight.shape, F32, FETCH)
    embed_out = (embed_weight.shape, F32, FETCH)
    vector_out = (vectors.shape, F32, HOLD)
    kernel_out = (kernel_rows.shape, F32, HOLD)
    made = run_kernel(
        [update_shared_stage(tap_count, own, embed_rows, rate)],
        dict(
            where=(common_where, SCALAR),
            near0=hold(common_near[0]),
            near1=hold(common_near[1]),
            far0=hold(common_far[0]),
            far1=hold(common_far[1]),
            head=fetch(head_weight),
            head_moment=fetch(head_moment),
            embed=fetch(embed_weight),
            embed_moment=fetch(embed_moment),
            vectors=fetch(vectors),
            vector_moment=fetch(vector_moment),
            vector_average=fetch(vector_average),
            kernels=fetch(kernel_rows),
            kernel_moment=fetch(jnp.transpose(kernel_moment, (0, 2, 1))),
            kernel_average=fetch(jnp.transpose(kernel_average, (0, 2, 1))),
        ),
        dict(
            new_head=head_out,
            new_head_moment=head_out,
            new_embed=embed_out,
            new_embed_moment=embed_out,
            new_vectors=vector_out,
            new_vector_moment=vector_out,
            new_vector_average=vector_out,
            new_kernels=kernel_out,
            new_kernel_moment=kernel_out,
            new_kernel_average=kernel_out,
            loss=((1, LANES), F32, HOLD),
        ),
        dict(
            packed=pltpu.VMEM((-(-vectors.shape[0] // 8) * 8, width), F32),
            small=pltpu.VMEM((small_rows, width), F32),
        ),
        limit=SMALL_LIMIT,
    )
    return (
        made.loss[0, 0],
        made.new_embed,
        made.new_embed_moment,
        made.new_head,
        made.new_head_moment,
        made.new_vectors,
        made.new_vector_moment,
        made.new_vector_average,
        *results,
        *[
            jnp.transpose(array, (0, 2, 1))
            for array in (made.new_kernels, made.new_kernel_moment, made.new_kernel_average)
        ],
    )


def solution(mesh):
    split = P(None, None, None, "chan")
    taps = P(None, None, "chan")
    return jax.shard_map(
        shards,
        mesh=mesh,
        in_specs=(P(("dp", "chan"), None), P("dp"), P("dp"), P("dp", None, None))
        + (P(),) * 7
        + (split,) * 9
        + (taps,) * 3,
        out_specs=(P(),) * 8 + (split,) * 9 + (taps,) * 3,
        check_vma=False,
    )
```

```python
import math

import jax
import jax.numpy as jnp
from jax import lax
from jax.experimental import pallas as pl
from jax.experimental.pallas import tpu as pltpu
from jax.sharding import PartitionSpec as P

PATCH_IN = 768
GRID = 16
BLOCKS = 2
IMAGE_ROWS = GRID * GRID
LANES = 128

EPS = 1e-05
MOMENTUM = 0.9
AVERAGE = 0.5
KEEP_RATE = 0.8
KERNEL_SIZES = (3, 5, 7)
KERNEL_STARTS = (0, 9, 34)
MLP_PARTS = 1
ROOT_HALF = math.sqrt(0.5)
DENSITY = 1.0 / math.sqrt(2.0 * math.pi)
VMEM_LIMIT = 44 << 20
SMALL_LIMIT = 14 << 20
F32 = jnp.float32
BF16 = jnp.bfloat16


def matmul(left, right):
    return jnp.dot(left, right, preferred_element_type=F32)


def contract_rows(left, right):
    return lax.dot_general(left, right, (((0,), (0,)), ((), ())), preferred_element_type=F32)


def times_transposed(left, right):
    return lax.dot_general(left, right, (((1,), (1,)), ((), ())), preferred_element_type=F32)


def normalize(values):
    average = jnp.mean(values, axis=-1, keepdims=True)
    centred = values - average
    variance = jnp.mean(centred * centred, axis=-1, keepdims=True)
    scale = lax.rsqrt(variance + EPS)
    return (centred * scale, scale)


def norm_backward(grad, unit, scale, gain):
    d_unit = grad * gain
    mean_one = jnp.mean(d_unit, axis=-1, keepdims=True)
    mean_two = jnp.mean(d_unit * unit, axis=-1, keepdims=True)
    return (d_unit - mean_one - unit * mean_two) * scale


def column_sum(values):
    return jnp.sum(values, axis=0, keepdims=True)


def gelu_pair(values):
    cumulative = 0.5 + 0.5 * lax.erf(values * ROOT_HALF)
    density = DENSITY * jnp.exp(-0.5 * values * values)
    return (values * cumulative, cumulative + values * density)


def nesterov(weight, moment, gradient, rate):
    new_moment = MOMENTUM * moment + gradient
    new_weight = weight - rate * (gradient + MOMENTUM * new_moment)
    return (new_weight, new_moment)


def after(value, *others):
    return lax.optimization_barrier((value, others))[0]


class Links:
    def __init__(self):
        chan = lax.axis_size("chan")
        self.ny = 1 << ((chan.bit_length() - 1) // 2)
        self.nz = chan // self.ny
        self.nc = 2
        self.nx = lax.axis_size("dp") // self.nc
        self.chan = chan
        self.place = lax.axis_index("chan")
        self.z = self.place // self.ny
        self.y = self.place % self.ny
        group = lax.axis_index("dp")
        self.x = group // self.nc
        self.core = group % self.nc
        self.sizes = {"z": self.nz, "y": self.ny, "x": self.nx}

    def bits(self, axis):
        return [1 << k for k in reversed(range((self.sizes[axis] - 1).bit_length()))]

    def swap(self, values, axis, step):
        if axis in ("z", "y"):
            step = step * self.ny if axis == "z" else step
            return lax.ppermute(values, "chan", [(i, i ^ step) for i in range(self.chan)])
        step = step * self.nc if axis == "x" else step
        return lax.ppermute(values, "dp", [(i, i ^ step) for i in range(self.nx * self.nc)])

    def swap_core(self, values):
        return self.swap(values, "core", 1)

    def cross_x(self, values):
        total = values
        for step in self.bits("x"):
            low = total.astype(values.dtype)
            total = low.astype(F32) + self.swap(low, "x", step).astype(F32)
        return total.astype(F32)

    def mask_of(self, axis, step):
        return tuple(step if name == axis else 0 for name in ("z", "y", "x"))

    def here(self):
        return jnp.stack([self.core, self.place, self.x, self.y, self.z]).astype(jnp.int32)

    def places(self, masks):
        return [
            ((self.z ^ mask_z) * self.ny + (self.y ^ mask_y), self.x ^ mask_x)
            for mask_z, mask_y, mask_x in masks
        ]

    def where(self, rows):
        return jnp.stack([self.core, self.place] + rows).astype(jnp.int32)

    def both_halves(self, summed):
        other = self.swap_core(summed)
        first = self.core == 0
        return (jnp.where(first, summed, other), jnp.where(first, other, summed))


def join(left, right):
    return tuple(a ^ b for a, b in zip(left, right))


def total(terms):
    result = terms[0].astype(F32)
    for term in terms[1:]:
        result = result + term.astype(F32)
    return result.astype(BF16)


class Chain:
    def __init__(self, links, terms, rows, order):
        self.terms = terms
        self.rows = rows
        self.order = list(order)
        self.dims = [("z", k) for k in reversed(range(len(links.bits("z"))))]
        self.dims += [("y", k) for k in reversed(range(len(links.bits("y"))))]

    def low(self):
        parts = [
            lax.slice_in_dim(array[0], first, first + self.rows) for array, first in self.terms
        ]
        return total(parts)


def halve(links, chains):
    arrays = []
    plans = []
    groups = []
    outs = []
    for chain in chains:
        axis, level = chain.order.pop(0)
        places = []
        for array, _first in chain.terms:
            found = [k for k, other in enumerate(arrays) if other is array]
            if not found:
                arrays.append(array)
            places.append(found[0] if found else len(arrays) - 1)
        lead = 1 << len(chain.dims)
        if axis == "x":
            before, behind, rows, count = 0, lead, chain.rows // 2, lead
        else:
            at = chain.dims.index((axis, level))
            before, behind = 1 << at, lead >> (at + 1)
            rows, count = chain.rows, lead // 2
            chain.dims.pop(at)
        key = (axis, level, count)
        mates = [group for group in groups if group[0] == key]
        if mates:
            group = mates[0]
        else:
            group = [key, 0]
            groups.append(group)
        plans.append((chain, places, before, behind, rows, count, group, group[1]))
        group[1] += rows
    width = arrays[0].shape[-1]
    for key, rows in groups:
        outs.append(jax.ShapeDtypeStruct((key[2], rows, width), BF16))
    for _chain, _places, _before, _behind, rows, count, _group, _at in plans:
        outs.append(jax.ShapeDtypeStruct((count, rows, width), BF16))

    def body(here_ref, *refs):
        ins, sends = refs[: len(arrays)], refs[len(arrays) : len(arrays) + len(groups)]
        keeps = refs[len(arrays) + len(groups) :]
        index = dict(y=here_ref[3], z=here_ref[4], x=here_ref[2])
        for plan, keep in zip(plans, keeps):
            chain, places, before, behind, rows, count, group, at = plan
            axis, level, _count = group[0]
            bit = index[axis] >> level & 1
            send = sends[groups.index(group)]
            for side, target, first_row in ((1 - bit, send, at), (bit, keep, 0)):
                for out in range(count):
                    summed = None
                    for place, (_array, first) in zip(places, chain.terms):
                        if axis == "x":
                            start = pl.multiple_of(first + side * rows, 8 if rows % 16 else 16)
                            value = ins[place][out, pl.ds(start, rows), :]
                        else:
                            source = (out // behind * 2 + side) * behind + out % behind
                            value = ins[place][source, first : first + rows, :]
                        value = value.astype(F32)
                        summed = value if summed is None else summed + value
                    target[out, first_row : first_row + rows, :] = summed.astype(BF16)

    made = pl.pallas_call(
        body,
        name=halve.__name__,
        in_specs=[pl.BlockSpec(memory_space=pltpu.SMEM)]
        + [pl.BlockSpec(memory_space=pltpu.VMEM) for _ in arrays],
        out_specs=[pl.BlockSpec(memory_space=pltpu.VMEM) for _ in outs],
        out_shape=outs,
        compiler_params=pltpu.CompilerParams(vmem_limit_bytes=SMALL_LIMIT),
    )(links.here(), *arrays)
    moves = [(sent, key[0], 1 << key[1]) for sent, (key, _rows) in zip(made, groups)]

    def take(received):
        for plan, keep in zip(plans, made[len(groups) :]):
            chain, _places, _before, _behind, rows, _count, group, at = plan
            chain.terms = [(keep, 0), (received[groups.index(group)], at)]
            chain.rows = rows

    return (moves, take)


class Reduction:
    def __init__(self, links, kept, received, cuts):
        self.links = links
        count = kept.shape[1]
        quantum = 16 * links.nx
        cut = 2 * count // (3 + cuts) // quantum * quantum if links.nx > 1 else 0
        over_x = [("x", k) for k in reversed(range(len(links.bits("x"))))]
        over_y = [("y", k) for k in range(len(links.bits("y")))]
        over_z = [("z", k) for k in range(len(links.bits("z")))]
        terms = lambda first: [(kept, first), (received, first)]
        self.plain = Chain(links, terms(cuts * cut), count - cuts * cut, over_y + over_z)
        self.cut = []
        if cut:
            orders = [over_x + over_y + over_z, over_z[:1] + over_x + over_y + over_z[1:]]
            self.cut = [
                Chain(links, terms(k * cut), cut, order) for k, order in enumerate(orders[:cuts])
            ]
        self.sums = links.bits("x")[::-1]
        self.gathers = list(self.sums) if cut else []
        self.plain_rows = None
        self.cut_rows = None

    def open(self):
        return [chain for chain in [self.plain] + self.cut if chain.order]

    def done(self):
        return not self.open() and not self.sums and not self.gathers

    def ready(self):
        return not self.open() and not self.sums

    def last_moves(self):
        moves, takes = [], []
        if not self.plain.order and self.sums:
            if self.plain_rows is None:
                self.plain_rows = self.plain.low()
            low = self.plain_rows.astype(BF16)
            moves.append((low, "x", self.sums.pop(0)))

            def take_sum(received):
                self.plain_rows = low.astype(F32) + received.astype(F32)

            takes.append(take_sum)
        if self.gathers and not any(chain.order for chain in self.cut):
            if self.cut_rows is None:
                self.cut_rows = jnp.stack([chain.low() for chain in self.cut])
            part = self.cut_rows
            step = self.gathers.pop(0)
            moves.append((part, "x", step))

            def take_part(received):
                first = jnp.concatenate([part, received], axis=1)
                second = jnp.concatenate([received, part], axis=1)
                self.cut_rows = jnp.where(self.links.x & step == 0, first, second)

            takes.append(take_part)
        return (moves, takes)

    def tail(self, count):
        return self.plain_rows[self.plain_rows.shape[0] - count :]

    def result(self):
        rows = self.plain_rows.astype(F32)
        if self.cut_rows is None:
            return rows
        width = rows.shape[-1]
        return jnp.concatenate([self.cut_rows.astype(F32).reshape(-1, width), rows])


def next_round(links, reductions):
    lasts = [reduction.last_moves() for reduction in reductions]
    chains = [chain for reduction in reductions for chain in reduction.open()]
    moves, take = halve(links, chains) if chains else ([], None)
    count = len(moves)
    for more, _takes in lasts:
        moves = moves + more
    takes = [one for _more, some in lasts for one in some]

    def take_all(received):
        if take is not None:
            take(received[:count])
        for one, part in zip(takes, received[count:]):
            one(part)

    return (moves, take_all)


class Gather:
    def __init__(self, links, own):
        self.links = links
        self.stack = own[None]
        self.masks = [(0, 0, 0)]
        self.parts = None

    def moves(self, axis, step):
        return [(self.stack, axis, step)]

    def take(self, received, axis, step, keep_apart=False):
        if keep_apart:
            self.parts = [self.stack, received]
        else:
            self.stack = jnp.concatenate([self.stack, received], axis=0)
        extra = self.links.mask_of(axis, step)
        self.masks = self.masks + [join(mask, extra) for mask in self.masks]

    def early(self, axis):
        *steps, last = self.links.bits(axis)
        for step in steps:
            self.take(self.links.swap(self.stack, axis, step), axis, step)
        return (axis, last)

    def direct(self):
        return [(self.stack, "z", step) for step in range(1, self.links.nz)]

    def take_direct(self, received):
        self.stack = jnp.concatenate([self.stack] + received, axis=0)
        self.masks = [self.links.mask_of("z", step) for step in range(self.links.nz)]


class Pieces:
    def __init__(self, where, near, far, matrices, slots):
        self.where = where
        self.near = near
        self.far = far
        self.matrices = matrices
        self.slots = slots
        self.width = near[0].shape[-1]

    def rows(self, name):
        return sum(entry[3] for entry in self.matrices[name][1])

    def count(self, name):
        return len(self.matrices[name][1])

    def arrays(self):
        return [*self.near, *self.far]

    def copies(self, name, where, parts, target, sems):
        half, entries = self.matrices[name]
        near, far = parts[: len(self.near)], parts[len(self.near) :]
        pairs = []
        for at, (array, slot, first, count, entry) in enumerate(entries):
            if len(target.shape) == 3:
                room = target.at[where[2 + entry]]
            else:
                start = pl.multiple_of(where[2 + entry], 8 if count % 16 else 16)
                room = target.at[pl.ds(start, count), :]
            rows = pl.ds(first, count)
            pairs.append(
                tuple(
                    pltpu.make_async_copy(part[array].at[slot, rows, :], room, sems.at[at])
                    for part in (near, far)
                )
            )
        mine = where[0] == half

        def start():
            @pl.when(mine)
            def _():
                for pair in pairs:
                    pair[0].start()

            @pl.when(jnp.logical_not(mine))
            def _():
                for pair in pairs:
                    pair[1].start()

        def wait():
            for pair in pairs:
                pair[0].wait()

        return (start, wait)


class Room:
    def __init__(self):
        self.refs = {}
        self.waits = {}
        self.flushes = []
        self.pending = []

    def __getitem__(self, key):
        wait = self.waits.pop(key, None)
        if wait is not None:
            wait()
        return self.refs[key]

    def __getattr__(self, key):
        return self[key]

    def flush(self, *refs):
        rest = []
        for ref, copy in self.flushes:
            if any(ref is one for one in refs):
                copy.start()
                self.pending.append(copy)
            else:
                rest.append((ref, copy))
        self.flushes = rest

    def flush_next(self, *refs):
        for ref in refs:
            at = [k for k, item in enumerate(self.flushes) if item[0] is ref][0]
            copy = self.flushes.pop(at)[1]
            copy.start()
            self.pending.append(copy)

    def finish(self):
        self.flush(*[ref for ref, _copy in self.flushes])
        for copy in self.pending:
            copy.wait()


class Box(dict):
    __getattr__ = dict.__getitem__


class View:
    def __init__(self, room, names):
        self.room = room
        self.names = names

    def __getitem__(self, key):
        return self.room[self.names.get(key, key)]

    def __getattr__(self, key):
        return self[key]

    def flush(self, *refs):
        self.room.flush(*refs)


def renamed(stage, **names):
    def call(room):
        stage(View(room, names))

    call.__name__ = stage.__name__
    return call


HOLD, FETCH, SCALAR = range(3)


def run_kernel(stages, inputs, outputs, temps=(), weights=(), pinned=True, limit=VMEM_LIMIT):
    temps = dict(temps)
    operands, in_specs, scratch, plan = [], [], [], []

    def scratch_for(shape):
        scratch.append(shape)
        return len(scratch) - 1

    for key, (array, mode) in inputs.items():
        operands.append(array)
        if mode == HOLD:
            in_specs.append(pl.BlockSpec(memory_space=pltpu.VMEM))
            plan.append((key, mode, None))
        elif mode == SCALAR:
            in_specs.append(pl.BlockSpec(memory_space=pltpu.SMEM))
            plan.append((key, mode, None))
        else:
            operands[-1] = pltpu.with_memory_space_constraint(array, pltpu.HBM)
            in_specs.append(pl.BlockSpec(memory_space=pltpu.HBM))
            place = scratch_for(pltpu.VMEM(array.shape, array.dtype))
            plan.append((key, mode, (place, scratch_for(pltpu.SemaphoreType.DMA))))
    loads = []
    for pieces, names in weights:
        first = len(operands)
        operands.append(pieces.where)
        in_specs.append(pl.BlockSpec(memory_space=pltpu.SMEM))
        for array in pieces.arrays():
            if pinned:
                array = pltpu.with_memory_space_constraint(array, pltpu.HBM)
            operands.append(array)
            in_specs.append(pl.BlockSpec(memory_space=pltpu.HBM if pinned else pl.ANY))
        for matrix, apart in names.items():
            shape = (pieces.rows(matrix), pieces.width)
            if apart:
                shape = (pieces.slots, shape[0] // pieces.slots, shape[1])
            place = scratch_for(pltpu.VMEM(shape, BF16))
            sems = scratch_for(pltpu.SemaphoreType.DMA((pieces.count(matrix),)))
            loads.append((matrix, pieces, first, place, sems))
    out_specs, out_shapes, out_plan = [], [], []
    for key, (shape, dtype, mode, *cuts) in outputs.items():
        if mode == HOLD:
            out_specs.append(pl.BlockSpec(memory_space=pltpu.VMEM))
            out_shapes.append(jax.ShapeDtypeStruct(shape, dtype))
            out_plan.append((key, None))
        else:
            out_specs.append(pl.BlockSpec(memory_space=pltpu.HBM))
            out_shapes.append(pltpu.HBM(shape, dtype))
            place = scratch_for(pltpu.VMEM(shape, dtype))
            cuts = cuts or [()]
            sems = [scratch_for(pltpu.SemaphoreType.DMA) for _ in cuts]
            out_plan.append((key, (place, sems, cuts)))
    temp_plan = [(key, scratch_for(shape)) for key, shape in temps.items()]

    def body(*refs):
        ins = refs[: len(operands)]
        outs = refs[len(operands) : len(operands) + len(out_specs)]
        rooms = refs[len(operands) + len(out_specs) :]
        room = Room()
        def load(group):
            for matrix, pieces, first, place, sems in loads:
                if pieces is group:
                    where = ins[first]
                    parts = ins[first + 1 : first + 1 + len(pieces.arrays())]
                    start, wait = pieces.copies(matrix, where, parts, rooms[place], rooms[sems])
                    start()
                    room.refs[matrix] = rooms[place]
                    room.waits[matrix] = wait
                    room.refs.update(where=where)

        for pieces, _names in weights[:1]:
            load(pieces)
        for ref, (key, mode, more) in zip(ins, plan):
            if mode == FETCH:
                place, sem = more
                copy = pltpu.make_async_copy(ref, rooms[place], rooms[sem])
                copy.start()
                room.refs[key] = rooms[place]
                room.waits[key] = copy.wait
            else:
                room.refs[key] = ref
        for pieces, _names in weights[1:]:
            load(pieces)
        for ref, (key, more) in zip(outs, out_plan):
            if more is None:
                room.refs[key] = ref
            else:
                place, sems, cuts = more
                room.refs[key] = rooms[place]
                for sem, cut in zip(sems, cuts):
                    source, target = rooms[place], ref
                    if cut:
                        source, target = source.at[cut], target.at[cut]
                    copy = pltpu.make_async_copy(source, target, rooms[sem])
                    room.flushes.append((rooms[place], copy))
        for key, place in temp_plan:
            room.refs[key] = rooms[place]
        for stage in stages:
            stage(room)
        for key in list(room.waits):
            room[key]
        room.finish()

    results = pl.pallas_call(
        body,
        name=stages[-1].__name__,
        in_specs=in_specs,
        out_specs=out_specs,
        out_shape=out_shapes,
        scratch_shapes=scratch,
        compiler_params=pltpu.CompilerParams(vmem_limit_bytes=limit),
    )(*operands)
    return Box(zip(outputs, results))


MASKED, COUNTED, VALID, KEEP = 0, 1, 2, 3


def column(room, index):
    return room.columns[:, index : index + 1]


def keep_of(room, block, branch):
    return column(room, KEEP + 2 * block + branch)


def vector(room, row):
    return room.vectors[row : row + 1, :]


def low_gates(room, block):
    return room.vectors[10 * block + 6 : 10 * block + 10, :].astype(BF16)


def correlate(padded, taps, level, flip):
    width = KERNEL_SIZES[level]
    first = KERNEL_STARTS[level]
    margin = width // 2
    lanes = padded.shape[-1]
    sums = [None] * GRID
    for dx in range(width):
        weights = []
        for dy in range(width):
            tap = dy * width + dx
            if flip:
                tap = width * width - 1 - tap
            weights.append(jnp.broadcast_to(taps[first + tap : first + tap + 1, :], (GRID, lanes)))
        for row in range(GRID):
            window = padded[row, 8 - margin + dx : 8 - margin + dx + GRID, :]
            for dy in range(width):
                out = row - dy + margin
                if 0 <= out < GRID:
                    term = window * weights[dy]
                    sums[out] = term if sums[out] is None else sums[out] + term
    return sums


def correlate_taps(padded, grads, d_taps, at_lanes, level):
    width = KERNEL_SIZES[level]
    first = KERNEL_STARTS[level]
    margin = width // 2
    for dx in range(width):
        sums = [None] * width
        for row in range(GRID):
            window = padded[row, 8 - margin + dx : 8 - margin + dx + GRID, :]
            for dy in range(width):
                out = row - dy + margin
                if 0 <= out < GRID:
                    term = window * grads[out]
                    sums[dy] = term if sums[dy] is None else sums[dy] + term
        for dy in range(width):
            tap = first + dy * width + dx
            d_taps[tap : tap + 1, at_lanes] = column_sum(sums[dy])


def clear_margins(padded):
    lanes = padded.shape[-1]
    for row in range(GRID):
        padded[row, 0:8, :] = jnp.zeros((8, lanes), F32)
        padded[row, 8 + GRID : 16 + GRID, :] = jnp.zeros((8, lanes), F32)


def rows_at(row):
    return slice(row * GRID, (row + 1) * GRID)


def gate_part(gates, row, level, lanes):
    part = gates[rows_at(row), level * LANES : (level + 1) * LANES]
    return part if lanes == LANES else part[:, 0:1]


def lane_range(group, groups, lanes):
    if groups == 1:
        return slice(0, lanes)
    if isinstance(group, int):
        return slice(group * lanes, (group + 1) * lanes)
    return pl.ds(pl.multiple_of(group * lanes, lanes), lanes)


def tap_room(tap_count):
    return -(-tap_count // 8) * 8


def split_three(values):
    high = values.astype(BF16)
    rest = values - high.astype(F32)
    middle = rest.astype(BF16)
    return (high, middle, (rest - middle.astype(F32)).astype(BF16))


def pack_rows(here, sources, taps):
    width = sources[0][0].shape[3]
    counts = [rows // parts for _array, _block, _first, rows, parts in sources]
    rows = sum(counts) + (0 if taps is None else taps.shape[1])

    def body(here_ref, *refs):
        wide_refs = refs[: len(sources)]
        rest = refs[len(sources) :]
        out_ref = rest[0] if taps is None else rest[1]
        buffers = rest[-1 - len(sources) : -1]
        sems = rest[-1]
        if taps is not None:
            tap_buffer, tap_sem = rest[2:4]
            tap_copy = pltpu.make_async_copy(rest[0], tap_buffer, tap_sem)
            tap_copy.start()
        copies = []
        for at, (ref, (_array, block, first, _rows, parts)) in enumerate(zip(wide_refs, sources)):
            if parts > 1:
                first = pl.multiple_of(first + here_ref[2] * counts[at], 8)
            source = ref.at[block, here_ref[0], pl.ds(first, counts[at]), :]
            copies.append(pltpu.make_async_copy(source, buffers[at], sems.at[at]))
            copies[-1].start()
        row = sum(counts)
        if taps is not None:
            own, count = taps.shape[1:]
            out_ref[row : row + own, :] = jnp.zeros((own, width), BF16)
            tap_copy.wait()
            splits = [split_three(tap_buffer[b]) for b in range(BLOCKS)]
            wide = (splits[0][0], splits[1][0], splits[0][1])
            thin = (splits[1][1], splits[0][2], splits[1][2])
            for chosen, at_core in ((wide, 0), (thin, 1)):

                @pl.when(here_ref[0] == at_core)
                def _():
                    for index, part in enumerate(chosen):
                        at = index * LANES
                        out_ref[row : row + own, at : at + count] = part

        row = 0
        for copy, buffer, count in zip(copies, buffers, counts):
            copy.wait()
            out_ref[row : row + count, :] = buffer[...].astype(BF16)
            row += count

    extra = [] if taps is None else [taps]
    return pl.pallas_call(
        body,
        name=pack_rows.__name__,
        in_specs=[pl.BlockSpec(memory_space=pltpu.SMEM)]
        + [pl.BlockSpec(memory_space=pltpu.HBM) for _ in sources]
        + [pl.BlockSpec(memory_space=pltpu.HBM) for _ in extra],
        out_specs=pl.BlockSpec(memory_space=pltpu.VMEM),
        out_shape=jax.ShapeDtypeStruct((rows, width), BF16),
        scratch_shapes=[
            item
            for array in extra
            for item in (pltpu.VMEM(array.shape, F32), pltpu.SemaphoreType.DMA)
        ]
        + [pltpu.VMEM((count, width), F32) for count in counts]
        + [pltpu.SemaphoreType.DMA((len(sources),))],
        compiler_params=pltpu.CompilerParams(vmem_limit_bytes=SMALL_LIMIT),
    )(
        here,
        *[pltpu.with_memory_space_constraint(array, pltpu.HBM) for array, *_rest in sources],
        *[pltpu.with_memory_space_constraint(array, pltpu.HBM) for array in extra],
    )


def taps_stage(tap_count, groups, lanes):
    room_rows = tap_room(tap_count)
    used = BLOCKS * room_rows

    def join_taps(room):
        wide = room.wide[...]
        thin = room.thin[...]
        shape = (used, wide.shape[1])
        row = lax.broadcasted_iota(jnp.int32, shape, 0)
        lane = lax.broadcasted_iota(jnp.int32, shape, 1)
        upper = row >= room_rows
        tap = jnp.where(upper, row - room_rows, row)
        tap = jnp.where(tap < tap_count, tap, -8 * LANES)

        def chosen(lower_places, upper_places):
            marks = jnp.zeros(shape, F32)
            for places, side in ((lower_places, False), (upper_places, True)):
                for place in places:
                    hit = jnp.logical_and(lane == tap + place * LANES, upper == side)
                    marks = jnp.where(hit, 1.0, marks)
            return marks.astype(BF16)

        taps = times_transposed(chosen((0, 2), (1,)), wide)
        taps = taps + times_transposed(chosen((1,), (0, 2)), thin)
        for b in range(BLOCKS):
            for j in range(groups):
                room.taps[b, j] = taps[
                    b * room_rows : (b + 1) * room_rows, j * lanes : (j + 1) * lanes
                ]

    return join_taps


def inputs_stage(block, groups, lanes):
    def focal_inputs(room):
        unit, _scale = normalize(room.x[...])
        first = unit * vector(room, 10 * block) + vector(room, 10 * block + 1)
        first = first.astype(BF16)
        width = first.shape[1]
        gate_low = low_gates(room, block)
        for level in range(4):
            spread = jnp.broadcast_to(gate_low[level : level + 1], (LANES, width))
            room.gates[:, level * LANES : (level + 1) * LANES] = times_transposed(
                first, spread
            )
        key = room.key
        for j in range(groups):
            room.context[j] = times_transposed(first, key[j * lanes : (j + 1) * lanes, :])
        room.query_out[...] = times_transposed(first, room.query[...])
        room.flush(room.gates, room.context, room.query_out)

    return focal_inputs


def focal_stage(block, groups, lanes):
    def focal_levels(room):
        padded = room.padded
        taps, context, gates, low, pool = room.taps, room.context, room.gates, room.low, room.pool
        fields = [room.k1, room.k2, room.k3]
        slopes = [room.s1, room.s2, room.s3]
        clear_margins(padded)
        valid = room.image_columns[:, VALID : VALID + 1]
        valid_total = column_sum(valid)

        def group(j, carry):
            tap = taps.at[block, j]
            for row in range(GRID):
                padded[row, 8 : 8 + GRID, :] = context[j, rows_at(row), :]
            for level in range(3):
                sums = correlate(padded, tap, level, False)
                for row in range(GRID):
                    value, slope = gelu_pair(sums[row])
                    fields[level][j, rows_at(row), :] = value
                    slopes[level][j, rows_at(row), :] = slope
                    if level < 2:
                        padded[row, 8 : 8 + GRID, :] = value
            mean = column_sum(fields[2][j] * valid) / valid_total
            pooled, pooled_slope = gelu_pair(mean)
            pool[j, 0:1, :] = pooled
            pool[j, 1:2, :] = pooled_slope / valid_total
            pool[j, 2:8, :] = jnp.zeros((6, lanes), F32)
            at = lane_range(j, groups, lanes)
            for row in range(GRID):
                summed = pooled * gate_part(gates, row, 3, lanes)
                for level in range(3):
                    summed = summed + fields[level][j, rows_at(row), :] * gate_part(
                        gates, row, level, lanes
                    )
                low[rows_at(row), at] = summed.astype(BF16)
            return carry

        if groups > 1:
            lax.fori_loop(0, groups, group, 0)
        else:
            group(0, 0)
        room.flush(room.k1, room.k2, room.k3, room.s1, room.s2, room.s3, room.pool, room.low)

    return focal_levels


def mix_stage(block):
    def mix_forward(room):
        modulator = times_transposed(room.low[...], room.mix[...])
        room.mod[...] = modulator
        room.flush(room.mod)
        product = (room.query_out[...] * modulator).astype(BF16)
        branch = matmul(product, room.proj[...]) + vector(room, 10 * block + 4)
        room.middle[...] = room.x[...] + keep_of(room, block, 0) * branch

    return mix_forward


def mlp_stage(block):
    def mlp_forward(room):
        middle = room.middle[...]
        unit, _scale = normalize(middle)
        second = unit * vector(room, 10 * block + 2) + vector(room, 10 * block + 3)
        second = second.astype(BF16)
        up = room.up
        step = up.shape[0] // 4
        for part in range(4):
            at = slice(part * step, (part + 1) * step)
            value, slope = gelu_pair(times_transposed(second, up[at, :]))
            room.hidden[:, at] = value.astype(BF16)
            room.slope[:, at] = slope
        room.flush(room.hidden, room.slope)
        lowered = matmul(room.hidden[...], room.down[...]) + vector(room, 10 * block + 5)
        room.out[...] = middle + keep_of(room, block, 1) * lowered

    return mlp_forward


def embed_stage(room):
    outer = 10 * BLOCKS
    embedded = matmul(room.patches[...], room.embed[...].astype(BF16))
    embedded = embedded + vector(room, outer)
    room.embedded[...] = embedded
    room.flush(room.embedded)
    unit, _scale = normalize(embedded)
    mask = column(room, MASKED)
    state = unit * vector(room, outer + 1) + vector(room, outer + 2)
    room.x[...] = state * (1.0 - mask) + vector(room, outer + 5) * mask


def store_halves(core, kept, sent, at, first, second):
    chan, _rows, width = kept.shape
    rows = first.shape[0] // chan
    first = first.reshape(chan, rows, width).astype(BF16)
    second = second.reshape(chan, rows, width).astype(BF16)

    @pl.when(core == 0)
    def _():
        kept[:, at : at + rows, :] = first
        sent[:, at : at + rows, :] = second

    @pl.when(core != 0)
    def _():
        kept[:, at : at + rows, :] = second
        sent[:, at : at + rows, :] = first


def head_stage(at):
    def head_step(room):
        outer = 10 * BLOCKS
        gain = vector(room, outer + 3)
        unit, scale = normalize(room.x[...])
        low = (unit * gain + vector(room, outer + 4)).astype(BF16)
        head_low = room.head[...].astype(BF16)
        error = matmul(low, head_low) - room.patches[...].astype(F32)
        denom = jnp.max(room.counts[...] + room.counts_twin[...]) * PATCH_IN
        weighted = column(room, COUNTED) * error
        loss = column_sum(weighted * error) / denom
        d_pred = (2.0 * weighted / denom).astype(BF16)
        grad = contract_rows(low, d_pred)
        half = grad.shape[1] // 2
        core = room.where[0]
        store_halves(core, room.kept, room.sent, at, grad[:, :half], grad[:, half:])
        d_final = times_transposed(d_pred, head_low)
        room.d_out[...] = norm_backward(d_final, unit, scale, gain)
        sums = room.sums
        width = low.shape[1]
        sums[0:1, :] = column_sum(d_final * unit)
        sums[1:2, :] = column_sum(d_final)
        parts = [loss[:, at : at + width] for at in range(0, loss.shape[1], width)]
        sums[2:3, :] = sum(parts[1:], parts[0])
        sums[3:8, :] = jnp.zeros((5, width), F32)

    return head_step


def mlp_back_stage(block, at):
    def mlp_backward(room):
        d_residual = room.d_in[...]
        d_down = d_residual * keep_of(room, block, 1)
        d_low = d_down.astype(BF16)
        unit, scale = normalize(room.middle[...])
        gain = vector(room, 10 * block + 2)
        second = (unit * gain + vector(room, 10 * block + 3)).astype(BF16)
        down, hidden, slope, up = room.down, room.hidden, room.slope, room.up
        d_second = None
        count = MLP_PARTS
        step = down.shape[0] // count
        grads = []
        for part in range(count):
            here = slice(part * step, (part + 1) * step)
            d_pre = (times_transposed(d_low, down[here, :]) * slope[:, here]).astype(BF16)
            grads.append((contract_rows(d_pre, second), contract_rows(hidden[:, here], d_low)))
            term = matmul(d_pre, up[here, :])
            d_second = term if d_second is None else d_second + term
        core = room.where[0]
        chan = room.kept.shape[0]
        for part, (grad_up, grad_down) in enumerate(grads):
            places = slice(part * (chan // count), (part + 1) * (chan // count))
            kept, sent = room.kept.at[places], room.sent.at[places]
            store_halves(core, kept, sent, at, grad_up, grad_down)
        room.d_out[...] = d_residual + norm_backward(d_second, unit, scale, gain)
        sums = room.sums
        width = d_low.shape[1]
        sums[0:1, :] = column_sum(d_second * unit)
        sums[1:2, :] = column_sum(d_second)
        sums[2:3, :] = column_sum(d_down)
        sums[3:8, :] = jnp.zeros((5, width), F32)

    return mlp_backward


def mix_back_stage(block, groups, lanes, at):
    def mix_backward(room):
        d_proj = room.d_in[...] * keep_of(room, block, 0)
        d_low = d_proj.astype(BF16)
        d_product = times_transposed(d_low, room.proj[...])
        modulator = room.mod[...]
        query = room.query_out[...]
        d_mod = (d_product * query).astype(BF16)
        mix = room.mix
        for j in range(groups):
            room.d_sum[j] = matmul(d_mod, mix[:, j * lanes : (j + 1) * lanes])
        room.d_query[...] = (d_product * modulator).astype(BF16)
        product = (query * modulator).astype(BF16)
        grad_proj = contract_rows(product, d_low)
        grad_mix = contract_rows(d_mod, room.low[...])
        core = room.where[0]
        store_halves(core, room.kept, room.sent, at, grad_mix, grad_proj)
        sums = room.sums
        width = d_low.shape[1]
        sums[0:1, :] = column_sum(d_proj)
        sums[1:8, :] = jnp.zeros((7, width), F32)

    return mix_backward


def focal_back_stage(block, groups, lanes):
    def levels_backward(room):
        padded = room.padded
        d_padded = room.d_padded
        clear_margins(padded)
        clear_margins(d_padded)
        d_all, gates, taps, pool = room.d_sum, room.gates, room.taps, room.pool
        fields = [room.context, room.k1, room.k2, room.k3]
        slopes = [room.s1, room.s2, room.s3]
        d_context, d_gates, d_taps = room.d_context, room.d_gates, room.d_taps
        valid = room.image_columns[:, VALID : VALID + 1]
        d_gates[...] = jnp.zeros(d_gates.shape, F32)
        d_taps[...] = jnp.zeros(d_taps.shape, F32)

        def fold(values):
            if lanes == LANES:
                return values
            summed = jnp.sum(values, axis=-1, keepdims=True) / LANES
            return jnp.broadcast_to(summed, (values.shape[0], LANES))

        def group(j, carry):
            tap = taps.at[block, j]
            at = lane_range(j, groups, lanes)
            d_pooled = jnp.zeros((1, lanes), F32)
            for row in range(GRID):
                d_pooled = d_pooled + column_sum(
                    d_all[j, rows_at(row), :] * gate_part(gates, row, 3, lanes)
                )
            d_mean = d_pooled * pool[j, 1:2, :]
            d_field = [d_mean * valid[rows_at(row)] for row in range(GRID)]
            for level in (2, 1, 0):
                d_pre = []
                for row in range(GRID):
                    here = rows_at(row)
                    grad = d_field[row] + d_all[j, here, :] * gate_part(gates, row, level, lanes)
                    grad = grad * slopes[level][j, here, :]
                    d_pre.append(grad)
                    d_padded[row, 8 : 8 + GRID, :] = grad
                    padded[row, 8 : 8 + GRID, :] = fields[level][j, here, :]
                correlate_taps(padded, d_pre, d_taps, at, level)
                d_field = correlate(d_padded, tap, level, True)
            for row in range(GRID):
                d_context[rows_at(row), at] = d_field[row].astype(BF16)
            whole = d_all[j]
            for level in range(3):
                here = slice(level * LANES, (level + 1) * LANES)
                d_gates[:, here] = d_gates[:, here] + fold(whole * fields[level + 1][j])
            here = slice(3 * LANES, 4 * LANES)
            d_gates[:, here] = d_gates[:, here] + fold(whole * pool[j, 0:1, :])
            return carry

        for j in range(groups):
            group(j, 0)
        room.flush(room.d_taps)

    return levels_backward


def inputs_back_stage(block, at):
    def inputs_backward(room):
        unit, scale = normalize(room.x[...])
        gain = vector(room, 10 * block)
        first_wide = (unit * gain + vector(room, 10 * block + 1)).astype(BF16)
        first = first_wide
        first_wide = first.astype(F32)
        rows, width = first.shape
        gate_low = low_gates(room, block).astype(F32)
        sums = room.input_sums
        sums[...] = jnp.zeros((8, width), F32)
        d_first = jnp.zeros((rows, width), F32)
        d_gates = room.d_gates
        for level in range(4):
            here = slice(level * LANES, (level + 1) * LANES)
            col = jnp.sum(d_gates[:, here], axis=-1, keepdims=True)
            d_first = d_first + col * gate_low[level : level + 1]
            sums[2 + level : 3 + level, :] = column_sum(col * first_wide)
        d_query = room.d_query[...]
        d_context = room.d_context[...]
        d_first = d_first + matmul(d_query, room.query[...])
        d_first = d_first + matmul(d_context, room.key[...])
        room.d_out[...] = room.d_in[...] + norm_backward(d_first, unit, scale, gain)
        sums[0:1, :] = column_sum(d_first * unit)
        sums[1:2, :] = column_sum(d_first)
        grad_query = contract_rows(d_query, first)
        grad_key = contract_rows(d_context, first)
        kept, sent = room.kept, room.sent
        core = room.where[0]
        store_halves(core, kept, sent, at, grad_query, grad_key)

    return inputs_backward


def sums_start(tap_count):
    return BLOCKS * tap_room(tap_count)


def small_rows_for(tap_count, chan):
    used = sums_start(tap_count) + 8 * (2 + 3 * BLOCKS)
    return -(-used // (16 * chan)) * (16 * chan)


def embed_back_stage(tap_count, sum_keys, tap_keys, first_row):
    outer = 10 * BLOCKS

    def embed_backward(room):
        mask = column(room, MASKED)
        d_residual = room.d_out[...]
        d_start = d_residual * (1.0 - mask)
        unit, scale = normalize(room.embedded[...])
        d_embed = norm_backward(d_start, unit, scale, vector(room, outer + 1))
        small = room.small
        small[...] = jnp.zeros(small.shape, F32)
        for b, key in enumerate(tap_keys):
            at = b * tap_room(tap_count)
            taps = room.d_taps if key is None else room[key]
            small[at : at + taps.shape[0], :] = taps[...]
        at = sums_start(tap_count)
        small[at : at + 1, :] = column_sum(d_embed)
        small[at + 1 : at + 2, :] = column_sum(d_start * unit)
        small[at + 2 : at + 3, :] = column_sum(d_start)
        small[at + 3 : at + 4, :] = column_sum(d_residual * mask)
        for key in sum_keys:
            at += 8
            small[at : at + 8, :] = room[key][...]
        grad = contract_rows(room.patches[...], d_embed.astype(BF16))
        core = room.where[0]
        kept, sent = room.kept, room.sent
        half = grad.shape[0] // 2
        row = first_row
        store_halves(core, kept, sent, row, grad[:half], grad[half:])
        row += half // kept.shape[0]
        half = small.shape[0] // 2
        store_halves(core, kept, sent, row, small[:half], small[half:])

    return embed_backward


def update_shared_stage(tap_count, own, part, rate):
    def update_shared(room):
        width = room.near0.shape[2]
        core = room.where[0]
        small_half = room.small.shape[0] // 2
        small_part = room.near0.shape[1] - 2 * part
        half_rows = room.embed.shape[0] // 2
        for half, parts in ((core, (room.near0, room.near1)), (1 - core, (room.far0, room.far1))):
            across = pl.ds(pl.multiple_of(half * width, width), width)
            entry = 2
            for ref in parts:
                for slot in range(ref.shape[0]):
                    place = room.where[entry]
                    entry += 1
                    gradient = ref[slot].astype(F32)
                    down = pl.ds(pl.multiple_of(place * part, 8), part)
                    new_weight, new_moment = nesterov(
                        room.head[down, across],
                        room.head_moment[down, across],
                        gradient[:part],
                        rate,
                    )
                    room.new_head[down, across] = new_weight
                    room.new_head_moment[down, across] = new_moment
                    down = pl.ds(pl.multiple_of(half * half_rows + place * part, 8), part)
                    new_weight, new_moment = nesterov(
                        room.embed[down, :],
                        room.embed_moment[down, :],
                        gradient[part : 2 * part],
                        rate,
                    )
                    room.new_embed[down, :] = new_weight
                    room.new_embed_moment[down, :] = new_moment
                    at = pl.multiple_of(half * small_half + place * small_part, 8)
                    room.small[pl.ds(at, small_part), :] = gradient[2 * part :]
        room.flush(room.new_head, room.new_head_moment, room.new_embed, room.new_embed_moment)
        grads = room.small[...]
        small = grads.astype(BF16)

        def sum_row(index, row):
            at = sums_start(tap_count) + 8 * index + row
            return grads[at : at + 1]

        rows = []
        for b in range(BLOCKS):
            inputs_at, mlp_at, mix_at = 1 + 3 * b, 2 + 3 * b, 3 + 3 * b
            rows += [sum_row(inputs_at, 0), sum_row(inputs_at, 1)]
            rows += [sum_row(mlp_at, 0), sum_row(mlp_at, 1)]
            rows += [sum_row(mix_at, 0), sum_row(mlp_at, 2)]
            rows += [sum_row(inputs_at, 2 + level) for level in range(4)]
        head_at = 1 + 3 * BLOCKS
        rows += [sum_row(0, 0), sum_row(0, 1), sum_row(0, 2)]
        rows += [sum_row(head_at, 0), sum_row(head_at, 1), sum_row(0, 3)]
        packed = room.packed
        for at, row in enumerate(rows):
            packed[at : at + 1, :] = row
        gradient = packed[0 : len(rows), :]
        new_weight, new_moment = nesterov(
            room.vectors[...], room.vector_moment[...], gradient, rate
        )
        room.new_vectors[...] = new_weight
        room.new_vector_moment[...] = new_moment
        room.new_vector_average[...] = (
            AVERAGE * room.vector_average[...] + (1.0 - AVERAGE) * new_weight
        )
        loss = jnp.sum(sum_row(head_at, 2), axis=-1, keepdims=True)
        room.loss[...] = jnp.broadcast_to(loss, room.loss.shape)
        first = room.where[1] * own
        source = lax.broadcasted_iota(jnp.int32, (own, width), 1)
        wanted = first + lax.broadcasted_iota(jnp.int32, (own, width), 0)
        chosen = (source == wanted).astype(F32).astype(BF16)
        for b in range(BLOCKS):
            at = b * tap_room(tap_count)
            gradient = times_transposed(chosen, small[at : at + tap_room(tap_count)])
            gradient = gradient[:, :tap_count]
            new_weight, new_moment = nesterov(
                room.kernels[b], room.kernel_moment[b], gradient, rate
            )
            room.new_kernels[b] = new_weight
            room.new_kernel_moment[b] = new_moment
            room.new_kernel_average[b] = (
                AVERAGE * room.kernel_average[b] + (1.0 - AVERAGE) * new_weight
            )

    return update_shared


class Shares:
    def __init__(self, local_rows, chan_size):
        self.count = max(1, IMAGE_ROWS // local_rows)
        self.groups = [
            list(range(first, first + self.count)) for first in range(0, chan_size, self.count)
        ]

    def to_images(self, values):
        whole = lax.all_to_all(
            values[0], "chan", 1, 0, axis_index_groups=self.groups, tiled=True
        )
        return whole[None]

    def to_rows(self, values):
        return lax.all_to_all(values, "chan", 0, 1, axis_index_groups=self.groups, tiled=True)

    def all_rows(self, values):
        return lax.all_gather(
            values, "chan", axis=0, axis_index_groups=self.groups, tiled=True
        )

    def sum_rows(self, values):
        return lax.psum_scatter(
            values, "chan", scatter_dimension=0, axis_index_groups=self.groups, tiled=True
        )

    def channels(self, values):
        size = values.shape[-1] // self.count
        place = lax.axis_index("chan") % self.count
        return lax.dynamic_slice_in_dim(values, place * size, size, values.ndim - 1)

    def spread(self, values):
        size = values.shape[1]
        place = lax.axis_index("chan") % self.count
        whole = jnp.zeros((values.shape[0], size * self.count), values.dtype)
        return lax.dynamic_update_slice_in_dim(whole, values, place * size, 1)


def hold(array):
    return (array, HOLD)


def fetch(array):
    return (array, FETCH)


def fetch_all(made, names):
    return {name: fetch(made[name]) for name in names}


def shards(
    patches,
    valid_mask,
    target_mask,
    keep_mask,
    embed_weight,
    embed_moment,
    head_weight,
    head_moment,
    vectors,
    vector_moment,
    vector_average,
    focal_input,
    focal_moment,
    focal_average,
    mixers,
    mixer_moment,
    mixer_average,
    mlp_weights,
    mlp_moment,
    mlp_average,
    kernels,
    kernel_moment,
    kernel_average,
):
    links = Links()
    rows, patch_in = patches.shape
    group_rows = valid_mask.shape[0]
    own = focal_input.shape[-1]
    own_hidden = mlp_weights.shape[-1]
    hidden_width = own_hidden * links.chan
    tap_count = kernels.shape[1]
    width = vectors.shape[1]
    shares = Shares(rows, links.chan)
    shared = shares.count > 1
    channels = width // shares.count
    lanes = LANES if channels % LANES == 0 else channels
    groups = channels // lanes
    room_rows = tap_room(tap_count)
    cut_rows = own_hidden // 2 if links.nx > 1 and own_hidden % (16 * links.nx) == 0 else 0
    plain_rows = own_hidden - cut_rows
    cut_part = cut_rows // links.nx

    def together(values, moves):
        got = [links.swap(*move) for move in moves]
        return lax.optimization_barrier((values, got))

    def beside(call, gate, moves):
        made = call(after(gate, *[move[0] for move in moves]))
        made, got = together(dict(made), moves)
        return (Box(made), got)

    here = links.here()
    focal_rows = jnp.transpose(focal_input, (0, 2, 3, 1))
    mixer_rows = jnp.transpose(mixers, (0, 1, 3, 2))
    mlp_rows = jnp.transpose(mlp_weights, (0, 1, 3, 2))
    kernel_rows = jnp.transpose(kernels, (0, 2, 1))
    focal_layout = dict(query=(0, 0), mix=(0, own), key=(1, 0), proj=(1, own))
    first_layout = dict(focal_layout, wide=(0, 2 * own), thin=(1, 2 * own))
    mlp_layout = dict(up=(0, 0), down=(1, 0))

    def slots_of(parts):
        return [(k, d) for k, part in enumerate(parts) for d in range(part.shape[0])]

    def pieces_of(gather, far, layout, count, apart=False):
        rows = [place * (1 if apart else count) for place, _x in links.places(gather.masks)]
        slots = slots_of(gather.parts)
        matrices = {
            name: (half, [(k, d, first, count, at) for at, (k, d) in enumerate(slots)])
            for name, (half, first) in layout.items()
        }
        return Pieces(links.where(rows), gather.parts, far, matrices, len(slots))

    def cut_pieces(gather, crossed, masks, far):
        rows, entries = [], []
        for (k, d), (place, x) in zip(slots_of(gather.parts), links.places(gather.masks)):
            entries.append((k, d, 0, plain_rows, len(rows)))
            rows.append(place * own_hidden)
            entries.append((k, d, plain_rows, cut_part, len(rows)))
            rows.append(place * own_hidden + plain_rows + x * cut_part)
        for (k, d), (place, x) in zip(slots_of(crossed), links.places(masks)):
            entries.append((k + len(gather.parts), d, 0, cut_part, len(rows)))
            rows.append(place * own_hidden + plain_rows + x * cut_part)
        matrices = dict(up=(0, entries), down=(1, entries))
        return Pieces(links.where(rows), gather.parts + crossed, far, matrices, links.chan)

    first_row = links.place * rows
    validity = valid_mask.astype(F32)
    masked = target_mask.astype(F32)
    keep_rows = jnp.repeat(
        keep_mask.reshape(keep_mask.shape[0], -1).astype(F32) / KEEP_RATE, IMAGE_ROWS, axis=0
    )
    table = jnp.concatenate(
        [
            masked[:, None],
            (masked * validity)[:, None],
            validity[:, None],
            keep_rows,
            jnp.zeros((group_rows, 1), F32),
        ],
        axis=1,
    )
    columns = lax.dynamic_slice_in_dim(table, first_row, rows)
    image_columns = columns
    if shared:
        image_columns = lax.dynamic_slice_in_dim(
            table, first_row // IMAGE_ROWS * IMAGE_ROWS, IMAGE_ROWS
        )
    group_count = jnp.broadcast_to(jnp.sum(validity * masked), (8, LANES))
    basic = dict(vectors=fetch(vectors), columns=fetch(columns))
    grid_columns = dict(image_columns=fetch(image_columns))

    whole = (rows, width)
    focal = [None] * BLOCKS
    mlp = [None] * BLOCKS
    focal[0] = Gather(
        links, pack_rows(
            here, [(focal_rows, 0, 0, own, 1), (mixer_rows, 0, 0, own, 1)], kernel_rows
        )
    )
    moves = focal[0].direct()
    embedded = run_kernel(
        [embed_stage],
        dict(patches=fetch(patches), embed=fetch(embed_weight), **basic),
        dict(x=(whole, F32, HOLD), embedded=(whole, F32, FETCH)),
    )
    sources = [(mlp_rows, 0, 0, plain_rows, 1)]
    if cut_rows:
        sources.append((mlp_rows, 0, plain_rows, cut_rows, links.nx))
    packed = pack_rows(here, sources, None)
    (x, packed), got = together((embedded.x, packed), moves)
    focal[0].take_direct(got)
    mlp[0] = Gather(links, packed)
    z_first, *z_rest = links.bits("z")
    y_move = focal[0].early("y")
    (move,) = mlp[0].moves("z", z_first)
    packed = (
        pack_rows(here, [(focal_rows, 1, 0, own, 1), (mixer_rows, 1, 0, own, 1)], None),
        pack_rows(here, [(mlp_rows, 1, 0, own_hidden, 1)], None),
    )
    packed, got = together(packed, [move])
    mlp[0].take(got[0], "z", z_first)
    focal[1] = Gather(links, packed[0])
    mlp[1] = Gather(links, packed[1])

    def take_z(gather, received):
        for step, one in zip(z_rest, received):
            gather.take(one, "z", step)

    moves = [(mlp[0].stack, "z", step) for step in z_rest]
    moves += [(focal[0].stack, *y_move), (focal[1].stack, "z", z_first)]
    x, got = together(x, moves)
    take_z(mlp[0], got[:-2])
    focal[0].take(got[-2], *y_move, True)
    focal[1].take(got[-1], "z", z_first)

    def twins(gather, values):
        values, got = together(values, [(part, "core", 1) for part in gather.parts])
        return (values, got)

    y_move = mlp[0].early("y")
    x, far = twins(focal[0], after(x, mlp[0].stack))
    focal_pieces = [pieces_of(focal[0], far, first_layout, own), None]
    mlp_pieces = [None, None]

    field_shape = (groups, IMAGE_ROWS, lanes)
    field = (field_shape, F32, FETCH)
    padded = pltpu.VMEM((GRID, GRID + 16, lanes), F32)
    gates_out = dict(gates=((IMAGE_ROWS, 4 * LANES), F32, FETCH))
    focal_out = dict(k1=field, k2=field, k3=field, s1=field, s2=field, s3=field)
    focal_out.update(pool=((groups, 8, lanes), F32, FETCH))
    mixed_out = dict(mod=(whole, F32, FETCH), middle=(whole, F32, HOLD))
    query_out = dict(query_out=(whole, F32, FETCH))
    low_out = dict(low=(whole, BF16, FETCH))
    mlp_out = dict(
        hidden=((rows, hidden_width), BF16, FETCH), slope=((rows, hidden_width), F32, FETCH)
    )
    weights_in = dict(key=0, query=0, mix=0, proj=0)
    up_down = dict(up=0, down=0)
    taps_shape = (BLOCKS, groups, room_rows, lanes)

    def focal_apart(b, x, taps):
        pieces = focal_pieces[b]
        made = run_kernel(
            [inputs_stage(b, 1, width)],
            dict(x=hold(x), **basic),
            dict(
                gates=((rows, 4 * LANES), F32, FETCH),
                context=((1, rows, width), F32, FETCH),
                **query_out,
            ),
            {},
            [(pieces, dict(key=0, query=0))],
        )
        made.update(gates=shares.all_rows(made.gates), context=shares.to_images(made.context))
        made.update(
            run_kernel(
                [focal_stage(b, groups, lanes)],
                dict(
                    context=fetch(made.context),
                    gates=fetch(made.gates),
                    taps=fetch(taps),
                    **grid_columns,
                ),
                dict(low=((IMAGE_ROWS, channels), BF16, FETCH), **focal_out),
                dict(padded=padded),
            )
        )
        made.update(low=shares.to_rows(made.low))
        made.update(
            run_kernel(
                [mix_stage(b)],
                dict(
                    x=hold(x), low=fetch(made.low), query_out=fetch(made.query_out), **basic
                ),
                mixed_out,
                {},
                [(pieces, dict(mix=0, proj=0))],
            )
        )
        return made

    def focal_stages(b):
        return [inputs_stage(b, groups, lanes), focal_stage(b, groups, lanes), mix_stage(b)]

    focal_made_out = dict(
        context=field, **gates_out, **query_out, **focal_out, **low_out, **mixed_out
    )

    def first_focal(x):
        if shared:
            taps = run_kernel(
                [taps_stage(tap_count, 1, width)],
                {},
                dict(taps=((BLOCKS, 1, room_rows, width), F32, FETCH)),
                {},
                [(focal_pieces[0], dict(wide=0, thin=0))],
            ).taps
            taps = shares.channels(taps)
            return Box(focal_apart(0, x, taps), taps=taps)
        return run_kernel(
            [taps_stage(tap_count, groups, lanes)] + focal_stages(0),
            dict(x=hold(x), **basic, **grid_columns),
            dict(taps=(taps_shape, F32, FETCH), **focal_made_out),
            dict(padded=padded),
            [(focal_pieces[0], dict(wide=0, thin=0, **weights_in))],
        )

    moves = [(mlp[0].stack, *y_move)]
    moves += [(focal[1].stack, "z", step) for step in z_rest[:1]]
    moves += [(mlp[1].stack, "z", z_first)]
    x_first, *x_rest = links.bits("x")
    saved = [Box(x=x), Box()]
    made, got = beside(first_focal, x, moves)
    saved[0].update(made)
    taps = made.taps
    mlp[0].take(got[0], *y_move, True)
    take_z(focal[1], got[1:-1])
    mlp[1].take(got[-1], "z", z_first)
    y_move = focal[1].early("y")
    moves = [(focal[1].stack, *y_move)]
    moves += [(mlp[1].stack, "z", step) for step in z_rest]
    crossed, crossed_masks = [], []
    if cut_rows:
        cut_stack = jnp.concatenate([part[:, plain_rows:] for part in mlp[0].parts])
        cut_gather = Gather(links, cut_stack[0])
        cut_gather.stack, cut_gather.masks = cut_stack, mlp[0].masks
        x_move = cut_gather.early("x")
        moves += [(cut_gather.stack, *x_move)]
    group_count = after(group_count, saved[0].middle)
    moves.insert(0, (group_count, "core", 1))
    middle, got = together(saved[0].middle, moves)
    group_count = group_count + got.pop(0)
    focal[1].take(got[0], *y_move, True)
    take_z(mlp[1], got[1 : 1 + len(z_rest)])
    if cut_rows:
        held = cut_stack.shape[0]
        cut_gather.take(got[-1], *x_move, True)
        crossed = [cut_gather.parts[0][held:], cut_gather.parts[1]]
        crossed = [part for part in crossed if part.shape[0]]
        crossed_masks = cut_gather.masks[held:]
    y_move = mlp[1].early("y")
    arrays = mlp[0].parts + crossed
    moves = [(part, "core", 1) for part in arrays + focal[1].parts]
    middle, got = together(after(middle, mlp[1].stack), moves)
    far, far_focal = got[: len(arrays)], got[len(arrays) :]
    if cut_rows:
        mlp_pieces[0] = cut_pieces(mlp[0], crossed, crossed_masks, far)
    else:
        mlp_pieces[0] = pieces_of(mlp[0], far, mlp_layout, own_hidden)
    focal_pieces[1] = pieces_of(focal[1], far_focal, focal_layout, own)

    def second_focal(middle):
        inputs = dict(middle=hold(middle), **basic)
        outputs = dict(out=(whole, F32, FETCH), **mlp_out)
        if shared:
            made = run_kernel(
                [mlp_stage(0)], inputs, outputs, {}, [(mlp_pieces[0], up_down)]
            )
            lower = Box(hidden=made.hidden, slope=made.slope)
            return Box(focal_apart(1, made.out, taps), x=made.out, lower=dict(lower))
        made = run_kernel(
            [renamed(mlp_stage(0), middle=0, out=1)]
            + [renamed(stage, x=1) for stage in focal_stages(1)],
            {0: hold(middle), **basic, **grid_columns, **dict(taps=fetch(taps))},
            {1: (whole, F32, FETCH), **mlp_out, **focal_made_out},
            dict(padded=padded),
            [(mlp_pieces[0], up_down), (focal_pieces[1], weights_in)],
        )
        lower = dict(hidden=made.hidden, slope=made.slope)
        upper = Box({key: made[key] for key in focal_made_out})
        upper.update(x=made[1], lower=lower)
        return upper

    moves = [(mlp[1].stack, *y_move), (group_count, "x", x_first)]
    made, got = beside(second_focal, middle, moves)
    mlp[1].take(got[0], *y_move, True)
    counts_twin = got[1]
    for step in x_rest:
        group_count = group_count + counts_twin
        counts_twin = links.swap(group_count, "x", step)
    saved[0].update(made.lower)
    saved[1].update(made)
    middle, far = twins(mlp[1], saved[1].middle)
    mlp_pieces[1] = pieces_of(mlp[1], far, mlp_layout, own_hidden)

    sums_out = ((8, width), F32, FETCH)
    embed_rows = patch_in // (2 * links.chan)
    small_rows = small_rows_for(tap_count, links.chan)
    small_part = small_rows // (2 * links.chan)
    hidden_shape = (rows, hidden_width)
    mix_at = own_hidden
    upper_lead = own_hidden + own
    head_at = upper_lead + own
    lower_lead = own_hidden + own
    upper_count = head_at + embed_rows
    lower_count = lower_lead + own + embed_rows + small_part
    d_shape = (1, rows, width) if shared else field_shape
    levels_names = dict(context=0, gates=0, k1=0, k2=0, k3=0, s1=0, s2=0, s3=0, pool=0)
    mix_names = dict(query_out=0, mod=0, low=0)
    levels_temps = dict(padded=padded, d_padded=padded)
    between = dict(
        d_context=pltpu.VMEM(whole, BF16),
        d_gates=pltpu.VMEM((rows, 4 * LANES), F32),
        **levels_temps,
    )
    tap_shape = (room_rows, width)

    def pair_of(count):
        shape = (links.chan, count, width)
        return dict(kept=(shape, BF16, HOLD), sent=(shape, BF16, HOLD))

    def levels_in(b):
        return dict(taps=fetch(taps), **fetch_all(saved[b], levels_names), **grid_columns)

    head_names = dict(x=0, d_out=1, sums=5)
    head_first = upper_lead if shared else head_at
    first_stages = [
        renamed(mlp_stage(1), out=0),
        renamed(head_stage(head_first), **head_names),
        renamed(mlp_back_stage(1, 0), d_in=1, d_out=2, sums=3),
        renamed(mix_back_stage(1, d_shape[0], d_shape[2], mix_at), d_in=2, sums=4),
    ]
    first_in = dict(
        middle=hold(middle),
        head=fetch(head_weight),
        patches=fetch(patches),
        counts=hold(group_count),
        counts_twin=hold(counts_twin),
        **basic,
        **fetch_all(saved[1], mix_names),
    )
    first_temps = {
        0: pltpu.VMEM(whole, F32),
        1: pltpu.VMEM(whole, F32),
        **dict(hidden=pltpu.VMEM(hidden_shape, BF16), slope=pltpu.VMEM(hidden_shape, F32)),
    }
    sums_outs = {3: sums_out, 4: sums_out, 5: sums_out}
    mlp_weights_in = (mlp_pieces[1], up_down)
    mixer_in = dict(proj=0, mix=0)
    inputs_in = dict(query=0, key=0)

    def levels_apart(b, d_sum):
        made = run_kernel(
            [focal_back_stage(b, groups, lanes)],
            dict(d_sum=fetch(shares.to_images(d_sum)), **levels_in(b)),
            dict(
                d_context=((IMAGE_ROWS, channels), BF16, FETCH),
                d_gates=((IMAGE_ROWS, 4 * LANES), F32, FETCH),
                d_taps=((room_rows, channels), F32, FETCH),
            ),
            levels_temps,
        )
        return Box(
            d_context=shares.to_rows(made.d_context),
            d_gates=shares.sum_rows(made.d_gates),
            d_taps=shares.spread(made.d_taps),
        )

    def joined(first, second):
        return Box(
            kept=jnp.concatenate([first.kept, second.kept], axis=1),
            sent=jnp.concatenate([first.sent, second.sent], axis=1),
        )

    if shared:
        first = run_kernel(
            first_stages,
            first_in,
            {
                2: (whole, F32, HOLD),
                **sums_outs,
                **dict(d_query=(whole, BF16, HOLD), d_sum=(d_shape, F32, HOLD)),
                **pair_of(upper_lead + embed_rows),
            },
            first_temps,
            [mlp_weights_in, (focal_pieces[1], mixer_in)],
        )
        levels = levels_apart(1, first.d_sum)
        second = run_kernel(
            [inputs_back_stage(1, 0)],
            dict(
                d_in=hold(first[2]),
                d_query=hold(first.d_query),
                d_context=fetch(levels.d_context),
                d_gates=fetch(levels.d_gates),
                x=fetch(saved[1].x),
                **basic,
            ),
            dict(d_out=(whole, F32, HOLD), input_sums=sums_out, **pair_of(own)),
            {},
            [(focal_pieces[1], inputs_in)],
        )
        pair = joined(first, second)
        pair = Box(
            (key, jnp.concatenate([array[:, :upper_lead], array[:, -own:], array[:, upper_lead:-own]], 1))
            for key, array in pair.items()
        )
        d_x, d_taps = second.d_out, levels.d_taps
        upper_sums = [second.input_sums, first[3], first[4], first[5]]
    else:
        first = run_kernel(
            first_stages
            + [
                focal_back_stage(1, groups, lanes),
                renamed(inputs_back_stage(1, upper_lead), d_in=2),
            ],
            dict(x=fetch(saved[1].x), **levels_in(1)) | first_in,
            {
                **sums_outs,
                **dict(
                    d_out=(whole, F32, HOLD),
                    input_sums=sums_out,
                    d_taps=(tap_shape, F32, FETCH),
                ),
                **pair_of(upper_count),
            },
            {
                2: pltpu.VMEM(whole, F32),
                **first_temps,
                **dict(d_query=pltpu.VMEM(whole, BF16), d_sum=pltpu.VMEM(d_shape, F32)),
                **between,
            },
            [mlp_weights_in, (focal_pieces[1], mixer_in | inputs_in)],
        )
        pair = first
        d_x, d_taps = first.d_out, first.d_taps
        upper_sums = [first.input_sums, first[3], first[4], first[5]]

    lower_stages = [
        renamed(mlp_back_stage(0, 0), d_out=2, sums=3),
        renamed(mix_back_stage(0, d_shape[0], d_shape[2], mix_at), d_in=2, sums=4),
    ]
    lower_names = dict(hidden=0, slope=0, middle=0)
    sum_keys = [10, 3, 4, 11, 12, 13, 14]
    last_in = {
        **dict(zip(sum_keys[3:], (fetch(array) for array in upper_sums))),
        15: fetch(d_taps),
        **dict(patches=fetch(patches), embedded=fetch(embedded.embedded), x=fetch(saved[0].x)),
    }

    def last_stages(at):
        return [
            renamed(inputs_back_stage(0, at), d_in=2, d_out=1, input_sums=10),
            renamed(
                embed_back_stage(tap_count, sum_keys, [None, 15], at + own), d_out=1
            ),
        ]

    last_temps = {
        1: pltpu.VMEM(whole, F32),
        10: pltpu.VMEM((8, width), F32),
        **dict(small=pltpu.VMEM((small_rows, width), F32)),
    }

    def lower_back(d_x):
        inputs = dict(
            d_in=hold(d_x),
            **fetch_all(saved[0], lower_names),
            **basic,
            **fetch_all(saved[0], mix_names),
        )
        weights = [(mlp_pieces[0], dict(down=0, up=0)), (focal_pieces[0], mixer_in)]
        if shared:
            first = run_kernel(
                lower_stages,
                inputs,
                {
                    2: (whole, F32, HOLD),
                    3: sums_out,
                    4: sums_out,
                    **dict(d_query=(whole, BF16, HOLD), d_sum=(d_shape, F32, HOLD)),
                    **pair_of(lower_lead),
                },
                {},
                weights,
            )
            levels = levels_apart(0, first.d_sum)
            second = run_kernel(
                last_stages(0),
                {
                    2: hold(first[2]),
                    3: fetch(first[3]),
                    4: fetch(first[4]),
                    **last_in,
                    **dict(
                        d_query=hold(first.d_query),
                        d_context=fetch(levels.d_context),
                        d_gates=fetch(levels.d_gates),
                        d_taps=fetch(levels.d_taps),
                        **basic,
                    ),
                },
                pair_of(lower_count - lower_lead),
                last_temps,
                [(focal_pieces[0], inputs_in)],
            )
            return joined(first, second)
        return run_kernel(
            lower_stages + [focal_back_stage(0, groups, lanes)] + last_stages(lower_lead),
            {**inputs, **levels_in(0), **last_in},
            pair_of(lower_count),
            {
                2: pltpu.VMEM(whole, F32),
                3: pltpu.VMEM((8, width), F32),
                4: pltpu.VMEM((8, width), F32),
                **last_temps,
                **dict(d_query=pltpu.VMEM(whole, BF16), d_sum=pltpu.VMEM(d_shape, F32)),
                **dict(d_taps=pltpu.VMEM(tap_shape, F32)),
                **between,
            },
            [weights[0], (focal_pieces[0], mixer_in | inputs_in)],
        )

    (d_x, upper_kept), got = together((d_x, pair.kept), [(pair.sent, "core", 1)])
    upper = Reduction(links, upper_kept, got[0], 1)
    moves, take = next_round(links, [upper])
    made, got = beside(lower_back, d_x, moves)
    take(got)
    moves, take = next_round(links, [upper])
    lower_kept, got = together(made.kept, moves + [(made.sent, "core", 1)])
    take(got[:-1])
    lower = Reduction(links, lower_kept, got[-1], 2)
    rate = 0.2 * math.sqrt(group_rows * lax.axis_size("dp"))
    gate = here
    turn = [lower]
    while not (lower.ready() and upper.done()):
        moves, take = next_round(links, turn)
        gate, got = together(gate, moves)
        take(got)
        turn = [lower, upper]
    common = Gather(
        links,
        jnp.concatenate(
            [
                upper.tail(embed_rows).astype(BF16),
                lower.tail(embed_rows + small_part).astype(BF16),
            ]
        ),
    )
    more, takes = lower.last_moves()
    gate, got = together(gate, [(common.stack, "z", z_first)] + more)
    common.take(got[0], "z", z_first)
    for one, part in zip(takes, got[1:]):
        one(part)
    for step in z_rest:
        common.take(links.swap(common.stack, "z", step), "z", step)
    while not lower.done():
        more, takes = lower.last_moves()
        takes[0](links.swap(*more[0]))
    upper_rows, lower_rows = upper.result(), lower.result()
    y_move = common.early("y")
    common.take(links.swap(common.stack, *y_move), *y_move, True)
    rows_early = jnp.concatenate(
        [
            upper_rows[:own_hidden],
            lower_rows[:own_hidden],
            upper_rows[mix_at : mix_at + own],
            upper_rows[upper_lead:head_at],
            lower_rows[mix_at : lower_lead + own],
        ]
    )
    rows_early, _stack = lax.optimization_barrier((rows_early, common.stack))
    halves = links.both_halves(rows_early)
    ends = (own_hidden, 2 * own_hidden)
    grad_mlp = jnp.stack(
        [
            jnp.stack([part[ends[0] : ends[1]] for part in halves]),
            jnp.stack([part[: ends[0]] for part in halves]),
        ]
    )
    places = [ends[1] + k * own for k in range(5)]
    mix_one, inputs_one, mix_zero, inputs_zero = (
        [part[first:end] for part in halves] for first, end in zip(places, places[1:])
    )
    grad_focal = jnp.stack([jnp.stack(inputs_zero), jnp.stack(inputs_one)])
    grad_mixer = jnp.stack([jnp.stack(mix_zero), jnp.stack(mix_one)])
    results = []
    for weight, moment, average, gradient, order, back in (
        (focal_input, focal_moment, focal_average, grad_focal, (0, 2, 3, 1), (0, 3, 1, 2)),
        (mixers, mixer_moment, mixer_average, grad_mixer, (0, 1, 3, 2), (0, 1, 3, 2)),
        (mlp_weights, mlp_moment, mlp_average, grad_mlp, (0, 1, 3, 2), (0, 1, 3, 2)),
    ):
        weight, moment, average = (
            jnp.transpose(array, order) for array in (weight, moment, average)
        )
        new_weight, new_moment = nesterov(weight, moment, gradient, rate)
        new_average = AVERAGE * average + (1.0 - AVERAGE) * new_weight
        results.extend(
            jnp.transpose(array, back) for array in (new_weight, new_moment, new_average)
        )
    there, results = lax.optimization_barrier((common.parts[1], results))
    common_near = [common.parts[0], there]
    common_far = [links.swap_core(part) for part in common_near]
    common_where = links.where([place for place, _x in links.places(common.masks)])
    head_out = (head_weight.shape, F32, FETCH)
    embed_out = (embed_weight.shape, F32, FETCH)
    vector_out = (vectors.shape, F32, HOLD)
    kernel_out = (kernel_rows.shape, F32, HOLD)
    made = run_kernel(
        [update_shared_stage(tap_count, own, embed_rows, rate)],
        dict(
            where=(common_where, SCALAR),
            near0=hold(common_near[0]),
            near1=hold(common_near[1]),
            far0=hold(common_far[0]),
            far1=hold(common_far[1]),
            head=fetch(head_weight),
            head_moment=fetch(head_moment),
            embed=fetch(embed_weight),
            embed_moment=fetch(embed_moment),
            vectors=fetch(vectors),
            vector_moment=fetch(vector_moment),
            vector_average=fetch(vector_average),
            kernels=fetch(kernel_rows),
            kernel_moment=fetch(jnp.transpose(kernel_moment, (0, 2, 1))),
            kernel_average=fetch(jnp.transpose(kernel_average, (0, 2, 1))),
        ),
        dict(
            new_head=head_out,
            new_head_moment=head_out,
            new_embed=embed_out,
            new_embed_moment=embed_out,
            new_vectors=vector_out,
            new_vector_moment=vector_out,
            new_vector_average=vector_out,
            new_kernels=kernel_out,
            new_kernel_moment=kernel_out,
            new_kernel_average=kernel_out,
            loss=((1, LANES), F32, HOLD),
        ),
        dict(
            packed=pltpu.VMEM((-(-vectors.shape[0] // 8) * 8, width), F32),
            small=pltpu.VMEM((small_rows, width), F32),
        ),
        limit=SMALL_LIMIT,
    )
    return (
        made.loss[0, 0],
        made.new_embed,
        made.new_embed_moment,
        made.new_head,
        made.new_head_moment,
        made.new_vectors,
        made.new_vector_moment,
        made.new_vector_average,
        *results,
        *[
            jnp.transpose(array, (0, 2, 1))
            for array in (made.new_kernels, made.new_kernel_moment, made.new_kernel_average)
        ],
    )


def solution(mesh):
    split = P(None, None, None, "chan")
    taps = P(None, None, "chan")
    return jax.shard_map(
        shards,
        mesh=mesh,
        in_specs=(P(("dp", "chan"), None), P("dp"), P("dp"), P("dp", None, None))
        + (P(),) * 7
        + (split,) * 9
        + (taps,) * 3,
        out_specs=(P(),) * 8 + (split,) * 9 + (taps,) * 3,
        check_vma=False,
    )
```
